32 devices in a mesh: wide: 8 (over z, y), narrow: 4 (over x, core).
Axes of the slice: x: 2, y: 2, z: 4, core: 2. Of those that a mesh axis runs over, the one named last changes fastest.
Arguments:
- tokens: bfloat16 [16384, 768], P(('wide', 'narrow')), may hold values from -6 to 6
- band_mask: int32 [32, 8], P(('wide', 'narrow')), may hold values from 0 to 1, as said below
- out_grad: bfloat16 [16384, 768], P(('wide', 'narrow')), may hold values from -6 to 6
- norm1_gain: float32 [768], P(('wide', 'narrow')), may hold values from 0.1 to 1.9
- norm1_shift: float32 [768], P(('wide', 'narrow')), may hold values from -3 to 3
- qkv_weight: float32 [768, 2304], P(('wide', 'narrow')), may hold values from -0.21875 to 0.21875
- qv_bias: float32 [1536], P(('wide', 'narrow')), may hold values from -3 to 3
- out_weight: float32 [768, 768], P(('wide', 'narrow')), may hold values from -4 to 4
- out_bias: float32 [768], P(('wide', 'narrow')), may hold values from -3 to 3
- norm2_gain: float32 [768], P(('wide', 'narrow')), may hold values from 0.1 to 1.9
- norm2_shift: float32 [768], P(('wide', 'narrow')), may hold values from -3 to 3
- up_weight: float32 [768, 3072], P(('wide', 'narrow')), may hold values from -0.21875 to 0.21875
- up_bias: float32 [3072], P(('wide', 'narrow')), may hold values from -3 to 3
- down_weight: float32 [3072, 768], P(('wide', 'narrow')), may hold values from -0.109375 to 0.109375
- down_bias: float32 [768], P(('wide', 'narrow')), may hold values from -3 to 3
Outputs:
- output: bfloat16 [16384, 768], P(('wide', 'narrow'))
- input_grad: bfloat16 [16384, 768], P(('wide', 'narrow'))
- norm1_gain_grad: float32 [768], P(('wide', 'narrow'))
- norm1_shift_grad: float32 [768], P(('wide', 'narrow'))
- qkv_weight_grad: float32 [768, 2304], P(('wide', 'narrow'))
- qv_bias_grad: float32 [1536], P(('wide', 'narrow'))
- out_weight_grad: float32 [768, 768], P(('wide', 'narrow'))
- out_bias_grad: float32 [768], P(('wide', 'narrow'))
- norm2_gain_grad: float32 [768], P(('wide', 'narrow'))
- norm2_shift_grad: float32 [768], P(('wide', 'narrow'))
- up_weight_grad: float32 [768, 3072], P(('wide', 'narrow'))
- up_bias_grad: float32 [3072], P(('wide', 'narrow'))
- down_weight_grad: float32 [3072, 768], P(('wide', 'narrow'))
- down_bias_grad: float32 [768], P(('wide', 'narrow'))
The draws below stay inside these ranges and needn't reach their ends.
Inputs may be any that keep to these rules, and one draw needn't show every extreme that they name: `band_mask`: each cube keeps at least 6 of its 8 spectral groups, and some cube keeps exactly that many.
All inputs are finite; a program needn't handle non-finite values.
Results may differ from the reference program's by a relative error of at most 0.012.
The reference program's roundings to bfloat16 on the way count: a program that leaves them out, or rounds other values in their place, can miss the bound.
Values may be sent and summed in bfloat16 or wider, within the bound.
A program may use at most 192 MiB of HBM per device.

```python
import math
import jax
import jax.numpy as jnp
from jax import lax

D = 768
HEADS = 12
HEAD = 64
FF = 3072
G = 8
S = 64
CUBES = 32
TOKENS = 16384


def draw_band_mask(key, part):
    row_keys = jax.random.split(jax.random.fold_in(key, 17), CUBES)

    def one_row(row_key):
        count_key, order_key = jax.random.split(row_key)
        dropped = jax.random.randint(count_key, (), 0, G // 4 + 1)
        ranking = jax.random.permutation(order_key, G)
        return (ranking >= dropped).astype(jnp.int32)
    return jax.vmap(one_row)(row_keys)


def strengthened(drawn, rng, source, target, blocks, factor):
    owner, partner = [(jnp.arange(drawn.shape[position]) // (drawn.shape[position] // blocks)).reshape([-1 if axis == position else 1 for axis in range(drawn.ndim)]) for position in (source, target)]
    chosen = jax.random.permutation(rng, blocks)[partner]
    strong = (owner == chosen) | (owner == (partner + blocks // 2) % blocks)
    return jnp.where(strong, factor * drawn, drawn)


def levels(own_key, shape, cuts, smallest, high):
    def one(dim, blocks):
        heights = jax.random.uniform(jax.random.fold_in(jax.random.fold_in(own_key, 6), dim), (blocks,), jnp.float32, smallest / len(cuts), high / len(cuts))
        return jnp.repeat(jnp.exp(heights), shape[dim] // blocks).reshape((-1,) + (1,) * (len(shape) - dim - 1))

    level = one(*cuts[0])
    for cut in cuts[1:]:
        level = level * one(*cut)
    return level


def scatter_about(rng, shape, scale, limit, shards=(), held_as=jnp.bfloat16):
    factor_of = levels(rng, shape, shards, -0.22, 0.18) if shards else 1.0
    entries = jax.random.normal(rng, shape, jnp.float32) * scale * factor_of
    return jnp.minimum(jnp.maximum(entries, -limit), limit).astype(held_as)


def bell_draw_with(stream_key, shape, spread, most, shards, heavy, held_as=jnp.bfloat16):
    drawn = spread * jax.random.normal(stream_key, shape, jnp.float32)
    if shards:
        drawn = drawn * levels(stream_key, shape, shards, -0.22, 0.18)
    return jnp.clip(strengthened(drawn, jax.random.fold_in(stream_key, 3), *heavy), -most, most).astype(held_as)


def setup_inputs(seed: int = 0) -> dict:
    key_list = jax.random.split(jax.random.key(seed), 16)
    return {
        "tokens": bell_draw_with(key_list[0], (TOKENS, D), 1.0, 6.0, ((0, 32),), (0, 1, 32, 2.75)),
        "band_mask": draw_band_mask(jax.random.fold_in(key_list[15], 71), 0),
        "out_grad": bell_draw_with(key_list[2], (TOKENS, D), 1.0, 6.0, ((0, 32),), (0, 1, 32, 2.75)),
        "norm1_gain": jnp.clip(1.0 + 0.18 * jax.random.normal(key_list[3], (D,), jnp.float32), 0.1, 1.9),
        "norm1_shift": scatter_about(key_list[4], (D,), 0.5, 3.0, ((0, 32),), jnp.float32),
        "qkv_weight": scatter_about(key_list[5], (D, 3 * D), D ** -0.5, 0.21875, ((0, 32),), jnp.float32),
        "qv_bias": scatter_about(key_list[6], (2 * D,), 0.5, 3.0, ((0, 32),), jnp.float32),
        "out_weight": scatter_about(key_list[7], (D, D), 2 ** -0.5, 4.0, ((0, 32),), jnp.float32),
        "out_bias": scatter_about(key_list[8], (D,), 0.5, 3.0, ((0, 32),), jnp.float32),
        "norm2_gain": jnp.clip(1.0 + 0.18 * jax.random.normal(key_list[9], (D,), jnp.float32), 0.1, 1.9),
        "norm2_shift": scatter_about(key_list[10], (D,), 0.5, 3.0, ((0, 32),), jnp.float32),
        "up_weight": scatter_about(key_list[11], (D, FF), D ** -0.5, 0.21875, ((0, 32),), jnp.float32),
        "up_bias": scatter_about(key_list[12], (FF,), 0.5, 3.0, ((0, 32),), jnp.float32),
        "down_weight": scatter_about(key_list[13], (FF, D), FF ** -0.5, 0.109375, ((0, 32),), jnp.float32),
        "down_bias": scatter_about(key_list[14], (D,), 0.5, 3.0, ((0, 32),), jnp.float32),
    }


FULL_PRECISION = lax.Precision.HIGHEST

@jax.custom_vjp
def low(v):
    return lax.optimization_barrier(v.astype(jnp.bfloat16)).astype(jnp.float32)

@jax.custom_vjp
def low_back(v):
    return v

def low_keep(v):
    return (low(v), None)

def low_pass(kept, grad):
    return (grad,)

def back_keep(v):
    return (v, None)

def back_low(kept, grad):
    return (low(grad),)
low.defvjp(low_keep, low_pass)
low_back.defvjp(back_keep, back_low)

def layer_norm(values, gain, shift):
    centre = lax.optimization_barrier(jnp.mean(values, axis=1, keepdims=True))
    centred = values - centre
    factor = lax.rsqrt(lax.optimization_barrier(jnp.mean(centred * centred, axis=1, keepdims=True)) + 1e-05)
    return centred * factor * gain + shift

def forward(inputs, params, present):
    gain_one, shift_one, w_qkv, b_qv, w_out, b_out, gain_two, shift_two, w_up, b_up, w_down, b_down = tuple((low(item) for item in params))
    width = inputs.shape[1]
    normed_one = low(layer_norm(inputs, gain_one, shift_one))
    bias_full = jnp.concatenate([b_qv[:width], jnp.zeros((width,), b_qv.dtype), b_qv[width:]])
    joined = jnp.dot(normed_one, w_qkv, precision=FULL_PRECISION) + bias_full
    queries = low_back(low(joined[:, :width])).reshape(-1, HEADS, HEAD)
    key_rows = low_back(low(joined[:, width:2 * width])).reshape(-1, HEADS, HEAD)
    value_rows = low_back(low(joined[:, 2 * width:])).reshape(-1, HEADS, HEAD)
    scores = jnp.einsum('qhd,khd->hqk', queries, key_rows, precision=FULL_PRECISION) * (1.0 / math.sqrt(HEAD))
    scores = low_back(scores)
    scores = jnp.where(present[None, None, :] > 0.5, scores, -jnp.inf)
    largest = lax.optimization_barrier(jnp.max(scores, axis=2, keepdims=True))
    expo = jnp.exp(scores - largest)
    probs = low(expo / lax.optimization_barrier(jnp.sum(expo, axis=2, keepdims=True)))
    mixture = jnp.einsum('hqk,khd->qhd', probs, value_rows, precision=FULL_PRECISION).reshape(-1, width)
    mixture = low_back(low(mixture))
    attention = low_back(jnp.dot(mixture, w_out, precision=FULL_PRECISION) + b_out)
    middle = inputs + present[:, None] * attention
    normed_two = low(layer_norm(middle, gain_two, shift_two))
    hidden = low_back(jnp.dot(normed_two, w_up, precision=FULL_PRECISION) + b_up)
    active = low(jax.nn.gelu(hidden, approximate=False))
    branch = low_back(jnp.dot(active, w_down, precision=FULL_PRECISION) + b_down)
    return middle + present[:, None] * branch

def reference(tokens, band_mask, out_grad, norm1_gain, norm1_shift, qkv_weight, qv_bias, out_weight, out_bias, norm2_gain, norm2_shift, up_weight, up_bias, down_weight, down_bias):
    params = (norm1_gain, norm1_shift, qkv_weight, qv_bias, out_weight, out_bias, norm2_gain, norm2_shift, up_weight, up_bias, down_weight, down_bias)
    cube_inputs = tokens.reshape(CUBES, G * S, D)
    cube_upstream = out_grad.reshape(CUBES, G * S, D)

    def one_cube(totals, items):
        inputs, upstream, groups_live = items
        present = jnp.repeat(groups_live.astype(jnp.float32), S)
        result, pullback = jax.vjp(lambda values, weights: forward(values, weights, present), inputs.astype(jnp.float32), params)
        input_grad, param_grads = pullback(upstream.astype(jnp.float32))
        totals = tuple((left + right for left, right in zip(totals, param_grads)))
        return (totals, (result.astype(jnp.bfloat16), input_grad.astype(jnp.bfloat16)))
    start = tuple((jnp.zeros_like(item) for item in params))
    grads, (results, input_grads) = lax.scan(one_cube, start, (cube_inputs, cube_upstream, band_mask))
    return (results.reshape(TOKENS, D), input_grads.reshape(TOKENS, D), grads[0], grads[1], grads[2], grads[3], grads[4], grads[5], grads[6], grads[7], grads[8], grads[9], grads[10], grads[11])
```

```python
import functools
import math

import jax
import jax.numpy as jnp
from jax import lax
from jax.experimental import pallas as pl
from jax.experimental.pallas import tpu as pltpu
from jax.sharding import PartitionSpec as P

HEAD = 64
HEAD_GROUP = 4
QBLOCK = 512


NORM_EPSILON = 1e-05


def normalize(values, gain, shift):
    centre = jnp.mean(values, axis=1, keepdims=True)
    centred = values - centre
    factor = lax.rsqrt(jnp.mean(centred * centred, axis=1, keepdims=True) + NORM_EPSILON)
    normed = centred * factor
    return (normed * gain + shift, normed, factor)


def normalize_back(upstream, normed, factor, gain):
    gain_grad = jnp.sum(upstream * normed, axis=0)
    shift_grad = jnp.sum(upstream, axis=0)
    scaled = upstream * gain
    inner = (
        scaled
        - jnp.mean(scaled, axis=1, keepdims=True)
        - normed * jnp.mean(scaled * normed, axis=1, keepdims=True)
    )
    return (factor * inner, gain_grad, shift_grad)


def gelu_slope(values):
    cumulative = 0.5 * (1.0 + lax.erf(values * (1.0 / math.sqrt(2.0))))
    return cumulative + values * jnp.exp(-0.5 * values * values) * (1.0 / math.sqrt(2.0 * math.pi))


def to_groups(matrix, count):
    return matrix.reshape(matrix.shape[0], count, -1).transpose(1, 0, 2)


def from_groups(stacked):
    return stacked.transpose(1, 0, 2).reshape(stacked.shape[1], -1)


def attend_forward(query_cols, key_cols, value_cols, key_live):
    row_count, span_cols = key_cols.shape
    head_width = span_cols // HEAD_GROUP
    scaling = 1.0 / math.sqrt(head_width)
    key_rows = key_cols.reshape(row_count, HEAD_GROUP, head_width)
    value_rows = value_cols.reshape(row_count, HEAD_GROUP, head_width)
    query_blocks = query_cols.reshape(row_count // QBLOCK, QBLOCK, HEAD_GROUP, head_width)

    def one_block(query_rows):
        scores = (
            jnp.einsum("qhd,khd->hqk", query_rows, key_rows, preferred_element_type=jnp.float32)
            * scaling
        )
        scores = jnp.where(key_live[None, None, :], scores, -jnp.inf)
        largest = jnp.max(scores, axis=2, keepdims=True)
        expo = jnp.exp(scores - largest)
        totals = jnp.sum(expo, axis=2, keepdims=True)
        weights_low = (expo / totals).astype(jnp.bfloat16)
        mixture = jnp.einsum(
            "hqk,khd->qhd", weights_low, value_rows, preferred_element_type=jnp.float32
        )
        return (mixture.reshape(QBLOCK, span_cols), largest[:, :, 0] + jnp.log(totals[:, :, 0]))

    mixture, logsum = lax.map(one_block, query_blocks)
    return (mixture.reshape(row_count, span_cols), logsum)


def attend_backward(query_cols, key_cols, value_cols, grad_cols, logsum, key_live):
    row_count, span_cols = key_cols.shape
    head_width = span_cols // HEAD_GROUP
    scaling = 1.0 / math.sqrt(head_width)
    key_rows = key_cols.reshape(row_count, HEAD_GROUP, head_width)
    value_rows = value_cols.reshape(row_count, HEAD_GROUP, head_width)
    query_blocks = query_cols.reshape(row_count // QBLOCK, QBLOCK, HEAD_GROUP, head_width)
    grad_blocks = grad_cols.reshape(row_count // QBLOCK, QBLOCK, HEAD_GROUP, head_width)

    def one_block(carry, items):
        key_acc, value_acc = carry
        query_rows, grad_rows, block_logsum = items
        scores = (
            jnp.einsum("qhd,khd->hqk", query_rows, key_rows, preferred_element_type=jnp.float32)
            * scaling
        )
        scores = jnp.where(key_live[None, None, :], scores, -jnp.inf)
        probs = jnp.exp(scores - block_logsum[:, :, None])
        value_acc = value_acc + jnp.einsum(
            "hqk,qhd->khd",
            probs.astype(jnp.bfloat16),
            grad_rows,
            preferred_element_type=jnp.float32,
        )
        prob_grad = jnp.einsum(
            "qhd,khd->hqk", grad_rows, value_rows, preferred_element_type=jnp.float32
        )
        inner = jnp.sum(probs * prob_grad, axis=2, keepdims=True)
        score_grad = (probs * (prob_grad - inner)).astype(jnp.bfloat16)
        query_grad = (
            jnp.einsum("hqk,khd->qhd", score_grad, key_rows, preferred_element_type=jnp.float32)
            * scaling
        )
        key_acc = (
            key_acc
            + jnp.einsum("hqk,qhd->khd", score_grad, query_rows, preferred_element_type=jnp.float32)
            * scaling
        )
        return ((key_acc, value_acc), query_grad.reshape(QBLOCK, span_cols))

    empty = jnp.zeros((row_count, HEAD_GROUP, head_width), jnp.float32)
    (key_grad, value_grad), query_grad = lax.scan(
        one_block, (empty, empty), (query_blocks, grad_blocks, logsum)
    )
    return (
        query_grad.reshape(row_count, span_cols),
        key_grad.reshape(row_count, span_cols),
        value_grad.reshape(row_count, span_cols),
    )


def body_plain(
    tokens,
    band_mask,
    out_grad,
    norm1_gain,
    norm1_shift,
    qkv_weight,
    qv_bias,
    out_weight,
    out_bias,
    norm2_gain,
    norm2_shift,
    up_weight,
    up_bias,
    down_weight,
    down_bias,
):
    row_count, width = tokens.shape
    group_count = width // (HEAD_GROUP * HEAD)
    present = jnp.repeat(band_mask[0].astype(jnp.float32), row_count // band_mask.shape[1])
    key_live = present > 0.5
    column_mask = present[:, None]
    gain_one, shift_one, w_qkv, b_qv, w_out, b_out = (
        lax.all_gather(norm1_gain.astype(jnp.bfloat16), ("wide", "narrow"), axis=0, tiled=True),
        lax.all_gather(norm1_shift.astype(jnp.bfloat16), ("wide", "narrow"), axis=0, tiled=True),
        lax.all_gather(qkv_weight.astype(jnp.bfloat16), ("wide", "narrow"), axis=0, tiled=True),
        lax.all_gather(qv_bias.astype(jnp.bfloat16), ("wide", "narrow"), axis=0, tiled=True),
        lax.all_gather(out_weight.astype(jnp.bfloat16), ("wide", "narrow"), axis=0, tiled=True),
        lax.all_gather(out_bias.astype(jnp.bfloat16), ("wide", "narrow"), axis=0, tiled=True),
    )
    inputs = tokens.astype(jnp.float32)
    normed_one, unit_one, factor_one = normalize(
        inputs, gain_one.astype(jnp.float32), shift_one.astype(jnp.float32)
    )
    normed_one = normed_one.astype(jnp.bfloat16)
    bias_wide = b_qv.astype(jnp.float32)
    bias_full = jnp.concatenate(
        [bias_wide[:width], jnp.zeros((width,), jnp.float32), bias_wide[width:]]
    )
    joined = (jnp.dot(normed_one, w_qkv, preferred_element_type=jnp.float32) + bias_full).astype(
        jnp.bfloat16
    )
    query_groups = to_groups(joined[:, :width], group_count)
    key_groups = to_groups(joined[:, width : 2 * width], group_count)
    value_groups = to_groups(joined[:, 2 * width :], group_count)
    mixture, logsum = lax.map(
        lambda items: attend_forward(items[0], items[1], items[2], key_live),
        (query_groups, key_groups, value_groups),
    )
    mixture = from_groups(mixture).astype(jnp.bfloat16)
    attention = jnp.dot(mixture, w_out, preferred_element_type=jnp.float32) + b_out.astype(
        jnp.float32
    )
    middle = inputs + column_mask * attention
    gain_two, shift_two, w_up, b_up, w_down, b_down = (
        lax.all_gather(norm2_gain.astype(jnp.bfloat16), ("wide", "narrow"), axis=0, tiled=True),
        lax.all_gather(norm2_shift.astype(jnp.bfloat16), ("wide", "narrow"), axis=0, tiled=True),
        lax.all_gather(up_weight.astype(jnp.bfloat16), ("wide", "narrow"), axis=0, tiled=True),
        lax.all_gather(up_bias.astype(jnp.bfloat16), ("wide", "narrow"), axis=0, tiled=True),
        lax.all_gather(down_weight.astype(jnp.bfloat16), ("wide", "narrow"), axis=0, tiled=True),
        lax.all_gather(down_bias.astype(jnp.bfloat16), ("wide", "narrow"), axis=0, tiled=True),
    )
    normed_two, unit_two, factor_two = normalize(
        middle, gain_two.astype(jnp.float32), shift_two.astype(jnp.float32)
    )
    normed_two = normed_two.astype(jnp.bfloat16)
    hidden = jnp.dot(normed_two, w_up, preferred_element_type=jnp.float32) + b_up.astype(
        jnp.float32
    )
    active = jax.nn.gelu(hidden, approximate=False).astype(jnp.bfloat16)
    branch = jnp.dot(active, w_down, preferred_element_type=jnp.float32) + b_down.astype(
        jnp.float32
    )
    output = (middle + column_mask * branch).astype(jnp.bfloat16)
    back_gain_two, back_shift_two, back_up, back_up_bias, back_down, back_down_bias = (
        lax.all_gather(norm2_gain.astype(jnp.bfloat16), ("wide", "narrow"), axis=0, tiled=True),
        lax.all_gather(norm2_shift.astype(jnp.bfloat16), ("wide", "narrow"), axis=0, tiled=True),
        lax.all_gather(up_weight.astype(jnp.bfloat16), ("wide", "narrow"), axis=0, tiled=True),
        lax.all_gather(up_bias.astype(jnp.bfloat16), ("wide", "narrow"), axis=0, tiled=True),
        lax.all_gather(down_weight.astype(jnp.bfloat16), ("wide", "narrow"), axis=0, tiled=True),
        lax.all_gather(down_bias.astype(jnp.bfloat16), ("wide", "narrow"), axis=0, tiled=True),
    )
    upstream = out_grad.astype(jnp.float32)
    branch_grad = (column_mask * upstream).astype(jnp.bfloat16)
    down_weight_grad = jnp.einsum(
        "tf,td->fd", active, branch_grad, preferred_element_type=jnp.float32
    )
    down_bias_grad = jnp.sum(branch_grad.astype(jnp.float32), axis=0)
    active_grad = jnp.einsum(
        "td,fd->tf", branch_grad, back_down, preferred_element_type=jnp.float32
    )
    hidden_grad = (active_grad * gelu_slope(hidden)).astype(jnp.bfloat16)
    up_weight_grad = jnp.einsum(
        "td,tf->df", normed_two, hidden_grad, preferred_element_type=jnp.float32
    )
    up_bias_grad = jnp.sum(hidden_grad.astype(jnp.float32), axis=0)
    normed_two_grad = jnp.einsum(
        "tf,df->td", hidden_grad, back_up, preferred_element_type=jnp.float32
    )
    middle_part, norm2_gain_grad, norm2_shift_grad = normalize_back(
        normed_two_grad, unit_two, factor_two, back_gain_two.astype(jnp.float32)
    )
    (
        norm2_gain_grad,
        norm2_shift_grad,
        up_weight_grad,
        up_bias_grad,
        down_weight_grad,
        down_bias_grad,
    ) = (
        lax.psum_scatter(norm2_gain_grad, ("wide", "narrow"), scatter_dimension=0, tiled=True),
        lax.psum_scatter(norm2_shift_grad, ("wide", "narrow"), scatter_dimension=0, tiled=True),
        lax.psum_scatter(up_weight_grad, ("wide", "narrow"), scatter_dimension=0, tiled=True),
        lax.psum_scatter(up_bias_grad, ("wide", "narrow"), scatter_dimension=0, tiled=True),
        lax.psum_scatter(down_weight_grad, ("wide", "narrow"), scatter_dimension=0, tiled=True),
        lax.psum_scatter(down_bias_grad, ("wide", "narrow"), scatter_dimension=0, tiled=True),
    )
    middle_grad = upstream + middle_part
    back_gain_one, back_shift_one, back_qkv, back_qv, back_out, back_out_bias = (
        lax.all_gather(norm1_gain.astype(jnp.bfloat16), ("wide", "narrow"), axis=0, tiled=True),
        lax.all_gather(norm1_shift.astype(jnp.bfloat16), ("wide", "narrow"), axis=0, tiled=True),
        lax.all_gather(qkv_weight.astype(jnp.bfloat16), ("wide", "narrow"), axis=0, tiled=True),
        lax.all_gather(qv_bias.astype(jnp.bfloat16), ("wide", "narrow"), axis=0, tiled=True),
        lax.all_gather(out_weight.astype(jnp.bfloat16), ("wide", "narrow"), axis=0, tiled=True),
        lax.all_gather(out_bias.astype(jnp.bfloat16), ("wide", "narrow"), axis=0, tiled=True),
    )
    attention_grad = (column_mask * middle_grad).astype(jnp.bfloat16)
    out_weight_grad = jnp.einsum(
        "te,td->ed", mixture, attention_grad, preferred_element_type=jnp.float32
    )
    out_bias_grad = jnp.sum(attention_grad.astype(jnp.float32), axis=0)
    mixture_grad = jnp.einsum(
        "td,ed->te", attention_grad, back_out, preferred_element_type=jnp.float32
    ).astype(jnp.bfloat16)
    grad_groups = to_groups(mixture_grad, group_count)
    query_grad, key_grad, value_grad = lax.map(
        lambda items: attend_backward(items[0], items[1], items[2], items[3], items[4], key_live),
        (query_groups, key_groups, value_groups, grad_groups, logsum),
    )
    query_grad = from_groups(query_grad).astype(jnp.bfloat16)
    key_grad = from_groups(key_grad).astype(jnp.bfloat16)
    value_grad = from_groups(value_grad).astype(jnp.bfloat16)
    joined_grad = jnp.concatenate([query_grad, key_grad, value_grad], axis=1)
    qkv_weight_grad = jnp.einsum(
        "td,tc->dc", normed_one, joined_grad, preferred_element_type=jnp.float32
    )
    qv_bias_grad = jnp.concatenate(
        [
            jnp.sum(query_grad.astype(jnp.float32), axis=0),
            jnp.sum(value_grad.astype(jnp.float32), axis=0),
        ]
    )
    normed_one_grad = jnp.einsum(
        "tc,dc->td", joined_grad, back_qkv, preferred_element_type=jnp.float32
    )
    input_part, norm1_gain_grad, norm1_shift_grad = normalize_back(
        normed_one_grad, unit_one, factor_one, back_gain_one.astype(jnp.float32)
    )
    input_grad = (middle_grad + input_part).astype(jnp.bfloat16)
    (
        norm1_gain_grad,
        norm1_shift_grad,
        qkv_weight_grad,
        qv_bias_grad,
        out_weight_grad,
        out_bias_grad,
    ) = (
        lax.psum_scatter(norm1_gain_grad, ("wide", "narrow"), scatter_dimension=0, tiled=True),
        lax.psum_scatter(norm1_shift_grad, ("wide", "narrow"), scatter_dimension=0, tiled=True),
        lax.psum_scatter(qkv_weight_grad, ("wide", "narrow"), scatter_dimension=0, tiled=True),
        lax.psum_scatter(qv_bias_grad, ("wide", "narrow"), scatter_dimension=0, tiled=True),
        lax.psum_scatter(out_weight_grad, ("wide", "narrow"), scatter_dimension=0, tiled=True),
        lax.psum_scatter(out_bias_grad, ("wide", "narrow"), scatter_dimension=0, tiled=True),
    )
    return (
        output,
        input_grad,
        norm1_gain_grad,
        norm1_shift_grad,
        qkv_weight_grad,
        qv_bias_grad,
        out_weight_grad,
        out_bias_grad,
        norm2_gain_grad,
        norm2_shift_grad,
        up_weight_grad,
        up_bias_grad,
        down_weight_grad,
        down_bias_grad,
    )


import functools

MESH_ID = pl.DeviceIdType.MESH
VIA_X = (0, 2)
VIA_Y = (1, 3)


class Place:
    def __init__(self):
        wide = lax.axis_index("wide")
        narrow = lax.axis_index("narrow")
        self.z = wide // 2
        self.y = wide % 2
        self.x = narrow // 2
        self.c = narrow % 2
        self.q = self.y * 2 + self.x
        self.qx = self.y * 2 + (1 - self.x)
        self.qy = (1 - self.y) * 2 + self.x
        self.qd = (1 - self.y) * 2 + (1 - self.x)

    def zk(self, k):
        if k == 0:
            return self.z
        if k == 3:
            return 3 - self.z
        if k == 2:
            return (self.z + 2) % 4
        return self.z + 1 - 2 * (self.z % 2)

    def at_z(self, k):
        return (self.zk(k) * 2 + self.y, self.x * 2 + self.c)

    def at_x(self):
        return (self.z * 2 + self.y, (1 - self.x) * 2 + self.c)

    def at_y(self):
        return (self.z * 2 + 1 - self.y, self.x * 2 + self.c)

    def at_c(self):
        return (self.z * 2 + self.y, self.x * 2 + 1 - self.c)

    def half(self, c, size):
        return pl.ds(pl.multiple_of(c * size, 128), size)


def meet(place):
    barrier = pltpu.get_barrier_semaphore()
    peers = [place.at_z(1), place.at_z(2), place.at_z(3), place.at_x(), place.at_y(), place.at_c()]
    for peer in peers:
        pl.semaphore_signal(barrier, inc=1, device_id=peer, device_id_type=MESH_ID)
    pl.semaphore_wait(barrier, len(peers))


def remote(source, target, send, recv, peer):
    return pltpu.make_async_remote_copy(
        src_ref=source,
        dst_ref=target,
        send_sem=send,
        recv_sem=recv,
        device_id=peer,
        device_id_type=MESH_ID,
    )


class Gather:
    COUNT = 19

    def __init__(self, place, own, block, column, send, recv):
        self.p = place
        self.own = own
        self.block = block
        self.column = column
        self.send = send
        self.recv = recv
        self.sent = []

    def _go(self, source, target, index, peer):
        copy = remote(source, target, self.send.at[index], self.recv.at[index], peer)
        copy.start()
        self.sent.append(copy)

    def _got(self, target, index, peer):
        remote(target, target, self.send.at[index], self.recv.at[index], peer).wait_recv()

    def start_z(self):
        p = self.p
        for k in (1, 3, 2):
            self._go(self.own, self.block(p.z, p.q), k - 1, p.at_z(k))

    def start_xy(self):
        p = self.p
        self._go(self.own, self.block(p.z, p.q), 3, p.at_x())
        self._go(self.own, self.block(p.z, p.q), 9, p.at_y())

    def z_got(self, k):
        p = self.p
        here = self.block(p.zk(k), p.q)
        self._got(here, k - 1, p.at_z(k))
        self._go(here, here, 3 + k, p.at_x())
        self._go(here, here, 9 + k, p.at_y())

    def own_column(self):
        p = self.p
        self._go(self.column(p.q), self.column(p.q), 15, p.at_c())

    def xy_got(self, k):
        p = self.p
        from_x = self.block(p.zk(k), p.qx)
        self._got(from_x, 3 + k, p.at_x())
        if k in VIA_X:
            self._go(from_x, from_x, 13 + VIA_X.index(k), p.at_y())
        from_y = self.block(p.zk(k), p.qy)
        self._got(from_y, 9 + k, p.at_y())
        if k in VIA_Y:
            self._go(from_y, from_y, 7 + VIA_Y.index(k), p.at_x())

    def xy_columns(self):
        p = self.p
        self._go(self.column(p.qx), self.column(p.qx), 16, p.at_c())
        self._go(self.column(p.qy), self.column(p.qy), 17, p.at_c())

    def d_got(self):
        p = self.p
        for i, k in enumerate(VIA_X):
            self._got(self.block(p.zk(k), p.qd), 13 + i, p.at_y())
        for i, k in enumerate(VIA_Y):
            self._got(self.block(p.zk(k), p.qd), 7 + i, p.at_x())
        self._go(self.column(p.qd), self.column(p.qd), 18, p.at_c())

    def c_got(self, other_column):
        p = self.p
        for i, q in enumerate((p.q, p.qx, p.qy, p.qd)):
            self._got(other_column(q), 15 + i, p.at_c())

    def finish(self):
        for copy in self.sent:
            copy.wait_send()


def gather_kernel(shapes, *refs):
    n = len(shapes)
    shards = refs[:n]
    small = refs[n]
    wide = refs[n + 1 : 2 * n + 1]
    wide_small = refs[2 * n + 1]
    owns = refs[2 * n + 2 : 3 * n + 2]
    sibs = refs[3 * n + 2 : 4 * n + 2]
    send, recv, pre_send, pre_recv, local = refs[4 * n + 2 :]
    place = Place()
    meet(place)
    pre = []
    for i in range(n):
        half = shapes[i][1] // 2
        copy = remote(
            shards[i].at[:, place.half(1 - place.c, half)],
            sibs[i],
            pre_send.at[i],
            pre_recv.at[i],
            place.at_c(),
        )
        copy.start()
        pre.append(copy)
    pieces = [
        Gather(
            place,
            small,
            lambda zz, q: wide_small.at[zz, q, place.c],
            lambda q: wide_small.at[:, q, place.c],
            send.at[n],
            recv.at[n],
        )
    ]
    copies = [pltpu.make_async_copy(small, wide_small.at[place.z, place.q, place.c], local.at[n])]
    copies[0].start()
    pieces[0].start_z()
    pieces[0].start_xy()
    for i in range(n):
        rows, width = shapes[i]
        half = width // 2
        pre[i].wait_recv()
        mine = shards[i][:, place.half(place.c, half)]
        theirs = sibs[i][...]
        first = place.c == 0
        owns[i][...] = jnp.concatenate(
            [jnp.where(first, mine, theirs), jnp.where(first, theirs, mine)], axis=0
        ).astype(jnp.bfloat16)
        cols = place.half(place.c, half)
        piece = Gather(
            place,
            owns[i],
            lambda zz, q, i=i, cols=cols: wide[i].at[zz, q, :, cols],
            lambda q, i=i, cols=cols: wide[i].at[:, q, :, cols],
            send.at[i],
            recv.at[i],
        )
        pieces.append(piece)
        copy = pltpu.make_async_copy(owns[i], piece.block(place.z, place.q), local.at[i])
        copy.start()
        copies.append(copy)
        piece.start_z()
        if i == 0:
            piece.start_xy()
    for j, piece in enumerate(pieces):
        for k in (1, 3, 2):
            piece.z_got(k)
        copies[j].wait()
        piece.own_column()
        if 1 <= j < n:
            pieces[j + 1].start_xy()
        for k in (0, 1, 3, 2):
            piece.xy_got(k)
        piece.xy_columns()
        piece.d_got()
    for j, piece in enumerate(pieces):
        if j == 0:
            piece.c_got(lambda q: wide_small.at[:, q, 1 - place.c])
        else:
            cols = place.half(1 - place.c, shapes[j - 1][1] // 2)
            piece.c_got(lambda q, j=j, cols=cols: wide[j - 1].at[:, q, :, cols])
    for copy in pre:
        copy.wait_send()
    for piece in pieces:
        piece.finish()


def gather_all(shards, small):
    shapes = tuple(s.shape for s in shards)
    n = len(shapes)
    vmem = pl.BlockSpec(memory_space=pltpu.VMEM)
    return pl.pallas_call(
        functools.partial(gather_kernel, shapes),
        out_shape=tuple(
            jax.ShapeDtypeStruct((4, 4, 2 * r, w), jnp.bfloat16) for r, w in shapes
        )
        + (jax.ShapeDtypeStruct((4, 4, 2, 8, 128), jnp.float32),),
        in_specs=[vmem] * (n + 1),
        out_specs=(vmem,) * (n + 1),
        scratch_shapes=[pltpu.VMEM((2 * r, w // 2), jnp.bfloat16) for r, w in shapes]
        + [pltpu.VMEM((r, w // 2), jnp.float32) for r, w in shapes]
        + [
            pltpu.SemaphoreType.DMA((n + 1, Gather.COUNT)),
            pltpu.SemaphoreType.DMA((n + 1, Gather.COUNT)),
            pltpu.SemaphoreType.DMA((n,)),
            pltpu.SemaphoreType.DMA((n,)),
            pltpu.SemaphoreType.DMA((n + 1,)),
        ],
        compiler_params=pltpu.CompilerParams(
            collective_id=0, has_side_effects=True, vmem_limit_bytes=60 << 20
        ),
        name="gather_all",
    )(*shards, small)


class Scatter:
    COUNT = 19

    def __init__(self, place, mine, total, dx, dy, xr, yr, zr, send, recv):
        self.p = place
        self.mine = mine
        self.total = total
        self.dx, self.dy, self.xr, self.yr, self.zr = dx, dy, xr, yr, zr
        self.send = send
        self.recv = recv
        self.sent = []

    def _go(self, source, target, index, peer):
        copy = remote(source, target, self.send.at[index], self.recv.at[index], peer)
        copy.start()
        self.sent.append(copy)

    def _got(self, target, index, peer):
        remote(target, target, self.send.at[index], self.recv.at[index], peer).wait_recv()

    def _add(self, target, other):
        target[...] = (target[...].astype(jnp.float32) + other[...].astype(jnp.float32)).astype(
            target.dtype
        )

    def columns(self):
        p = self.p
        return (p.qd, p.qx, p.qy, p.q)

    def give(self, other):
        for i, q in enumerate(self.columns()):
            self._go(other(q), self.total.at[:, q], 15 + i, self.p.at_c())

    def take(self, i):
        q = self.columns()[i]
        self._got(self.total.at[:, q], 15 + i, self.p.at_c())
        for zz in range(4):
            self._add(self.total.at[zz, q], self.mine(zz, q))

    def diagonal(self):
        p = self.p
        self.take(0)
        for i in range(2):
            self._go(self.total.at[p.zk(VIA_X[i]), p.qd], self.dx.at[i], 7 + i, p.at_x())
            self._go(self.total.at[p.zk(VIA_Y[i]), p.qd], self.dy.at[i], 13 + i, p.at_y())

    def cross(self):
        p = self.p
        self.take(1)
        self.take(2)
        for k in (1, 3, 2, 0):
            here = self.total.at[p.zk(k), p.qx]
            if k in VIA_Y:
                i = VIA_Y.index(k)
                self._got(self.dy.at[i], 13 + i, p.at_y())
                self._add(here, self.dy.at[i])
            self._go(here, self.xr.at[k], 3 + k, p.at_x())
            here = self.total.at[p.zk(k), p.qy]
            if k in VIA_X:
                i = VIA_X.index(k)
                self._got(self.dx.at[i], 7 + i, p.at_x())
                self._add(here, self.dx.at[i])
            self._go(here, self.yr.at[k], 9 + k, p.at_y())

    def _plane(self, k):
        p = self.p
        self._got(self.xr.at[k], 3 + k, p.at_x())
        self._got(self.yr.at[k], 9 + k, p.at_y())
        here = self.total.at[p.zk(k), p.q]
        return here, (
            here[...].astype(jnp.float32)
            + self.xr[k].astype(jnp.float32)
            + self.yr[k].astype(jnp.float32)
        )

    def spread(self):
        p = self.p
        self.take(3)
        for k in (1, 3, 2):
            here, value = self._plane(k)
            here[...] = value.astype(here.dtype)
            self._go(here, self.zr.at[k - 1], k - 1, p.at_z(k))

    def last(self):
        p = self.p
        _, value = self._plane(0)
        for k in (1, 3, 2):
            self._got(self.zr.at[k - 1], k - 1, p.at_z(k))
            value = value + self.zr[k - 1].astype(jnp.float32)
        return value

    def finish(self):
        for copy in self.sent:
            copy.wait_send()


def scatter_kernel(shapes, *refs):
    n = len(shapes)
    parts = refs[: n + 1]
    outs = refs[n + 1 : 2 * n + 2]
    at = 2 * n + 2
    bufs = []
    for _ in range(n + 1):
        bufs.append(refs[at : at + 6])
        at += 6
    finals = refs[at : at + n]
    others = refs[at + n : at + 2 * n]
    send, recv, end_send, end_recv = refs[at + 2 * n :]
    place = Place()
    meet(place)
    pieces = []
    for i in range(n + 1):
        if i < n:
            half = shapes[i][1] // 2
            cols = place.half(place.c, half)
            rest = place.half(1 - place.c, half)
            mine = lambda zz, q, i=i, cols=cols: parts[i].at[zz, q, :, cols]
            other = lambda q, i=i, rest=rest: parts[i].at[:, q, :, rest]
        else:
            mine = lambda zz, q, i=i: parts[i].at[zz, q, place.c]
            other = lambda q, i=i: parts[i].at[:, q, 1 - place.c]
        piece = Scatter(place, mine, *bufs[i], send.at[i], recv.at[i])
        pieces.append(piece)
        piece.give(other)
    ends = []
    for i, piece in enumerate(pieces):
        piece.diagonal()
        piece.cross()
        if i:
            pieces[i - 1].spread()
    pieces[n].spread()
    for i in range(n):
        rows, width = shapes[i]
        half = width // 2
        finals[i][...] = pieces[i].last()
        keep = pl.ds(pl.multiple_of(place.c * rows, 8), rows)
        pass_on = pl.ds(pl.multiple_of((1 - place.c) * rows, 8), rows)
        copy = remote(
            finals[i].at[pass_on], others[i], end_send.at[i], end_recv.at[i], place.at_c()
        )
        copy.start()
        ends.append(copy)
        outs[i][:, place.half(place.c, half)] = finals[i][keep]
    outs[n][...] = pieces[n].last()
    for i in range(n):
        half = shapes[i][1] // 2
        ends[i].wait_recv()
        outs[i][:, place.half(1 - place.c, half)] = others[i][...]
    for copy in ends:
        copy.wait_send()
    for piece in pieces:
        piece.finish()


def scatter_all(parts, small):
    shapes = tuple((g.shape[2] // 2, g.shape[3]) for g in parts)
    n = len(shapes)
    vmem = pl.BlockSpec(memory_space=pltpu.VMEM)
    scratch = []
    for tail, kind in [((2 * r, w // 2), jnp.bfloat16) for r, w in shapes] + [((8, 128), jnp.float32)]:
        scratch += [
            pltpu.VMEM((4, 4) + tail, kind),
            pltpu.VMEM((2,) + tail, kind),
            pltpu.VMEM((2,) + tail, kind),
            pltpu.VMEM((4,) + tail, kind),
            pltpu.VMEM((4,) + tail, kind),
            pltpu.VMEM((3,) + tail, kind),
        ]
    return pl.pallas_call(
        functools.partial(scatter_kernel, shapes),
        out_shape=tuple(jax.ShapeDtypeStruct((r, w), jnp.float32) for r, w in shapes)
        + (jax.ShapeDtypeStruct((8, 128), jnp.float32),),
        in_specs=[vmem] * (n + 1),
        out_specs=(vmem,) * (n + 1),
        scratch_shapes=scratch
        + [pltpu.VMEM((2 * r, w // 2), jnp.float32) for r, w in shapes]
        + [pltpu.VMEM((r, w // 2), jnp.float32) for r, w in shapes]
        + [
            pltpu.SemaphoreType.DMA((n + 1, Scatter.COUNT)),
            pltpu.SemaphoreType.DMA((n + 1, Scatter.COUNT)),
            pltpu.SemaphoreType.DMA((n,)),
            pltpu.SemaphoreType.DMA((n,)),
        ],
        compiler_params=pltpu.CompilerParams(
            collective_id=1, has_side_effects=True, vmem_limit_bytes=60 << 20
        ),
        name="scatter_all",
    )(*parts, small)


def pack_small(vectors):
    return jnp.stack([jnp.pad(v, (0, 128 - v.shape[0])) for v in vectors])


def unpack_small(wide_small, sizes):
    rows = wide_small.reshape(32, 8, 128)
    return [rows[:, i, :m].reshape(32 * m).astype(jnp.bfloat16) for i, m in enumerate(sizes)]


def pack_grads(vectors):
    rows = [jnp.pad(v.reshape(32, -1), ((0, 0), (0, 128 - v.shape[0] // 32))) for v in vectors]
    return jnp.stack(rows, axis=1).reshape(4, 4, 2, 8, 128)


def body(
    tokens,
    band_mask,
    out_grad,
    norm1_gain,
    norm1_shift,
    qkv_weight,
    qv_bias,
    out_weight,
    out_bias,
    norm2_gain,
    norm2_shift,
    up_weight,
    up_bias,
    down_weight,
    down_bias,
):
    row_count, width = tokens.shape
    group_count = width // (HEAD_GROUP * HEAD)
    present = jnp.repeat(band_mask[0].astype(jnp.float32), row_count // band_mask.shape[1])
    key_live = present > 0.5
    column_mask = present[:, None]
    smalls = (norm1_gain, norm1_shift, qv_bias, out_bias, norm2_gain, norm2_shift, up_bias, down_bias)
    sizes = [v.shape[0] for v in smalls]
    *gathered, wide_small = gather_all((qkv_weight, out_weight, up_weight, down_weight), pack_small(smalls))
    w_qkv, w_out, w_up, w_down = [g.reshape(-1, g.shape[-1]) for g in gathered]
    gain_one, shift_one, b_qv, b_out, gain_two, shift_two, b_up, b_down = unpack_small(wide_small, sizes)
    inputs = tokens.astype(jnp.float32)
    normed_one, unit_one, factor_one = normalize(
        inputs, gain_one.astype(jnp.float32), shift_one.astype(jnp.float32)
    )
    normed_one = normed_one.astype(jnp.bfloat16)
    bias_wide = b_qv.astype(jnp.float32)
    bias_full = jnp.concatenate(
        [bias_wide[:width], jnp.zeros((width,), jnp.float32), bias_wide[width:]]
    )
    joined = (jnp.dot(normed_one, w_qkv, preferred_element_type=jnp.float32) + bias_full).astype(
        jnp.bfloat16
    )
    query_groups = to_groups(joined[:, :width], group_count)
    key_groups = to_groups(joined[:, width : 2 * width], group_count)
    value_groups = to_groups(joined[:, 2 * width :], group_count)
    mixture, logsum = lax.map(
        lambda items: attend_forward(items[0], items[1], items[2], key_live),
        (query_groups, key_groups, value_groups),
    )
    mixture = from_groups(mixture).astype(jnp.bfloat16)
    attention = jnp.dot(mixture, w_out, preferred_element_type=jnp.float32) + b_out.astype(
        jnp.float32
    )
    middle = inputs + column_mask * attention
    normed_two, unit_two, factor_two = normalize(
        middle, gain_two.astype(jnp.float32), shift_two.astype(jnp.float32)
    )
    normed_two = normed_two.astype(jnp.bfloat16)
    hidden = jnp.dot(normed_two, w_up, preferred_element_type=jnp.float32) + b_up.astype(
        jnp.float32
    )
    active = jax.nn.gelu(hidden, approximate=False).astype(jnp.bfloat16)
    branch = jnp.dot(active, w_down, preferred_element_type=jnp.float32) + b_down.astype(
        jnp.float32
    )
    output = (middle + column_mask * branch).astype(jnp.bfloat16)
    upstream = out_grad.astype(jnp.float32)
    branch_grad = (column_mask * upstream).astype(jnp.bfloat16)
    down_weight_grad = jnp.einsum(
        "tf,td->fd", active, branch_grad, preferred_element_type=jnp.float32
    )
    down_bias_grad = jnp.sum(branch_grad.astype(jnp.float32), axis=0)
    active_grad = jnp.einsum(
        "td,fd->tf", branch_grad, w_down, preferred_element_type=jnp.float32
    )
    hidden_grad = (active_grad * gelu_slope(hidden)).astype(jnp.bfloat16)
    up_weight_grad = jnp.einsum(
        "td,tf->df", normed_two, hidden_grad, preferred_element_type=jnp.float32
    )
    up_bias_grad = jnp.sum(hidden_grad.astype(jnp.float32), axis=0)
    normed_two_grad = jnp.einsum(
        "tf,df->td", hidden_grad, w_up, preferred_element_type=jnp.float32
    )
    middle_part, norm2_gain_grad, norm2_shift_grad = normalize_back(
        normed_two_grad, unit_two, factor_two, gain_two.astype(jnp.float32)
    )
    middle_grad = upstream + middle_part
    attention_grad = (column_mask * middle_grad).astype(jnp.bfloat16)
    out_weight_grad = jnp.einsum(
        "te,td->ed", mixture, attention_grad, preferred_element_type=jnp.float32
    )
    out_bias_grad = jnp.sum(attention_grad.astype(jnp.float32), axis=0)
    mixture_grad = jnp.einsum(
        "td,ed->te", attention_grad, w_out, preferred_element_type=jnp.float32
    ).astype(jnp.bfloat16)
    grad_groups = to_groups(mixture_grad, group_count)
    query_grad, key_grad, value_grad = lax.map(
        lambda items: attend_backward(items[0], items[1], items[2], items[3], items[4], key_live),
        (query_groups, key_groups, value_groups, grad_groups, logsum),
    )
    query_grad = from_groups(query_grad).astype(jnp.bfloat16)
    key_grad = from_groups(key_grad).astype(jnp.bfloat16)
    value_grad = from_groups(value_grad).astype(jnp.bfloat16)
    joined_grad = jnp.concatenate([query_grad, key_grad, value_grad], axis=1)
    qkv_weight_grad = jnp.einsum(
        "td,tc->dc", normed_one, joined_grad, preferred_element_type=jnp.float32
    )
    qv_bias_grad = jnp.concatenate(
        [
            jnp.sum(query_grad.astype(jnp.float32), axis=0),
            jnp.sum(value_grad.astype(jnp.float32), axis=0),
        ]
    )
    normed_one_grad = jnp.einsum(
        "tc,dc->td", joined_grad, w_qkv, preferred_element_type=jnp.float32
    )
    input_part, norm1_gain_grad, norm1_shift_grad = normalize_back(
        normed_one_grad, unit_one, factor_one, gain_one.astype(jnp.float32)
    )
    input_grad = (middle_grad + input_part).astype(jnp.bfloat16)
    blocks = [
        g.astype(jnp.bfloat16).reshape(4, 4, -1, g.shape[1])
        for g in (down_weight_grad, up_weight_grad, out_weight_grad, qkv_weight_grad)
    ]
    small_grads = (
        norm1_gain_grad,
        norm1_shift_grad,
        qv_bias_grad,
        out_bias_grad,
        norm2_gain_grad,
        norm2_shift_grad,
        up_bias_grad,
        down_bias_grad,
    )
    down_weight_grad, up_weight_grad, out_weight_grad, qkv_weight_grad, tile = scatter_all(
        blocks, pack_grads(small_grads)
    )
    (
        norm1_gain_grad,
        norm1_shift_grad,
        qv_bias_grad,
        out_bias_grad,
        norm2_gain_grad,
        norm2_shift_grad,
        up_bias_grad,
        down_bias_grad,
    ) = [tile[i, :m] for i, m in enumerate(sizes)]
    return (
        output,
        input_grad,
        norm1_gain_grad,
        norm1_shift_grad,
        qkv_weight_grad,
        qv_bias_grad,
        out_weight_grad,
        out_bias_grad,
        norm2_gain_grad,
        norm2_shift_grad,
        up_weight_grad,
        up_bias_grad,
        down_weight_grad,
        down_bias_grad,
    )


def solution(mesh):
    placed = (
        P(("wide", "narrow"), None),
        P(("wide", "narrow"), None),
        P(("wide", "narrow"), None),
        P(("wide", "narrow")),
        P(("wide", "narrow")),
        P(("wide", "narrow"), None),
        P(("wide", "narrow")),
        P(("wide", "narrow"), None),
        P(("wide", "narrow")),
        P(("wide", "narrow")),
        P(("wide", "narrow")),
        P(("wide", "narrow"), None),
        P(("wide", "narrow")),
        P(("wide", "narrow"), None),
        P(("wide", "narrow")),
    )
    fitted = dict(mesh.shape) == {"wide": 8, "narrow": 4}
    return jax.shard_map(
        body if fitted else body_plain,
        mesh=mesh,
        in_specs=placed,
        out_specs=(
            P(("wide", "narrow"), None),
            P(("wide", "narrow"), None),
            P(("wide", "narrow")),
            P(("wide", "narrow")),
            P(("wide", "narrow"), None),
            P(("wide", "narrow")),
            P(("wide", "narrow"), None),
            P(("wide", "narrow")),
            P(("wide", "narrow")),
            P(("wide", "narrow")),
            P(("wide", "narrow"), None),
            P(("wide", "narrow")),
            P(("wide", "narrow"), None),
            P(("wide", "narrow")),
        ),
        check_vma=False,
    )
```

```python
import functools
import math

import jax
import jax.numpy as jnp
from jax import lax
from jax.experimental import pallas as pl
from jax.experimental.pallas import tpu as pltpu
from jax.sharding import PartitionSpec as P

HEAD = 64
HEAD_GROUP = 4
QBLOCK = 512


NORM_EPSILON = 1e-05
VMEM_BYTES = 62 << 20
AXES = ("wide", "narrow")


def normalize(values, gain, shift):
    centre = jnp.mean(values, axis=1, keepdims=True)
    centred = values - centre
    factor = lax.rsqrt(jnp.mean(centred * centred, axis=1, keepdims=True) + NORM_EPSILON)
    normed = centred * factor
    return (normed * gain + shift, normed, factor)


def normalize_back(upstream, normed, factor, gain):
    gain_grad = jnp.sum(upstream * normed, axis=0)
    shift_grad = jnp.sum(upstream, axis=0)
    scaled = upstream * gain
    inner = (
        scaled
        - jnp.mean(scaled, axis=1, keepdims=True)
        - normed * jnp.mean(scaled * normed, axis=1, keepdims=True)
    )
    return (factor * inner, gain_grad, shift_grad)


def gelu_slope(values):
    cumulative = 0.5 * (1.0 + lax.erf(values * (1.0 / math.sqrt(2.0))))
    return cumulative + values * jnp.exp(-0.5 * values * values) * (1.0 / math.sqrt(2.0 * math.pi))


def to_groups(matrix, count):
    return matrix.reshape(matrix.shape[0], count, -1).transpose(1, 0, 2)


def from_groups(stacked):
    return stacked.transpose(1, 0, 2).reshape(stacked.shape[1], -1)


def attend_forward(query_cols, key_cols, value_cols, key_live):
    row_count, span_cols = key_cols.shape
    head_width = span_cols // HEAD_GROUP
    scaling = 1.0 / math.sqrt(head_width)
    key_rows = key_cols.reshape(row_count, HEAD_GROUP, head_width)
    value_rows = value_cols.reshape(row_count, HEAD_GROUP, head_width)
    query_blocks = query_cols.reshape(row_count // QBLOCK, QBLOCK, HEAD_GROUP, head_width)

    def one_block(query_rows):
        scores = (
            jnp.einsum("qhd,khd->hqk", query_rows, key_rows, preferred_element_type=jnp.float32)
            * scaling
        )
        scores = jnp.where(key_live[None, None, :], scores, -jnp.inf)
        largest = jnp.max(scores, axis=2, keepdims=True)
        expo = jnp.exp(scores - largest)
        totals = jnp.sum(expo, axis=2, keepdims=True)
        weights_low = (expo / totals).astype(jnp.bfloat16)
        mixture = jnp.einsum(
            "hqk,khd->qhd", weights_low, value_rows, preferred_element_type=jnp.float32
        )
        return (mixture.reshape(QBLOCK, span_cols), largest[:, :, 0] + jnp.log(totals[:, :, 0]))

    mixture, logsum = lax.map(one_block, query_blocks)
    return (mixture.reshape(row_count, span_cols), logsum)


def attend_backward(query_cols, key_cols, value_cols, grad_cols, logsum, key_live):
    row_count, span_cols = key_cols.shape
    head_width = span_cols // HEAD_GROUP
    scaling = 1.0 / math.sqrt(head_width)
    key_rows = key_cols.reshape(row_count, HEAD_GROUP, head_width)
    value_rows = value_cols.reshape(row_count, HEAD_GROUP, head_width)
    query_blocks = query_cols.reshape(row_count // QBLOCK, QBLOCK, HEAD_GROUP, head_width)
    grad_blocks = grad_cols.reshape(row_count // QBLOCK, QBLOCK, HEAD_GROUP, head_width)

    def one_block(carry, items):
        key_acc, value_acc = carry
        query_rows, grad_rows, block_logsum = items
        scores = (
            jnp.einsum("qhd,khd->hqk", query_rows, key_rows, preferred_element_type=jnp.float32)
            * scaling
        )
        scores = jnp.where(key_live[None, None, :], scores, -jnp.inf)
        probs = jnp.exp(scores - block_logsum[:, :, None])
        value_acc = value_acc + jnp.einsum(
            "hqk,qhd->khd",
            probs.astype(jnp.bfloat16),
            grad_rows,
            preferred_element_type=jnp.float32,
        )
        prob_grad = jnp.einsum(
            "qhd,khd->hqk", grad_rows, value_rows, preferred_element_type=jnp.float32
        )
        inner = jnp.sum(probs * prob_grad, axis=2, keepdims=True)
        score_grad = (probs * (prob_grad - inner)).astype(jnp.bfloat16)
        query_grad = (
            jnp.einsum("hqk,khd->qhd", score_grad, key_rows, preferred_element_type=jnp.float32)
            * scaling
        )
        key_acc = (
            key_acc
            + jnp.einsum("hqk,qhd->khd", score_grad, query_rows, preferred_element_type=jnp.float32)
            * scaling
        )
        return ((key_acc, value_acc), query_grad.reshape(QBLOCK, span_cols))

    empty = jnp.zeros((row_count, HEAD_GROUP, head_width), jnp.float32)
    (key_grad, value_grad), query_grad = lax.scan(
        one_block, (empty, empty), (query_blocks, grad_blocks, logsum)
    )
    return (
        query_grad.reshape(row_count, span_cols),
        key_grad.reshape(row_count, span_cols),
        value_grad.reshape(row_count, span_cols),
    )


def gathered(shard):
    return lax.all_gather(shard.astype(jnp.bfloat16), AXES, axis=0, tiled=True)


def scattered(part):
    return lax.psum_scatter(part, AXES, scatter_dimension=0, tiled=True)


def body_plain(
    tokens,
    band_mask,
    out_grad,
    norm1_gain,
    norm1_shift,
    qkv_weight,
    qv_bias,
    out_weight,
    out_bias,
    norm2_gain,
    norm2_shift,
    up_weight,
    up_bias,
    down_weight,
    down_bias,
):
    row_count, width = tokens.shape
    group_count = width // (HEAD_GROUP * HEAD)
    present = jnp.repeat(band_mask[0].astype(jnp.float32), row_count // band_mask.shape[1])
    key_live = present > 0.5
    column_mask = present[:, None]
    gain_one, shift_one, w_qkv, b_qv, w_out, b_out = (
        gathered(norm1_gain),
        gathered(norm1_shift),
        gathered(qkv_weight),
        gathered(qv_bias),
        gathered(out_weight),
        gathered(out_bias),
    )
    inputs = tokens.astype(jnp.float32)
    normed_one, unit_one, factor_one = normalize(
        inputs, gain_one.astype(jnp.float32), shift_one.astype(jnp.float32)
    )
    normed_one = normed_one.astype(jnp.bfloat16)
    bias_wide = b_qv.astype(jnp.float32)
    bias_full = jnp.concatenate(
        [bias_wide[:width], jnp.zeros((width,), jnp.float32), bias_wide[width:]]
    )
    joined = (jnp.dot(normed_one, w_qkv, preferred_element_type=jnp.float32) + bias_full).astype(
        jnp.bfloat16
    )
    query_groups = to_groups(joined[:, :width], group_count)
    key_groups = to_groups(joined[:, width : 2 * width], group_count)
    value_groups = to_groups(joined[:, 2 * width :], group_count)
    mixture, logsum = lax.map(
        lambda items: attend_forward(items[0], items[1], items[2], key_live),
        (query_groups, key_groups, value_groups),
    )
    mixture = from_groups(mixture).astype(jnp.bfloat16)
    attention = jnp.dot(mixture, w_out, preferred_element_type=jnp.float32) + b_out.astype(
        jnp.float32
    )
    middle = inputs + column_mask * attention
    gain_two, shift_two, w_up, b_up, w_down, b_down = (
        gathered(norm2_gain),
        gathered(norm2_shift),
        gathered(up_weight),
        gathered(up_bias),
        gathered(down_weight),
        gathered(down_bias),
    )
    normed_two, unit_two, factor_two = normalize(
        middle, gain_two.astype(jnp.float32), shift_two.astype(jnp.float32)
    )
    normed_two = normed_two.astype(jnp.bfloat16)
    hidden = jnp.dot(normed_two, w_up, preferred_element_type=jnp.float32) + b_up.astype(
        jnp.float32
    )
    active = jax.nn.gelu(hidden, approximate=False).astype(jnp.bfloat16)
    branch = jnp.dot(active, w_down, preferred_element_type=jnp.float32) + b_down.astype(
        jnp.float32
    )
    output = (middle + column_mask * branch).astype(jnp.bfloat16)
    upstream = out_grad.astype(jnp.float32)
    branch_grad = (column_mask * upstream).astype(jnp.bfloat16)
    down_weight_grad = jnp.einsum(
        "tf,td->fd", active, branch_grad, preferred_element_type=jnp.float32
    )
    down_bias_grad = jnp.sum(branch_grad.astype(jnp.float32), axis=0)
    active_grad = jnp.einsum(
        "td,fd->tf", branch_grad, w_down, preferred_element_type=jnp.float32
    )
    hidden_grad = (active_grad * gelu_slope(hidden)).astype(jnp.bfloat16)
    up_weight_grad = jnp.einsum(
        "td,tf->df", normed_two, hidden_grad, preferred_element_type=jnp.float32
    )
    up_bias_grad = jnp.sum(hidden_grad.astype(jnp.float32), axis=0)
    normed_two_grad = jnp.einsum(
        "tf,df->td", hidden_grad, w_up, preferred_element_type=jnp.float32
    )
    middle_part, norm2_gain_grad, norm2_shift_grad = normalize_back(
        normed_two_grad, unit_two, factor_two, gain_two.astype(jnp.float32)
    )
    (
        norm2_gain_grad,
        norm2_shift_grad,
        up_weight_grad,
        up_bias_grad,
        down_weight_grad,
        down_bias_grad,
    ) = (
        scattered(norm2_gain_grad),
        scattered(norm2_shift_grad),
        scattered(up_weight_grad),
        scattered(up_bias_grad),
        scattered(down_weight_grad),
        scattered(down_bias_grad),
    )
    middle_grad = upstream + middle_part
    attention_grad = (column_mask * middle_grad).astype(jnp.bfloat16)
    out_weight_grad = jnp.einsum(
        "te,td->ed", mixture, attention_grad, preferred_element_type=jnp.float32
    )
    out_bias_grad = jnp.sum(attention_grad.astype(jnp.float32), axis=0)
    mixture_grad = jnp.einsum(
        "td,ed->te", attention_grad, w_out, preferred_element_type=jnp.float32
    ).astype(jnp.bfloat16)
    grad_groups = to_groups(mixture_grad, group_count)
    query_grad, key_grad, value_grad = lax.map(
        lambda items: attend_backward(items[0], items[1], items[2], items[3], items[4], key_live),
        (query_groups, key_groups, value_groups, grad_groups, logsum),
    )
    query_grad = from_groups(query_grad).astype(jnp.bfloat16)
    key_grad = from_groups(key_grad).astype(jnp.bfloat16)
    value_grad = from_groups(value_grad).astype(jnp.bfloat16)
    joined_grad = jnp.concatenate([query_grad, key_grad, value_grad], axis=1)
    qkv_weight_grad = jnp.einsum(
        "td,tc->dc", normed_one, joined_grad, preferred_element_type=jnp.float32
    )
    qv_bias_grad = jnp.concatenate(
        [
            jnp.sum(query_grad.astype(jnp.float32), axis=0),
            jnp.sum(value_grad.astype(jnp.float32), axis=0),
        ]
    )
    normed_one_grad = jnp.einsum(
        "tc,dc->td", joined_grad, w_qkv, preferred_element_type=jnp.float32
    )
    input_part, norm1_gain_grad, norm1_shift_grad = normalize_back(
        normed_one_grad, unit_one, factor_one, gain_one.astype(jnp.float32)
    )
    input_grad = (middle_grad + input_part).astype(jnp.bfloat16)
    (
        norm1_gain_grad,
        norm1_shift_grad,
        qkv_weight_grad,
        qv_bias_grad,
        out_weight_grad,
        out_bias_grad,
    ) = (
        scattered(norm1_gain_grad),
        scattered(norm1_shift_grad),
        scattered(qkv_weight_grad),
        scattered(qv_bias_grad),
        scattered(out_weight_grad),
        scattered(out_bias_grad),
    )
    return (
        output,
        input_grad,
        norm1_gain_grad,
        norm1_shift_grad,
        qkv_weight_grad,
        qv_bias_grad,
        out_weight_grad,
        out_bias_grad,
        norm2_gain_grad,
        norm2_shift_grad,
        up_weight_grad,
        up_bias_grad,
        down_weight_grad,
        down_bias_grad,
    )


MESH_ID = pl.DeviceIdType.MESH
VIA_X = (0, 2)
VIA_Y = (1, 3)
ORDER = (1, 3, 2)
SCORE_SCALE = math.log2(math.e) / math.sqrt(HEAD)
TILE = 384


class Place:
    def __init__(self):
        wide = lax.axis_index("wide")
        narrow = lax.axis_index("narrow")
        z, y = wide // 2, wide % 2
        x, c = narrow // 2, narrow % 2
        self.z, self.c = z, c
        self.zs = (z, z + 1 - 2 * (z % 2), (z + 2) % 4, 3 - z)
        self.q = y * 2 + x
        self.qx = y * 2 + (1 - x)
        self.qy = (1 - y) * 2 + x
        self.qd = (1 - y) * 2 + (1 - x)
        self.to_z = tuple((zz * 2 + y, x * 2 + c) for zz in self.zs)
        self.to_x = (z * 2 + y, (1 - x) * 2 + c)
        self.to_y = (z * 2 + 1 - y, x * 2 + c)
        self.to_c = (z * 2 + y, x * 2 + 1 - c)


def span(start, size, step):
    return pl.ds(pl.multiple_of(start, step), size)


def meet(place):
    barrier = pltpu.get_barrier_semaphore()
    peers = place.to_z[1:] + (place.to_x, place.to_y, place.to_c)
    for peer in peers:
        pl.semaphore_signal(barrier, inc=1, device_id=peer, device_id_type=MESH_ID)
    pl.semaphore_wait(barrier, len(peers))


def remote(source, target, send, recv, peer):
    return pltpu.make_async_remote_copy(
        src_ref=source,
        dst_ref=target,
        send_sem=send,
        recv_sem=recv,
        device_id=peer,
        device_id_type=MESH_ID,
    )


class Piece:
    COUNT = 19

    def __init__(self, place, send, recv):
        self.p = place
        self.send = send
        self.recv = recv
        self.sent = []

    def go(self, source, target, index, peer):
        remote(source(), target(), self.send.at[index], self.recv.at[index], peer).start()
        self.sent.append((source, target, index, peer))

    def got(self, target, index, peer):
        remote(target, target, self.send.at[index], self.recv.at[index], peer).wait_recv()

    def finish(self):
        for source, target, index, peer in self.sent:
            remote(source(), target(), self.send.at[index], self.recv.at[index], peer).wait_send()


class Gather(Piece):
    def __init__(self, place, own, block, column, other, send, recv):
        super().__init__(place, send, recv)
        self.own = own
        self.block = block
        self.column = column
        self.other = other

    def start_z(self):
        p = self.p
        for k in ORDER:
            self.go(self.own, lambda: self.block(p.z, p.q), k - 1, p.to_z[k])

    def start_xy(self):
        p = self.p
        self.go(self.own, lambda: self.block(p.z, p.q), 3, p.to_x)
        self.go(self.own, lambda: self.block(p.z, p.q), 9, p.to_y)

    def z(self, k):
        p = self.p
        here = lambda: self.block(p.zs[k], p.q)
        self.got(here(), k - 1, p.to_z[k])
        self.go(here, here, 3 + k, p.to_x)
        self.go(here, here, 9 + k, p.to_y)

    def share(self, index, q):
        column = lambda: self.column(q)
        self.go(column, column, index, self.p.to_c)

    def own_column(self):
        self.share(15, self.p.q)

    def xy(self, k):
        p = self.p
        from_x = lambda: self.block(p.zs[k], p.qx)
        self.got(from_x(), 3 + k, p.to_x)
        if k in VIA_X:
            self.go(from_x, from_x, 13 + VIA_X.index(k), p.to_y)
        from_y = lambda: self.block(p.zs[k], p.qy)
        self.got(from_y(), 9 + k, p.to_y)
        if k in VIA_Y:
            self.go(from_y, from_y, 7 + VIA_Y.index(k), p.to_x)

    def xy_columns(self):
        self.share(16, self.p.qx)
        self.share(17, self.p.qy)

    def d(self):
        p = self.p
        for i, k in enumerate(VIA_X):
            self.got(self.block(p.zs[k], p.qd), 13 + i, p.to_y)
        for i, k in enumerate(VIA_Y):
            self.got(self.block(p.zs[k], p.qd), 7 + i, p.to_x)
        self.share(18, p.qd)

    def c(self):
        p = self.p
        for i, q in enumerate((p.q, p.qx, p.qy, p.qd)):
            self.got(self.other(q), 15 + i, p.to_c)


class Scatter(Piece):
    def __init__(self, place, bufs, send, recv):
        super().__init__(place, send, recv)
        self.total, self.dx, self.dy, self.xr, self.yr, self.zr = bufs
        self.columns = (place.qd, place.qx, place.qy, place.q)

    def add(self, target, other):
        target[...] = (target[...].astype(jnp.float32) + other[...].astype(jnp.float32)).astype(
            target.dtype
        )

    def give(self, other):
        for i, q in enumerate(self.columns):
            self.go(
                lambda q=q: other(q), lambda q=q: self.total.at[:, q], 15 + i, self.p.to_c
            )

    def arrive(self, i):
        self.got(self.total.at[:, self.columns[i]], 15 + i, self.p.to_c)

    def take(self, i, mine):
        self.arrive(i)
        q = self.columns[i]
        for zz in range(4):
            self.add(self.total.at[zz, q], mine(zz, q))

    def diagonal(self):
        p = self.p
        for i in range(2):
            self.go(
                lambda i=i: self.total.at[p.zs[VIA_X[i]], p.qd],
                lambda i=i: self.dx.at[i],
                7 + i,
                p.to_x,
            )
            self.go(
                lambda i=i: self.total.at[p.zs[VIA_Y[i]], p.qd],
                lambda i=i: self.dy.at[i],
                13 + i,
                p.to_y,
            )

    def cross(self, k):
        p = self.p
        on_x = lambda: self.total.at[p.zs[k], p.qx]
        on_y = lambda: self.total.at[p.zs[k], p.qy]
        if k in VIA_Y:
            i = VIA_Y.index(k)
            self.go(on_y, lambda: self.yr.at[k], 9 + k, p.to_y)
            self.got(self.dy.at[i], 13 + i, p.to_y)
            self.add(on_x(), self.dy.at[i])
            self.go(on_x, lambda: self.xr.at[k], 3 + k, p.to_x)
        else:
            i = VIA_X.index(k)
            self.go(on_x, lambda: self.xr.at[k], 3 + k, p.to_x)
            self.got(self.dx.at[i], 7 + i, p.to_x)
            self.add(on_y(), self.dx.at[i])
            self.go(on_y, lambda: self.yr.at[k], 9 + k, p.to_y)

    def plane(self, k):
        p = self.p
        self.got(self.xr.at[k], 3 + k, p.to_x)
        self.got(self.yr.at[k], 9 + k, p.to_y)
        here = self.total.at[p.zs[k], p.q]
        return here, (
            here[...].astype(jnp.float32)
            + self.xr[k].astype(jnp.float32)
            + self.yr[k].astype(jnp.float32)
        )

    def spread(self, k):
        here, value = self.plane(k)
        here[...] = value.astype(here.dtype)
        self.go(
            lambda: self.total.at[self.p.zs[k], self.p.q],
            lambda: self.zr.at[k - 1],
            k - 1,
            self.p.to_z[k],
        )

    def last(self):
        p = self.p
        _, value = self.plane(0)
        for k in ORDER:
            self.got(self.zr.at[k - 1], k - 1, p.to_z[k])
            value = value + self.zr[k - 1].astype(jnp.float32)
        return value


def scatter_buffers(tail, kind):
    return [
        pltpu.VMEM((4, 4) + tail, kind),
        pltpu.VMEM((2,) + tail, kind),
        pltpu.VMEM((2,) + tail, kind),
        pltpu.VMEM((4,) + tail, kind),
        pltpu.VMEM((4,) + tail, kind),
        pltpu.VMEM((3,) + tail, kind),
    ]


WANTED = (
    "vec",
    "turned_two",
    "middle",
    "up_wide",
    "mixed_turned",
    "out_wide",
    "joined",
    "logsum",
    "turned_one",
    "qkv_wide",
)
MATRICES = ("qkv", "out", "up", "down")


def triples(**named):
    return [(name, one, two) for name, (one, two) in named.items()]


def pairs_of(**named):
    return list(named.items())


class Named:
    def __init__(self, names, refs):
        assert len(names) == len(refs)
        self.__dict__.update(zip(names, refs))


def loop(count, compute, slots=()):
    def step(i, carry):
        compute(i)
        for j, steps in enumerate(slots):
            if steps:

                @pl.when(i == j)
                def _(steps=steps):
                    for one in steps:
                        one()

        return carry

    lax.fori_loop(0, count, step, 0)


def dot(left, right):
    return jnp.dot(left, right, preferred_element_type=jnp.float32)


def dot_nt(left, right):
    return lax.dot_general(
        left, right, (((1,), (1,)), ((), ())), preferred_element_type=jnp.float32
    )


def dot_tn(left, right):
    return lax.dot_general(
        left, right, (((0,), (0,)), ((), ())), preferred_element_type=jnp.float32
    )


def head_only(values, e):
    lane = lax.broadcasted_iota(jnp.int32, values.shape, 1)
    return jnp.where((lane // HEAD) == e, values, jnp.zeros_like(values))


def fill_present(present, mask):
    groups = mask.shape[1]
    rows = present.shape[0] // groups
    for g in range(groups):
        present[g * rows : (g + 1) * rows, :] = jnp.full(
            (rows, 128), mask[0, g].astype(jnp.float32)
        )


def segments(width):
    return ((0, width, width // 32), (width, 2 * width, width // 16), (3 * width, 4 * width, width // 8))


def selection(width):
    parts = []
    for _, size, m in segments(width):
        lane = lax.broadcasted_iota(jnp.int32, (1, size), 1).astype(jnp.float32)
        rest = lane - m * jnp.floor((lane + 0.5) * (1.0 / m))
        row = lax.broadcasted_iota(jnp.int32, (128, size), 0).astype(jnp.float32)
        parts.append(jnp.where(row == rest, 1.0, 0.0).astype(jnp.bfloat16))
    return jnp.concatenate(parts, axis=1)


def owners(width):
    parts = []
    for _, size, m in segments(width):
        lane = lax.broadcasted_iota(jnp.int32, (1, size), 1).astype(jnp.float32)
        parts.append(jnp.floor((lane + 0.5) * (1.0 / m)))
    return jnp.concatenate(parts, axis=1)


def unit(values):
    centred = values - jnp.mean(values, axis=1, keepdims=True)
    factor = lax.rsqrt(jnp.mean(centred * centred, axis=1, keepdims=True) + NORM_EPSILON)
    return centred * factor, factor


def forward_kernel(names, *refs):
    r = Named(names, refs)
    place = Place()
    tokens, width = r.tokens.shape
    hidden = r.act.shape[0] * TILE
    pairs = width // 128
    shards = (r.qkv_shard, r.out_shard, r.up_shard, r.down_shard)
    owns = (r.qkv_own, r.out_own, r.up_own, r.down_own)
    sibs = (r.qkv_sib, r.out_sib, r.up_sib, r.down_sib)
    wides = (r.qkv_wide, r.out_wide, r.up_wide, r.down_wide)
    meet(place)
    first = place.c == 0

    def before(i):
        half = shards[i].shape[1] // 2
        return remote(
            shards[i].at[:, span((1 - place.c) * half, half, 128)],
            sibs[i],
            r.pre_send.at[i],
            r.pre_recv.at[i],
            place.to_c,
        )

    for i in range(4):
        before(i).start()
    small = Gather(
        place,
        lambda: r.small,
        lambda zz, q: r.small_wide.at[zz, q, place.c],
        lambda q: r.small_wide.at[:, q, place.c],
        lambda q: r.small_wide.at[:, q, 1 - place.c],
        r.send.at[6],
        r.recv.at[6],
    )
    local = [pltpu.make_async_copy(r.small, r.small_wide.at[place.z, place.q, place.c], r.local.at[4])]
    local[0].start()
    small.start_z()
    small.start_xy()

    cuts = (
        (0, 0, 48, 0, 1152),
        (1, 0, 48, 0, 384),
        (2, 0, 48, 0, 768),
        (2, 0, 48, 768, 768),
        (3, 0, 96, 0, 384),
        (3, 96, 96, 0, 384),
    )
    pieces = []
    for j, (i, row, rows, col, cols) in enumerate(cuts):
        half = shards[i].shape[1] // 2

        def at(c, row=row, rows=rows, col=col, cols=cols, half=half):
            return (pl.ds(row, rows), span(c * half + col, cols, 128))

        pieces.append(
            Gather(
                place,
                lambda i=i, row=row, rows=rows, col=col, cols=cols: owns[i].at[
                    pl.ds(row, rows), pl.ds(col, cols)
                ],
                lambda zz, q, i=i, at=at: wides[i].at[(zz, q) + at(place.c)],
                lambda q, i=i, at=at: wides[i].at[(slice(None), q) + at(place.c)],
                lambda q, i=i, at=at: wides[i].at[(slice(None), q) + at(1 - place.c)],
                r.send.at[j],
                r.recv.at[j],
            )
        )
    for i in range(4):
        half = shards[i].shape[1] // 2
        cols = span(place.c * half, half, 128)
        before(i).wait_recv()
        mine = shards[i][:, cols]
        theirs = sibs[i][...]
        owns[i][...] = jnp.concatenate(
            [jnp.where(first, mine, theirs), jnp.where(first, theirs, mine)], axis=0
        ).astype(jnp.bfloat16)
        copy = pltpu.make_async_copy(
            owns[i], wides[i].at[place.z, place.q, :, cols], r.local.at[i]
        )
        copy.start()
        local.append(copy)
        for j, cut in enumerate(cuts):
            if cut[0] == i:
                pieces[j].start_z()
        if i == 0:
            pieces[0].start_xy()
    fill_present(r.present, r.mask)
    for copy in local:
        copy.wait()
    p0, p1, p2, p3, p4, p5 = pieces

    def z_steps(piece):
        return [lambda k=k: piece.z(k) for k in ORDER] + [piece.own_column]

    def xy_steps(piece):
        return [lambda k=k: piece.xy(k) for k in (0, 1, 3, 2)]

    def run(steps):
        for one in steps:
            one()

    outgoing = []

    def write(source, target, index):
        copy = pltpu.make_async_copy(source, target, r.write.at[index])
        copy.start()
        outgoing.append(copy)

    run(z_steps(small)[:3])
    run(z_steps(p0))
    small.own_column()
    run(xy_steps(small))
    small.xy_columns()
    p1.start_xy()
    p0.xy(0)
    small.d()
    small.c()

    rows = r.small_wide[...].reshape(256, 128).astype(jnp.bfloat16)
    picked = dot(rows, selection(width))
    owner = owners(width)
    total = jnp.zeros((8, 7 * width), jnp.float32)
    for d in range(32):
        total = total + jnp.where(owner == d, picked[d * 8 : d * 8 + 8], 0.0)
    r.vec[...] = total
    r.bias[:, 0:width] = total[2:3, width : 2 * width]
    r.bias[:, width : 2 * width] = jnp.zeros((1, width), jnp.float32)
    r.bias[:, 2 * width : 3 * width] = total[2:3, 2 * width : 3 * width]
    write(r.vec, r.vec_out, 0)

    def first_norm(t):
        rows = span(t * 128, 128, 128)
        normed, _ = unit(r.tokens[rows, :].astype(jnp.float32))
        value = normed * r.vec[0:1, 0:width] + r.vec[1:2, 0:width]
        r.normed[rows, :] = value.astype(jnp.bfloat16)
        r.turned_one[:, rows] = value.T.astype(jnp.bfloat16)

    loop(tokens // 128, first_norm)
    write(r.turned_one, r.turned_one_out, 1)
    run(xy_steps(p0)[1:])
    p0.xy_columns()
    run(z_steps(p1))
    p0.d()
    p2.start_xy()
    p0.c()
    write(r.qkv_wide, r.qkv_wide_out, 2)

    def project(t):
        cols = span(t * width, width, 128)
        r.joined[:, cols] = (
            dot(r.normed[...], r.qkv_wide[:, :, :, cols].reshape(width, width)) + r.bias[:, cols]
        ).astype(jnp.bfloat16)

    xy1 = xy_steps(p1)
    loop(3, project, [xy1[:2], xy1[2:3], xy1[3:] + [p1.xy_columns]])
    write(r.joined, r.joined_out, 3)

    def attend(hp):
        cols = span(hp * 128, 128, 128)
        query = r.joined[:, cols]
        key = r.joined[:, span(width + hp * 128, 128, 128)]
        value = r.joined[:, span(2 * width + hp * 128, 128, 128)].T
        live = r.present[:, 0:1] > 0.5
        mixed = []
        for e in range(2):
            scores = dot_nt(head_only(key, e), query) * SCORE_SCALE
            scores = jnp.where(live, scores, -jnp.inf)
            largest = jnp.max(scores, axis=0, keepdims=True)
            expo = jnp.exp2(scores - largest)
            totals = jnp.sum(expo, axis=0, keepdims=True)
            probs = (expo * (1.0 / totals)).astype(jnp.bfloat16)
            mixed.append(dot(value[HEAD * e : HEAD * (e + 1)], probs))
            r.logsum[hp, e : e + 1, :] = largest + jnp.log2(totals)
        both = jnp.concatenate(mixed, axis=0)
        r.mixed_turned[cols, :] = both.astype(jnp.bfloat16)
        r.mixed[:, cols] = both.T.astype(jnp.bfloat16)

    z2 = z_steps(p2)
    xy2 = xy_steps(p2)
    loop(
        pairs,
        attend,
        [z2, [p1.d, p3.start_xy], xy2[:1], xy2[1:2], xy2[2:3], xy2[3:] + [p2.xy_columns]],
    )
    write(r.logsum, r.logsum_out, 4)
    write(r.mixed_turned, r.mixed_turned_out, 5)
    p1.c()
    run(z_steps(p3))
    write(r.out_wide, r.out_wide_out, 6)
    r.middle[...] = dot(r.mixed[...], r.out_wide[...].reshape(width, width))

    def second_norm(t):
        rows = span(t * 128, 128, 128)
        present = r.present[rows, 0:1]
        middle = r.tokens[rows, :].astype(jnp.float32) + present * (
            r.middle[rows, :] + r.vec[3:4, 0:width]
        )
        r.middle[rows, :] = middle
        normed, _ = unit(middle)
        value = normed * r.vec[4:5, 0:width] + r.vec[5:6, 0:width]
        r.normed[rows, :] = value.astype(jnp.bfloat16)
        r.turned_two[:, rows] = value.T.astype(jnp.bfloat16)
        r.grad_low[rows, :] = (present * r.out_grad[rows, :].astype(jnp.float32)).astype(
            jnp.bfloat16
        )

    loop(tokens // 128, second_norm)
    write(r.middle, r.middle_out, 7)
    write(r.turned_two, r.turned_two_out, 8)
    p2.d()
    p4.start_xy()
    p2.c()

    def expand(t):
        cols = span(t * TILE, TILE, 128)
        value = (
            dot(r.normed[...], r.up_wide[:, :, :, cols].reshape(width, TILE))
            + r.vec[6:7, span(3 * width + t * TILE, TILE, 128)]
        )
        cumulative = 0.5 * (1.0 + lax.erf(value * (1.0 / math.sqrt(2.0))))
        r.act[t] = (value * cumulative).astype(jnp.bfloat16)
        r.slope[t] = cumulative + value * jnp.exp(-0.5 * value * value) * (
            1.0 / math.sqrt(2.0 * math.pi)
        )

    def down_grad(t):
        grad = dot_tn(r.act[t], r.grad_low[...]).astype(jnp.bfloat16)
        r.down_grad[t // 2, pl.ds((t % 2) * 2, 2)] = grad.reshape(2, TILE // 2, width)

    xy3 = xy_steps(p3)
    loop(4, lambda u: expand(u + 2 * (u // 2)), [[s] for s in xy3])
    p3.xy_columns()
    run(z_steps(p4))
    loop(4, lambda u: down_grad(u + 2 * (u // 2)))
    p3.d()
    p5.start_xy()
    p3.c()
    write(r.up_wide, r.up_wide_out, 9)
    xy4 = xy_steps(p4)
    loop(4, lambda u: expand(u + 2 * (u // 2) + 2), [[s] for s in xy4])
    p4.xy_columns()
    write(r.act, r.act_out, 10)
    write(r.slope, r.slope_out, 11)
    run(z_steps(p5))
    loop(4, lambda u: down_grad(u + 2 * (u // 2) + 2))
    write(r.down_grad, r.down_grad_out, 12)
    p4.d()
    run(xy_steps(p5))
    p5.xy_columns()
    p4.c()
    p5.d()
    p5.c()
    write(r.down_wide, r.down_wide_out, 13)
    for i in range(4):
        before(i).wait_send()
    for piece in [small] + pieces:
        piece.finish()
    for copy in outgoing:
        copy.wait()


def forward_call(tokens, band_mask, out_grad, shards, small):
    bf16, f32 = jnp.bfloat16, jnp.float32
    count, width = tokens.shape
    shapes = [s.shape for s in shards]
    hidden = shapes[2][1]
    tiles = hidden // TILE
    vmem = pl.BlockSpec(memory_space=pltpu.VMEM)
    inputs = triples(
        tokens=(tokens, vmem),
        mask=(band_mask, pl.BlockSpec(memory_space=pltpu.SMEM)),
        out_grad=(out_grad, vmem),
        qkv_shard=(shards[0], vmem),
        out_shard=(shards[1], vmem),
        up_shard=(shards[2], vmem),
        down_shard=(shards[3], vmem),
        small=(small, vmem),
    )
    kept = triples(
        vec=((8, 7 * width), f32),
        turned_one=((width, count), bf16),
        qkv_wide=((4, 4, 2 * shapes[0][0], shapes[0][1]), bf16),
        joined=((count, 3 * width), bf16),
        logsum=((width // 128, 8, count), f32),
        mixed_turned=((width, count), bf16),
        out_wide=((4, 4, 2 * shapes[1][0], shapes[1][1]), bf16),
        middle=((count, width), f32),
        turned_two=((width, count), bf16),
        up_wide=((4, 4, 2 * shapes[2][0], shapes[2][1]), bf16),
        act=((tiles, count, TILE), bf16),
        slope=((tiles, count, TILE), f32),
        down_grad=((4, 4, 2 * shapes[3][0], shapes[3][1]), bf16),
        down_wide=((4, 4, 2 * shapes[3][0], shapes[3][1]), bf16),
    )
    scratch = [(name, pltpu.VMEM(shape, kind)) for name, shape, kind in kept]
    for name, (rows, cols) in zip(MATRICES, shapes):
        scratch.append((name + "_own", pltpu.VMEM((2 * rows, cols // 2), bf16)))
        scratch.append((name + "_sib", pltpu.VMEM((rows, cols // 2), f32)))
    scratch += pairs_of(
        small_wide=pltpu.VMEM((4, 4, 2, 8, 128), f32),
        present=pltpu.VMEM((count, 128), f32),
        bias=pltpu.VMEM((1, 3 * width), f32),
        normed=pltpu.VMEM((count, width), bf16),
        mixed=pltpu.VMEM((count, width), bf16),
        grad_low=pltpu.VMEM((count, width), bf16),
        send=pltpu.SemaphoreType.DMA((7, Piece.COUNT)),
        recv=pltpu.SemaphoreType.DMA((7, Piece.COUNT)),
        pre_send=pltpu.SemaphoreType.DMA((4,)),
        pre_recv=pltpu.SemaphoreType.DMA((4,)),
        local=pltpu.SemaphoreType.DMA((5,)),
        write=pltpu.SemaphoreType.DMA((len(kept),)),
    )
    names = (
        [name for name, _, _ in inputs]
        + [name + "_out" for name, _, _ in kept]
        + [name for name, _ in scratch]
    )
    results = pl.pallas_call(
        functools.partial(forward_kernel, names),
        out_shape=tuple(jax.ShapeDtypeStruct(shape, kind) for _, shape, kind in kept),
        in_specs=[spec for _, _, spec in inputs],
        out_specs=(pl.BlockSpec(memory_space=pl.ANY),) * len(kept),
        scratch_shapes=[kind for _, kind in scratch],
        compiler_params=pltpu.CompilerParams(
            collective_id=0, has_side_effects=True, vmem_limit_bytes=VMEM_BYTES
        ),
        name="forward",
    )(*[array for _, array, _ in inputs])
    return dict(zip([name for name, _, _ in kept], results))


def backward_kernel(names, *refs):
    r = Named(names, refs)
    place = Place()
    tokens, width = r.tokens.shape
    hidden = r.dpre.shape[1]
    pairs = width // 128
    tiles = hidden // TILE
    c = place.c

    def fetch(name, index):
        return pltpu.make_async_copy(getattr(r, name + "_in"), getattr(r, name), r.load.at[index])

    wanted = WANTED

    def need(*some):
        for name in some:
            fetch(name, wanted.index(name)).wait()

    def stream(t, slot):
        return (
            pltpu.make_async_copy(r.act_in.at[t], r.act.at[slot], r.tile.at[0, slot]),
            pltpu.make_async_copy(r.slope_in.at[t], r.slope.at[slot], r.tile.at[1, slot]),
            pltpu.make_async_copy(
                r.down_wide_in.at[t // 2, pl.ds((t % 2) * 2, 2)],
                r.down_tile.at[slot],
                r.tile.at[2, slot],
            ),
        )

    def down_mine(s):
        return pltpu.make_async_copy(
            r.down_grad_in.at[:, :, pl.ds(96 * s, 96), span(c * 384, 384, 128)],
            r.down_mine.at[s],
            r.mine.at[s],
        )

    for s in range(2):
        down_mine(s).start()
    for copy in stream(0, 0):
        copy.start()
    for i, name in enumerate(wanted):
        fetch(name, i).start()
    meet(place)
    pieces = []
    for j in range(9):
        bufs = [getattr(r, "piece%d_%d" % (j, b)) for b in range(6)]
        pieces.append(Scatter(place, bufs, r.send.at[j], r.recv.at[j]))
    d0, d1, u0, u1, o, q0, q1, q2, small = pieces
    for s, piece in enumerate((d0, d1)):
        piece.give(
            lambda q, s=s: r.down_grad_in.at[
                :, q, pl.ds(96 * s, 96), span((1 - c) * 384, 384, 128)
            ]
        )
    fill_present(r.present, r.mask)
    r.sums[...] = jnp.zeros_like(r.sums)
    r.acc[...] = jnp.zeros_like(r.acc)

    def mask_grad(t):
        rows = span(t * 128, 128, 128)
        low = (r.present[rows, 0:1] * r.out_grad[rows, :].astype(jnp.float32)).astype(jnp.bfloat16)
        r.grad_low[rows, :] = low
        r.sums[7:8, 0:width] += jnp.sum(low.astype(jnp.float32), axis=0, keepdims=True)

    loop(tokens // 128, mask_grad)

    def take_down(piece, s, i):
        if i == 0:
            down_mine(s).wait()
        piece.take(i, lambda zz, q: r.down_mine.at[s, zz, q])

    def narrow(t):
        slot = t % 2
        for copy in stream(t, slot):
            copy.wait()

        @pl.when(t + 1 < tiles)
        def _():
            for copy in stream(t + 1, 1 - slot):
                copy.start()

        cols = span(t * TILE, TILE, 128)
        weights = r.down_tile[slot].reshape(TILE, width)
        r.acc[...] += dot(r.act[slot], weights)
        grad = (dot_nt(r.grad_low[...], weights) * r.slope[slot]).astype(jnp.bfloat16)
        r.dpre[:, cols] = grad
        r.sums[6:7, span(3 * width + t * TILE, TILE, 128)] = jnp.sum(
            grad.astype(jnp.float32), axis=0, keepdims=True
        )

    def cross_steps(piece):
        return [lambda k=k: piece.cross(k) for k in (1, 3, 2, 0)]

    def spread_steps(piece):
        return [lambda k=k: piece.spread(k) for k in ORDER]

    def run(steps):
        for one in steps:
            one()

    xd0, xd1, xu0, xu1, xo = [cross_steps(p) for p in (d0, d1, u0, u1, o)]
    take_down(d0, 0, 0)
    d0.diagonal()
    loop(
        tiles,
        narrow,
        [
            [lambda: take_down(d0, 0, 1), lambda: take_down(d0, 0, 2)],
            [lambda: take_down(d1, 1, 0), d1.diagonal],
            xd0[:1],
            xd0[1:2] + [lambda: take_down(d1, 1, 1)],
            xd0[2:3] + [lambda: take_down(d1, 1, 2)],
            xd0[3:] + [lambda: take_down(d0, 0, 3)],
            [lambda: take_down(d1, 1, 3)],
            xd1[:1],
        ],
    )

    need("vec", "middle")

    def finish_output(t):
        rows = span(t * 128, 128, 128)
        r.output[rows, :] = (
            r.middle[rows, :]
            + r.present[rows, 0:1] * (r.acc[rows, :] + r.vec[7:8, 0:width])
        ).astype(jnp.bfloat16)

    need("turned_two", "up_wide")

    def up_part(side, s):
        cols = span(side * (hidden // 2) + 768 * s, 768, 128)
        return dot(r.turned_two[...], r.dpre[:, cols]).reshape(4, 4, 48, 768)

    for s, (piece, part) in enumerate(((u0, r.up_part0), (u1, r.up_part1))):
        part[...] = up_part(1 - c, s).astype(jnp.bfloat16)
        piece.give(lambda q, part=part: part.at[:, q])
    run(xd1[1:2])
    for s, piece in enumerate((u0, u1)):
        for i in range(4):
            piece.arrive(i)
        piece.total[...] = (
            piece.total[...].astype(jnp.float32) + up_part(c, s)
        ).astype(jnp.bfloat16)
        if s == 0:
            piece.diagonal()
            run(xd1[2:])
    run(spread_steps(d0))
    u1.diagonal()
    loop(tokens // 128, finish_output)
    r.acc[...] = dot_nt(r.dpre[...], r.up_wide[...].reshape(width, hidden))

    def second_back(t):
        rows = span(t * 128, 128, 128)
        normed, factor = unit(r.middle[rows, :])
        up = r.acc[rows, :]
        r.sums[4:5, 0:width] += jnp.sum(up * normed, axis=0, keepdims=True)
        r.sums[5:6, 0:width] += jnp.sum(up, axis=0, keepdims=True)
        scaled = up * r.vec[4:5, 0:width]
        inner = (
            scaled
            - jnp.mean(scaled, axis=1, keepdims=True)
            - normed * jnp.mean(scaled * normed, axis=1, keepdims=True)
        )
        grad = r.out_grad[rows, :].astype(jnp.float32) + factor * inner
        r.middle[rows, :] = grad
        low = (r.present[rows, 0:1] * grad).astype(jnp.bfloat16)
        r.attention_low[rows, :] = low
        r.sums[3:4, 0:width] += jnp.sum(low.astype(jnp.float32), axis=0, keepdims=True)

    loop(tokens // 128, second_back, [xu0[:1], xu0[1:2], xu0[2:3], xu0[3:]])
    need("mixed_turned", "out_wide")

    def out_part(side):
        cols = span(side * (width // 2), width // 2, 128)
        return dot(r.mixed_turned[...], r.attention_low[:, cols]).reshape(4, 4, 48, width // 2)

    r.out_part[...] = out_part(1 - c).astype(jnp.bfloat16)
    o.give(lambda q: r.out_part.at[:, q])
    r.mixed_grad[...] = dot_nt(r.attention_low[...], r.out_wide[...].reshape(width, width)).astype(
        jnp.bfloat16
    )
    for i in range(4):
        o.arrive(i)
    o.total[...] = (o.total[...].astype(jnp.float32) + out_part(c)).astype(jnp.bfloat16)
    o.diagonal()
    run(spread_steps(d1))
    need("joined", "logsum")

    def attend_back(hp):
        cols = span(hp * 128, 128, 128)
        key_cols = span(width + hp * 128, 128, 128)
        value_cols = span(2 * width + hp * 128, 128, 128)
        query = r.joined[:, cols]
        key = r.joined[:, key_cols]
        value = r.joined[:, value_cols]
        grad = r.mixed_grad[:, cols]
        turned = key.T
        live = r.present[:, 0:1] > 0.5
        value_grad = jnp.zeros((tokens, 128), jnp.float32)
        key_grad = jnp.zeros((tokens, 128), jnp.float32)
        query_grad = []
        for e in range(2):
            scores = dot_nt(head_only(key, e), query) * SCORE_SCALE
            scores = jnp.where(live, scores, -jnp.inf)
            probs = jnp.exp2(scores - r.logsum[hp, e : e + 1, :])
            back = dot_nt(head_only(value, e), grad)
            inner = jnp.sum(probs * back, axis=0, keepdims=True)
            score_grad = (probs * (back - inner)).astype(jnp.bfloat16)
            value_grad = value_grad + dot(probs.astype(jnp.bfloat16), head_only(grad, e))
            key_grad = key_grad + dot(score_grad, head_only(query, e))
            query_grad.append(dot(turned[HEAD * e : HEAD * (e + 1)], score_grad))
        scale = 1.0 / math.sqrt(HEAD)
        query_low = (jnp.concatenate(query_grad, axis=0).T * scale).astype(jnp.bfloat16)
        value_low = value_grad.astype(jnp.bfloat16)
        r.joined_grad[:, cols] = query_low
        r.joined_grad[:, key_cols] = (key_grad * scale).astype(jnp.bfloat16)
        r.joined_grad[:, value_cols] = value_low
        r.sums[2:3, span(width + hp * 128, 128, 128)] = jnp.sum(
            query_low.astype(jnp.float32), axis=0, keepdims=True
        )
        r.sums[2:3, span(2 * width + hp * 128, 128, 128)] = jnp.sum(
            value_low.astype(jnp.float32), axis=0, keepdims=True
        )

    loop(
        pairs,
        attend_back,
        [xu1[:1], xu1[1:2], xu1[2:3], xu1[3:] + spread_steps(u0)[:1], spread_steps(u0)[1:], xo],
    )

    need("turned_one", "qkv_wide")

    def qkv_part(side, s):
        cols = span(side * (3 * width // 2) + 384 * s, 384, 128)
        return dot(r.turned_one[...], r.joined_grad[:, cols]).reshape(4, 4, 48, 384)

    qs = (q0, q1, q2)
    for s, (piece, part) in enumerate(zip(qs, (r.qkv_part0, r.qkv_part1, r.qkv_part2))):
        part[...] = qkv_part(1 - c, s).astype(jnp.bfloat16)
        piece.give(lambda q, part=part: part.at[:, q])
    for s, piece in enumerate(qs):
        for i in range(4):
            piece.arrive(i)
        piece.total[...] = (
            piece.total[...].astype(jnp.float32) + qkv_part(c, s)
        ).astype(jnp.bfloat16)
        piece.diagonal()
    run(spread_steps(u1))
    r.acc[...] = dot_nt(r.joined_grad[...], r.qkv_wide[...].reshape(width, 3 * width))

    def first_back(t):
        rows = span(t * 128, 128, 128)
        normed, factor = unit(r.tokens[rows, :].astype(jnp.float32))
        up = r.acc[rows, :]
        r.sums[0:1, 0:width] += jnp.sum(up * normed, axis=0, keepdims=True)
        r.sums[1:2, 0:width] += jnp.sum(up, axis=0, keepdims=True)
        scaled = up * r.vec[0:1, 0:width]
        inner = (
            scaled
            - jnp.mean(scaled, axis=1, keepdims=True)
            - normed * jnp.mean(scaled * normed, axis=1, keepdims=True)
        )
        r.input_grad[rows, :] = (r.middle[rows, :] + factor * inner).astype(jnp.bfloat16)

    loop(tokens // 128, first_back)
    owner = owners(width)
    sums = r.sums[...]
    high = sums.astype(jnp.bfloat16)
    rest = sums - high.astype(jnp.float32)
    mid = rest.astype(jnp.bfloat16)
    low = (rest - mid.astype(jnp.float32)).astype(jnp.bfloat16)
    chosen = selection(width)
    tile = jnp.zeros((256, 128), jnp.float32)
    for part in (high, mid, low):
        part = part.astype(jnp.float32)
        spreaded = jnp.concatenate(
            [jnp.where(owner == d, part, 0.0) for d in range(32)], axis=0
        ).astype(jnp.bfloat16)
        tile = tile + dot_nt(spreaded, chosen)
    r.small_part[...] = tile.reshape(4, 4, 2, 8, 128)
    small.give(lambda q: r.small_part.at[:, q, 1 - c])
    run(cross_steps(q0))
    for i in range(4):
        small.take(i, lambda zz, q: r.small_part.at[zz, q, c])
    small.diagonal()
    run(spread_steps(o))
    run(cross_steps(q1))
    run(cross_steps(small))
    run(spread_steps(q0))
    run(cross_steps(q2))
    run(spread_steps(small))

    finals = (r.down_final, r.up_final, r.out_final, r.qkv_final)
    others = (r.down_other, r.up_other, r.out_other, r.qkv_other)
    results = (r.down_result, r.up_result, r.out_result, r.qkv_result)

    def swap(i):
        rows = results[i].shape[0]
        return remote(
            finals[i].at[span((1 - c) * rows, rows, 8)],
            others[i],
            r.end_send.at[i],
            r.end_recv.at[i],
            place.to_c,
        )

    def close(i):
        rows, cols = results[i].shape
        swap(i).start()
        results[i][:, span(c * (cols // 2), cols // 2, 128)] = finals[i][span(c * rows, rows, 8)]

    def settle(i):
        cols = results[i].shape[1]
        swap(i).wait_recv()
        results[i][:, span((1 - c) * (cols // 2), cols // 2, 128)] = others[i][...]

    r.down_final[0:96, :] = d0.last()
    r.down_final[96:192, :] = d1.last()
    close(0)
    r.up_final[:, 0:768] = u0.last()
    r.up_final[:, 768:1536] = u1.last()
    close(1)
    r.out_final[...] = o.last()
    close(2)
    run(spread_steps(q1))
    r.qkv_final[:, 0:384] = q0.last()
    run(spread_steps(q2))
    r.small_result[...] = small.last()
    r.qkv_final[:, 384:768] = q1.last()
    settle(0)
    settle(1)
    settle(2)
    r.qkv_final[:, 768:1152] = q2.last()
    close(3)
    settle(3)
    for i in range(4):
        swap(i).wait_send()
    for piece in pieces:
        piece.finish()


def backward_call(tokens, band_mask, out_grad, kept, shapes):
    bf16, f32 = jnp.bfloat16, jnp.float32
    count, width = tokens.shape
    hidden = shapes[2][1]
    vmem = pl.BlockSpec(memory_space=pltpu.VMEM)
    anywhere = pl.BlockSpec(memory_space=pl.ANY)
    inputs = triples(
        tokens=(tokens, vmem),
        mask=(band_mask, pl.BlockSpec(memory_space=pltpu.SMEM)),
        out_grad=(out_grad, vmem),
    ) + [(name + "_in", array, anywhere) for name, array in kept.items()]
    outs = triples(
        output=((count, width), bf16),
        input_grad=((count, width), bf16),
        qkv_result=(shapes[0], f32),
        out_result=(shapes[1], f32),
        up_result=(shapes[2], f32),
        down_result=(shapes[3], f32),
        small_result=((8, 128), f32),
    )
    tails = (
        [((96, 384), bf16)] * 2
        + [((48, 768), bf16)] * 2
        + [((48, 384), bf16)] * 4
        + [((8, 128), f32)]
    )
    scratch = []
    for j, (tail, kind) in enumerate(tails):
        for b, one in enumerate(scatter_buffers(tail, kind)):
            scratch.append(("piece%d_%d" % (j, b), one))
    for name in WANTED:
        scratch.append((name, pltpu.VMEM(kept[name].shape, kept[name].dtype)))
    for name, (rows, cols) in zip(MATRICES, shapes):
        scratch.append((name + "_final", pltpu.VMEM((2 * rows, cols // 2), f32)))
        scratch.append((name + "_other", pltpu.VMEM((rows, cols // 2), f32)))
    scratch += pairs_of(
        act=pltpu.VMEM((2, count, TILE), bf16),
        slope=pltpu.VMEM((2, count, TILE), f32),
        down_tile=pltpu.VMEM((2, 2, TILE // 2, width), bf16),
        down_mine=pltpu.VMEM((2, 4, 4, 96, 384), bf16),
        up_part0=pltpu.VMEM((4, 4, 48, 768), bf16),
        up_part1=pltpu.VMEM((4, 4, 48, 768), bf16),
        out_part=pltpu.VMEM((4, 4, 48, 384), bf16),
        qkv_part0=pltpu.VMEM((4, 4, 48, 384), bf16),
        qkv_part1=pltpu.VMEM((4, 4, 48, 384), bf16),
        qkv_part2=pltpu.VMEM((4, 4, 48, 384), bf16),
        small_part=pltpu.VMEM((4, 4, 2, 8, 128), f32),
        present=pltpu.VMEM((count, 128), f32),
        sums=pltpu.VMEM((8, 7 * width), f32),
        acc=pltpu.VMEM((count, width), f32),
        grad_low=pltpu.VMEM((count, width), bf16),
        dpre=pltpu.VMEM((count, hidden), bf16),
        attention_low=pltpu.VMEM((count, width), bf16),
        mixed_grad=pltpu.VMEM((count, width), bf16),
        joined_grad=pltpu.VMEM((count, 3 * width), bf16),
        send=pltpu.SemaphoreType.DMA((len(tails), Piece.COUNT)),
        recv=pltpu.SemaphoreType.DMA((len(tails), Piece.COUNT)),
        end_send=pltpu.SemaphoreType.DMA((4,)),
        end_recv=pltpu.SemaphoreType.DMA((4,)),
        load=pltpu.SemaphoreType.DMA((10,)),
        tile=pltpu.SemaphoreType.DMA((3, 2)),
        mine=pltpu.SemaphoreType.DMA((2,)),
    )
    names = (
        [name for name, _, _ in inputs] + [name for name, _, _ in outs] + [name for name, _ in scratch]
    )
    results = pl.pallas_call(
        functools.partial(backward_kernel, names),
        out_shape=tuple(jax.ShapeDtypeStruct(shape, kind) for _, shape, kind in outs),
        in_specs=[spec for _, _, spec in inputs],
        out_specs=(vmem,) * len(outs),
        scratch_shapes=[kind for _, kind in scratch],
        compiler_params=pltpu.CompilerParams(
            collective_id=1, has_side_effects=True, vmem_limit_bytes=VMEM_BYTES
        ),
        name="backward",
    )(*[array for _, array, _ in inputs])
    return dict(zip([name for name, _, _ in outs], results))


def body(
    tokens,
    band_mask,
    out_grad,
    norm1_gain,
    norm1_shift,
    qkv_weight,
    qv_bias,
    out_weight,
    out_bias,
    norm2_gain,
    norm2_shift,
    up_weight,
    up_bias,
    down_weight,
    down_bias,
):
    smalls = (norm1_gain, norm1_shift, qv_bias, out_bias, norm2_gain, norm2_shift, up_bias, down_bias)
    shards = (qkv_weight, out_weight, up_weight, down_weight)
    packed = jnp.stack([jnp.pad(v, (0, 128 - v.shape[0])) for v in smalls])
    kept = forward_call(tokens, band_mask, out_grad, shards, packed)
    done = backward_call(tokens, band_mask, out_grad, kept, [s.shape for s in shards])
    tile = done["small_result"]
    grads = [tile[i, : v.shape[0]] for i, v in enumerate(smalls)]
    return (
        done["output"],
        done["input_grad"],
        grads[0],
        grads[1],
        done["qkv_result"],
        grads[2],
        done["out_result"],
        grads[3],
        grads[4],
        grads[5],
        done["up_result"],
        grads[6],
        done["down_result"],
        grads[7],
    )


def solution(mesh):
    rows, flat = P(AXES, None), P(AXES)
    params = (flat, flat, rows, flat, rows, flat, flat, flat, rows, flat, rows, flat)
    fitted = tuple(mesh.shape[axis] for axis in AXES) == (8, 4)
    return jax.shard_map(
        body if fitted else body_plain,
        mesh=mesh,
        in_specs=(rows, rows, rows) + params,
        out_specs=(rows, rows) + params,
        check_vma=False,
    )
```

```python
import functools
import math

import jax
import jax.numpy as jnp
from jax import lax
from jax.experimental import pallas as pl
from jax.experimental.pallas import tpu as pltpu
from jax.sharding import PartitionSpec as P

HEAD = 64
HEAD_GROUP = 4
QBLOCK = 512


NORM_EPSILON = 1e-05
VMEM_BYTES = 62 << 20
AXES = ("wide", "narrow")


def normalize(values, gain, shift):
    centre = jnp.mean(values, axis=1, keepdims=True)
    centred = values - centre
    factor = lax.rsqrt(jnp.mean(centred * centred, axis=1, keepdims=True) + NORM_EPSILON)
    normed = centred * factor
    return (normed * gain + shift, normed, factor)


def normalize_back(upstream, normed, factor, gain):
    gain_grad = jnp.sum(upstream * normed, axis=0)
    shift_grad = jnp.sum(upstream, axis=0)
    scaled = upstream * gain
    inner = (
        scaled
        - jnp.mean(scaled, axis=1, keepdims=True)
        - normed * jnp.mean(scaled * normed, axis=1, keepdims=True)
    )
    return (factor * inner, gain_grad, shift_grad)


def gelu_slope(values):
    cumulative = 0.5 * (1.0 + lax.erf(values * (1.0 / math.sqrt(2.0))))
    return cumulative + values * jnp.exp(-0.5 * values * values) * (1.0 / math.sqrt(2.0 * math.pi))


def to_groups(matrix, count):
    return matrix.reshape(matrix.shape[0], count, -1).transpose(1, 0, 2)


def from_groups(stacked):
    return stacked.transpose(1, 0, 2).reshape(stacked.shape[1], -1)


def attend_forward(query_cols, key_cols, value_cols, key_live):
    row_count, span_cols = key_cols.shape
    head_width = span_cols // HEAD_GROUP
    scaling = 1.0 / math.sqrt(head_width)
    key_rows = key_cols.reshape(row_count, HEAD_GROUP, head_width)
    value_rows = value_cols.reshape(row_count, HEAD_GROUP, head_width)
    query_blocks = query_cols.reshape(row_count // QBLOCK, QBLOCK, HEAD_GROUP, head_width)

    def one_block(query_rows):
        scores = (
            jnp.einsum("qhd,khd->hqk", query_rows, key_rows, preferred_element_type=jnp.float32)
            * scaling
        )
        scores = jnp.where(key_live[None, None, :], scores, -jnp.inf)
        largest = jnp.max(scores, axis=2, keepdims=True)
        expo = jnp.exp(scores - largest)
        totals = jnp.sum(expo, axis=2, keepdims=True)
        weights_low = (expo / totals).astype(jnp.bfloat16)
        mixture = jnp.einsum(
            "hqk,khd->qhd", weights_low, value_rows, preferred_element_type=jnp.float32
        )
        return (mixture.reshape(QBLOCK, span_cols), largest[:, :, 0] + jnp.log(totals[:, :, 0]))

    mixture, logsum = lax.map(one_block, query_blocks)
    return (mixture.reshape(row_count, span_cols), logsum)


def attend_backward(query_cols, key_cols, value_cols, grad_cols, logsum, key_live):
    row_count, span_cols = key_cols.shape
    head_width = span_cols // HEAD_GROUP
    scaling = 1.0 / math.sqrt(head_width)
    key_rows = key_cols.reshape(row_count, HEAD_GROUP, head_width)
    value_rows = value_cols.reshape(row_count, HEAD_GROUP, head_width)
    query_blocks = query_cols.reshape(row_count // QBLOCK, QBLOCK, HEAD_GROUP, head_width)
    grad_blocks = grad_cols.reshape(row_count // QBLOCK, QBLOCK, HEAD_GROUP, head_width)

    def one_block(carry, items):
        key_acc, value_acc = carry
        query_rows, grad_rows, block_logsum = items
        scores = (
            jnp.einsum("qhd,khd->hqk", query_rows, key_rows, preferred_element_type=jnp.float32)
            * scaling
        )
        scores = jnp.where(key_live[None, None, :], scores, -jnp.inf)
        probs = jnp.exp(scores - block_logsum[:, :, None])
        value_acc = value_acc + jnp.einsum(
            "hqk,qhd->khd",
            probs.astype(jnp.bfloat16),
            grad_rows,
            preferred_element_type=jnp.float32,
        )
        prob_grad = jnp.einsum(
            "qhd,khd->hqk", grad_rows, value_rows, preferred_element_type=jnp.float32
        )
        inner = jnp.sum(probs * prob_grad, axis=2, keepdims=True)
        score_grad = (probs * (prob_grad - inner)).astype(jnp.bfloat16)
        query_grad = (
            jnp.einsum("hqk,khd->qhd", score_grad, key_rows, preferred_element_type=jnp.float32)
            * scaling
        )
        key_acc = (
            key_acc
            + jnp.einsum("hqk,qhd->khd", score_grad, query_rows, preferred_element_type=jnp.float32)
            * scaling
        )
        return ((key_acc, value_acc), query_grad.reshape(QBLOCK, span_cols))

    empty = jnp.zeros((row_count, HEAD_GROUP, head_width), jnp.float32)
    (key_grad, value_grad), query_grad = lax.scan(
        one_block, (empty, empty), (query_blocks, grad_blocks, logsum)
    )
    return (
        query_grad.reshape(row_count, span_cols),
        key_grad.reshape(row_count, span_cols),
        value_grad.reshape(row_count, span_cols),
    )


def gathered(shard):
    return lax.all_gather(shard.astype(jnp.bfloat16), AXES, axis=0, tiled=True)


def scattered(part):
    return lax.psum_scatter(part, AXES, scatter_dimension=0, tiled=True)


def body_plain(
    tokens,
    band_mask,
    out_grad,
    norm1_gain,
    norm1_shift,
    qkv_weight,
    qv_bias,
    out_weight,
    out_bias,
    norm2_gain,
    norm2_shift,
    up_weight,
    up_bias,
    down_weight,
    down_bias,
):
    row_count, width = tokens.shape
    group_count = width // (HEAD_GROUP * HEAD)
    present = jnp.repeat(band_mask[0].astype(jnp.float32), row_count // band_mask.shape[1])
    key_live = present > 0.5
    column_mask = present[:, None]
    gain_one, shift_one, w_qkv, b_qv, w_out, b_out = (
        gathered(norm1_gain),
        gathered(norm1_shift),
        gathered(qkv_weight),
        gathered(qv_bias),
        gathered(out_weight),
        gathered(out_bias),
    )
    inputs = tokens.astype(jnp.float32)
    normed_one, unit_one, factor_one = normalize(
        inputs, gain_one.astype(jnp.float32), shift_one.astype(jnp.float32)
    )
    normed_one = normed_one.astype(jnp.bfloat16)
    bias_wide = b_qv.astype(jnp.float32)
    bias_full = jnp.concatenate(
        [bias_wide[:width], jnp.zeros((width,), jnp.float32), bias_wide[width:]]
    )
    joined = (jnp.dot(normed_one, w_qkv, preferred_element_type=jnp.float32) + bias_full).astype(
        jnp.bfloat16
    )
    query_groups = to_groups(joined[:, :width], group_count)
    key_groups = to_groups(joined[:, width : 2 * width], group_count)
    value_groups = to_groups(joined[:, 2 * width :], group_count)
    mixture, logsum = lax.map(
        lambda items: attend_forward(items[0], items[1], items[2], key_live),
        (query_groups, key_groups, value_groups),
    )
    mixture = from_groups(mixture).astype(jnp.bfloat16)
    attention = jnp.dot(mixture, w_out, preferred_element_type=jnp.float32) + b_out.astype(
        jnp.float32
    )
    middle = inputs + column_mask * attention
    gain_two, shift_two, w_up, b_up, w_down, b_down = (
        gathered(norm2_gain),
        gathered(norm2_shift),
        gathered(up_weight),
        gathered(up_bias),
        gathered(down_weight),
        gathered(down_bias),
    )
    normed_two, unit_two, factor_two = normalize(
        middle, gain_two.astype(jnp.float32), shift_two.astype(jnp.float32)
    )
    normed_two = normed_two.astype(jnp.bfloat16)
    hidden = jnp.dot(normed_two, w_up, preferred_element_type=jnp.float32) + b_up.astype(
        jnp.float32
    )
    active = jax.nn.gelu(hidden, approximate=False).astype(jnp.bfloat16)
    branch = jnp.dot(active, w_down, preferred_element_type=jnp.float32) + b_down.astype(
        jnp.float32
    )
    output = (middle + column_mask * branch).astype(jnp.bfloat16)
    upstream = out_grad.astype(jnp.float32)
    branch_grad = (column_mask * upstream).astype(jnp.bfloat16)
    down_weight_grad = jnp.einsum(
        "tf,td->fd", active, branch_grad, preferred_element_type=jnp.float32
    )
    down_bias_grad = jnp.sum(branch_grad.astype(jnp.float32), axis=0)
    active_grad = jnp.einsum(
        "td,fd->tf", branch_grad, w_down, preferred_element_type=jnp.float32
    )
    hidden_grad = (active_grad * gelu_slope(hidden)).astype(jnp.bfloat16)
    up_weight_grad = jnp.einsum(
        "td,tf->df", normed_two, hidden_grad, preferred_element_type=jnp.float32
    )
    up_bias_grad = jnp.sum(hidden_grad.astype(jnp.float32), axis=0)
    normed_two_grad = jnp.einsum(
        "tf,df->td", hidden_grad, w_up, preferred_element_type=jnp.float32
    )
    middle_part, norm2_gain_grad, norm2_shift_grad = normalize_back(
        normed_two_grad, unit_two, factor_two, gain_two.astype(jnp.float32)
    )
    (
        norm2_gain_grad,
        norm2_shift_grad,
        up_weight_grad,
        up_bias_grad,
        down_weight_grad,
        down_bias_grad,
    ) = (
        scattered(norm2_gain_grad),
        scattered(norm2_shift_grad),
        scattered(up_weight_grad),
        scattered(up_bias_grad),
        scattered(down_weight_grad),
        scattered(down_bias_grad),
    )
    middle_grad = upstream + middle_part
    attention_grad = (column_mask * middle_grad).astype(jnp.bfloat16)
    out_weight_grad = jnp.einsum(
        "te,td->ed", mixture, attention_grad, preferred_element_type=jnp.float32
    )
    out_bias_grad = jnp.sum(attention_grad.astype(jnp.float32), axis=0)
    mixture_grad = jnp.einsum(
        "td,ed->te", attention_grad, w_out, preferred_element_type=jnp.float32
    ).astype(jnp.bfloat16)
    grad_groups = to_groups(mixture_grad, group_count)
    query_grad, key_grad, value_grad = lax.map(
        lambda items: attend_backward(items[0], items[1], items[2], items[3], items[4], key_live),
        (query_groups, key_groups, value_groups, grad_groups, logsum),
    )
    query_grad = from_groups(query_grad).astype(jnp.bfloat16)
    key_grad = from_groups(key_grad).astype(jnp.bfloat16)
    value_grad = from_groups(value_grad).astype(jnp.bfloat16)
    joined_grad = jnp.concatenate([query_grad, key_grad, value_grad], axis=1)
    qkv_weight_grad = jnp.einsum(
        "td,tc->dc", normed_one, joined_grad, preferred_element_type=jnp.float32
    )
    qv_bias_grad = jnp.concatenate(
        [
            jnp.sum(query_grad.astype(jnp.float32), axis=0),
            jnp.sum(value_grad.astype(jnp.float32), axis=0),
        ]
    )
    normed_one_grad = jnp.einsum(
        "tc,dc->td", joined_grad, w_qkv, preferred_element_type=jnp.float32
    )
    input_part, norm1_gain_grad, norm1_shift_grad = normalize_back(
        normed_one_grad, unit_one, factor_one, gain_one.astype(jnp.float32)
    )
    input_grad = (middle_grad + input_part).astype(jnp.bfloat16)
    (
        norm1_gain_grad,
        norm1_shift_grad,
        qkv_weight_grad,
        qv_bias_grad,
        out_weight_grad,
        out_bias_grad,
    ) = (
        scattered(norm1_gain_grad),
        scattered(norm1_shift_grad),
        scattered(qkv_weight_grad),
        scattered(qv_bias_grad),
        scattered(out_weight_grad),
        scattered(out_bias_grad),
    )
    return (
        output,
        input_grad,
        norm1_gain_grad,
        norm1_shift_grad,
        qkv_weight_grad,
        qv_bias_grad,
        out_weight_grad,
        out_bias_grad,
        norm2_gain_grad,
        norm2_shift_grad,
        up_weight_grad,
        up_bias_grad,
        down_weight_grad,
        down_bias_grad,
    )


MESH_ID = pl.DeviceIdType.MESH
VIA_X = (0, 2)
VIA_Y = (1, 3)
ORDER = (1, 3, 2)
SCORE_SCALE = math.log2(math.e) / math.sqrt(HEAD)
TILE = 384


class Place:
    def __init__(self):
        wide = lax.axis_index("wide")
        narrow = lax.axis_index("narrow")
        z, y = wide // 2, wide % 2
        x, c = narrow // 2, narrow % 2
        self.z, self.c = z, c
        self.zs = (z, z + 1 - 2 * (z % 2), (z + 2) % 4, 3 - z)
        self.q = y * 2 + x
        self.qx = y * 2 + (1 - x)
        self.qy = (1 - y) * 2 + x
        self.qd = (1 - y) * 2 + (1 - x)
        self.to_z = tuple((zz * 2 + y, x * 2 + c) for zz in self.zs)
        self.to_x = (z * 2 + y, (1 - x) * 2 + c)
        self.to_y = (z * 2 + 1 - y, x * 2 + c)
        self.to_c = (z * 2 + y, x * 2 + 1 - c)


def span(start, size, step):
    return pl.ds(pl.multiple_of(start, step), size)


def meet(place):
    barrier = pltpu.get_barrier_semaphore()
    peers = place.to_z[1:] + (place.to_x, place.to_y, place.to_c)
    for peer in peers:
        pl.semaphore_signal(barrier, inc=1, device_id=peer, device_id_type=MESH_ID)
    pl.semaphore_wait(barrier, len(peers))


def remote(source, target, send, recv, peer):
    return pltpu.make_async_remote_copy(
        src_ref=source,
        dst_ref=target,
        send_sem=send,
        recv_sem=recv,
        device_id=peer,
        device_id_type=MESH_ID,
    )


class Piece:
    COUNT = 19

    def __init__(self, place, send, recv):
        self.p = place
        self.send = send
        self.recv = recv
        self.sent = []

    def go(self, source, target, index, peer):
        remote(source(), target(), self.send.at[index], self.recv.at[index], peer).start()
        self.sent.append((source, target, index, peer))

    def got(self, target, index, peer):
        remote(target, target, self.send.at[index], self.recv.at[index], peer).wait_recv()

    def finish(self):
        for source, target, index, peer in self.sent:
            remote(source(), target(), self.send.at[index], self.recv.at[index], peer).wait_send()


class Gather(Piece):
    def __init__(self, place, own, block, column, other, send, recv):
        super().__init__(place, send, recv)
        self.own = own
        self.block = block
        self.column = column
        self.other = other

    def start_z(self):
        p = self.p
        for k in ORDER:
            self.go(self.own, lambda: self.block(p.z, p.q), k - 1, p.to_z[k])

    def start_xy(self):
        p = self.p
        self.go(self.own, lambda: self.block(p.z, p.q), 3, p.to_x)
        self.go(self.own, lambda: self.block(p.z, p.q), 9, p.to_y)

    def z(self, k):
        p = self.p
        here = lambda: self.block(p.zs[k], p.q)
        self.got(here(), k - 1, p.to_z[k])
        self.go(here, here, 3 + k, p.to_x)
        self.go(here, here, 9 + k, p.to_y)

    def share(self, index, q):
        column = lambda: self.column(q)
        self.go(column, column, index, self.p.to_c)

    def own_column(self):
        self.share(15, self.p.q)

    def xy(self, k):
        p = self.p
        from_x = lambda: self.block(p.zs[k], p.qx)
        self.got(from_x(), 3 + k, p.to_x)
        if k in VIA_X:
            self.go(from_x, from_x, 13 + VIA_X.index(k), p.to_y)
        from_y = lambda: self.block(p.zs[k], p.qy)
        self.got(from_y(), 9 + k, p.to_y)
        if k in VIA_Y:
            self.go(from_y, from_y, 7 + VIA_Y.index(k), p.to_x)

    def xy_columns(self):
        self.share(16, self.p.qx)
        self.share(17, self.p.qy)

    def d(self):
        p = self.p
        for i, k in enumerate(VIA_X):
            self.got(self.block(p.zs[k], p.qd), 13 + i, p.to_y)
        for i, k in enumerate(VIA_Y):
            self.got(self.block(p.zs[k], p.qd), 7 + i, p.to_x)
        self.share(18, p.qd)

    def c(self):
        p = self.p
        for i, q in enumerate((p.q, p.qx, p.qy, p.qd)):
            self.got(self.other(q), 15 + i, p.to_c)


class Scatter(Piece):
    def __init__(self, place, bufs, send, recv):
        super().__init__(place, send, recv)
        self.total, self.dx, self.dy, self.xr, self.yr, self.zr = bufs
        self.columns = (place.qd, place.qx, place.qy, place.q)

    def add(self, target, other):
        target[...] = (target[...].astype(jnp.float32) + other[...].astype(jnp.float32)).astype(
            target.dtype
        )

    def give(self, other):
        for i, q in enumerate(self.columns):
            self.go(
                lambda q=q: other(q), lambda q=q: self.total.at[:, q], 15 + i, self.p.to_c
            )

    def arrive(self, i):
        self.got(self.total.at[:, self.columns[i]], 15 + i, self.p.to_c)

    def take(self, i, mine):
        self.arrive(i)
        q = self.columns[i]
        for zz in range(4):
            self.add(self.total.at[zz, q], mine(zz, q))

    def diagonal(self):
        p = self.p
        for i in range(2):
            self.go(
                lambda i=i: self.total.at[p.zs[VIA_X[i]], p.qd],
                lambda i=i: self.dx.at[i],
                7 + i,
                p.to_x,
            )
            self.go(
                lambda i=i: self.total.at[p.zs[VIA_Y[i]], p.qd],
                lambda i=i: self.dy.at[i],
                13 + i,
                p.to_y,
            )

    def cross(self, k):
        p = self.p
        on_x = lambda: self.total.at[p.zs[k], p.qx]
        on_y = lambda: self.total.at[p.zs[k], p.qy]
        if k in VIA_Y:
            i = VIA_Y.index(k)
            self.go(on_y, lambda: self.yr.at[k], 9 + k, p.to_y)
            self.got(self.dy.at[i], 13 + i, p.to_y)
            self.add(on_x(), self.dy.at[i])
            self.go(on_x, lambda: self.xr.at[k], 3 + k, p.to_x)
        else:
            i = VIA_X.index(k)
            self.go(on_x, lambda: self.xr.at[k], 3 + k, p.to_x)
            self.got(self.dx.at[i], 7 + i, p.to_x)
            self.add(on_y(), self.dx.at[i])
            self.go(on_y, lambda: self.yr.at[k], 9 + k, p.to_y)

    def plane(self, k):
        p = self.p
        self.got(self.xr.at[k], 3 + k, p.to_x)
        self.got(self.yr.at[k], 9 + k, p.to_y)
        here = self.total.at[p.zs[k], p.q]
        return here, (
            here[...].astype(jnp.float32)
            + self.xr[k].astype(jnp.float32)
            + self.yr[k].astype(jnp.float32)
        )

    def spread(self, k):
        here, value = self.plane(k)
        here[...] = value.astype(here.dtype)
        self.go(
            lambda: self.total.at[self.p.zs[k], self.p.q],
            lambda: self.zr.at[k - 1],
            k - 1,
            self.p.to_z[k],
        )

    def last(self):
        p = self.p
        _, value = self.plane(0)
        for k in ORDER:
            self.got(self.zr.at[k - 1], k - 1, p.to_z[k])
            value = value + self.zr[k - 1].astype(jnp.float32)
        return value


def scatter_buffers(tail, kind):
    return [
        pltpu.VMEM((4, 4) + tail, kind),
        pltpu.VMEM((2,) + tail, kind),
        pltpu.VMEM((2,) + tail, kind),
        pltpu.VMEM((4,) + tail, kind),
        pltpu.VMEM((4,) + tail, kind),
        pltpu.VMEM((3,) + tail, kind),
    ]


WANTED = (
    "vec",
    "turned_two",
    "middle",
    "up_wide",
    "mixed_turned",
    "out_wide",
    "joined",
    "logsum",
    "turned_one",
    "qkv_wide",
)
MATRICES = ("qkv", "out", "up", "down")


def triples(**named):
    return [(name, one, two) for name, (one, two) in named.items()]


def pairs_of(**named):
    return list(named.items())


class Named:
    def __init__(self, names, refs):
        assert len(names) == len(refs)
        self.__dict__.update(zip(names, refs))


def loop(count, compute, slots=()):
    def step(i, carry):
        compute(i)
        for j, steps in enumerate(slots):
            if steps:

                @pl.when(i == j)
                def _(steps=steps):
                    for one in steps:
                        one()

        return carry

    lax.fori_loop(0, count, step, 0)


def dot(left, right):
    return jnp.dot(left, right, preferred_element_type=jnp.float32)


def dot_nt(left, right):
    return lax.dot_general(
        left, right, (((1,), (1,)), ((), ())), preferred_element_type=jnp.float32
    )


def dot_tn(left, right):
    return lax.dot_general(
        left, right, (((0,), (0,)), ((), ())), preferred_element_type=jnp.float32
    )


def head_only(values, e):
    lane = lax.broadcasted_iota(jnp.int32, values.shape, 1)
    return jnp.where((lane // HEAD) == e, values, jnp.zeros_like(values))


def fill_present(present, mask):
    groups = mask.shape[1]
    rows = present.shape[0] // groups
    for g in range(groups):
        present[g * rows : (g + 1) * rows, :] = jnp.full(
            (rows, 128), mask[0, g].astype(jnp.float32)
        )


def segments(width):
    return ((0, width, width // 32), (width, 2 * width, width // 16), (3 * width, 4 * width, width // 8))


def selection(width):
    parts = []
    for _, size, m in segments(width):
        lane = lax.broadcasted_iota(jnp.int32, (1, size), 1).astype(jnp.float32)
        rest = lane - m * jnp.floor((lane + 0.5) * (1.0 / m))
        row = lax.broadcasted_iota(jnp.int32, (128, size), 0).astype(jnp.float32)
        parts.append(jnp.where(row == rest, 1.0, 0.0).astype(jnp.bfloat16))
    return jnp.concatenate(parts, axis=1)


def owners(width):
    parts = []
    for _, size, m in segments(width):
        lane = lax.broadcasted_iota(jnp.int32, (1, size), 1).astype(jnp.float32)
        parts.append(jnp.floor((lane + 0.5) * (1.0 / m)))
    return jnp.concatenate(parts, axis=1)


def unit(values):
    centred = values - jnp.mean(values, axis=1, keepdims=True)
    factor = lax.rsqrt(jnp.mean(centred * centred, axis=1, keepdims=True) + NORM_EPSILON)
    return centred * factor, factor


def forward_kernel(names, *refs):
    r = Named(names, refs)
    place = Place()
    tokens, width = r.tokens.shape
    hidden = r.act.shape[0] * TILE
    pairs = width // 128
    shards = (r.qkv_shard, r.out_shard, r.up_shard, r.down_shard)
    owns = (r.qkv_own, r.out_own, r.up_own, r.down_own)
    sibs = (r.qkv_sib, r.out_sib, r.up_sib, r.down_sib)
    wides = (r.qkv_wide, r.out_wide, r.up_wide, r.down_wide)
    meet(place)
    first = place.c == 0

    def before(i):
        half = shards[i].shape[1] // 2
        return remote(
            shards[i].at[:, span((1 - place.c) * half, half, 128)],
            sibs[i],
            r.pre_send.at[i],
            r.pre_recv.at[i],
            place.to_c,
        )

    for i in range(4):
        before(i).start()
    r.small[...] = jnp.zeros_like(r.small)
    for i in range(8):
        vector = getattr(r, "vector%d" % i)
        r.small[i : i + 1, 0 : vector.shape[0]] = vector[...].reshape(1, -1)
    small = Gather(
        place,
        lambda: r.small,
        lambda zz, q: r.small_wide.at[zz, q, place.c],
        lambda q: r.small_wide.at[:, q, place.c],
        lambda q: r.small_wide.at[:, q, 1 - place.c],
        r.send.at[6],
        r.recv.at[6],
    )
    local = [pltpu.make_async_copy(r.small, r.small_wide.at[place.z, place.q, place.c], r.local.at[4])]
    local[0].start()
    small.start_z()
    small.start_xy()

    cuts = (
        (0, 0, 48, 0, 1152),
        (1, 0, 48, 0, 384),
        (2, 0, 48, 0, 768),
        (2, 0, 48, 768, 768),
        (3, 0, 96, 0, 384),
        (3, 96, 96, 0, 384),
    )
    pieces = []
    for j, (i, row, rows, col, cols) in enumerate(cuts):
        half = shards[i].shape[1] // 2

        def at(c, row=row, rows=rows, col=col, cols=cols, half=half):
            return (pl.ds(row, rows), span(c * half + col, cols, 128))

        pieces.append(
            Gather(
                place,
                lambda i=i, row=row, rows=rows, col=col, cols=cols: owns[i].at[
                    pl.ds(row, rows), pl.ds(col, cols)
                ],
                lambda zz, q, i=i, at=at: wides[i].at[(zz, q) + at(place.c)],
                lambda q, i=i, at=at: wides[i].at[(slice(None), q) + at(place.c)],
                lambda q, i=i, at=at: wides[i].at[(slice(None), q) + at(1 - place.c)],
                r.send.at[j],
                r.recv.at[j],
            )
        )
    for i in range(4):
        half = shards[i].shape[1] // 2
        cols = span(place.c * half, half, 128)
        before(i).wait_recv()
        mine = shards[i][:, cols]
        theirs = sibs[i][...]
        owns[i][...] = jnp.concatenate(
            [jnp.where(first, mine, theirs), jnp.where(first, theirs, mine)], axis=0
        ).astype(jnp.bfloat16)
        copy = pltpu.make_async_copy(
            owns[i], wides[i].at[place.z, place.q, :, cols], r.local.at[i]
        )
        copy.start()
        local.append(copy)
        for j, cut in enumerate(cuts):
            if cut[0] == i:
                pieces[j].start_z()
        if i == 0:
            pieces[0].start_xy()
    fill_present(r.present, r.mask)
    for copy in local:
        copy.wait()
    p0, p1, p2, p3, p4, p5 = pieces

    def z_steps(piece):
        return [lambda k=k: piece.z(k) for k in ORDER] + [piece.own_column]

    def xy_steps(piece):
        return [lambda k=k: piece.xy(k) for k in (0, 1, 3, 2)]

    def run(steps):
        for one in steps:
            one()

    outgoing = []

    def write(source, target, index):
        copy = pltpu.make_async_copy(source, target, r.write.at[index])
        copy.start()
        outgoing.append(copy)

    run(z_steps(small)[:3])
    run(z_steps(p0))
    small.own_column()
    run(xy_steps(small))
    small.xy_columns()
    p1.start_xy()
    p0.xy(0)
    small.d()
    small.c()

    rows = r.small_wide[...].reshape(256, 128).astype(jnp.bfloat16)
    picked = dot(rows, selection(width))
    owner = owners(width)
    total = jnp.zeros((8, 7 * width), jnp.float32)
    for d in range(32):
        total = total + jnp.where(owner == d, picked[d * 8 : d * 8 + 8], 0.0)
    r.vec[...] = total
    r.bias[:, 0:width] = total[2:3, width : 2 * width]
    r.bias[:, width : 2 * width] = jnp.zeros((1, width), jnp.float32)
    r.bias[:, 2 * width : 3 * width] = total[2:3, 2 * width : 3 * width]
    write(r.vec, r.vec_out, 0)

    def first_norm(t):
        rows = span(t * 128, 128, 128)
        normed, _ = unit(r.tokens[rows, :].astype(jnp.float32))
        value = normed * r.vec[0:1, 0:width] + r.vec[1:2, 0:width]
        r.normed[rows, :] = value.astype(jnp.bfloat16)
        r.turned_one[:, rows] = value.T.astype(jnp.bfloat16)

    loop(tokens // 128, first_norm)
    write(r.turned_one, r.turned_one_out, 1)
    run(xy_steps(p0)[1:])
    p0.xy_columns()
    run(z_steps(p1))
    p0.d()
    p2.start_xy()
    p0.c()
    write(r.qkv_wide, r.qkv_wide_out, 2)

    def project(t):
        cols = span(t * width, width, 128)
        r.joined[:, cols] = (
            dot(r.normed[...], r.qkv_wide[:, :, :, cols].reshape(width, width)) + r.bias[:, cols]
        ).astype(jnp.bfloat16)

    xy1 = xy_steps(p1)
    loop(3, project, [xy1[:2], xy1[2:3], xy1[3:] + [p1.xy_columns]])
    write(r.joined, r.joined_out, 3)

    def attend(hp):
        cols = span(hp * 128, 128, 128)
        query = r.joined[:, cols]
        key = r.joined[:, span(width + hp * 128, 128, 128)]
        value = r.joined[:, span(2 * width + hp * 128, 128, 128)].T
        live = r.present[:, 0:1] > 0.5
        mixed = []
        for e in range(2):
            scores = dot_nt(head_only(key, e), query) * SCORE_SCALE
            scores = jnp.where(live, scores, -jnp.inf)
            largest = jnp.max(scores, axis=0, keepdims=True)
            expo = jnp.exp2(scores - largest)
            totals = jnp.sum(expo, axis=0, keepdims=True)
            probs = (expo * (1.0 / totals)).astype(jnp.bfloat16)
            mixed.append(dot(value[HEAD * e : HEAD * (e + 1)], probs))
            r.logsum[hp, e : e + 1, :] = largest + jnp.log2(totals)
        both = jnp.concatenate(mixed, axis=0)
        r.mixed_turned[cols, :] = both.astype(jnp.bfloat16)
        r.mixed[:, cols] = both.T.astype(jnp.bfloat16)

    z2 = z_steps(p2)
    xy2 = xy_steps(p2)
    loop(
        pairs,
        attend,
        [z2, [p1.d, p3.start_xy], xy2[:1], xy2[1:2], xy2[2:3], xy2[3:] + [p2.xy_columns]],
    )
    write(r.logsum, r.logsum_out, 4)
    write(r.mixed_turned, r.mixed_turned_out, 5)
    p1.c()
    run(z_steps(p3))
    write(r.out_wide, r.out_wide_out, 6)
    r.middle[...] = dot(r.mixed[...], r.out_wide[...].reshape(width, width))

    def second_norm(t):
        rows = span(t * 128, 128, 128)
        present = r.present[rows, 0:1]
        middle = r.tokens[rows, :].astype(jnp.float32) + present * (
            r.middle[rows, :] + r.vec[3:4, 0:width]
        )
        r.middle[rows, :] = middle
        normed, _ = unit(middle)
        value = normed * r.vec[4:5, 0:width] + r.vec[5:6, 0:width]
        r.normed[rows, :] = value.astype(jnp.bfloat16)
        r.turned_two[:, rows] = value.T.astype(jnp.bfloat16)
        r.grad_low[rows, :] = (present * r.out_grad[rows, :].astype(jnp.float32)).astype(
            jnp.bfloat16
        )

    loop(tokens // 128, second_norm)
    write(r.middle, r.middle_out, 7)
    write(r.turned_two, r.turned_two_out, 8)
    p2.d()
    p4.start_xy()
    p2.c()

    def expand(t):
        cols = span(t * TILE, TILE, 128)
        value = (
            dot(r.normed[...], r.up_wide[:, :, :, cols].reshape(width, TILE))
            + r.vec[6:7, span(3 * width + t * TILE, TILE, 128)]
        )
        cumulative = 0.5 * (1.0 + lax.erf(value * (1.0 / math.sqrt(2.0))))
        r.act[t] = (value * cumulative).astype(jnp.bfloat16)
        r.slope[t] = cumulative + value * jnp.exp(-0.5 * value * value) * (
            1.0 / math.sqrt(2.0 * math.pi)
        )

    def down_grad(t):
        grad = dot_tn(r.act[t], r.grad_low[...]).astype(jnp.bfloat16)
        r.down_grad[t // 2, pl.ds((t % 2) * 2, 2)] = grad.reshape(2, TILE // 2, width)

    xy3 = xy_steps(p3)
    loop(4, lambda u: expand(u + 2 * (u // 2)), [[s] for s in xy3])
    p3.xy_columns()
    run(z_steps(p4))
    loop(4, lambda u: down_grad(u + 2 * (u // 2)))
    p3.d()
    p5.start_xy()
    p3.c()
    write(r.up_wide, r.up_wide_out, 9)
    xy4 = xy_steps(p4)
    loop(4, lambda u: expand(u + 2 * (u // 2) + 2), [[s] for s in xy4])
    p4.xy_columns()
    write(r.act, r.act_out, 10)
    write(r.slope, r.slope_out, 11)
    run(z_steps(p5))
    loop(4, lambda u: down_grad(u + 2 * (u // 2) + 2))
    write(r.down_grad, r.down_grad_out, 12)
    p4.d()
    run(xy_steps(p5))
    p5.xy_columns()
    p4.c()
    p5.d()
    p5.c()
    write(r.down_wide, r.down_wide_out, 13)
    for i in range(4):
        before(i).wait_send()
    for piece in [small] + pieces:
        piece.finish()
    for copy in outgoing:
        copy.wait()


def forward_call(tokens, band_mask, out_grad, shards, smalls):
    bf16, f32 = jnp.bfloat16, jnp.float32
    count, width = tokens.shape
    shapes = [s.shape for s in shards]
    hidden = shapes[2][1]
    tiles = hidden // TILE
    vmem = pl.BlockSpec(memory_space=pltpu.VMEM)
    inputs = triples(
        tokens=(tokens, vmem),
        mask=(band_mask, pl.BlockSpec(memory_space=pltpu.SMEM)),
        out_grad=(out_grad, vmem),
        qkv_shard=(shards[0], vmem),
        out_shard=(shards[1], vmem),
        up_shard=(shards[2], vmem),
        down_shard=(shards[3], vmem),
    ) + [("vector%d" % i, v, vmem) for i, v in enumerate(smalls)]
    kept = triples(
        vec=((8, 7 * width), f32),
        turned_one=((width, count), bf16),
        qkv_wide=((4, 4, 2 * shapes[0][0], shapes[0][1]), bf16),
        joined=((count, 3 * width), bf16),
        logsum=((width // 128, 8, count), f32),
        mixed_turned=((width, count), bf16),
        out_wide=((4, 4, 2 * shapes[1][0], shapes[1][1]), bf16),
        middle=((count, width), f32),
        turned_two=((width, count), bf16),
        up_wide=((4, 4, 2 * shapes[2][0], shapes[2][1]), bf16),
        act=((tiles, count, TILE), bf16),
        slope=((tiles, count, TILE), f32),
        down_grad=((4, 4, 2 * shapes[3][0], shapes[3][1]), bf16),
        down_wide=((4, 4, 2 * shapes[3][0], shapes[3][1]), bf16),
    )
    scratch = [(name, pltpu.VMEM(shape, kind)) for name, shape, kind in kept]
    for name, (rows, cols) in zip(MATRICES, shapes):
        scratch.append((name + "_own", pltpu.VMEM((2 * rows, cols // 2), bf16)))
        scratch.append((name + "_sib", pltpu.VMEM((rows, cols // 2), f32)))
    scratch += pairs_of(
        small=pltpu.VMEM((8, 128), f32),
        small_wide=pltpu.VMEM((4, 4, 2, 8, 128), f32),
        present=pltpu.VMEM((count, 128), f32),
        bias=pltpu.VMEM((1, 3 * width), f32),
        normed=pltpu.VMEM((count, width), bf16),
        mixed=pltpu.VMEM((count, width), bf16),
        grad_low=pltpu.VMEM((count, width), bf16),
        send=pltpu.SemaphoreType.DMA((7, Piece.COUNT)),
        recv=pltpu.SemaphoreType.DMA((7, Piece.COUNT)),
        pre_send=pltpu.SemaphoreType.DMA((4,)),
        pre_recv=pltpu.SemaphoreType.DMA((4,)),
        local=pltpu.SemaphoreType.DMA((5,)),
        write=pltpu.SemaphoreType.DMA((len(kept),)),
    )
    names = (
        [name for name, _, _ in inputs]
        + [name + "_out" for name, _, _ in kept]
        + [name for name, _ in scratch]
    )
    results = pl.pallas_call(
        functools.partial(forward_kernel, names),
        out_shape=tuple(jax.ShapeDtypeStruct(shape, kind) for _, shape, kind in kept),
        in_specs=[spec for _, _, spec in inputs],
        out_specs=(pl.BlockSpec(memory_space=pl.ANY),) * len(kept),
        scratch_shapes=[kind for _, kind in scratch],
        compiler_params=pltpu.CompilerParams(
            collective_id=0, has_side_effects=True, vmem_limit_bytes=VMEM_BYTES
        ),
        name="forward",
    )(*[array for _, array, _ in inputs])
    return dict(zip([name for name, _, _ in kept], results))


def backward_kernel(names, *refs):
    r = Named(names, refs)
    place = Place()
    tokens, width = r.tokens.shape
    hidden = r.dpre.shape[1]
    pairs = width // 128
    tiles = hidden // TILE
    c = place.c

    def fetch(name, index):
        return pltpu.make_async_copy(getattr(r, name + "_in"), getattr(r, name), r.load.at[index])

    wanted = WANTED

    def need(*some):
        for name in some:
            fetch(name, wanted.index(name)).wait()

    def stream(t, slot):
        return (
            pltpu.make_async_copy(r.act_in.at[t], r.act.at[slot], r.tile.at[0, slot]),
            pltpu.make_async_copy(r.slope_in.at[t], r.slope.at[slot], r.tile.at[1, slot]),
            pltpu.make_async_copy(
                r.down_wide_in.at[t // 2, pl.ds((t % 2) * 2, 2)],
                r.down_tile.at[slot],
                r.tile.at[2, slot],
            ),
        )

    def down_mine(s):
        return pltpu.make_async_copy(
            r.down_grad_in.at[:, :, pl.ds(96 * s, 96), span(c * 384, 384, 128)],
            r.down_mine.at[s],
            r.mine.at[s],
        )

    for s in range(2):
        down_mine(s).start()
    for copy in stream(0, 0):
        copy.start()
    for i, name in enumerate(wanted):
        fetch(name, i).start()
    meet(place)
    pieces = []
    for j in range(9):
        bufs = [getattr(r, "piece%d_%d" % (j, b)) for b in range(6)]
        pieces.append(Scatter(place, bufs, r.send.at[j], r.recv.at[j]))
    d0, d1, u0, u1, o, q0, q1, q2, small = pieces
    for s, piece in enumerate((d0, d1)):
        piece.give(
            lambda q, s=s: r.down_grad_in.at[
                :, q, pl.ds(96 * s, 96), span((1 - c) * 384, 384, 128)
            ]
        )
    fill_present(r.present, r.mask)
    r.sums[...] = jnp.zeros_like(r.sums)
    r.acc[...] = jnp.zeros_like(r.acc)

    def mask_grad(t):
        rows = span(t * 128, 128, 128)
        low = (r.present[rows, 0:1] * r.out_grad[rows, :].astype(jnp.float32)).astype(jnp.bfloat16)
        r.grad_low[rows, :] = low
        r.sums[7:8, 0:width] += jnp.sum(low.astype(jnp.float32), axis=0, keepdims=True)

    loop(tokens // 128, mask_grad)

    def take_down(piece, s, i):
        if i == 0:
            down_mine(s).wait()
        piece.take(i, lambda zz, q: r.down_mine.at[s, zz, q])

    def narrow(t):
        slot = t % 2
        for copy in stream(t, slot):
            copy.wait()

        @pl.when(t + 1 < tiles)
        def _():
            for copy in stream(t + 1, 1 - slot):
                copy.start()

        cols = span(t * TILE, TILE, 128)
        weights = r.down_tile[slot].reshape(TILE, width)
        r.acc[...] += dot(r.act[slot], weights)
        grad = (dot_nt(r.grad_low[...], weights) * r.slope[slot]).astype(jnp.bfloat16)
        r.dpre[:, cols] = grad
        r.sums[6:7, span(3 * width + t * TILE, TILE, 128)] = jnp.sum(
            grad.astype(jnp.float32), axis=0, keepdims=True
        )

    def cross_steps(piece):
        return [lambda k=k: piece.cross(k) for k in (1, 3, 2, 0)]

    def spread_steps(piece):
        return [lambda k=k: piece.spread(k) for k in ORDER]

    def run(steps):
        for one in steps:
            one()

    xd0, xd1, xu0, xu1, xo = [cross_steps(p) for p in (d0, d1, u0, u1, o)]
    take_down(d0, 0, 0)
    d0.diagonal()
    loop(
        tiles,
        narrow,
        [
            [lambda: take_down(d0, 0, 1), lambda: take_down(d0, 0, 2)],
            [lambda: take_down(d1, 1, 0), d1.diagonal],
            xd0[:1],
            xd0[1:2] + [lambda: take_down(d1, 1, 1)],
            xd0[2:3] + [lambda: take_down(d1, 1, 2)],
            xd0[3:] + [lambda: take_down(d0, 0, 3)],
            [lambda: take_down(d1, 1, 3)],
            xd1[:1],
        ],
    )

    need("vec", "middle")

    def finish_output(t):
        rows = span(t * 128, 128, 128)
        r.output[rows, :] = (
            r.middle[rows, :]
            + r.present[rows, 0:1] * (r.acc[rows, :] + r.vec[7:8, 0:width])
        ).astype(jnp.bfloat16)

    need("turned_two", "up_wide")

    def up_part(side, s):
        cols = span(side * (hidden // 2) + 768 * s, 768, 128)
        return dot(r.turned_two[...], r.dpre[:, cols]).reshape(4, 4, 48, 768)

    for s, (piece, part) in enumerate(((u0, r.up_part0), (u1, r.up_part1))):
        part[...] = up_part(1 - c, s).astype(jnp.bfloat16)
        piece.give(lambda q, part=part: part.at[:, q])
    run(xd1[1:2])
    for s, piece in enumerate((u0, u1)):
        for i in range(4):
            piece.arrive(i)
        piece.total[...] = (
            piece.total[...].astype(jnp.float32) + up_part(c, s)
        ).astype(jnp.bfloat16)
        if s == 0:
            piece.diagonal()
            run(xd1[2:])
    run(spread_steps(d0))
    u1.diagonal()
    loop(tokens // 128, finish_output)
    r.acc[...] = dot_nt(r.dpre[...], r.up_wide[...].reshape(width, hidden))

    def second_back(t):
        rows = span(t * 128, 128, 128)
        normed, factor = unit(r.middle[rows, :])
        up = r.acc[rows, :]
        r.sums[4:5, 0:width] += jnp.sum(up * normed, axis=0, keepdims=True)
        r.sums[5:6, 0:width] += jnp.sum(up, axis=0, keepdims=True)
        scaled = up * r.vec[4:5, 0:width]
        inner = (
            scaled
            - jnp.mean(scaled, axis=1, keepdims=True)
            - normed * jnp.mean(scaled * normed, axis=1, keepdims=True)
        )
        grad = r.out_grad[rows, :].astype(jnp.float32) + factor * inner
        r.middle[rows, :] = grad
        low = (r.present[rows, 0:1] * grad).astype(jnp.bfloat16)
        r.attention_low[rows, :] = low
        r.sums[3:4, 0:width] += jnp.sum(low.astype(jnp.float32), axis=0, keepdims=True)

    loop(tokens // 128, second_back, [xu0[:1], xu0[1:2], xu0[2:3], xu0[3:]])
    need("mixed_turned", "out_wide")

    def out_part(side):
        cols = span(side * (width // 2), width // 2, 128)
        return dot(r.mixed_turned[...], r.attention_low[:, cols]).reshape(4, 4, 48, width // 2)

    r.out_part[...] = out_part(1 - c).astype(jnp.bfloat16)
    o.give(lambda q: r.out_part.at[:, q])
    r.mixed_grad[...] = dot_nt(r.attention_low[...], r.out_wide[...].reshape(width, width)).astype(
        jnp.bfloat16
    )
    for i in range(4):
        o.arrive(i)
    o.total[...] = (o.total[...].astype(jnp.float32) + out_part(c)).astype(jnp.bfloat16)
    o.diagonal()
    run(spread_steps(d1))
    need("joined", "logsum")

    def attend_back(hp):
        cols = span(hp * 128, 128, 128)
        key_cols = span(width + hp * 128, 128, 128)
        value_cols = span(2 * width + hp * 128, 128, 128)
        query = r.joined[:, cols]
        key = r.joined[:, key_cols]
        value = r.joined[:, value_cols]
        grad = r.mixed_grad[:, cols]
        turned = key.T
        live = r.present[:, 0:1] > 0.5
        value_grad = jnp.zeros((tokens, 128), jnp.float32)
        key_grad = jnp.zeros((tokens, 128), jnp.float32)
        query_grad = []
        for e in range(2):
            scores = dot_nt(head_only(key, e), query) * SCORE_SCALE
            scores = jnp.where(live, scores, -jnp.inf)
            probs = jnp.exp2(scores - r.logsum[hp, e : e + 1, :])
            back = dot_nt(head_only(value, e), grad)
            inner = jnp.sum(probs * back, axis=0, keepdims=True)
            score_grad = (probs * (back - inner)).astype(jnp.bfloat16)
            value_grad = value_grad + dot(probs.astype(jnp.bfloat16), head_only(grad, e))
            key_grad = key_grad + dot(score_grad, head_only(query, e))
            query_grad.append(dot(turned[HEAD * e : HEAD * (e + 1)], score_grad))
        scale = 1.0 / math.sqrt(HEAD)
        query_low = (jnp.concatenate(query_grad, axis=0).T * scale).astype(jnp.bfloat16)
        value_low = value_grad.astype(jnp.bfloat16)
        r.joined_grad[:, cols] = query_low
        r.joined_grad[:, key_cols] = (key_grad * scale).astype(jnp.bfloat16)
        r.joined_grad[:, value_cols] = value_low
        r.sums[2:3, span(width + hp * 128, 128, 128)] = jnp.sum(
            query_low.astype(jnp.float32), axis=0, keepdims=True
        )
        r.sums[2:3, span(2 * width + hp * 128, 128, 128)] = jnp.sum(
            value_low.astype(jnp.float32), axis=0, keepdims=True
        )

    loop(
        pairs,
        attend_back,
        [xu1[:1], xu1[1:2], xu1[2:3], xu1[3:] + spread_steps(u0)[:1], spread_steps(u0)[1:], xo],
    )

    need("turned_one", "qkv_wide")

    def qkv_part(side, s):
        cols = span(side * (3 * width // 2) + 384 * s, 384, 128)
        return dot(r.turned_one[...], r.joined_grad[:, cols]).reshape(4, 4, 48, 384)

    qs = (q0, q1, q2)
    for s, (piece, part) in enumerate(zip(qs, (r.qkv_part0, r.qkv_part1, r.qkv_part2))):
        part[...] = qkv_part(1 - c, s).astype(jnp.bfloat16)
        piece.give(lambda q, part=part: part.at[:, q])
    for s, piece in enumerate(qs):
        for i in range(4):
            piece.arrive(i)
        piece.total[...] = (
            piece.total[...].astype(jnp.float32) + qkv_part(c, s)
        ).astype(jnp.bfloat16)
        piece.diagonal()
    run(spread_steps(u1))
    r.acc[...] = dot_nt(r.joined_grad[...], r.qkv_wide[...].reshape(width, 3 * width))

    def first_back(t):
        rows = span(t * 128, 128, 128)
        normed, factor = unit(r.tokens[rows, :].astype(jnp.float32))
        up = r.acc[rows, :]
        r.sums[0:1, 0:width] += jnp.sum(up * normed, axis=0, keepdims=True)
        r.sums[1:2, 0:width] += jnp.sum(up, axis=0, keepdims=True)
        scaled = up * r.vec[0:1, 0:width]
        inner = (
            scaled
            - jnp.mean(scaled, axis=1, keepdims=True)
            - normed * jnp.mean(scaled * normed, axis=1, keepdims=True)
        )
        r.input_grad[rows, :] = (r.middle[rows, :] + factor * inner).astype(jnp.bfloat16)

    loop(tokens // 128, first_back)
    owner = owners(width)
    sums = r.sums[...]
    high = sums.astype(jnp.bfloat16)
    rest = sums - high.astype(jnp.float32)
    mid = rest.astype(jnp.bfloat16)
    low = (rest - mid.astype(jnp.float32)).astype(jnp.bfloat16)
    chosen = selection(width)
    tile = jnp.zeros((256, 128), jnp.float32)
    for part in (high, mid, low):
        part = part.astype(jnp.float32)
        spreaded = jnp.concatenate(
            [jnp.where(owner == d, part, 0.0) for d in range(32)], axis=0
        ).astype(jnp.bfloat16)
        tile = tile + dot_nt(spreaded, chosen)
    r.small_part[...] = tile.reshape(4, 4, 2, 8, 128)
    small.give(lambda q: r.small_part.at[:, q, 1 - c])
    run(cross_steps(q0))
    for i in range(4):
        small.take(i, lambda zz, q: r.small_part.at[zz, q, c])
    small.diagonal()
    run(spread_steps(o))
    run(cross_steps(q1))
    run(cross_steps(small))
    run(spread_steps(q0))
    run(cross_steps(q2))
    run(spread_steps(small))

    finals = (r.down_final, r.up_final, r.out_final, r.qkv_final)
    others = (r.down_other, r.up_other, r.out_other, r.qkv_other)
    results = (r.down_result, r.up_result, r.out_result, r.qkv_result)

    def swap(i):
        rows = results[i].shape[0]
        return remote(
            finals[i].at[span((1 - c) * rows, rows, 8)],
            others[i],
            r.end_send.at[i],
            r.end_recv.at[i],
            place.to_c,
        )

    def close(i):
        rows, cols = results[i].shape
        swap(i).start()
        results[i][:, span(c * (cols // 2), cols // 2, 128)] = finals[i][span(c * rows, rows, 8)]

    def settle(i):
        cols = results[i].shape[1]
        swap(i).wait_recv()
        results[i][:, span((1 - c) * (cols // 2), cols // 2, 128)] = others[i][...]

    r.down_final[0:96, :] = d0.last()
    r.down_final[96:192, :] = d1.last()
    close(0)
    r.up_final[:, 0:768] = u0.last()
    r.up_final[:, 768:1536] = u1.last()
    close(1)
    r.out_final[...] = o.last()
    close(2)
    run(spread_steps(q1))
    r.qkv_final[:, 0:384] = q0.last()
    run(spread_steps(q2))
    r.small_result[...] = small.last()
    r.qkv_final[:, 384:768] = q1.last()
    settle(0)
    settle(1)
    settle(2)
    r.qkv_final[:, 768:1152] = q2.last()
    close(3)
    settle(3)
    for i in range(4):
        swap(i).wait_send()
    for piece in pieces:
        piece.finish()


def backward_call(tokens, band_mask, out_grad, kept, shapes):
    bf16, f32 = jnp.bfloat16, jnp.float32
    count, width = tokens.shape
    hidden = shapes[2][1]
    vmem = pl.BlockSpec(memory_space=pltpu.VMEM)
    anywhere = pl.BlockSpec(memory_space=pl.ANY)
    inputs = triples(
        tokens=(tokens, vmem),
        mask=(band_mask, pl.BlockSpec(memory_space=pltpu.SMEM)),
        out_grad=(out_grad, vmem),
    ) + [(name + "_in", array, anywhere) for name, array in kept.items()]
    outs = triples(
        output=((count, width), bf16),
        input_grad=((count, width), bf16),
        qkv_result=(shapes[0], f32),
        out_result=(shapes[1], f32),
        up_result=(shapes[2], f32),
        down_result=(shapes[3], f32),
        small_result=((8, 128), f32),
    )
    tails = (
        [((96, 384), bf16)] * 2
        + [((48, 768), bf16)] * 2
        + [((48, 384), bf16)] * 4
        + [((8, 128), f32)]
    )
    scratch = []
    for j, (tail, kind) in enumerate(tails):
        for b, one in enumerate(scatter_buffers(tail, kind)):
            scratch.append(("piece%d_%d" % (j, b), one))
    for name in WANTED:
        scratch.append((name, pltpu.VMEM(kept[name].shape, kept[name].dtype)))
    for name, (rows, cols) in zip(MATRICES, shapes):
        scratch.append((name + "_final", pltpu.VMEM((2 * rows, cols // 2), f32)))
        scratch.append((name + "_other", pltpu.VMEM((rows, cols // 2), f32)))
    scratch += pairs_of(
        act=pltpu.VMEM((2, count, TILE), bf16),
        slope=pltpu.VMEM((2, count, TILE), f32),
        down_tile=pltpu.VMEM((2, 2, TILE // 2, width), bf16),
        down_mine=pltpu.VMEM((2, 4, 4, 96, 384), bf16),
        up_part0=pltpu.VMEM((4, 4, 48, 768), bf16),
        up_part1=pltpu.VMEM((4, 4, 48, 768), bf16),
        out_part=pltpu.VMEM((4, 4, 48, 384), bf16),
        qkv_part0=pltpu.VMEM((4, 4, 48, 384), bf16),
        qkv_part1=pltpu.VMEM((4, 4, 48, 384), bf16),
        qkv_part2=pltpu.VMEM((4, 4, 48, 384), bf16),
        small_part=pltpu.VMEM((4, 4, 2, 8, 128), f32),
        present=pltpu.VMEM((count, 128), f32),
        sums=pltpu.VMEM((8, 7 * width), f32),
        acc=pltpu.VMEM((count, width), f32),
        grad_low=pltpu.VMEM((count, width), bf16),
        dpre=pltpu.VMEM((count, hidden), bf16),
        attention_low=pltpu.VMEM((count, width), bf16),
        mixed_grad=pltpu.VMEM((count, width), bf16),
        joined_grad=pltpu.VMEM((count, 3 * width), bf16),
        send=pltpu.SemaphoreType.DMA((len(tails), Piece.COUNT)),
        recv=pltpu.SemaphoreType.DMA((len(tails), Piece.COUNT)),
        end_send=pltpu.SemaphoreType.DMA((4,)),
        end_recv=pltpu.SemaphoreType.DMA((4,)),
        load=pltpu.SemaphoreType.DMA((10,)),
        tile=pltpu.SemaphoreType.DMA((3, 2)),
        mine=pltpu.SemaphoreType.DMA((2,)),
    )
    names = (
        [name for name, _, _ in inputs] + [name for name, _, _ in outs] + [name for name, _ in scratch]
    )
    results = pl.pallas_call(
        functools.partial(backward_kernel, names),
        out_shape=tuple(jax.ShapeDtypeStruct(shape, kind) for _, shape, kind in outs),
        in_specs=[spec for _, _, spec in inputs],
        out_specs=(vmem,) * len(outs),
        scratch_shapes=[kind for _, kind in scratch],
        compiler_params=pltpu.CompilerParams(
            collective_id=1, has_side_effects=True, vmem_limit_bytes=VMEM_BYTES
        ),
        name="backward",
    )(*[array for _, array, _ in inputs])
    return results


def deliver_kernel(count, *refs):
    sources, tile = refs[:count], refs[count]
    targets = refs[count + 1 : 2 * count + 1]
    vectors = refs[2 * count + 1 : -1]
    copies = [
        pltpu.make_async_copy(source, target, refs[-1].at[i])
        for i, (source, target) in enumerate(zip(sources, targets))
    ]
    for copy in copies:
        copy.start()
    for i, vector in enumerate(vectors):
        vector[...] = tile[i, 0 : vector.shape[0]]
    for copy in copies:
        copy.wait()


def deliver(whole, tile, sizes):
    count = len(whole)
    anywhere = pl.BlockSpec(memory_space=pl.ANY)
    vmem = pl.BlockSpec(memory_space=pltpu.VMEM)
    return pl.pallas_call(
        functools.partial(deliver_kernel, count),
        out_shape=[jax.ShapeDtypeStruct(a.shape, a.dtype) for a in whole]
        + [jax.ShapeDtypeStruct((m,), jnp.float32) for m in sizes],
        in_specs=[anywhere] * count + [vmem],
        out_specs=[anywhere] * count + [vmem] * len(sizes),
        scratch_shapes=[pltpu.SemaphoreType.DMA((count,))],
        name="deliver",
    )(*whole, tile)


def body(
    tokens,
    band_mask,
    out_grad,
    norm1_gain,
    norm1_shift,
    qkv_weight,
    qv_bias,
    out_weight,
    out_bias,
    norm2_gain,
    norm2_shift,
    up_weight,
    up_bias,
    down_weight,
    down_bias,
):
    smalls = (norm1_gain, norm1_shift, qv_bias, out_bias, norm2_gain, norm2_shift, up_bias, down_bias)
    shards = (qkv_weight, out_weight, up_weight, down_weight)
    kept = forward_call(tokens, band_mask, out_grad, shards, smalls)
    *whole, tile = backward_call(tokens, band_mask, out_grad, kept, [s.shape for s in shards])
    output, input_grad, qkv, out, up, down, *grads = deliver(
        whole, tile, [v.shape[0] for v in smalls]
    )
    return (
        output,
        input_grad,
        grads[0],
        grads[1],
        qkv,
        grads[2],
        out,
        grads[3],
        grads[4],
        grads[5],
        up,
        grads[6],
        down,
        grads[7],
    )


def solution(mesh):
    rows, flat = P(AXES, None), P(AXES)
    params = (flat, flat, rows, flat, rows, flat, flat, flat, rows, flat, rows, flat)
    fitted = tuple(mesh.shape[axis] for axis in AXES) == (8, 4)
    return jax.shard_map(
        body if fitted else body_plain,
        mesh=mesh,
        in_specs=(rows, rows, rows) + params,
        out_specs=(rows, rows) + params,
        check_vma=False,
    )
```

```python
import functools
import math

import jax
import jax.numpy as jnp
from jax import lax
from jax.experimental import pallas as pl
from jax.experimental.pallas import tpu as pltpu
from jax.sharding import PartitionSpec as P

HEAD = 64
HEAD_GROUP = 4
QBLOCK = 512


NORM_EPSILON = 1e-05
VMEM_BYTES = 127 << 19
AXES = ("wide", "narrow")


def normalize(values, gain, shift):
    centre = jnp.mean(values, axis=1, keepdims=True)
    centred = values - centre
    factor = lax.rsqrt(jnp.mean(centred * centred, axis=1, keepdims=True) + NORM_EPSILON)
    normed = centred * factor
    return (normed * gain + shift, normed, factor)


def normalize_back(upstream, normed, factor, gain):
    gain_grad = jnp.sum(upstream * normed, axis=0)
    shift_grad = jnp.sum(upstream, axis=0)
    scaled = upstream * gain
    inner = (
        scaled
        - jnp.mean(scaled, axis=1, keepdims=True)
        - normed * jnp.mean(scaled * normed, axis=1, keepdims=True)
    )
    return (factor * inner, gain_grad, shift_grad)


def gelu_slope(values):
    cumulative = 0.5 * (1.0 + lax.erf(values * (1.0 / math.sqrt(2.0))))
    return cumulative + values * jnp.exp(-0.5 * values * values) * (1.0 / math.sqrt(2.0 * math.pi))


def to_groups(matrix, count):
    return matrix.reshape(matrix.shape[0], count, -1).transpose(1, 0, 2)


def from_groups(stacked):
    return stacked.transpose(1, 0, 2).reshape(stacked.shape[1], -1)


def attend_forward(query_cols, key_cols, value_cols, key_live):
    row_count, span_cols = key_cols.shape
    head_width = span_cols // HEAD_GROUP
    scaling = 1.0 / math.sqrt(head_width)
    key_rows = key_cols.reshape(row_count, HEAD_GROUP, head_width)
    value_rows = value_cols.reshape(row_count, HEAD_GROUP, head_width)
    query_blocks = query_cols.reshape(row_count // QBLOCK, QBLOCK, HEAD_GROUP, head_width)

    def one_block(query_rows):
        scores = (
            jnp.einsum("qhd,khd->hqk", query_rows, key_rows, preferred_element_type=jnp.float32)
            * scaling
        )
        scores = jnp.where(key_live[None, None, :], scores, -jnp.inf)
        largest = jnp.max(scores, axis=2, keepdims=True)
        expo = jnp.exp(scores - largest)
        totals = jnp.sum(expo, axis=2, keepdims=True)
        weights_low = (expo / totals).astype(jnp.bfloat16)
        mixture = jnp.einsum(
            "hqk,khd->qhd", weights_low, value_rows, preferred_element_type=jnp.float32
        )
        return (mixture.reshape(QBLOCK, span_cols), largest[:, :, 0] + jnp.log(totals[:, :, 0]))

    mixture, logsum = lax.map(one_block, query_blocks)
    return (mixture.reshape(row_count, span_cols), logsum)


def attend_backward(query_cols, key_cols, value_cols, grad_cols, logsum, key_live):
    row_count, span_cols = key_cols.shape
    head_width = span_cols // HEAD_GROUP
    scaling = 1.0 / math.sqrt(head_width)
    key_rows = key_cols.reshape(row_count, HEAD_GROUP, head_width)
    value_rows = value_cols.reshape(row_count, HEAD_GROUP, head_width)
    query_blocks = query_cols.reshape(row_count // QBLOCK, QBLOCK, HEAD_GROUP, head_width)
    grad_blocks = grad_cols.reshape(row_count // QBLOCK, QBLOCK, HEAD_GROUP, head_width)

    def one_block(carry, items):
        key_acc, value_acc = carry
        query_rows, grad_rows, block_logsum = items
        scores = (
            jnp.einsum("qhd,khd->hqk", query_rows, key_rows, preferred_element_type=jnp.float32)
            * scaling
        )
        scores = jnp.where(key_live[None, None, :], scores, -jnp.inf)
        probs = jnp.exp(scores - block_logsum[:, :, None])
        value_acc = value_acc + jnp.einsum(
            "hqk,qhd->khd",
            probs.astype(jnp.bfloat16),
            grad_rows,
            preferred_element_type=jnp.float32,
        )
        prob_grad = jnp.einsum(
            "qhd,khd->hqk", grad_rows, value_rows, preferred_element_type=jnp.float32
        )
        inner = jnp.sum(probs * prob_grad, axis=2, keepdims=True)
        score_grad = (probs * (prob_grad - inner)).astype(jnp.bfloat16)
        query_grad = (
            jnp.einsum("hqk,khd->qhd", score_grad, key_rows, preferred_element_type=jnp.float32)
            * scaling
        )
        key_acc = (
            key_acc
            + jnp.einsum("hqk,qhd->khd", score_grad, query_rows, preferred_element_type=jnp.float32)
            * scaling
        )
        return ((key_acc, value_acc), query_grad.reshape(QBLOCK, span_cols))

    empty = jnp.zeros((row_count, HEAD_GROUP, head_width), jnp.float32)
    (key_grad, value_grad), query_grad = lax.scan(
        one_block, (empty, empty), (query_blocks, grad_blocks, logsum)
    )
    return (
        query_grad.reshape(row_count, span_cols),
        key_grad.reshape(row_count, span_cols),
        value_grad.reshape(row_count, span_cols),
    )


def gathered(shard):
    return lax.all_gather(shard.astype(jnp.bfloat16), AXES, axis=0, tiled=True)


def scattered(part):
    return lax.psum_scatter(part, AXES, scatter_dimension=0, tiled=True)


def body_plain(
    tokens,
    band_mask,
    out_grad,
    norm1_gain,
    norm1_shift,
    qkv_weight,
    qv_bias,
    out_weight,
    out_bias,
    norm2_gain,
    norm2_shift,
    up_weight,
    up_bias,
    down_weight,
    down_bias,
):
    row_count, width = tokens.shape
    group_count = width // (HEAD_GROUP * HEAD)
    present = jnp.repeat(band_mask[0].astype(jnp.float32), row_count // band_mask.shape[1])
    key_live = present > 0.5
    column_mask = present[:, None]
    gain_one, shift_one, w_qkv, b_qv, w_out, b_out = (
        gathered(norm1_gain),
        gathered(norm1_shift),
        gathered(qkv_weight),
        gathered(qv_bias),
        gathered(out_weight),
        gathered(out_bias),
    )
    inputs = tokens.astype(jnp.float32)
    normed_one, unit_one, factor_one = normalize(
        inputs, gain_one.astype(jnp.float32), shift_one.astype(jnp.float32)
    )
    normed_one = normed_one.astype(jnp.bfloat16)
    bias_wide = b_qv.astype(jnp.float32)
    bias_full = jnp.concatenate(
        [bias_wide[:width], jnp.zeros((width,), jnp.float32), bias_wide[width:]]
    )
    joined = (jnp.dot(normed_one, w_qkv, preferred_element_type=jnp.float32) + bias_full).astype(
        jnp.bfloat16
    )
    query_groups = to_groups(joined[:, :width], group_count)
    key_groups = to_groups(joined[:, width : 2 * width], group_count)
    value_groups = to_groups(joined[:, 2 * width :], group_count)
    mixture, logsum = lax.map(
        lambda items: attend_forward(items[0], items[1], items[2], key_live),
        (query_groups, key_groups, value_groups),
    )
    mixture = from_groups(mixture).astype(jnp.bfloat16)
    attention = jnp.dot(mixture, w_out, preferred_element_type=jnp.float32) + b_out.astype(
        jnp.float32
    )
    middle = inputs + column_mask * attention
    gain_two, shift_two, w_up, b_up, w_down, b_down = (
        gathered(norm2_gain),
        gathered(norm2_shift),
        gathered(up_weight),
        gathered(up_bias),
        gathered(down_weight),
        gathered(down_bias),
    )
    normed_two, unit_two, factor_two = normalize(
        middle, gain_two.astype(jnp.float32), shift_two.astype(jnp.float32)
    )
    normed_two = normed_two.astype(jnp.bfloat16)
    hidden = jnp.dot(normed_two, w_up, preferred_element_type=jnp.float32) + b_up.astype(
        jnp.float32
    )
    active = jax.nn.gelu(hidden, approximate=False).astype(jnp.bfloat16)
    branch = jnp.dot(active, w_down, preferred_element_type=jnp.float32) + b_down.astype(
        jnp.float32
    )
    output = (middle + column_mask * branch).astype(jnp.bfloat16)
    upstream = out_grad.astype(jnp.float32)
    branch_grad = (column_mask * upstream).astype(jnp.bfloat16)
    down_weight_grad = jnp.einsum(
        "tf,td->fd", active, branch_grad, preferred_element_type=jnp.float32
    )
    down_bias_grad = jnp.sum(branch_grad.astype(jnp.float32), axis=0)
    active_grad = jnp.einsum(
        "td,fd->tf", branch_grad, w_down, preferred_element_type=jnp.float32
    )
    hidden_grad = (active_grad * gelu_slope(hidden)).astype(jnp.bfloat16)
    up_weight_grad = jnp.einsum(
        "td,tf->df", normed_two, hidden_grad, preferred_element_type=jnp.float32
    )
    up_bias_grad = jnp.sum(hidden_grad.astype(jnp.float32), axis=0)
    normed_two_grad = jnp.einsum(
        "tf,df->td", hidden_grad, w_up, preferred_element_type=jnp.float32
    )
    middle_part, norm2_gain_grad, norm2_shift_grad = normalize_back(
        normed_two_grad, unit_two, factor_two, gain_two.astype(jnp.float32)
    )
    (
        norm2_gain_grad,
        norm2_shift_grad,
        up_weight_grad,
        up_bias_grad,
        down_weight_grad,
        down_bias_grad,
    ) = (
        scattered(norm2_gain_grad),
        scattered(norm2_shift_grad),
        scattered(up_weight_grad),
        scattered(up_bias_grad),
        scattered(down_weight_grad),
        scattered(down_bias_grad),
    )
    middle_grad = upstream + middle_part
    attention_grad = (column_mask * middle_grad).astype(jnp.bfloat16)
    out_weight_grad = jnp.einsum(
        "te,td->ed", mixture, attention_grad, preferred_element_type=jnp.float32
    )
    out_bias_grad = jnp.sum(attention_grad.astype(jnp.float32), axis=0)
    mixture_grad = jnp.einsum(
        "td,ed->te", attention_grad, w_out, preferred_element_type=jnp.float32
    ).astype(jnp.bfloat16)
    grad_groups = to_groups(mixture_grad, group_count)
    query_grad, key_grad, value_grad = lax.map(
        lambda items: attend_backward(items[0], items[1], items[2], items[3], items[4], key_live),
        (query_groups, key_groups, value_groups, grad_groups, logsum),
    )
    query_grad = from_groups(query_grad).astype(jnp.bfloat16)
    key_grad = from_groups(key_grad).astype(jnp.bfloat16)
    value_grad = from_groups(value_grad).astype(jnp.bfloat16)
    joined_grad = jnp.concatenate([query_grad, key_grad, value_grad], axis=1)
    qkv_weight_grad = jnp.einsum(
        "td,tc->dc", normed_one, joined_grad, preferred_element_type=jnp.float32
    )
    qv_bias_grad = jnp.concatenate(
        [
            jnp.sum(query_grad.astype(jnp.float32), axis=0),
            jnp.sum(value_grad.astype(jnp.float32), axis=0),
        ]
    )
    normed_one_grad = jnp.einsum(
        "tc,dc->td", joined_grad, w_qkv, preferred_element_type=jnp.float32
    )
    input_part, norm1_gain_grad, norm1_shift_grad = normalize_back(
        normed_one_grad, unit_one, factor_one, gain_one.astype(jnp.float32)
    )
    input_grad = (middle_grad + input_part).astype(jnp.bfloat16)
    (
        norm1_gain_grad,
        norm1_shift_grad,
        qkv_weight_grad,
        qv_bias_grad,
        out_weight_grad,
        out_bias_grad,
    ) = (
        scattered(norm1_gain_grad),
        scattered(norm1_shift_grad),
        scattered(qkv_weight_grad),
        scattered(qv_bias_grad),
        scattered(out_weight_grad),
        scattered(out_bias_grad),
    )
    return (
        output,
        input_grad,
        norm1_gain_grad,
        norm1_shift_grad,
        qkv_weight_grad,
        qv_bias_grad,
        out_weight_grad,
        out_bias_grad,
        norm2_gain_grad,
        norm2_shift_grad,
        up_weight_grad,
        up_bias_grad,
        down_weight_grad,
        down_bias_grad,
    )


MESH_ID = pl.DeviceIdType.MESH
VIA_X = (0, 2)
VIA_Y = (1, 3)
ORDER = (1, 3, 2)
SCORE_SCALE = math.log2(math.e) / math.sqrt(HEAD)
TILE = 384


class Place:
    def __init__(self):
        wide = lax.axis_index("wide")
        narrow = lax.axis_index("narrow")
        z, y = wide // 2, wide % 2
        x, c = narrow // 2, narrow % 2
        self.z, self.c = z, c
        self.zs = (z, z + 1 - 2 * (z % 2), (z + 2) % 4, 3 - z)
        self.q = y * 2 + x
        self.qx = y * 2 + (1 - x)
        self.qy = (1 - y) * 2 + x
        self.qd = (1 - y) * 2 + (1 - x)
        self.to_z = tuple((zz * 2 + y, x * 2 + c) for zz in self.zs)
        self.to_x = (z * 2 + y, (1 - x) * 2 + c)
        self.to_y = (z * 2 + 1 - y, x * 2 + c)
        self.to_c = (z * 2 + y, x * 2 + 1 - c)


def span(start, size, step):
    return pl.ds(pl.multiple_of(start, step), size)


def meet(place):
    barrier = pltpu.get_barrier_semaphore()
    peers = place.to_z[1:] + (place.to_x, place.to_y, place.to_c)
    for peer in peers:
        pl.semaphore_signal(barrier, inc=1, device_id=peer, device_id_type=MESH_ID)
    pl.semaphore_wait(barrier, len(peers))


def remote(source, target, send, recv, peer):
    return pltpu.make_async_remote_copy(
        src_ref=source,
        dst_ref=target,
        send_sem=send,
        recv_sem=recv,
        device_id=peer,
        device_id_type=MESH_ID,
    )


class Piece:
    COUNT = 19

    def __init__(self, place, send, recv):
        self.p = place
        self.send = send
        self.recv = recv
        self.sent = []

    def go(self, source, target, index, peer):
        remote(source(), target(), self.send.at[index], self.recv.at[index], peer).start()
        self.sent.append((source, target, index, peer))

    def got(self, target, index, peer):
        remote(target, target, self.send.at[index], self.recv.at[index], peer).wait_recv()

    def left(self, source, target, index, peer):
        remote(source(), target(), self.send.at[index], self.recv.at[index], peer).wait_send()

    def finish(self):
        for one in self.sent:
            self.left(*one)


class Gather(Piece):
    def __init__(self, place, own, block, column, other, send, recv):
        super().__init__(place, send, recv)
        self.own = own
        self.block = block
        self.column = column
        self.other = other

    def start_z(self):
        p = self.p
        for k in ORDER:
            self.go(self.own, lambda: self.block(p.z, p.q), k - 1, p.to_z[k])

    def start_xy(self):
        p = self.p
        self.go(self.own, lambda: self.block(p.z, p.q), 3, p.to_x)
        self.go(self.own, lambda: self.block(p.z, p.q), 9, p.to_y)

    def z(self, k):
        p = self.p
        here = lambda: self.block(p.zs[k], p.q)
        self.got(here(), k - 1, p.to_z[k])
        self.go(here, here, 3 + k, p.to_x)
        self.go(here, here, 9 + k, p.to_y)

    def share(self, index, q):
        column = lambda: self.column(q)
        self.go(column, column, index, self.p.to_c)

    def own_column(self):
        self.share(15, self.p.q)

    def xy(self, k):
        p = self.p
        from_x = lambda: self.block(p.zs[k], p.qx)
        self.got(from_x(), 3 + k, p.to_x)
        if k in VIA_X:
            self.go(from_x, from_x, 13 + VIA_X.index(k), p.to_y)
        from_y = lambda: self.block(p.zs[k], p.qy)
        self.got(from_y(), 9 + k, p.to_y)
        if k in VIA_Y:
            self.go(from_y, from_y, 7 + VIA_Y.index(k), p.to_x)

    def xy_columns(self):
        self.share(16, self.p.qx)
        self.share(17, self.p.qy)

    def d(self):
        p = self.p
        for i, k in enumerate(VIA_X):
            self.got(self.block(p.zs[k], p.qd), 13 + i, p.to_y)
        for i, k in enumerate(VIA_Y):
            self.got(self.block(p.zs[k], p.qd), 7 + i, p.to_x)
        self.share(18, p.qd)

    def c(self):
        p = self.p
        for i, q in enumerate((p.q, p.qx, p.qy, p.qd)):
            self.got(self.other(q), 15 + i, p.to_c)


class Scatter(Piece):
    def __init__(self, place, block, column, bufs, send, recv):
        super().__init__(place, send, recv)
        self.block, self.column = block, column
        self.dx, self.dy, self.xr, self.yr, self.zr = bufs
        self.columns = (place.qd, place.qx, place.qy, place.q)

    def add(self, target, other):
        target[...] = (target[...].astype(jnp.float32) + other[...].astype(jnp.float32)).astype(
            target.dtype
        )

    def give(self, other):
        for i, q in enumerate(self.columns):
            self.go(
                lambda q=q: other(q), lambda q=q: self.column(q), 15 + i, self.p.to_c
            )

    def given(self):
        for source, target, index, peer in self.sent:
            if index >= 15:
                self.left(source, target, index, peer)
        self.sent = [one for one in self.sent if one[2] < 15]

    def arrive(self, i):
        self.got(self.column(self.columns[i]), 15 + i, self.p.to_c)

    def take(self, i, mine):
        self.arrive(i)
        q = self.columns[i]
        for zz in range(4):
            self.add(self.block(zz, q), mine(zz, q))

    def diagonal(self):
        p = self.p
        for i in range(2):
            self.go(
                lambda i=i: self.block(p.zs[VIA_X[i]], p.qd),
                lambda i=i: self.dx.at[i],
                7 + i,
                p.to_x,
            )
            self.go(
                lambda i=i: self.block(p.zs[VIA_Y[i]], p.qd),
                lambda i=i: self.dy.at[i],
                13 + i,
                p.to_y,
            )

    def cross(self, k):
        p = self.p
        on_x = lambda: self.block(p.zs[k], p.qx)
        on_y = lambda: self.block(p.zs[k], p.qy)
        if k in VIA_Y:
            i = VIA_Y.index(k)
            self.go(on_y, lambda: self.yr.at[k], 9 + k, p.to_y)
            self.got(self.dy.at[i], 13 + i, p.to_y)
            self.add(on_x(), self.dy.at[i])
            self.go(on_x, lambda: self.xr.at[k], 3 + k, p.to_x)
        else:
            i = VIA_X.index(k)
            self.go(on_x, lambda: self.xr.at[k], 3 + k, p.to_x)
            self.got(self.dx.at[i], 7 + i, p.to_x)
            self.add(on_y(), self.dx.at[i])
            self.go(on_y, lambda: self.yr.at[k], 9 + k, p.to_y)

    def plane(self, k):
        p = self.p
        self.got(self.xr.at[k], 3 + k, p.to_x)
        self.got(self.yr.at[k], 9 + k, p.to_y)
        here = self.block(p.zs[k], p.q)
        return here, (
            here[...].astype(jnp.float32)
            + self.xr[k].astype(jnp.float32)
            + self.yr[k].astype(jnp.float32)
        )

    def spread(self, k):
        here, value = self.plane(k)
        here[...] = value.astype(here.dtype)
        self.go(
            lambda: self.block(self.p.zs[k], self.p.q),
            lambda: self.zr.at[k - 1],
            k - 1,
            self.p.to_z[k],
        )

    def last(self):
        p = self.p
        _, value = self.plane(0)
        for k in ORDER:
            self.got(self.zr.at[k - 1], k - 1, p.to_z[k])
            value = value + self.zr[k - 1].astype(jnp.float32)
        return value


def scatter_buffers(tail, kind):
    return [
        pltpu.VMEM((2,) + tail, kind),
        pltpu.VMEM((2,) + tail, kind),
        pltpu.VMEM((4,) + tail, kind),
        pltpu.VMEM((4,) + tail, kind),
        pltpu.VMEM((3,) + tail, kind),
    ]


MATRICES = ("qkv", "out", "up", "down")


def triples(**named):
    return [(name, one, two) for name, (one, two) in named.items()]


def pairs_of(**named):
    return list(named.items())


class Named:
    def __init__(self, names, refs):
        assert len(names) == len(refs)
        self.__dict__.update(zip(names, refs))


def loop(count, compute, slots=()):
    def step(i, carry):
        compute(i)
        for j, steps in enumerate(slots):
            if steps:

                @pl.when(i == j)
                def _(steps=steps):
                    for one in steps:
                        one()

        return carry

    lax.fori_loop(0, count, step, 0)


def dot(left, right):
    return jnp.dot(left, right, preferred_element_type=jnp.float32)


def dot_nt(left, right):
    return lax.dot_general(
        left, right, (((1,), (1,)), ((), ())), preferred_element_type=jnp.float32
    )


def dot_tn(left, right):
    return lax.dot_general(
        left, right, (((0,), (0,)), ((), ())), preferred_element_type=jnp.float32
    )


def head_only(values, e):
    lane = lax.broadcasted_iota(jnp.int32, values.shape, 1)
    return jnp.where((lane // HEAD) == e, values, jnp.zeros_like(values))


def fill_present(present, mask):
    groups = mask.shape[1]
    rows = present.shape[0] // groups
    for g in range(groups):
        present[g * rows : (g + 1) * rows, :] = jnp.full(
            (rows, 128), mask[0, g].astype(jnp.float32)
        )


def segments(width):
    return ((0, width, width // 32), (width, 2 * width, width // 16), (3 * width, 4 * width, width // 8))


def selection(width):
    parts = []
    for _, size, m in segments(width):
        lane = lax.broadcasted_iota(jnp.int32, (1, size), 1).astype(jnp.float32)
        rest = lane - m * jnp.floor((lane + 0.5) * (1.0 / m))
        row = lax.broadcasted_iota(jnp.int32, (128, size), 0).astype(jnp.float32)
        parts.append(jnp.where(row == rest, 1.0, 0.0).astype(jnp.bfloat16))
    return jnp.concatenate(parts, axis=1)


def owners(width):
    parts = []
    for _, size, m in segments(width):
        lane = lax.broadcasted_iota(jnp.int32, (1, size), 1).astype(jnp.float32)
        parts.append(jnp.floor((lane + 0.5) * (1.0 / m)))
    return jnp.concatenate(parts, axis=1)


def unit(values):
    centred = values - jnp.mean(values, axis=1, keepdims=True)
    factor = lax.rsqrt(jnp.mean(centred * centred, axis=1, keepdims=True) + NORM_EPSILON)
    return centred * factor, factor


def run(steps):
    for one in steps:
        one()


def layer_kernel(names, *refs):
    r = Named(names, refs)
    place = Place()
    c = place.c
    tokens, width = r.tokens.shape
    hidden = r.act.shape[1]
    pairs = width // 128
    tiles = hidden // TILE
    shards = (r.qkv_shard, r.out_shard, r.up_shard, r.down_shard)
    sibs = (r.qkv_sib, r.out_sib, r.up_sib, r.down_sib)
    wides = (r.qkv_wide, r.out_wide, r.up_wide, r.down_wide)
    meet(place)

    def before(i):
        half = shards[i].shape[1] // 2
        return remote(
            shards[i].at[:, span((1 - c) * half, half, 128)],
            sibs[i],
            r.pre_send.at[i],
            r.pre_recv.at[i],
            place.to_c,
        )

    for i in range(4):
        before(i).start()
    r.small_wide[place.z, place.q, c] = jnp.zeros((8, 128), jnp.float32)
    for i in range(8):
        vector = getattr(r, "vector%d" % i)
        r.small_wide[place.z, place.q, c, i : i + 1, 0 : vector.shape[0]] = vector[...].reshape(1, -1)
    gather_small = Gather(
        place,
        lambda: r.small_wide.at[place.z, place.q, c],
        lambda zz, q: r.small_wide.at[zz, q, c],
        lambda q: r.small_wide.at[:, q, c],
        lambda q: r.small_wide.at[:, q, 1 - c],
        r.gather_send.at[8],
        r.gather_recv.at[8],
    )
    gather_small.start_z()
    gather_small.start_xy()

    cuts = (
        (0, 0, 48, 0, 384),
        (0, 0, 48, 384, 384),
        (0, 0, 48, 768, 384),
        (1, 0, 48, 0, 384),
        (2, 0, 48, 0, 768),
        (2, 0, 48, 768, 768),
        (3, 0, 96, 0, 384),
        (3, 96, 96, 0, 384),
    )
    pieces = []
    for j, (i, row, rows, col, cols) in enumerate(cuts):
        half = shards[i].shape[1] // 2

        def at(side, row=row, rows=rows, col=col, cols=cols, half=half):
            return (pl.ds(row, rows), span(side * half + col, cols, 128))

        block = lambda zz, q, i=i, at=at: wides[i].at[(zz, q) + at(c)]
        pieces.append(
            Gather(
                place,
                lambda block=block: block(place.z, place.q),
                block,
                lambda q, i=i, at=at: wides[i].at[(slice(None), q) + at(c)],
                lambda q, i=i, at=at: wides[i].at[(slice(None), q) + at(1 - c)],
                r.gather_send.at[j],
                r.gather_recv.at[j],
            )
        )
    for i in range(4):
        half = shards[i].shape[1] // 2
        cols = span(c * half, half, 128)
        before(i).wait_recv()
        mine = shards[i][:, cols]
        theirs = sibs[i][...]
        wides[i][place.z, place.q, :, cols] = jnp.concatenate(
            [jnp.where(c == 0, mine, theirs), jnp.where(c == 0, theirs, mine)], axis=0
        ).astype(jnp.bfloat16)
        for j, cut in enumerate(cuts):
            if cut[0] == i:
                pieces[j].start_z()
                if j == 0:
                    pieces[0].start_xy()
    fill_present(r.present, r.mask)
    r.sums[...] = jnp.zeros_like(r.sums)

    def z_steps(j):
        piece = pieces[j]
        return (
            ([piece.start_xy] if j else [])
            + [lambda k=k: piece.z(k) for k in ORDER]
            + [piece.own_column]
        )

    def xy_steps(j):
        piece = pieces[j]
        return [lambda k=k: piece.xy(k) for k in (0, 1, 3, 2)] + [piece.xy_columns]

    def period(j):
        return (
            (z_steps(j + 1) if j + 1 < len(pieces) else [])
            + xy_steps(j)
            + ([pieces[j - 1].d] if j else [])
        )

    run([lambda k=k: gather_small.z(k) for k in ORDER])
    run(z_steps(0))
    gather_small.own_column()
    run([lambda k=k: gather_small.xy(k) for k in range(4)])
    gather_small.xy_columns()
    run(z_steps(1))
    run(xy_steps(0)[:2])
    gather_small.d()
    gather_small.c()

    r.chosen[...] = selection(width)
    r.owner[...] = owners(width)
    r.vec[...] = jnp.zeros_like(r.vec)

    def unpack(zz):
        rows = r.small_wide[zz].reshape(64, 128).astype(jnp.bfloat16)
        picked = dot(rows, r.chosen[...])
        owner = r.owner[...] - (zz * 8).astype(jnp.float32)
        total = r.vec[...]
        for d in range(8):
            total = total + jnp.where(owner == d, picked[d * 8 : d * 8 + 8], 0.0)
        r.vec[...] = total

    loop(4, unpack)
    run(xy_steps(0)[2:])
    r.bias[:, 0:width] = r.vec[2:3, width : 2 * width]
    r.bias[:, width : 2 * width] = jnp.zeros((1, width), jnp.float32)
    r.bias[:, 2 * width : 3 * width] = r.vec[2:3, 2 * width : 3 * width]

    def first_norm(t):
        rows = span(t * 128, 128, 128)
        normed, _ = unit(r.tokens[rows, :].astype(jnp.float32))
        value = normed * r.vec[0:1, 0:width] + r.vec[1:2, 0:width]
        r.normed[rows, :] = value.astype(jnp.bfloat16)
        r.turned_one[:, rows] = value.T.astype(jnp.bfloat16)

    def mask_grad(t):
        rows = span(t * 128, 128, 128)
        low = (r.present[rows, 0:1] * r.out_grad[rows, :].astype(jnp.float32)).astype(jnp.bfloat16)
        r.grad_low[rows, :] = low
        r.sums[7:8, 0:width] += jnp.sum(low.astype(jnp.float32), axis=0, keepdims=True)

    steps = period(1)
    loop(tokens // 128, first_norm, [steps[0:2], steps[2:3], steps[3:4], steps[4:5]])
    run(steps[5:])
    steps = period(2)
    loop(tokens // 128, mask_grad, [steps[0:2], steps[2:3], steps[3:4], steps[4:5]])
    run(steps[5:])
    steps = period(3)
    run(steps[:4])
    pieces[2].d()
    run(steps[4:-1])
    for j in range(3):
        pieces[j].c()

    def project(t):
        cols = span(t * width, width, 128)
        r.joined[:, cols] = (
            dot(r.normed[...], r.qkv_wide[:, :, :, cols].reshape(width, width)) + r.bias[:, cols]
        ).astype(jnp.bfloat16)

    steps = period(4)
    loop(3, project, [steps[0:2], steps[2:4], steps[4:5]])

    def attend(hp):
        cols = span(hp * 128, 128, 128)
        query = r.joined[:, cols]
        key = r.joined[:, span(width + hp * 128, 128, 128)]
        value = r.joined[:, span(2 * width + hp * 128, 128, 128)].T
        live = r.present[:, 0:1] > 0.5
        mixed = []
        for e in range(2):
            scores = dot_nt(head_only(key, e), query) * SCORE_SCALE
            scores = jnp.where(live, scores, -jnp.inf)
            largest = jnp.max(scores, axis=0, keepdims=True)
            expo = jnp.exp2(scores - largest)
            totals = jnp.sum(expo, axis=0, keepdims=True)
            probs = (expo * (1.0 / totals)).astype(jnp.bfloat16)
            mixed.append(dot(value[HEAD * e : HEAD * (e + 1)], probs))
            r.logsum[hp, e : e + 1, :] = largest + jnp.log2(totals)
        both = jnp.concatenate(mixed, axis=0)
        r.mixed_turned[cols, :] = both.astype(jnp.bfloat16)
        r.mixed[:, cols] = both.T.astype(jnp.bfloat16)

    later = period(5)
    loop(
        pairs,
        attend,
        [steps[5:6], steps[6:7], steps[7:8], steps[8:], later[0:3], later[3:5]],
    )
    pieces[3].c()
    r.middle[...] = dot(r.mixed[...], r.out_wide[...].reshape(width, width))

    def second_norm(t):
        rows = span(t * 128, 128, 128)
        present = r.present[rows, 0:1]
        middle = r.tokens[rows, :].astype(jnp.float32) + present * (
            r.middle[rows, :] + r.vec[3:4, 0:width]
        )
        r.middle[rows, :] = middle
        normed, _ = unit(middle)
        value = normed * r.vec[4:5, 0:width] + r.vec[5:6, 0:width]
        r.normed[rows, :] = value.astype(jnp.bfloat16)
        r.turned_two[:, rows] = value.T.astype(jnp.bfloat16)

    loop(tokens // 128, second_norm, [later[5:6], later[6:7], later[7:8], later[8:9]])
    run(later[9:])
    pieces[4].c()

    def slope_out(t, slot):
        return pltpu.make_async_copy(r.slope.at[slot], r.slope_far.at[t], r.slope_send.at[slot])

    def slope_in(t, slot):
        return pltpu.make_async_copy(r.slope_far.at[t], r.slope.at[slot], r.slope_recv.at[slot])

    def expand(t, u):
        slot = u % 2

        @pl.when(u >= 2)
        def _():
            slope_out(t, slot).wait()

        cols = span(t * TILE, TILE, 128)
        value = (
            dot(r.normed[...], r.up_wide[:, :, :, cols].reshape(width, TILE))
            + r.vec[6:7, span(3 * width + t * TILE, TILE, 128)]
        )
        cumulative = 0.5 * (1.0 + lax.erf(value * (1.0 / math.sqrt(2.0))))
        r.act[:, cols] = (value * cumulative).astype(jnp.bfloat16)
        r.slope[slot] = cumulative + value * jnp.exp(-0.5 * value * value) * (
            1.0 / math.sqrt(2.0 * math.pi)
        )
        slope_out(t, slot).start()

    def down_grad(t):
        cols = span(t * TILE, TILE, 128)
        grad = dot_tn(r.act[:, cols], r.grad_low[...]).astype(jnp.bfloat16)
        r.down_part[t // 2, pl.ds((t % 2) * 2, 2)] = grad.reshape(2, TILE // 2, width)

    steps = period(6)
    loop(4, lambda u: expand(u + 2 * (u // 2), u), [steps[0:2], steps[2:4], steps[4:5], steps[5:6]])
    loop(4, lambda u: down_grad(u + 2 * (u // 2)), [steps[6:7], steps[7:8], steps[8:9], steps[9:]])
    pieces[5].c()
    steps = period(7)
    loop(4, lambda u: expand(u + 2 * (u // 2) + 2, u + 4), [[s] for s in steps[0:4]])
    loop(4, lambda u: down_grad(u + 2 * (u // 2) + 2), [steps[4:5], steps[5:6]])
    for u in (6, 7):
        slope_out(0, u % 2).wait()
    slope_in(0, 0).start()

    def scatter(j, block, column):
        bufs = [getattr(r, "piece%d_%d" % (j, b)) for b in range(5)]
        return Scatter(place, block, column, bufs, r.scatter_send.at[j], r.scatter_recv.at[j])

    d0, d1 = [
        scatter(
            s,
            lambda zz, q, s=s: r.down_total.at[zz, q, pl.ds(96 * s, 96)],
            lambda q, s=s: r.down_total.at[:, q, pl.ds(96 * s, 96)],
        )
        for s in range(2)
    ]
    u0, u1 = [
        scatter(
            2 + s,
            lambda zz, q, s=s: r.up_total.at[s, zz, q],
            lambda q, s=s: r.up_total.at[s, :, q],
        )
        for s in range(2)
    ]
    o = scatter(4, lambda zz, q: r.out_total.at[zz, q], lambda q: r.out_total.at[:, q])
    qs = [
        scatter(
            5 + s,
            lambda zz, q, s=s: r.qkv_total.at[s, zz, q],
            lambda q, s=s: r.qkv_total.at[s, :, q],
        )
        for s in range(3)
    ]
    small = scatter(8, lambda zz, q: r.small_total.at[zz, q], lambda q: r.small_total.at[:, q])

    def take_down(piece, s, i):
        piece.take(
            i, lambda zz, q: r.down_part.at[zz, q, pl.ds(96 * s, 96), span(c * 384, 384, 128)]
        )

    def cross_steps(piece):
        return [lambda k=k: piece.cross(k) for k in (1, 3, 2, 0)]

    def spread_steps(piece):
        return [lambda k=k: piece.spread(k) for k in ORDER]

    for s, piece in enumerate((d0, d1)):
        piece.give(
            lambda q, s=s: r.down_part.at[
                :, q, pl.ds(96 * s, 96), span((1 - c) * 384, 384, 128)
            ]
        )
    pieces[7].d()
    take_down(d0, 0, 0)
    d0.diagonal()
    take_down(d1, 1, 0)
    d1.diagonal()
    pieces[6].c()
    pieces[7].c()
    r.acc[...] = jnp.zeros_like(r.acc)

    def narrow(t):
        slot = t % 2
        slope_in(t, slot).wait()

        @pl.when(t + 1 < tiles)
        def _():
            slope_in(t + 1, 1 - slot).start()

        cols = span(t * TILE, TILE, 128)
        weights = r.down_wide[t // 2, pl.ds((t % 2) * 2, 2)].reshape(TILE, width)
        r.acc[...] += dot(r.act[:, cols], weights)
        grad = (dot_nt(r.grad_low[...], weights) * r.slope[slot]).astype(jnp.bfloat16)
        r.act[:, cols] = grad
        r.sums[6:7, span(3 * width + t * TILE, TILE, 128)] = jnp.sum(
            grad.astype(jnp.float32), axis=0, keepdims=True
        )

    xd0, xd1, xu0, xu1, xo = [cross_steps(p) for p in (d0, d1, u0, u1, o)]
    loop(
        tiles,
        narrow,
        [
            [lambda: take_down(d0, 0, 1), lambda: take_down(d0, 0, 2)],
            xd0[:1],
            xd0[1:2],
            xd0[2:3] + [lambda: take_down(d1, 1, 1)],
            xd0[3:] + [lambda: take_down(d1, 1, 2)],
            xd1[:1] + [lambda: take_down(d0, 0, 3)],
            xd1[1:2],
            [lambda: take_down(d1, 1, 3)],
        ],
    )

    def finish_output(t):
        rows = span(t * 128, 128, 128)
        r.output[rows, :] = (
            r.middle[rows, :]
            + r.present[rows, 0:1] * (r.acc[rows, :] + r.vec[7:8, 0:width])
        ).astype(jnp.bfloat16)

    def up_part(side, s):
        cols = span(side * (hidden // 2) + 768 * s, 768, 128)
        return dot(r.turned_two[...], r.act[:, cols]).reshape(4, 4, 48, 768)

    for s, piece in enumerate((u0, u1)):
        r.up_part[s] = up_part(1 - c, s).astype(jnp.bfloat16)
        piece.give(lambda q, s=s: r.up_part.at[s, :, q])
    run(xd1[2:3])
    for s, piece in enumerate((u0, u1)):
        for i in range(4):
            piece.arrive(i)
        r.up_total[s] = (r.up_total[s].astype(jnp.float32) + up_part(c, s)).astype(jnp.bfloat16)
        if s == 0:
            piece.diagonal()
            run(xd1[3:])
    run(spread_steps(d0))
    u1.diagonal()
    loop(tokens // 128, finish_output)
    r.acc[...] = dot_nt(r.act[...], r.up_wide[...].reshape(width, hidden))

    def norm_back(up, normed, factor, index):
        r.sums[index : index + 1, 0:width] += jnp.sum(up * normed, axis=0, keepdims=True)
        r.sums[index + 1 : index + 2, 0:width] += jnp.sum(up, axis=0, keepdims=True)
        scaled = up * r.vec[index : index + 1, 0:width]
        return factor * (
            scaled
            - jnp.mean(scaled, axis=1, keepdims=True)
            - normed * jnp.mean(scaled * normed, axis=1, keepdims=True)
        )

    def second_back(t):
        rows = span(t * 128, 128, 128)
        normed, factor = unit(r.middle[rows, :])
        grad = r.out_grad[rows, :].astype(jnp.float32) + norm_back(
            r.acc[rows, :], normed, factor, 4
        )
        r.middle[rows, :] = grad
        low = (r.present[rows, 0:1] * grad).astype(jnp.bfloat16)
        r.normed[rows, :] = low
        r.sums[3:4, 0:width] += jnp.sum(low.astype(jnp.float32), axis=0, keepdims=True)

    loop(tokens // 128, second_back, [xu0[:1], xu0[1:2], xu0[2:3], xu0[3:]])

    def out_part(side):
        cols = span(side * (width // 2), width // 2, 128)
        return dot(r.mixed_turned[...], r.normed[:, cols]).reshape(4, 4, 48, width // 2)

    r.out_part[...] = out_part(1 - c).astype(jnp.bfloat16)
    o.give(lambda q: r.out_part.at[:, q])
    r.mixed[...] = dot_nt(r.normed[...], r.out_wide[...].reshape(width, width)).astype(jnp.bfloat16)
    for i in range(4):
        o.arrive(i)
    r.out_total[...] = (r.out_total[...].astype(jnp.float32) + out_part(c)).astype(jnp.bfloat16)
    o.diagonal()
    run(spread_steps(d1))

    def attend_back(hp):
        cols = span(hp * 128, 128, 128)
        key_cols = span(width + hp * 128, 128, 128)
        value_cols = span(2 * width + hp * 128, 128, 128)
        query = r.joined[:, cols]
        key = r.joined[:, key_cols]
        value = r.joined[:, value_cols]
        grad = r.mixed[:, cols]
        turned = key.T
        live = r.present[:, 0:1] > 0.5
        value_grad = jnp.zeros((tokens, 128), jnp.float32)
        key_grad = jnp.zeros((tokens, 128), jnp.float32)
        query_grad = []
        for e in range(2):
            scores = dot_nt(head_only(key, e), query) * SCORE_SCALE
            scores = jnp.where(live, scores, -jnp.inf)
            probs = jnp.exp2(scores - r.logsum[hp, e : e + 1, :])
            back = dot_nt(head_only(value, e), grad)
            inner = jnp.sum(probs * back, axis=0, keepdims=True)
            score_grad = (probs * (back - inner)).astype(jnp.bfloat16)
            value_grad = value_grad + dot(probs.astype(jnp.bfloat16), head_only(grad, e))
            key_grad = key_grad + dot(score_grad, head_only(query, e))
            query_grad.append(dot(turned[HEAD * e : HEAD * (e + 1)], score_grad))
        scale = 1.0 / math.sqrt(HEAD)
        query_low = (jnp.concatenate(query_grad, axis=0).T * scale).astype(jnp.bfloat16)
        value_low = value_grad.astype(jnp.bfloat16)
        r.joined[:, cols] = query_low
        r.joined[:, key_cols] = (key_grad * scale).astype(jnp.bfloat16)
        r.joined[:, value_cols] = value_low
        r.sums[2:3, span(width + hp * 128, 128, 128)] = jnp.sum(
            query_low.astype(jnp.float32), axis=0, keepdims=True
        )
        r.sums[2:3, span(2 * width + hp * 128, 128, 128)] = jnp.sum(
            value_low.astype(jnp.float32), axis=0, keepdims=True
        )

    loop(
        pairs,
        attend_back,
        [xu1[:1], xu1[1:2], xu1[2:3], xu1[3:] + spread_steps(u0)[:1], spread_steps(u0)[1:], xo],
    )

    def qkv_part(side, s):
        cols = span(side * (3 * width // 2) + 384 * s, 384, 128)
        return dot(r.turned_one[...], r.joined[:, cols]).reshape(4, 4, 48, 384)

    u0.given()
    u1.given()
    for s, piece in enumerate(qs):
        cols = pl.ds(384 * (s % 2), 384)
        r.up_part[s // 2, :, :, :, cols] = qkv_part(1 - c, s).astype(jnp.bfloat16)
        piece.give(lambda q, s=s, cols=cols: r.up_part.at[s // 2, :, q, :, cols])
    for s, piece in enumerate(qs):
        for i in range(4):
            piece.arrive(i)
        r.qkv_total[s] = (r.qkv_total[s].astype(jnp.float32) + qkv_part(c, s)).astype(jnp.bfloat16)
        piece.diagonal()
    run(spread_steps(u1))
    r.acc[...] = dot_nt(r.joined[...], r.qkv_wide[...].reshape(width, 3 * width))

    def first_back(t):
        rows = span(t * 128, 128, 128)
        normed, factor = unit(r.tokens[rows, :].astype(jnp.float32))
        part = norm_back(r.acc[rows, :], normed, factor, 0)
        r.input_grad[rows, :] = (r.middle[rows, :] + part).astype(jnp.bfloat16)

    loop(tokens // 128, first_back)

    def pack(zz):
        sums = r.sums[...]
        owner = r.owner[...] - (zz * 8).astype(jnp.float32)
        tile = jnp.zeros((64, 128), jnp.float32)
        for _ in range(3):
            part = sums.astype(jnp.bfloat16).astype(jnp.float32)
            sums = sums - part
            rows = jnp.concatenate(
                [jnp.where(owner == d, part, 0.0) for d in range(8)], axis=0
            ).astype(jnp.bfloat16)
            tile = tile + dot_nt(rows, r.chosen[...])
        r.small_part[zz] = tile.reshape(4, 2, 8, 128)

    loop(4, pack)
    small.give(lambda q: r.small_part.at[:, q, 1 - c])
    run(cross_steps(qs[0]))
    for i in range(4):
        small.take(i, lambda zz, q: r.small_part.at[zz, q, c])
    small.diagonal()
    run(spread_steps(o))
    run(cross_steps(qs[1]))
    run(cross_steps(small))
    run(spread_steps(qs[0]))
    run(cross_steps(qs[2]))
    run(spread_steps(small))

    finals = (r.down_final, r.up_final, r.out_final, r.qkv_final)
    results = (r.down_result, r.up_result, r.out_result, r.qkv_result)

    def swap(i, side):
        rows, cols = results[i].shape
        return remote(
            finals[i].at[span((1 - c) * rows, rows, 8)],
            results[i].at[:, span(side * (cols // 2), cols // 2, 128)],
            r.end_send.at[i],
            r.end_recv.at[i],
            place.to_c,
        )

    def close(i):
        rows, cols = results[i].shape
        swap(i, c).start()
        results[i][:, span(c * (cols // 2), cols // 2, 128)] = finals[i][span(c * rows, rows, 8)]

    r.down_final[0:96, :] = d0.last()
    r.down_final[96:192, :] = d1.last()
    close(0)
    r.up_final[:, 0:768] = u0.last()
    r.up_final[:, 768:1536] = u1.last()
    close(1)
    r.out_final[...] = o.last()
    close(2)
    run(spread_steps(qs[1]))
    r.qkv_final[:, 0:384] = qs[0].last()
    run(spread_steps(qs[2]))
    r.small_result[...] = small.last()
    r.qkv_final[:, 384:768] = qs[1].last()
    r.qkv_final[:, 768:1152] = qs[2].last()
    close(3)
    for i in range(4):
        swap(i, 1 - c).wait_recv()
    for i in range(4):
        before(i).wait_send()
        swap(i, c).wait_send()
    for piece in [gather_small] + pieces + [d0, d1, u0, u1, o] + qs + [small]:
        piece.finish()


def layer_call(tokens, band_mask, out_grad, shards, smalls):
    bf16, f32 = jnp.bfloat16, jnp.float32
    count, width = tokens.shape
    shapes = [s.shape for s in shards]
    hidden = shapes[2][1]
    tiles = hidden // TILE
    vmem = pl.BlockSpec(memory_space=pltpu.VMEM)
    anywhere = pl.BlockSpec(memory_space=pl.ANY)
    inputs = triples(
        tokens=(tokens, vmem),
        mask=(band_mask, pl.BlockSpec(memory_space=pltpu.SMEM)),
        out_grad=(out_grad, vmem),
        qkv_shard=(shards[0], vmem),
        out_shard=(shards[1], vmem),
        up_shard=(shards[2], vmem),
        down_shard=(shards[3], vmem),
    ) + [("vector%d" % i, v, vmem) for i, v in enumerate(smalls)]
    outs = triples(
        slope_far=((tiles, count, TILE), f32),
        output=((count, width), bf16),
        input_grad=((count, width), bf16),
        qkv_result=(shapes[0], f32),
        out_result=(shapes[1], f32),
        up_result=(shapes[2], f32),
        down_result=(shapes[3], f32),
        small_result=((8, 128), f32),
    )
    tails = (
        [((96, 384), bf16)] * 2
        + [((48, 768), bf16)] * 2
        + [((48, 384), bf16)] * 4
        + [((8, 128), f32)]
    )
    scratch = []
    for j, (tail, kind) in enumerate(tails):
        for b, one in enumerate(scatter_buffers(tail, kind)):
            scratch.append(("piece%d_%d" % (j, b), one))
    for name, (rows, cols) in zip(MATRICES, shapes):
        scratch.append((name + "_wide", pltpu.VMEM((4, 4, 2 * rows, cols), bf16)))
        scratch.append((name + "_sib", pltpu.VMEM((rows, cols // 2), f32)))
        scratch.append((name + "_final", pltpu.VMEM((2 * rows, cols // 2), f32)))
    scratch += pairs_of(
        small_wide=pltpu.VMEM((4, 4, 2, 8, 128), f32),
        small_part=pltpu.VMEM((4, 4, 2, 8, 128), f32),
        small_total=pltpu.VMEM((4, 4, 8, 128), f32),
        down_part=pltpu.VMEM((4, 4, 192, width), bf16),
        down_total=pltpu.VMEM((4, 4, 192, 384), bf16),
        up_part=pltpu.VMEM((2, 4, 4, 48, 768), bf16),
        up_total=pltpu.VMEM((2, 4, 4, 48, 768), bf16),
        out_part=pltpu.VMEM((4, 4, 48, 384), bf16),
        out_total=pltpu.VMEM((4, 4, 48, 384), bf16),
        qkv_total=pltpu.VMEM((3, 4, 4, 48, 384), bf16),
        present=pltpu.VMEM((count, 128), f32),
        vec=pltpu.VMEM((8, 7 * width), f32),
        sums=pltpu.VMEM((8, 7 * width), f32),
        bias=pltpu.VMEM((1, 3 * width), f32),
        chosen=pltpu.VMEM((128, 7 * width), bf16),
        owner=pltpu.VMEM((1, 7 * width), f32),
        logsum=pltpu.VMEM((width // 128, 8, count), f32),
        turned_one=pltpu.VMEM((width, count), bf16),
        turned_two=pltpu.VMEM((width, count), bf16),
        mixed_turned=pltpu.VMEM((width, count), bf16),
        normed=pltpu.VMEM((count, width), bf16),
        mixed=pltpu.VMEM((count, width), bf16),
        grad_low=pltpu.VMEM((count, width), bf16),
        joined=pltpu.VMEM((count, 3 * width), bf16),
        middle=pltpu.VMEM((count, width), f32),
        acc=pltpu.VMEM((count, width), f32),
        act=pltpu.VMEM((count, hidden), bf16),
        slope=pltpu.VMEM((2, count, TILE), f32),
        gather_send=pltpu.SemaphoreType.DMA((9, Piece.COUNT)),
        gather_recv=pltpu.SemaphoreType.DMA((9, Piece.COUNT)),
        scatter_send=pltpu.SemaphoreType.DMA((9, Piece.COUNT)),
        scatter_recv=pltpu.SemaphoreType.DMA((9, Piece.COUNT)),
        pre_send=pltpu.SemaphoreType.DMA((4,)),
        pre_recv=pltpu.SemaphoreType.DMA((4,)),
        end_send=pltpu.SemaphoreType.DMA((4,)),
        end_recv=pltpu.SemaphoreType.DMA((4,)),
        slope_send=pltpu.SemaphoreType.DMA((2,)),
        slope_recv=pltpu.SemaphoreType.DMA((2,)),
    )
    names = (
        [name for name, _, _ in inputs] + [name for name, _, _ in outs] + [name for name, _ in scratch]
    )
    results = pl.pallas_call(
        functools.partial(layer_kernel, names),
        out_shape=tuple(jax.ShapeDtypeStruct(shape, kind) for _, shape, kind in outs),
        in_specs=[spec for _, _, spec in inputs],
        out_specs=(anywhere,) + (vmem,) * (len(outs) - 1),
        scratch_shapes=[kind for _, kind in scratch],
        compiler_params=pltpu.CompilerParams(
            collective_id=0, has_side_effects=True, vmem_limit_bytes=VMEM_BYTES
        ),
        name="layer",
    )(*[array for _, array, _ in inputs])
    return results[1:]


def deliver_kernel(count, *refs):
    sources, tile = refs[:count], refs[count]
    targets = refs[count + 1 : 2 * count + 1]
    vectors = refs[2 * count + 1 : -count - 2]
    stages = refs[-count - 2 : -2]
    get, put = refs[-2:]
    arriving = [
        pltpu.make_async_copy(sources[i], stages[i], get.at[i]) for i in range(count)
    ]
    leaving = [pltpu.make_async_copy(stages[i], targets[i], put.at[i]) for i in range(count)]
    for copy in arriving:
        copy.start()
    for i, vector in enumerate(vectors):
        vector[...] = tile[i, 0 : vector.shape[0]]
    for first, second in zip(arriving, leaving):
        first.wait()
        second.start()
    for copy in leaving:
        copy.wait()


def deliver(whole, tile, sizes):
    count = len(whole)
    anywhere = pl.BlockSpec(memory_space=pl.ANY)
    vmem = pl.BlockSpec(memory_space=pltpu.VMEM)
    return pl.pallas_call(
        functools.partial(deliver_kernel, count),
        out_shape=[jax.ShapeDtypeStruct(a.shape, a.dtype) for a in whole]
        + [jax.ShapeDtypeStruct((m,), jnp.float32) for m in sizes],
        in_specs=[anywhere] * count + [vmem],
        out_specs=[anywhere] * count + [vmem] * len(sizes),
        scratch_shapes=[pltpu.VMEM(a.shape, a.dtype) for a in whole]
        + [pltpu.SemaphoreType.DMA((count,))] * 2,
        compiler_params=pltpu.CompilerParams(vmem_limit_bytes=VMEM_BYTES),
        name="deliver",
    )(*whole, tile)


def body(
    tokens,
    band_mask,
    out_grad,
    norm1_gain,
    norm1_shift,
    qkv_weight,
    qv_bias,
    out_weight,
    out_bias,
    norm2_gain,
    norm2_shift,
    up_weight,
    up_bias,
    down_weight,
    down_bias,
):
    smalls = (norm1_gain, norm1_shift, qv_bias, out_bias, norm2_gain, norm2_shift, up_bias, down_bias)
    shards = (qkv_weight, out_weight, up_weight, down_weight)
    *whole, tile = layer_call(tokens, band_mask, out_grad, shards, smalls)
    output, input_grad, qkv, out, up, down, *grads = deliver(
        whole, tile, [v.shape[0] for v in smalls]
    )
    return (
        output,
        input_grad,
        grads[0],
        grads[1],
        qkv,
        grads[2],
        out,
        grads[3],
        grads[4],
        grads[5],
        up,
        grads[6],
        down,
        grads[7],
    )


def solution(mesh):
    rows, flat = P(AXES, None), P(AXES)
    params = (flat, flat, rows, flat, rows, flat, flat, flat, rows, flat, rows, flat)
    fitted = tuple(mesh.shape[axis] for axis in AXES) == (8, 4)
    return jax.shard_map(
        body if fitted else body_plain,
        mesh=mesh,
        in_specs=(rows, rows, rows) + params,
        out_specs=(rows, rows) + params,
        check_vma=False,
    )
```

```python
import functools
import math

import jax
import jax.numpy as jnp
from jax import lax
from jax.experimental import pallas as pl
from jax.experimental.pallas import tpu as pltpu
from jax.sharding import PartitionSpec as P

HEAD = 64
HEAD_GROUP = 4
QBLOCK = 512


NORM_EPSILON = 1e-05
VMEM_BYTES = 62 << 20
AXES = ("wide", "narrow")


def normalize(values, gain, shift):
    centre = jnp.mean(values, axis=1, keepdims=True)
    centred = values - centre
    factor = lax.rsqrt(jnp.mean(centred * centred, axis=1, keepdims=True) + NORM_EPSILON)
    normed = centred * factor
    return (normed * gain + shift, normed, factor)


def normalize_back(upstream, normed, factor, gain):
    gain_grad = jnp.sum(upstream * normed, axis=0)
    shift_grad = jnp.sum(upstream, axis=0)
    scaled = upstream * gain
    inner = (
        scaled
        - jnp.mean(scaled, axis=1, keepdims=True)
        - normed * jnp.mean(scaled * normed, axis=1, keepdims=True)
    )
    return (factor * inner, gain_grad, shift_grad)


def gelu_slope(values):
    cumulative = 0.5 * (1.0 + lax.erf(values * (1.0 / math.sqrt(2.0))))
    return cumulative + values * jnp.exp(-0.5 * values * values) * (1.0 / math.sqrt(2.0 * math.pi))


def to_groups(matrix, count):
    return matrix.reshape(matrix.shape[0], count, -1).transpose(1, 0, 2)


def from_groups(stacked):
    return stacked.transpose(1, 0, 2).reshape(stacked.shape[1], -1)


def attend_forward(query_cols, key_cols, value_cols, key_live):
    row_count, span_cols = key_cols.shape
    head_width = span_cols // HEAD_GROUP
    scaling = 1.0 / math.sqrt(head_width)
    key_rows = key_cols.reshape(row_count, HEAD_GROUP, head_width)
    value_rows = value_cols.reshape(row_count, HEAD_GROUP, head_width)
    query_blocks = query_cols.reshape(row_count // QBLOCK, QBLOCK, HEAD_GROUP, head_width)

    def one_block(query_rows):
        scores = (
            jnp.einsum("qhd,khd->hqk", query_rows, key_rows, preferred_element_type=jnp.float32)
            * scaling
        )
        scores = jnp.where(key_live[None, None, :], scores, -jnp.inf)
        largest = jnp.max(scores, axis=2, keepdims=True)
        expo = jnp.exp(scores - largest)
        totals = jnp.sum(expo, axis=2, keepdims=True)
        weights_low = (expo / totals).astype(jnp.bfloat16)
        mixture = jnp.einsum(
            "hqk,khd->qhd", weights_low, value_rows, preferred_element_type=jnp.float32
        )
        return (mixture.reshape(QBLOCK, span_cols), largest[:, :, 0] + jnp.log(totals[:, :, 0]))

    mixture, logsum = lax.map(one_block, query_blocks)
    return (mixture.reshape(row_count, span_cols), logsum)


def attend_backward(query_cols, key_cols, value_cols, grad_cols, logsum, key_live):
    row_count, span_cols = key_cols.shape
    head_width = span_cols // HEAD_GROUP
    scaling = 1.0 / math.sqrt(head_width)
    key_rows = key_cols.reshape(row_count, HEAD_GROUP, head_width)
    value_rows = value_cols.reshape(row_count, HEAD_GROUP, head_width)
    query_blocks = query_cols.reshape(row_count // QBLOCK, QBLOCK, HEAD_GROUP, head_width)
    grad_blocks = grad_cols.reshape(row_count // QBLOCK, QBLOCK, HEAD_GROUP, head_width)

    def one_block(carry, items):
        key_acc, value_acc = carry
        query_rows, grad_rows, block_logsum = items
        scores = (
            jnp.einsum("qhd,khd->hqk", query_rows, key_rows, preferred_element_type=jnp.float32)
            * scaling
        )
        scores = jnp.where(key_live[None, None, :], scores, -jnp.inf)
        probs = jnp.exp(scores - block_logsum[:, :, None])
        value_acc = value_acc + jnp.einsum(
            "hqk,qhd->khd",
            probs.astype(jnp.bfloat16),
            grad_rows,
            preferred_element_type=jnp.float32,
        )
        prob_grad = jnp.einsum(
            "qhd,khd->hqk", grad_rows, value_rows, preferred_element_type=jnp.float32
        )
        inner = jnp.sum(probs * prob_grad, axis=2, keepdims=True)
        score_grad = (probs * (prob_grad - inner)).astype(jnp.bfloat16)
        query_grad = (
            jnp.einsum("hqk,khd->qhd", score_grad, key_rows, preferred_element_type=jnp.float32)
            * scaling
        )
        key_acc = (
            key_acc
            + jnp.einsum("hqk,qhd->khd", score_grad, query_rows, preferred_element_type=jnp.float32)
            * scaling
        )
        return ((key_acc, value_acc), query_grad.reshape(QBLOCK, span_cols))

    empty = jnp.zeros((row_count, HEAD_GROUP, head_width), jnp.float32)
    (key_grad, value_grad), query_grad = lax.scan(
        one_block, (empty, empty), (query_blocks, grad_blocks, logsum)
    )
    return (
        query_grad.reshape(row_count, span_cols),
        key_grad.reshape(row_count, span_cols),
        value_grad.reshape(row_count, span_cols),
    )


def gathered(shard):
    return lax.all_gather(shard.astype(jnp.bfloat16), AXES, axis=0, tiled=True)


def scattered(part):
    return lax.psum_scatter(part, AXES, scatter_dimension=0, tiled=True)


def body_plain(
    tokens,
    band_mask,
    out_grad,
    norm1_gain,
    norm1_shift,
    qkv_weight,
    qv_bias,
    out_weight,
    out_bias,
    norm2_gain,
    norm2_shift,
    up_weight,
    up_bias,
    down_weight,
    down_bias,
):
    row_count, width = tokens.shape
    group_count = width // (HEAD_GROUP * HEAD)
    present = jnp.repeat(band_mask[0].astype(jnp.float32), row_count // band_mask.shape[1])
    key_live = present > 0.5
    column_mask = present[:, None]
    gain_one, shift_one, w_qkv, b_qv, w_out, b_out = (
        gathered(norm1_gain),
        gathered(norm1_shift),
        gathered(qkv_weight),
        gathered(qv_bias),
        gathered(out_weight),
        gathered(out_bias),
    )
    inputs = tokens.astype(jnp.float32)
    normed_one, unit_one, factor_one = normalize(
        inputs, gain_one.astype(jnp.float32), shift_one.astype(jnp.float32)
    )
    normed_one = normed_one.astype(jnp.bfloat16)
    bias_wide = b_qv.astype(jnp.float32)
    bias_full = jnp.concatenate(
        [bias_wide[:width], jnp.zeros((width,), jnp.float32), bias_wide[width:]]
    )
    joined = (jnp.dot(normed_one, w_qkv, preferred_element_type=jnp.float32) + bias_full).astype(
        jnp.bfloat16
    )
    query_groups = to_groups(joined[:, :width], group_count)
    key_groups = to_groups(joined[:, width : 2 * width], group_count)
    value_groups = to_groups(joined[:, 2 * width :], group_count)
    mixture, logsum = lax.map(
        lambda items: attend_forward(items[0], items[1], items[2], key_live),
        (query_groups, key_groups, value_groups),
    )
    mixture = from_groups(mixture).astype(jnp.bfloat16)
    attention = jnp.dot(mixture, w_out, preferred_element_type=jnp.float32) + b_out.astype(
        jnp.float32
    )
    middle = inputs + column_mask * attention
    gain_two, shift_two, w_up, b_up, w_down, b_down = (
        gathered(norm2_gain),
        gathered(norm2_shift),
        gathered(up_weight),
        gathered(up_bias),
        gathered(down_weight),
        gathered(down_bias),
    )
    normed_two, unit_two, factor_two = normalize(
        middle, gain_two.astype(jnp.float32), shift_two.astype(jnp.float32)
    )
    normed_two = normed_two.astype(jnp.bfloat16)
    hidden = jnp.dot(normed_two, w_up, preferred_element_type=jnp.float32) + b_up.astype(
        jnp.float32
    )
    active = jax.nn.gelu(hidden, approximate=False).astype(jnp.bfloat16)
    branch = jnp.dot(active, w_down, preferred_element_type=jnp.float32) + b_down.astype(
        jnp.float32
    )
    output = (middle + column_mask * branch).astype(jnp.bfloat16)
    upstream = out_grad.astype(jnp.float32)
    branch_grad = (column_mask * upstream).astype(jnp.bfloat16)
    down_weight_grad = jnp.einsum(
        "tf,td->fd", active, branch_grad, preferred_element_type=jnp.float32
    )
    down_bias_grad = jnp.sum(branch_grad.astype(jnp.float32), axis=0)
    active_grad = jnp.einsum(
        "td,fd->tf", branch_grad, w_down, preferred_element_type=jnp.float32
    )
    hidden_grad = (active_grad * gelu_slope(hidden)).astype(jnp.bfloat16)
    up_weight_grad = jnp.einsum(
        "td,tf->df", normed_two, hidden_grad, preferred_element_type=jnp.float32
    )
    up_bias_grad = jnp.sum(hidden_grad.astype(jnp.float32), axis=0)
    normed_two_grad = jnp.einsum(
        "tf,df->td", hidden_grad, w_up, preferred_element_type=jnp.float32
    )
    middle_part, norm2_gain_grad, norm2_shift_grad = normalize_back(
        normed_two_grad, unit_two, factor_two, gain_two.astype(jnp.float32)
    )
    (
        norm2_gain_grad,
        norm2_shift_grad,
        up_weight_grad,
        up_bias_grad,
        down_weight_grad,
        down_bias_grad,
    ) = (
        scattered(norm2_gain_grad),
        scattered(norm2_shift_grad),
        scattered(up_weight_grad),
        scattered(up_bias_grad),
        scattered(down_weight_grad),
        scattered(down_bias_grad),
    )
    middle_grad = upstream + middle_part
    attention_grad = (column_mask * middle_grad).astype(jnp.bfloat16)
    out_weight_grad = jnp.einsum(
        "te,td->ed", mixture, attention_grad, preferred_element_type=jnp.float32
    )
    out_bias_grad = jnp.sum(attention_grad.astype(jnp.float32), axis=0)
    mixture_grad = jnp.einsum(
        "td,ed->te", attention_grad, w_out, preferred_element_type=jnp.float32
    ).astype(jnp.bfloat16)
    grad_groups = to_groups(mixture_grad, group_count)
    query_grad, key_grad, value_grad = lax.map(
        lambda items: attend_backward(items[0], items[1], items[2], items[3], items[4], key_live),
        (query_groups, key_groups, value_groups, grad_groups, logsum),
    )
    query_grad = from_groups(query_grad).astype(jnp.bfloat16)
    key_grad = from_groups(key_grad).astype(jnp.bfloat16)
    value_grad = from_groups(value_grad).astype(jnp.bfloat16)
    joined_grad = jnp.concatenate([query_grad, key_grad, value_grad], axis=1)
    qkv_weight_grad = jnp.einsum(
        "td,tc->dc", normed_one, joined_grad, preferred_element_type=jnp.float32
    )
    qv_bias_grad = jnp.concatenate(
        [
            jnp.sum(query_grad.astype(jnp.float32), axis=0),
            jnp.sum(value_grad.astype(jnp.float32), axis=0),
        ]
    )
    normed_one_grad = jnp.einsum(
        "tc,dc->td", joined_grad, w_qkv, preferred_element_type=jnp.float32
    )
    input_part, norm1_gain_grad, norm1_shift_grad = normalize_back(
        normed_one_grad, unit_one, factor_one, gain_one.astype(jnp.float32)
    )
    input_grad = (middle_grad + input_part).astype(jnp.bfloat16)
    (
        norm1_gain_grad,
        norm1_shift_grad,
        qkv_weight_grad,
        qv_bias_grad,
        out_weight_grad,
        out_bias_grad,
    ) = (
        scattered(norm1_gain_grad),
        scattered(norm1_shift_grad),
        scattered(qkv_weight_grad),
        scattered(qv_bias_grad),
        scattered(out_weight_grad),
        scattered(out_bias_grad),
    )
    return (
        output,
        input_grad,
        norm1_gain_grad,
        norm1_shift_grad,
        qkv_weight_grad,
        qv_bias_grad,
        out_weight_grad,
        out_bias_grad,
        norm2_gain_grad,
        norm2_shift_grad,
        up_weight_grad,
        up_bias_grad,
        down_weight_grad,
        down_bias_grad,
    )


MESH_ID = pl.DeviceIdType.MESH
VIA_X = (0, 2)
VIA_Y = (1, 3)
ORDER = (1, 3, 2)
SCORE_SCALE = math.log2(math.e) / math.sqrt(HEAD)
TILE = 384


class Place:
    def __init__(self):
        wide = lax.axis_index("wide")
        narrow = lax.axis_index("narrow")
        z, y = wide // 2, wide % 2
        x, c = narrow // 2, narrow % 2
        self.z, self.c = z, c
        self.zs = (z, z + 1 - 2 * (z % 2), (z + 2) % 4, 3 - z)
        self.q = y * 2 + x
        self.qx = y * 2 + (1 - x)
        self.qy = (1 - y) * 2 + x
        self.qd = (1 - y) * 2 + (1 - x)
        self.to_z = tuple((zz * 2 + y, x * 2 + c) for zz in self.zs)
        self.to_x = (z * 2 + y, (1 - x) * 2 + c)
        self.to_y = (z * 2 + 1 - y, x * 2 + c)
        self.to_c = (z * 2 + y, x * 2 + 1 - c)


def span(start, size, step):
    return pl.ds(pl.multiple_of(start, step), size)


def meet(place):
    barrier = pltpu.get_barrier_semaphore()
    peers = place.to_z[1:] + (place.to_x, place.to_y, place.to_c)
    for peer in peers:
        pl.semaphore_signal(barrier, inc=1, device_id=peer, device_id_type=MESH_ID)
    pl.semaphore_wait(barrier, len(peers))


def remote(source, target, send, recv, peer):
    return pltpu.make_async_remote_copy(
        src_ref=source,
        dst_ref=target,
        send_sem=send,
        recv_sem=recv,
        device_id=peer,
        device_id_type=MESH_ID,
    )


class Piece:
    COUNT = 19

    def __init__(self, place, send, recv, slots, z_send=None):
        self.p = place
        self.send, self.recv, self.slots, self.z_send = send, recv, slots, z_send
        self.sent = []

    def pair(self, index):
        own = self.send if index >= 3 or self.z_send is None else self.z_send
        return own.at[index], self.recv.at[self.slots[index]]

    def go(self, source, target, index, peer):
        remote(source(), target(), *self.pair(index), peer).start()
        self.sent.append((source, target, index, peer))

    def got(self, target, index, peer):
        remote(target, target, *self.pair(index), peer).wait_recv()

    def finish(self):
        for source, target, index, peer in self.sent:
            remote(source(), target(), *self.pair(index), peer).wait_send()
        self.sent = []


class Gather(Piece):
    SLOTS = (0, 1, 2, 3, 4, 5, 6, 11, 11, 7, 8, 9, 10, 11, 11, 12, 12, 12, 12)

    def __init__(self, place, block, column, others, send, recv, z_send):
        super().__init__(place, send, recv, self.SLOTS, z_send)
        self.block, self.column, self.others = block, column, others

    def own(self):
        return self.block(self.p.z, self.p.q)

    def start_z(self):
        p = self.p
        for k in ORDER:
            self.go(self.own, self.own, k - 1, p.to_z[k])

    def start_xy(self):
        p = self.p
        self.go(self.own, self.own, 3, p.to_x)
        self.go(self.own, self.own, 9, p.to_y)

    def z(self, k):
        p = self.p
        here = lambda: self.block(p.zs[k], p.q)
        self.got(here(), k - 1, p.to_z[k])
        self.go(here, here, 3 + k, p.to_x)
        self.go(here, here, 9 + k, p.to_y)

    def share(self, index, q):
        column = lambda: self.column(q)
        self.go(column, column, index, self.p.to_c)

    def own_column(self):
        self.share(15, self.p.q)

    def xy(self, k):
        p = self.p
        from_x = lambda: self.block(p.zs[k], p.qx)
        self.got(from_x(), 3 + k, p.to_x)
        if k in VIA_X:
            self.go(from_x, from_x, 13 + VIA_X.index(k), p.to_y)
        from_y = lambda: self.block(p.zs[k], p.qy)
        self.got(from_y(), 9 + k, p.to_y)
        if k in VIA_Y:
            self.go(from_y, from_y, 7 + VIA_Y.index(k), p.to_x)

    def xy_columns(self):
        self.share(16, self.p.qx)
        self.share(17, self.p.qy)

    def d(self):
        p = self.p
        self.got(self.column(p.qd), 13, p.to_y)
        self.share(18, p.qd)

    def c(self):
        self.got(self.others(), 15, self.p.to_c)


class Scatter(Piece):
    SLOTS = (13, 13, 13, 5, 6, 7, 8, 1, 2, 9, 10, 11, 12, 3, 4, 0, 0, 0, 0)

    def __init__(self, place, block, column, whole, bufs, send, recv):
        super().__init__(place, send, recv, self.SLOTS)
        self.block, self.column, self.whole = block, column, whole
        self.dx, self.dy, self.xr, self.yr, self.zr = bufs

    def add(self, target, other):
        target[...] = (target[...].astype(jnp.float32) + other[...].astype(jnp.float32)).astype(
            target.dtype
        )

    def give(self, other):
        p = self.p
        for i, q in enumerate((p.qd, p.qx, p.qy, p.q)):
            self.go(lambda q=q: other(q), lambda q=q: self.column(q), 15 + i, p.to_c)

    def arrive(self):
        self.got(self.whole(), 15, self.p.to_c)

    def diagonal(self):
        p = self.p
        for i in range(2):
            self.go(
                lambda i=i: self.block(p.zs[VIA_X[i]], p.qd), lambda i=i: self.dx.at[i], 7 + i, p.to_x
            )
            self.go(
                lambda i=i: self.block(p.zs[VIA_Y[i]], p.qd), lambda i=i: self.dy.at[i], 13 + i, p.to_y
            )

    def cross(self, k):
        p = self.p
        on_x = lambda: self.block(p.zs[k], p.qx)
        on_y = lambda: self.block(p.zs[k], p.qy)
        if k in VIA_Y:
            i = VIA_Y.index(k)
            self.go(on_y, lambda: self.yr.at[k], 9 + k, p.to_y)
            self.got(self.dy.at[i], 13 + i, p.to_y)
            self.add(on_x(), self.dy.at[i])
            self.go(on_x, lambda: self.xr.at[k], 3 + k, p.to_x)
        else:
            i = VIA_X.index(k)
            self.go(on_x, lambda: self.xr.at[k], 3 + k, p.to_x)
            self.got(self.dx.at[i], 7 + i, p.to_x)
            self.add(on_y(), self.dx.at[i])
            self.go(on_y, lambda: self.yr.at[k], 9 + k, p.to_y)

    def plane(self, k):
        p = self.p
        self.got(self.xr.at[k], 3 + k, p.to_x)
        self.got(self.yr.at[k], 9 + k, p.to_y)
        here = self.block(p.zs[k], p.q)
        return here, (
            here[...].astype(jnp.float32)
            + self.xr[k].astype(jnp.float32)
            + self.yr[k].astype(jnp.float32)
        )

    def spread(self, k):
        p = self.p
        here, value = self.plane(k)
        here[...] = value.astype(here.dtype)
        self.go(lambda: self.block(p.zs[k], p.q), lambda: self.zr.at[k - 1], k - 1, p.to_z[k])

    def last(self):
        _, value = self.plane(0)
        self.got(self.zr, 0, self.p.to_z[1])
        for k in ORDER:
            value = value + self.zr[k - 1].astype(jnp.float32)
        return value


def scatter_buffers(tail, kind):
    return [
        pltpu.VMEM((2,) + tail, kind),
        pltpu.VMEM((2,) + tail, kind),
        pltpu.VMEM((4,) + tail, kind),
        pltpu.VMEM((4,) + tail, kind),
        pltpu.VMEM((3,) + tail, kind),
    ]


MATRICES = ("qkv", "out", "up", "down")


def triples(**named):
    return [(name, one, two) for name, (one, two) in named.items()]


def pairs_of(**named):
    return list(named.items())


class Named:
    def __init__(self, names, refs):
        assert len(names) == len(refs)
        self.__dict__.update(zip(names, refs))


def loop(first, count, compute, slots=()):
    def step(i, carry):
        compute(i)
        for j, steps in enumerate(slots):
            if steps:

                @pl.when(i == first + j)
                def _(steps=steps):
                    for one in steps:
                        one()

        return carry

    lax.fori_loop(first, first + count, step, 0)


def follow(order, steps, loops):
    at = 0
    while at < len(order):
        kind = order[at][0]
        if kind not in loops:
            steps[order[at]]()
            at += 1
            continue
        first, slots, end = order[at][1], [[]], at + 1
        held = []
        while end < len(order) and (order[end][0] not in loops or order[end][0] == kind):
            if order[end][0] == kind:
                slots[-1] += held
                held = []
                slots.append([])
                at = end
            else:
                held.append(steps[order[end]])
            end += 1
        if len(slots) == 1:
            loops[kind](jnp.int32(first))
        else:
            loop(first, len(slots), loops[kind], slots)
        at += 1


def dot(left, right):
    return jnp.dot(left, right, preferred_element_type=jnp.float32)


def dot_nt(left, right):
    return lax.dot_general(
        left, right, (((1,), (1,)), ((), ())), preferred_element_type=jnp.float32
    )


def dot_tn(left, right):
    return lax.dot_general(
        left, right, (((0,), (0,)), ((), ())), preferred_element_type=jnp.float32
    )


def head_only(values, e):
    lane = lax.broadcasted_iota(jnp.int32, values.shape, 1)
    return jnp.where((lane // HEAD) == e, values, jnp.zeros_like(values))


def fill_present(present, mask):
    groups = mask.shape[1]
    rows = present.shape[0] // groups
    for g in range(groups):
        present[g * rows : (g + 1) * rows, :] = jnp.full(
            (rows, 128), mask[0, g].astype(jnp.float32)
        )


def segments(width):
    return ((0, width, width // 32), (width, 2 * width, width // 16), (3 * width, 4 * width, width // 8))


def selection(size, m):
    lane = lax.broadcasted_iota(jnp.int32, (1, size), 1).astype(jnp.float32)
    rest = lane - m * jnp.floor((lane + 0.5) * (1.0 / m))
    row = lax.broadcasted_iota(jnp.int32, (128, size), 0).astype(jnp.float32)
    return jnp.where(row == rest, 1.0, 0.0).astype(jnp.bfloat16)


def owners(width):
    parts = []
    for _, size, m in segments(width):
        lane = lax.broadcasted_iota(jnp.int32, (1, size), 1).astype(jnp.float32)
        parts.append(jnp.floor((lane + 0.5) * (1.0 / m)))
    return jnp.concatenate(parts, axis=1)


def unit(values):
    centred = values - jnp.mean(values, axis=1, keepdims=True)
    factor = lax.rsqrt(jnp.mean(centred * centred, axis=1, keepdims=True) + NORM_EPSILON)
    return centred * factor, factor


(
    ATTENTION,
    CLOSE,
    CROSS,
    C_GOT,
    DIAGONAL,
    DOWN_HIGH,
    DOWN_LOW,
    DRAIN,
    D_GOT,
    EXPAND_HIGH,
    EXPAND_LOW,
    FINISH,
    FIRST_BACK,
    FIRST_NORM,
    FORM,
    GIVE,
    HEADS,
    HEADS_BACK,
    LAST,
    MASK_GRAD,
    NARROW,
    OUT_BACK,
    OWN_COLUMN,
    OWN_PART,
    PACK,
    QKV_BACK,
    SECOND_BACK,
    SECOND_NORM,
    SETTLE,
    SPREAD,
    START_XY,
    START_Z,
    UNPACK,
    UP_BACK,
    XY_COLUMNS,
    XY_GOT,
    Z_GOT,
) = range(37)
SEQUENCE = (
    (START_Z, 8),
    (START_XY, 8),
    (FORM, 0),
    (FORM, 1),
    (FORM, 2),
    (FORM, 3),
    (START_Z, 0),
    (START_Z, 1),
    (START_Z, 2),
    (START_Z, 3),
    (START_Z, 4),
    (START_Z, 5),
    (START_Z, 6),
    (START_Z, 7),
    (XY_GOT, 8, 0),
    (Z_GOT, 8, 1),
    (Z_GOT, 8, 3),
    (Z_GOT, 8, 2),
    (OWN_COLUMN, 8),
    (START_XY, 0),
    (START_XY, 1),
    (START_XY, 2),
    (MASK_GRAD, 0),
    (MASK_GRAD, 1),
    (START_XY, 3),
    (MASK_GRAD, 2),
    (XY_GOT, 8, 1),
    (XY_GOT, 8, 3),
    (XY_GOT, 8, 2),
    (XY_COLUMNS, 8),
    (MASK_GRAD, 3),
    (XY_GOT, 0, 0),
    (Z_GOT, 0, 3),
    (XY_GOT, 1, 0),
    (Z_GOT, 0, 2),
    (XY_GOT, 2, 0),
    (Z_GOT, 0, 1),
    (OWN_COLUMN, 0),
    (XY_GOT, 3, 0),
    (D_GOT, 8),
    (C_GOT, 8),
    (UNPACK,),
    (XY_GOT, 0, 2),
    (XY_GOT, 0, 3),
    (Z_GOT, 1, 3),
    (Z_GOT, 1, 2),
    (Z_GOT, 1, 1),
    (OWN_COLUMN, 1),
    (FIRST_NORM, 0),
    (FIRST_NORM, 1),
    (XY_GOT, 0, 1),
    (XY_COLUMNS, 0),
    (FIRST_NORM, 2),
    (FIRST_NORM, 3),
    (Z_GOT, 2, 3),
    (XY_GOT, 1, 3),
    (Z_GOT, 2, 2),
    (XY_GOT, 1, 2),
    (Z_GOT, 2, 1),
    (OWN_COLUMN, 2),
    (XY_GOT, 1, 1),
    (D_GOT, 0),
    (XY_COLUMNS, 1),
    (START_XY, 4),
    (XY_GOT, 2, 3),
    (C_GOT, 0),
    (HEADS, 0),
    (D_GOT, 1),
    (XY_GOT, 2, 1),
    (XY_GOT, 2, 2),
    (XY_COLUMNS, 2),
    (Z_GOT, 3, 1),
    (Z_GOT, 3, 3),
    (Z_GOT, 3, 2),
    (OWN_COLUMN, 3),
    (HEADS, 1),
    (C_GOT, 1),
    (XY_GOT, 4, 0),
    (START_XY, 5),
    (D_GOT, 2),
    (HEADS, 2),
    (C_GOT, 2),
    (XY_GOT, 3, 1),
    (XY_GOT, 3, 2),
    (XY_GOT, 3, 3),
    (XY_COLUMNS, 3),
    (Z_GOT, 4, 3),
    (HEADS, 3),
    (Z_GOT, 4, 1),
    (Z_GOT, 4, 2),
    (OWN_COLUMN, 4),
    (XY_GOT, 5, 0),
    (HEADS, 4),
    (D_GOT, 3),
    (XY_GOT, 4, 3),
    (HEADS, 5),
    (C_GOT, 3),
    (XY_GOT, 4, 1),
    (Z_GOT, 5, 3),
    (ATTENTION,),
    (XY_GOT, 4, 2),
    (XY_COLUMNS, 4),
    (SECOND_NORM, 0),
    (Z_GOT, 5, 2),
    (SECOND_NORM, 1),
    (SECOND_NORM, 2),
    (SECOND_NORM, 3),
    (Z_GOT, 5, 1),
    (OWN_COLUMN, 5),
    (XY_GOT, 5, 3),
    (D_GOT, 4),
    (START_XY, 6),
    (XY_GOT, 5, 2),
    (C_GOT, 4),
    (EXPAND_LOW, 0),
    (EXPAND_LOW, 1),
    (XY_GOT, 5, 1),
    (XY_COLUMNS, 5),
    (Z_GOT, 6, 3),
    (EXPAND_LOW, 2),
    (Z_GOT, 6, 2),
    (EXPAND_LOW, 3),
    (XY_GOT, 6, 0),
    (Z_GOT, 6, 1),
    (OWN_COLUMN, 6),
    (DOWN_LOW, 0),
    (DOWN_LOW, 1),
    (D_GOT, 5),
    (DOWN_LOW, 2),
    (DOWN_LOW, 3),
    (XY_GOT, 6, 3),
    (START_XY, 7),
    (C_GOT, 5),
    (EXPAND_HIGH, 0),
    (XY_GOT, 6, 2),
    (EXPAND_HIGH, 1),
    (Z_GOT, 7, 3),
    (EXPAND_HIGH, 2),
    (XY_GOT, 6, 1),
    (XY_COLUMNS, 6),
    (EXPAND_HIGH, 3),
    (Z_GOT, 7, 2),
    (DRAIN,),
    (DOWN_HIGH, 0),
    (Z_GOT, 7, 1),
    (XY_GOT, 7, 0),
    (OWN_COLUMN, 7),
    (DOWN_HIGH, 1),
    (DOWN_HIGH, 2),
    (XY_GOT, 7, 3),
    (DOWN_HIGH, 3),
    (GIVE, 0),
    (GIVE, 1),
    (D_GOT, 6),
    (XY_GOT, 7, 2),
    (XY_GOT, 7, 1),
    (XY_COLUMNS, 7),
    (OWN_PART, 0),
    (DIAGONAL, 0),
    (OWN_PART, 1),
    (D_GOT, 7),
    (DIAGONAL, 1),
    (C_GOT, 6),
    (CROSS, 0, 1),
    (CROSS, 0, 0),
    (CROSS, 0, 3),
    (C_GOT, 7),
    (NARROW, 0),
    (CROSS, 0, 2),
    (CROSS, 1, 1),
    (NARROW, 1),
    (CROSS, 1, 0),
    (CROSS, 1, 3),
    (NARROW, 2),
    (CROSS, 1, 2),
    (NARROW, 3),
    (SPREAD, 0, 1),
    (NARROW, 4),
    (NARROW, 5),
    (NARROW, 6),
    (SPREAD, 0, 3),
    (NARROW, 7),
    (SPREAD, 0, 2),
    (GIVE, 2),
    (SPREAD, 1, 1),
    (GIVE, 3),
    (SPREAD, 1, 3),
    (OWN_PART, 2),
    (SPREAD, 1, 2),
    (DIAGONAL, 2),
    (FINISH, 0),
    (FINISH, 1),
    (FINISH, 2),
    (FINISH, 3),
    (UP_BACK,),
    (CROSS, 2, 0),
    (CROSS, 2, 1),
    (LAST, 0),
    (OWN_PART, 3),
    (CROSS, 2, 2),
    (CROSS, 2, 3),
    (DIAGONAL, 3),
    (SECOND_BACK, 0),
    (SECOND_BACK, 1),
    (SECOND_BACK, 2),
    (SECOND_BACK, 3),
    (GIVE, 4),
    (OUT_BACK,),
    (SPREAD, 2, 1),
    (HEADS_BACK, 0),
    (SPREAD, 2, 3),
    (SPREAD, 2, 2),
    (LAST, 1),
    (CLOSE, 3),
    (OWN_PART, 4),
    (CROSS, 3, 0),
    (CROSS, 3, 1),
    (DIAGONAL, 4),
    (HEADS_BACK, 1),
    (CROSS, 3, 2),
    (CROSS, 3, 3),
    (SETTLE, 3),
    (GIVE, 5),
    (HEADS_BACK, 2),
    (SPREAD, 3, 1),
    (CROSS, 4, 0),
    (CROSS, 4, 1),
    (CROSS, 4, 2),
    (CROSS, 4, 3),
    (OWN_PART, 5),
    (DIAGONAL, 5),
    (SPREAD, 3, 2),
    (LAST, 2),
    (HEADS_BACK, 3),
    (SPREAD, 3, 3),
    (GIVE, 6),
    (SPREAD, 4, 1),
    (HEADS_BACK, 4),
    (SPREAD, 4, 3),
    (SPREAD, 4, 2),
    (CROSS, 5, 0),
    (CROSS, 5, 1),
    (CROSS, 5, 2),
    (CROSS, 5, 3),
    (OWN_PART, 6),
    (DIAGONAL, 6),
    (HEADS_BACK, 5),
    (SPREAD, 5, 1),
    (LAST, 3),
    (SPREAD, 5, 2),
    (CLOSE, 2),
    (GIVE, 7),
    (SPREAD, 5, 3),
    (CROSS, 6, 0),
    (CROSS, 6, 1),
    (SETTLE, 2),
    (LAST, 4),
    (CROSS, 6, 2),
    (CROSS, 6, 3),
    (CLOSE, 1),
    (OWN_PART, 7),
    (DIAGONAL, 7),
    (SETTLE, 1),
    (QKV_BACK,),
    (SPREAD, 6, 1),
    (SPREAD, 6, 3),
    (SPREAD, 6, 2),
    (CROSS, 7, 0),
    (CROSS, 7, 1),
    (LAST, 5),
    (CROSS, 7, 2),
    (CROSS, 7, 3),
    (FIRST_BACK, 0),
    (FIRST_BACK, 1),
    (FIRST_BACK, 2),
    (FIRST_BACK, 3),
    (PACK, 0),
    (SPREAD, 7, 1),
    (PACK, 1),
    (PACK, 2),
    (SPREAD, 7, 2),
    (PACK, 3),
    (GIVE, 8),
    (SPREAD, 7, 3),
    (LAST, 6),
    (OWN_PART, 8),
    (DIAGONAL, 8),
    (CROSS, 8, 0),
    (CROSS, 8, 1),
    (CROSS, 8, 2),
    (CROSS, 8, 3),
    (LAST, 7),
    (SPREAD, 8, 1),
    (SPREAD, 8, 2),
    (SPREAD, 8, 3),
    (CLOSE, 0),
    (SETTLE, 0),
    (LAST, 8),
)


def layer_kernel(names, *refs):
    r = Named(names, refs)
    place = Place()
    c = place.c
    tokens, width = r.tokens.shape
    hidden = r.act.shape[1]
    third = width // 2
    tiles = hidden // TILE
    shards = (r.qkv_shard, r.out_shard, r.up_shard, r.down_shard)
    meet(place)

    moves = [(0, g * width, third, (g,)) for g in range(3)] + [
        (i, 0, shards[i].shape[1] // 2, ()) for i in (1, 2, 3)
    ]
    sibs = (r.qkv_sib, r.out_sib, r.up_sib, r.down_sib)
    wides = (r.qkv_wide, r.out_wide, r.up_wide, r.down_wide)

    def before(m):
        i, start, cols, at = moves[m]
        source = shards[i].at[:, span(start + (1 - c) * cols, cols, 128)]
        target = sibs[i].at[at] if at else sibs[i]
        return remote(source, target, r.pre_send.at[m], r.pre_recv.at[m], place.to_c)

    for m in range(6):
        before(m).start()
    r.small_wide[place.z, place.q, c] = jnp.zeros((8, 128), jnp.float32)
    for i in range(8):
        vector = getattr(r, "vector%d" % i)
        r.small_wide[place.z, place.q, c, i : i + 1, 0 : vector.shape[0]] = vector[...].reshape(1, -1)

    def gather(j, block, column, others):
        lane = 4 if j == 8 else j % 4
        return Gather(
            place, block, column, others, r.send.at[lane], r.gather_recv.at[j], r.gather_z.at[j]
        )

    every = slice(None)
    pieces = []
    for s in range(3):
        cols = lambda side, s=s: span(side * third + 128 * s, 128, 128)
        pieces.append(
            gather(
                s,
                lambda zz, q, cols=cols: r.qkv_wide.at[:, zz, q, :, cols(c)],
                lambda q, cols=cols: r.qkv_wide.at[:, :, q, :, cols(c)],
                lambda cols=cols: r.qkv_wide.at[:, :, :, :, cols(1 - c)],
            )
        )
    cuts = (
        (1, 0, 48, 0, 384),
        (2, 0, 48, 0, 768),
        (2, 0, 48, 768, 768),
        (3, 0, 96, 0, 384),
        (3, 96, 96, 0, 384),
    )
    for j, (i, row, rows, col, cols) in enumerate(cuts):
        half = shards[i].shape[1] // 2

        def at(side, row=row, rows=rows, col=col, cols=cols, half=half):
            return (pl.ds(row, rows), span(side * half + col, cols, 128))

        pieces.append(
            gather(
                3 + j,
                lambda zz, q, i=i, at=at: wides[i].at[(zz, q) + at(c)],
                lambda q, i=i, at=at: wides[i].at[(every, q) + at(c)],
                lambda i=i, at=at: wides[i].at[(every, every) + at(1 - c)],
            )
        )
    pieces.append(
        gather(
            8,
            lambda zz, q: r.small_wide.at[zz, q, c],
            lambda q: r.small_wide.at[:, q, c],
            lambda: r.small_wide.at[:, :, 1 - c],
        )
    )

    def form(i):
        for m, (weight, start, cols, at) in enumerate(moves):
            if weight == i:
                before(m).wait_recv()
                mine = shards[i][:, span(start + c * cols, cols, 128)]
                theirs = sibs[i][at] if at else sibs[i][...]
                wides[i][at + (place.z, place.q, every, span(c * cols, cols, 128))] = jnp.concatenate(
                    [jnp.where(c == 0, mine, theirs), jnp.where(c == 0, theirs, mine)], axis=0
                ).astype(jnp.bfloat16)

    fill_present(r.present, r.mask)
    r.sums[...] = jnp.zeros_like(r.sums)
    r.owner[...] = owners(width)
    r.vec[...] = jnp.zeros_like(r.vec)

    def unpack():
        for zz in range(4):
            rows = r.small_wide[zz].reshape(64, 128).astype(jnp.bfloat16)
            for start, size, m in segments(width):
                lanes = slice(start, start + size)
                picked = dot(rows, selection(size, m))
                total = r.vec[:, lanes]
                for d in range(8):
                    total = total + jnp.where(
                        r.owner[:, lanes] == zz * 8 + d, picked[d * 8 : d * 8 + 8], 0.0
                    )
                r.vec[:, lanes] = total
        for s in range(3):
            r.bias[s] = jnp.zeros((8, 6 * 128), jnp.float32)
            for e in range(2):
                at = 128 * s + third * e
                r.bias[s, 0:1, 128 * e : 128 * e + 128] = r.vec[2:3, width + at : width + at + 128]
                r.bias[s, 0:1, 512 + 128 * e : 640 + 128 * e] = r.vec[
                    2:3, 2 * width + at : 2 * width + at + 128
                ]

    def first_norm(t):
        rows = span(t * 128, 128, 128)
        normed, _ = unit(r.tokens[rows, :].astype(jnp.float32))
        value = normed * r.vec[0:1, 0:width] + r.vec[1:2, 0:width]
        r.normed[rows, :] = value.astype(jnp.bfloat16)
        r.turned_one[:, rows] = value.T.astype(jnp.bfloat16)

    def mask_grad(t):
        rows = span(t * 128, 128, 128)
        low = (r.present[rows, 0:1] * r.out_grad[rows, :].astype(jnp.float32)).astype(jnp.bfloat16)
        r.grad_low[rows, :] = low
        r.sums[7:8, 0:width] += jnp.sum(low.astype(jnp.float32), axis=0, keepdims=True)

    def heads(i):
        s, e = i // 2, i % 2

        @pl.when(e == 0)
        def _():
            weights = [
                r.qkv_wide[g, :, :, :, span(half * third + s * 128, 128, 128)].reshape(width, 128)
                for g in range(3)
                for half in range(2)
            ]
            value = dot(r.normed[...], jnp.concatenate(weights, axis=1)) + r.bias[s, 0:1, :]
            value = value.astype(jnp.bfloat16)
            for g in range(3):
                for half in range(2):
                    at = (2 * g + half) * 128
                    r.joined[s + 3 * half, g] = value[:, at : at + 128]

        hp = s + 3 * e
        cols = span(hp * 128, 128, 128)
        query, key, value = r.joined[hp, 0], r.joined[hp, 1], r.joined[hp, 2].T
        live = r.present[:, 0:1] > 0.5
        mixed = []
        for e in range(2):
            scores = dot_nt(head_only(key, e), query) * SCORE_SCALE
            scores = jnp.where(live, scores, -jnp.inf)
            largest = jnp.max(scores, axis=0, keepdims=True)
            expo = jnp.exp2(scores - largest)
            totals = jnp.sum(expo, axis=0, keepdims=True)
            probs = (expo * (1.0 / totals)).astype(jnp.bfloat16)
            mixed.append(dot(value[HEAD * e : HEAD * (e + 1)], probs))
            r.logsum[hp, e : e + 1, :] = largest + jnp.log2(totals)
        both = jnp.concatenate(mixed, axis=0)
        r.mixed_turned[cols, :] = both.astype(jnp.bfloat16)
        r.mixed[:, cols] = both.T.astype(jnp.bfloat16)

    def attention():
        r.middle[...] = dot(r.mixed[...], r.out_wide[...].reshape(width, width))

    def second_norm(t):
        rows = span(t * 128, 128, 128)
        present = r.present[rows, 0:1]
        middle = r.tokens[rows, :].astype(jnp.float32) + present * (
            r.middle[rows, :] + r.vec[3:4, 0:width]
        )
        r.middle[rows, :] = middle
        normed, _ = unit(middle)
        value = normed * r.vec[4:5, 0:width] + r.vec[5:6, 0:width]
        r.normed[rows, :] = value.astype(jnp.bfloat16)
        r.turned_two[:, rows] = value.T.astype(jnp.bfloat16)

    def slope_out(t, slot):
        return pltpu.make_async_copy(r.slope.at[slot], r.slope_far.at[t], r.slope_send.at[slot])

    def slope_in(t, slot):
        return pltpu.make_async_copy(r.slope_far.at[t], r.slope.at[slot], r.slope_recv.at[slot])

    def expand(t, u):
        slot = u % 2

        @pl.when(u >= 2)
        def _():
            slope_out(t, slot).wait()

        cols = span(t * TILE, TILE, 128)
        value = (
            dot(r.normed[...], r.up_wide[:, :, :, cols].reshape(width, TILE))
            + r.vec[6:7, span(3 * width + t * TILE, TILE, 128)]
        )
        cumulative = 0.5 * (1.0 + lax.erf(value * (1.0 / math.sqrt(2.0))))
        r.act[:, cols] = (value * cumulative).astype(jnp.bfloat16)
        r.slope[slot] = cumulative + value * jnp.exp(-0.5 * value * value) * (
            1.0 / math.sqrt(2.0 * math.pi)
        )
        slope_out(t, slot).start()

    def down_grad(t):
        cols = span(t * TILE, TILE, 128)
        grad = dot_tn(r.act[:, cols], r.grad_low[...]).astype(jnp.bfloat16)
        r.down_part[t // 2, pl.ds((t % 2) * 2, 2)] = grad.reshape(2, TILE // 2, width)

    low_tile = lambda u: u + 2 * (u // 2)
    high_tile = lambda u: u + 2 * (u // 2) + 2

    def scatter(j, block, column, whole):
        bufs = [getattr(r, "piece%d_%d" % (j, b)) for b in range(5)]
        lane = 4 if j == 8 else j % 4
        return Scatter(
            place, block, column, whole, bufs, r.send.at[lane], r.scatter_recv.at[j]
        )

    sums = []
    for s in range(2):
        rows = pl.ds(96 * s, 96)
        sums.append(
            scatter(
                s,
                lambda zz, q, rows=rows: r.down_total.at[zz, q, rows],
                lambda q, rows=rows: r.down_total.at[:, q, rows],
                lambda rows=rows: r.down_total.at[:, :, rows],
            )
        )
    for s in range(2):
        sums.append(
            scatter(
                2 + s,
                lambda zz, q, s=s: r.up_total.at[s, zz, q],
                lambda q, s=s: r.up_total.at[s, :, q],
                lambda s=s: r.up_total.at[s],
            )
        )
    sums.append(
        scatter(
            4,
            lambda zz, q: r.out_total.at[zz, q],
            lambda q: r.out_total.at[:, q],
            lambda: r.out_total,
        )
    )
    for s in range(3):
        sums.append(
            scatter(
                5 + s,
                lambda zz, q, s=s: r.qkv_total.at[s, zz, q],
                lambda q, s=s: r.qkv_total.at[s, :, q],
                lambda s=s: r.qkv_total.at[s],
            )
        )
    sums.append(
        scatter(
            8,
            lambda zz, q: r.small_total.at[zz, q],
            lambda q: r.small_total.at[:, q],
            lambda: r.small_total,
        )
    )

    def up_part(side, s):
        cols = span(side * (hidden // 2) + 768 * s, 768, 128)
        return dot(r.turned_two[...], r.act[:, cols]).reshape(4, 4, 48, 768)

    def out_part(side):
        cols = span(side * third, third, 128)
        return dot(r.mixed_turned[...], r.normed[:, cols]).reshape(4, 4, 48, third)

    def qkv_part(side, s):
        hp = side * 3 + s
        grads = jnp.concatenate([r.joined[hp, g] for g in range(3)], axis=1)
        return dot(r.turned_one[...], grads)

    def other_part(p):
        if p in (2, 3):
            r.down_wide[:, :, 48 * (p - 2) : 48 * (p - 1), :] = up_part(1 - c, p - 2).astype(
                jnp.bfloat16
            )
        elif p == 4:
            r.down_wide[:, :, 96:144, 0:384] = out_part(1 - c).astype(jnp.bfloat16)
        else:
            value = qkv_part(1 - c, p - 5).astype(jnp.bfloat16)
            for g in range(3):
                r.down_part[:, :, 48 * g : 48 * g + 48, 128 * (p - 5) : 128 * (p - 4)] = value[
                    :, 128 * g : 128 * g + 128
                ].reshape(4, 4, 48, 128)

    def given(p):
        if p < 2:
            rows, cols = pl.ds(96 * p, 96), span((1 - c) * 384, 384, 128)
            return lambda q: r.down_part.at[:, q, rows, cols]
        if p < 4:
            return lambda q: r.down_wide.at[:, q, pl.ds(48 * (p - 2), 48)]
        if p == 4:
            return lambda q: r.down_wide.at[:, q, pl.ds(96, 48), pl.ds(0, 384)]
        if p < 8:
            return lambda q: r.down_part.at[:, q, pl.ds(0, 144), pl.ds(128 * (p - 5), 128)]
        return lambda q: r.small_part.at[:, q, 1 - c]

    def wide_sum(total, value):
        total[...] = (total[...].astype(jnp.float32) + value).astype(total.dtype)

    def own_part(p):
        sums[p].arrive()
        if p < 2:
            rows = pl.ds(96 * p, 96)
            mine = r.down_part[:, :, rows, span(c * 384, 384, 128)].astype(jnp.float32)
            wide_sum(r.down_total.at[:, :, rows], mine)
        elif p < 4:
            wide_sum(r.up_total.at[p - 2], up_part(c, p - 2))
        elif p == 4:
            wide_sum(r.out_total, out_part(c))
        elif p < 8:
            value = qkv_part(c, p - 5)
            for g in range(3):
                wide_sum(
                    r.qkv_total.at[p - 5, :, :, pl.ds(48 * g, 48)],
                    value[:, 128 * g : 128 * g + 128].reshape(4, 4, 48, 128),
                )
        else:
            wide_sum(r.small_total, r.small_part[:, :, c])

    def narrow(t):
        slot = t % 2

        @pl.when(t == 0)
        def _():
            slope_in(0, 0).start()
            r.acc[...] = jnp.zeros_like(r.acc)

        slope_in(t, slot).wait()

        @pl.when(t + 1 < tiles)
        def _():
            slope_in(t + 1, 1 - slot).start()

        cols = span(t * TILE, TILE, 128)
        weights = r.down_wide[t // 2, pl.ds((t % 2) * 2, 2)].reshape(TILE, width)
        r.acc[...] += dot(r.act[:, cols], weights)
        grad = (dot_nt(r.grad_low[...], weights) * r.slope[slot]).astype(jnp.bfloat16)
        r.act[:, cols] = grad
        r.sums[6:7, span(3 * width + t * TILE, TILE, 128)] = jnp.sum(
            grad.astype(jnp.float32), axis=0, keepdims=True
        )

    def drain_slope():
        for slot in range(2):
            slope_out(0, slot).wait()

    def finish_output(t):
        rows = span(t * 128, 128, 128)
        r.output[rows, :] = (
            r.middle[rows, :]
            + r.present[rows, 0:1] * (r.acc[rows, :] + r.vec[7:8, 0:width])
        ).astype(jnp.bfloat16)

    def up_back():
        r.acc[...] = dot_nt(r.act[...], r.up_wide[...].reshape(width, hidden))

    def norm_back(up, normed, factor, index):
        r.sums[index : index + 1, 0:width] += jnp.sum(up * normed, axis=0, keepdims=True)
        r.sums[index + 1 : index + 2, 0:width] += jnp.sum(up, axis=0, keepdims=True)
        scaled = up * r.vec[index : index + 1, 0:width]
        return factor * (
            scaled
            - jnp.mean(scaled, axis=1, keepdims=True)
            - normed * jnp.mean(scaled * normed, axis=1, keepdims=True)
        )

    def second_back(t):
        rows = span(t * 128, 128, 128)
        normed, factor = unit(r.middle[rows, :])
        grad = r.out_grad[rows, :].astype(jnp.float32) + norm_back(
            r.acc[rows, :], normed, factor, 4
        )
        r.middle[rows, :] = grad
        low = (r.present[rows, 0:1] * grad).astype(jnp.bfloat16)
        r.normed[rows, :] = low
        r.sums[3:4, 0:width] += jnp.sum(low.astype(jnp.float32), axis=0, keepdims=True)

    def out_back():
        r.mixed[...] = dot_nt(r.normed[...], r.out_wide[...].reshape(width, width)).astype(
            jnp.bfloat16
        )

    def heads_back(i):
        hp = i // 2 + 3 * (i % 2)
        cols = span(hp * 128, 128, 128)
        query, key, value = r.joined[hp, 0], r.joined[hp, 1], r.joined[hp, 2]
        grad = r.mixed[:, cols]
        turned = key.T
        live = r.present[:, 0:1] > 0.5
        value_grad = jnp.zeros((tokens, 128), jnp.float32)
        key_grad = jnp.zeros((tokens, 128), jnp.float32)
        query_grad = []
        for e in range(2):
            scores = dot_nt(head_only(key, e), query) * SCORE_SCALE
            scores = jnp.where(live, scores, -jnp.inf)
            probs = jnp.exp2(scores - r.logsum[hp, e : e + 1, :])
            back = dot_nt(head_only(value, e), grad)
            inner = jnp.sum(probs * back, axis=0, keepdims=True)
            score_grad = (probs * (back - inner)).astype(jnp.bfloat16)
            value_grad = value_grad + dot(probs.astype(jnp.bfloat16), head_only(grad, e))
            key_grad = key_grad + dot(score_grad, head_only(query, e))
            query_grad.append(dot(turned[HEAD * e : HEAD * (e + 1)], score_grad))
        scale = 1.0 / math.sqrt(HEAD)
        query_low = (jnp.concatenate(query_grad, axis=0).T * scale).astype(jnp.bfloat16)
        value_low = value_grad.astype(jnp.bfloat16)
        r.joined[hp, 0] = query_low
        r.joined[hp, 1] = (key_grad * scale).astype(jnp.bfloat16)
        r.joined[hp, 2] = value_low
        r.sums[2:3, span(width + hp * 128, 128, 128)] = jnp.sum(
            query_low.astype(jnp.float32), axis=0, keepdims=True
        )
        r.sums[2:3, span(2 * width + hp * 128, 128, 128)] = jnp.sum(
            value_low.astype(jnp.float32), axis=0, keepdims=True
        )

    def qkv_back():
        total = jnp.zeros((tokens, width), jnp.float32)
        for g in range(3):
            grads = jnp.concatenate([r.joined[hp, g] for hp in range(6)], axis=1)
            total = total + dot_nt(grads, r.qkv_wide[g].reshape(width, width))
        r.acc[...] = total

    def first_back(t):
        rows = span(t * 128, 128, 128)
        normed, factor = unit(r.tokens[rows, :].astype(jnp.float32))
        part = norm_back(r.acc[rows, :], normed, factor, 0)
        r.input_grad[rows, :] = (r.middle[rows, :] + part).astype(jnp.bfloat16)

    def pack(zz):
        first = (zz * 8).astype(jnp.float32)
        for index, (start, size, m) in zip((None, 2, 6), segments(width)):
            lanes = slice(start, start + size)
            left = r.sums[:, lanes] if index is None else r.sums[index : index + 1, lanes]
            owner = r.owner[:, lanes] - first
            chosen = selection(size, m)
            tile = 0.0
            for _ in range(2):
                part = left.astype(jnp.bfloat16).astype(jnp.float32)
                left = left - part
                rows = jnp.concatenate(
                    [jnp.where(owner == d, part, 0.0) for d in range(8)], axis=0
                ).astype(jnp.bfloat16)
                tile = tile + dot_nt(rows, chosen)
            if index is None:
                r.small_part[zz] = tile.reshape(4, 2, 8, 128)
            else:
                for d in range(8):
                    r.small_part[zz, d // 2, d % 2, index : index + 1, :] = tile[d : d + 1, :]

    results = (r.qkv_result, r.out_result, r.up_result, r.down_result)
    finals = (r.qkv_final, r.out_final, r.up_final, r.down_final)

    def swap(m, side):
        i, start, cols, at = moves[m]
        rows = results[i].shape[0]
        return remote(
            finals[i].at[at + (span((1 - c) * rows, rows, 8),)],
            results[i].at[:, span(start + side * cols, cols, 128)],
            r.end_send.at[m],
            r.end_recv.at[m],
            place.to_c,
        )

    def close(i):
        for m, (weight, start, cols, at) in enumerate(moves):
            if weight == i:
                rows = results[i].shape[0]
                swap(m, c).start()
                results[i][:, span(start + c * cols, cols, 128)] = finals[i][
                    at + (span(c * rows, rows, 8),)
                ]

    def settle(i):
        for m, move in enumerate(moves):
            if move[0] == i:
                swap(m, 1 - c).wait_recv()

    def last(p):
        value = sums[p].last()
        if p < 2:
            r.down_final[96 * p : 96 * p + 96, :] = value
        elif p < 4:
            r.up_final[:, 768 * (p - 2) : 768 * (p - 1)] = value
        elif p == 4:
            r.out_final[...] = value
        elif p < 8:
            for g in range(3):
                r.qkv_final[g, :, 128 * (p - 5) : 128 * (p - 4)] = value[48 * g : 48 * g + 48]
        else:
            r.small_result[...] = value

    def start_xy(j):
        if 4 <= j < 8:
            pieces[j - 4].finish()
        pieces[j].start_xy()

    def give(p):
        before_it = pieces[8] if p == 8 else (sums[p - 4] if p >= 4 else pieces[p + 4])
        before_it.finish()
        if 2 <= p < 8:
            other_part(p)
        sums[p].give(given(p))

    steps = {(UNPACK,): unpack, (ATTENTION,): attention, (DRAIN,): drain_slope}
    steps.update({(UP_BACK,): up_back, (OUT_BACK,): out_back, (QKV_BACK,): qkv_back})
    for i in range(4):
        steps[FORM, i] = functools.partial(form, i)
        steps[CLOSE, i] = functools.partial(close, i)
        steps[SETTLE, i] = functools.partial(settle, i)
    for j in range(9):
        piece, total = pieces[j], sums[j]
        steps[START_Z, j] = piece.start_z
        steps[START_XY, j] = functools.partial(start_xy, j)
        steps[OWN_COLUMN, j] = piece.own_column
        steps[XY_COLUMNS, j] = piece.xy_columns
        steps[D_GOT, j] = piece.d
        steps[C_GOT, j] = piece.c
        steps[GIVE, j] = functools.partial(give, j)
        steps[OWN_PART, j] = functools.partial(own_part, j)
        steps[DIAGONAL, j] = total.diagonal
        steps[LAST, j] = functools.partial(last, j)
        for k in range(4):
            steps[Z_GOT, j, k] = functools.partial(piece.z, k)
            steps[XY_GOT, j, k] = functools.partial(piece.xy, k)
            steps[CROSS, j, k] = functools.partial(total.cross, k)
            steps[SPREAD, j, k] = functools.partial(total.spread, k)
    loops = {
        FIRST_NORM: first_norm,
        MASK_GRAD: mask_grad,
        HEADS: heads,
        SECOND_NORM: second_norm,
        EXPAND_LOW: lambda u: expand(low_tile(u), u),
        EXPAND_HIGH: lambda u: expand(high_tile(u), u + 4),
        DOWN_LOW: lambda u: down_grad(low_tile(u)),
        DOWN_HIGH: lambda u: down_grad(high_tile(u)),
        NARROW: narrow,
        FINISH: finish_output,
        SECOND_BACK: second_back,
        HEADS_BACK: heads_back,
        FIRST_BACK: first_back,
        PACK: pack,
    }
    follow(SEQUENCE, steps, loops)
    for m in range(6):
        before(m).wait_send()
        swap(m, c).wait_send()
    for piece in pieces + sums:
        piece.finish()


def layer_call(tokens, band_mask, out_grad, shards, smalls):
    bf16, f32 = jnp.bfloat16, jnp.float32
    count, width = tokens.shape
    shapes = [s.shape for s in shards]
    hidden = shapes[2][1]
    tiles = hidden // TILE
    vmem = pl.BlockSpec(memory_space=pltpu.VMEM)
    anywhere = pl.BlockSpec(memory_space=pl.ANY)
    inputs = triples(
        tokens=(tokens, vmem),
        mask=(band_mask, pl.BlockSpec(memory_space=pltpu.SMEM)),
        out_grad=(out_grad, vmem),
        qkv_shard=(shards[0], vmem),
        out_shard=(shards[1], vmem),
        up_shard=(shards[2], vmem),
        down_shard=(shards[3], vmem),
    ) + [("vector%d" % i, v, vmem) for i, v in enumerate(smalls)]
    outs = triples(
        slope_far=((tiles, count, TILE), f32),
        output=((count, width), bf16),
        input_grad=((count, width), bf16),
        qkv_result=(shapes[0], f32),
        out_result=(shapes[1], f32),
        up_result=(shapes[2], f32),
        down_result=(shapes[3], f32),
        small_result=((8, 128), f32),
    )
    tails = (
        [((96, 384), bf16)] * 2
        + [((48, 768), bf16)] * 2
        + [((48, 384), bf16)]
        + [((144, 128), bf16)] * 3
        + [((8, 128), f32)]
    )
    scratch = []
    for j, (tail, kind) in enumerate(tails):
        for b, one in enumerate(scatter_buffers(tail, kind)):
            scratch.append(("piece%d_%d" % (j, b), one))
    scratch += pairs_of(
        qkv_wide=pltpu.VMEM((3, 4, 4, 48, width), bf16),
        out_wide=pltpu.VMEM((4, 4, 48, width), bf16),
        up_wide=pltpu.VMEM((4, 4, 48, hidden), bf16),
        down_wide=pltpu.VMEM((4, 4, 192, width), bf16),
        qkv_sib=pltpu.VMEM((3, 24, width // 2), f32),
        out_sib=pltpu.VMEM((24, width // 2), f32),
        up_sib=pltpu.VMEM((24, hidden // 2), f32),
        down_sib=pltpu.VMEM((96, width // 2), f32),
        qkv_final=pltpu.VMEM((3, 48, width // 2), f32),
        out_final=pltpu.VMEM((48, width // 2), f32),
        up_final=pltpu.VMEM((48, hidden // 2), f32),
        down_final=pltpu.VMEM((192, width // 2), f32),
        small_wide=pltpu.VMEM((4, 4, 2, 8, 128), f32),
        small_part=pltpu.VMEM((4, 4, 2, 8, 128), f32),
        small_total=pltpu.VMEM((4, 4, 8, 128), f32),
        down_part=pltpu.VMEM((4, 4, 192, width), bf16),
        down_total=pltpu.VMEM((4, 4, 192, 384), bf16),
        up_total=pltpu.VMEM((2, 4, 4, 48, 768), bf16),
        out_total=pltpu.VMEM((4, 4, 48, 384), bf16),
        qkv_total=pltpu.VMEM((3, 4, 4, 144, 128), bf16),
        present=pltpu.VMEM((count, 128), f32),
        vec=pltpu.VMEM((8, 7 * width), f32),
        sums=pltpu.VMEM((8, 7 * width), f32),
        bias=pltpu.VMEM((3, 8, width), f32),
        owner=pltpu.VMEM((1, 7 * width), f32),
        logsum=pltpu.VMEM((width // 128, 8, count), f32),
        turned_one=pltpu.VMEM((width, count), bf16),
        turned_two=pltpu.VMEM((width, count), bf16),
        mixed_turned=pltpu.VMEM((width, count), bf16),
        normed=pltpu.VMEM((count, width), bf16),
        mixed=pltpu.VMEM((count, width), bf16),
        grad_low=pltpu.VMEM((count, width), bf16),
        joined=pltpu.VMEM((width // 128, 3, count, 128), bf16),
        middle=pltpu.VMEM((count, width), f32),
        acc=pltpu.VMEM((count, width), f32),
        act=pltpu.VMEM((count, hidden), bf16),
        slope=pltpu.VMEM((2, count, TILE), f32),
        send=pltpu.SemaphoreType.DMA((5, Piece.COUNT)),
        gather_z=pltpu.SemaphoreType.DMA((9, 3)),
        gather_recv=pltpu.SemaphoreType.DMA((9, 13)),
        scatter_recv=pltpu.SemaphoreType.DMA((9, 14)),
        pre_send=pltpu.SemaphoreType.DMA((6,)),
        pre_recv=pltpu.SemaphoreType.DMA((6,)),
        end_send=pltpu.SemaphoreType.DMA((6,)),
        end_recv=pltpu.SemaphoreType.DMA((6,)),
        slope_send=pltpu.SemaphoreType.DMA((2,)),
        slope_recv=pltpu.SemaphoreType.DMA((2,)),
    )
    names = (
        [name for name, _, _ in inputs] + [name for name, _, _ in outs] + [name for name, _ in scratch]
    )
    results = pl.pallas_call(
        functools.partial(layer_kernel, names),
        out_shape=tuple(jax.ShapeDtypeStruct(shape, kind) for _, shape, kind in outs),
        in_specs=[spec for _, _, spec in inputs],
        out_specs=(anywhere,) + (vmem,) * (len(outs) - 1),
        scratch_shapes=[kind for _, kind in scratch],
        compiler_params=pltpu.CompilerParams(
            collective_id=0, has_side_effects=True, vmem_limit_bytes=VMEM_BYTES
        ),
        name="layer",
    )(*[array for _, array, _ in inputs])
    return results[1:]


def deliver_kernel(count, *refs):
    sources, tile = refs[:count], refs[count]
    targets = refs[count + 1 : 2 * count + 1]
    vectors = refs[2 * count + 1 : -count - 2]
    stages = refs[-count - 2 : -2]
    get, put = refs[-2:]
    arriving = [
        pltpu.make_async_copy(sources[i], stages[i], get.at[i]) for i in range(count)
    ]
    leaving = [pltpu.make_async_copy(stages[i], targets[i], put.at[i]) for i in range(count)]
    for copy in arriving:
        copy.start()
    for i, vector in enumerate(vectors):
        vector[...] = tile[i, 0 : vector.shape[0]]
    for first, second in zip(arriving, leaving):
        first.wait()
        second.start()
    for copy in leaving:
        copy.wait()


def deliver(whole, tile, sizes):
    count = len(whole)
    anywhere = pl.BlockSpec(memory_space=pl.ANY)
    vmem = pl.BlockSpec(memory_space=pltpu.VMEM)
    return pl.pallas_call(
        functools.partial(deliver_kernel, count),
        out_shape=[jax.ShapeDtypeStruct(a.shape, a.dtype) for a in whole]
        + [jax.ShapeDtypeStruct((m,), jnp.float32) for m in sizes],
        in_specs=[anywhere] * count + [vmem],
        out_specs=[anywhere] * count + [vmem] * len(sizes),
        scratch_shapes=[pltpu.VMEM(a.shape, a.dtype) for a in whole]
        + [pltpu.SemaphoreType.DMA((count,))] * 2,
        compiler_params=pltpu.CompilerParams(vmem_limit_bytes=VMEM_BYTES),
        name="deliver",
    )(*whole, tile)


def body(
    tokens,
    band_mask,
    out_grad,
    norm1_gain,
    norm1_shift,
    qkv_weight,
    qv_bias,
    out_weight,
    out_bias,
    norm2_gain,
    norm2_shift,
    up_weight,
    up_bias,
    down_weight,
    down_bias,
):
    smalls = (norm1_gain, norm1_shift, qv_bias, out_bias, norm2_gain, norm2_shift, up_bias, down_bias)
    shards = (qkv_weight, out_weight, up_weight, down_weight)
    *whole, tile = layer_call(tokens, band_mask, out_grad, shards, smalls)
    output, input_grad, qkv, out, up, down, *grads = deliver(
        whole, tile, [v.shape[0] for v in smalls]
    )
    return (
        output,
        input_grad,
        grads[0],
        grads[1],
        qkv,
        grads[2],
        out,
        grads[3],
        grads[4],
        grads[5],
        up,
        grads[6],
        down,
        grads[7],
    )


def solution(mesh):
    rows, flat = P(AXES, None), P(AXES)
    params = (flat, flat, rows, flat, rows, flat, flat, flat, rows, flat, rows, flat)
    fitted = tuple(mesh.shape[axis] for axis in AXES) == (8, 4)
    return jax.shard_map(
        body if fitted else body_plain,
        mesh=mesh,
        in_specs=(rows, rows, rows) + params,
        out_specs=(rows, rows) + params,
        check_vma=False,
    )
```

```python
import functools
import math

import jax
import jax.numpy as jnp
from jax import lax
from jax.experimental import pallas as pl
from jax.experimental.pallas import tpu as pltpu
from jax.sharding import PartitionSpec as P

HEAD = 64
HEAD_GROUP = 4
QBLOCK = 512


NORM_EPSILON = 1e-05
VMEM_BYTES = 62 << 20
AXES = ("wide", "narrow")


def normalize(values, gain, shift):
    centre = jnp.mean(values, axis=1, keepdims=True)
    centred = values - centre
    factor = lax.rsqrt(jnp.mean(centred * centred, axis=1, keepdims=True) + NORM_EPSILON)
    normed = centred * factor
    return (normed * gain + shift, normed, factor)


def normalize_back(upstream, normed, factor, gain):
    gain_grad = jnp.sum(upstream * normed, axis=0)
    shift_grad = jnp.sum(upstream, axis=0)
    scaled = upstream * gain
    inner = (
        scaled
        - jnp.mean(scaled, axis=1, keepdims=True)
        - normed * jnp.mean(scaled * normed, axis=1, keepdims=True)
    )
    return (factor * inner, gain_grad, shift_grad)


def gelu_slope(values):
    cumulative = 0.5 * (1.0 + lax.erf(values * (1.0 / math.sqrt(2.0))))
    return cumulative + values * jnp.exp(-0.5 * values * values) * (1.0 / math.sqrt(2.0 * math.pi))


def to_groups(matrix, count):
    return matrix.reshape(matrix.shape[0], count, -1).transpose(1, 0, 2)


def from_groups(stacked):
    return stacked.transpose(1, 0, 2).reshape(stacked.shape[1], -1)


def attend_forward(query_cols, key_cols, value_cols, key_live):
    row_count, span_cols = key_cols.shape
    head_width = span_cols // HEAD_GROUP
    scaling = 1.0 / math.sqrt(head_width)
    key_rows = key_cols.reshape(row_count, HEAD_GROUP, head_width)
    value_rows = value_cols.reshape(row_count, HEAD_GROUP, head_width)
    query_blocks = query_cols.reshape(row_count // QBLOCK, QBLOCK, HEAD_GROUP, head_width)

    def one_block(query_rows):
        scores = (
            jnp.einsum("qhd,khd->hqk", query_rows, key_rows, preferred_element_type=jnp.float32)
            * scaling
        )
        scores = jnp.where(key_live[None, None, :], scores, -jnp.inf)
        largest = jnp.max(scores, axis=2, keepdims=True)
        expo = jnp.exp(scores - largest)
        totals = jnp.sum(expo, axis=2, keepdims=True)
        weights_low = (expo / totals).astype(jnp.bfloat16)
        mixture = jnp.einsum(
            "hqk,khd->qhd", weights_low, value_rows, preferred_element_type=jnp.float32
        )
        return (mixture.reshape(QBLOCK, span_cols), largest[:, :, 0] + jnp.log(totals[:, :, 0]))

    mixture, logsum = lax.map(one_block, query_blocks)
    return (mixture.reshape(row_count, span_cols), logsum)


def attend_backward(query_cols, key_cols, value_cols, grad_cols, logsum, key_live):
    row_count, span_cols = key_cols.shape
    head_width = span_cols // HEAD_GROUP
    scaling = 1.0 / math.sqrt(head_width)
    key_rows = key_cols.reshape(row_count, HEAD_GROUP, head_width)
    value_rows = value_cols.reshape(row_count, HEAD_GROUP, head_width)
    query_blocks = query_cols.reshape(row_count // QBLOCK, QBLOCK, HEAD_GROUP, head_width)
    grad_blocks = grad_cols.reshape(row_count // QBLOCK, QBLOCK, HEAD_GROUP, head_width)

    def one_block(carry, items):
        key_acc, value_acc = carry
        query_rows, grad_rows, block_logsum = items
        scores = (
            jnp.einsum("qhd,khd->hqk", query_rows, key_rows, preferred_element_type=jnp.float32)
            * scaling
        )
        scores = jnp.where(key_live[None, None, :], scores, -jnp.inf)
        probs = jnp.exp(scores - block_logsum[:, :, None])
        value_acc = value_acc + jnp.einsum(
            "hqk,qhd->khd",
            probs.astype(jnp.bfloat16),
            grad_rows,
            preferred_element_type=jnp.float32,
        )
        prob_grad = jnp.einsum(
            "qhd,khd->hqk", grad_rows, value_rows, preferred_element_type=jnp.float32
        )
        inner = jnp.sum(probs * prob_grad, axis=2, keepdims=True)
        score_grad = (probs * (prob_grad - inner)).astype(jnp.bfloat16)
        query_grad = (
            jnp.einsum("hqk,khd->qhd", score_grad, key_rows, preferred_element_type=jnp.float32)
            * scaling
        )
        key_acc = (
            key_acc
            + jnp.einsum("hqk,qhd->khd", score_grad, query_rows, preferred_element_type=jnp.float32)
            * scaling
        )
        return ((key_acc, value_acc), query_grad.reshape(QBLOCK, span_cols))

    empty = jnp.zeros((row_count, HEAD_GROUP, head_width), jnp.float32)
    (key_grad, value_grad), query_grad = lax.scan(
        one_block, (empty, empty), (query_blocks, grad_blocks, logsum)
    )
    return (
        query_grad.reshape(row_count, span_cols),
        key_grad.reshape(row_count, span_cols),
        value_grad.reshape(row_count, span_cols),
    )


def gathered(shard):
    return lax.all_gather(shard.astype(jnp.bfloat16), AXES, axis=0, tiled=True)


def scattered(part):
    return lax.psum_scatter(part, AXES, scatter_dimension=0, tiled=True)


def body_plain(
    tokens,
    band_mask,
    out_grad,
    norm1_gain,
    norm1_shift,
    qkv_weight,
    qv_bias,
    out_weight,
    out_bias,
    norm2_gain,
    norm2_shift,
    up_weight,
    up_bias,
    down_weight,
    down_bias,
):
    row_count, width = tokens.shape
    group_count = width // (HEAD_GROUP * HEAD)
    present = jnp.repeat(band_mask[0].astype(jnp.float32), row_count // band_mask.shape[1])
    key_live = present > 0.5
    column_mask = present[:, None]
    gain_one, shift_one, w_qkv, b_qv, w_out, b_out = (
        gathered(norm1_gain),
        gathered(norm1_shift),
        gathered(qkv_weight),
        gathered(qv_bias),
        gathered(out_weight),
        gathered(out_bias),
    )
    inputs = tokens.astype(jnp.float32)
    normed_one, unit_one, factor_one = normalize(
        inputs, gain_one.astype(jnp.float32), shift_one.astype(jnp.float32)
    )
    normed_one = normed_one.astype(jnp.bfloat16)
    bias_wide = b_qv.astype(jnp.float32)
    bias_full = jnp.concatenate(
        [bias_wide[:width], jnp.zeros((width,), jnp.float32), bias_wide[width:]]
    )
    joined = (jnp.dot(normed_one, w_qkv, preferred_element_type=jnp.float32) + bias_full).astype(
        jnp.bfloat16
    )
    query_groups = to_groups(joined[:, :width], group_count)
    key_groups = to_groups(joined[:, width : 2 * width], group_count)
    value_groups = to_groups(joined[:, 2 * width :], group_count)
    mixture, logsum = lax.map(
        lambda items: attend_forward(items[0], items[1], items[2], key_live),
        (query_groups, key_groups, value_groups),
    )
    mixture = from_groups(mixture).astype(jnp.bfloat16)
    attention = jnp.dot(mixture, w_out, preferred_element_type=jnp.float32) + b_out.astype(
        jnp.float32
    )
    middle = inputs + column_mask * attention
    gain_two, shift_two, w_up, b_up, w_down, b_down = (
        gathered(norm2_gain),
        gathered(norm2_shift),
        gathered(up_weight),
        gathered(up_bias),
        gathered(down_weight),
        gathered(down_bias),
    )
    normed_two, unit_two, factor_two = normalize(
        middle, gain_two.astype(jnp.float32), shift_two.astype(jnp.float32)
    )
    normed_two = normed_two.astype(jnp.bfloat16)
    hidden = jnp.dot(normed_two, w_up, preferred_element_type=jnp.float32) + b_up.astype(
        jnp.float32
    )
    active = jax.nn.gelu(hidden, approximate=False).astype(jnp.bfloat16)
    branch = jnp.dot(active, w_down, preferred_element_type=jnp.float32) + b_down.astype(
        jnp.float32
    )
    output = (middle + column_mask * branch).astype(jnp.bfloat16)
    upstream = out_grad.astype(jnp.float32)
    branch_grad = (column_mask * upstream).astype(jnp.bfloat16)
    down_weight_grad = jnp.einsum(
        "tf,td->fd", active, branch_grad, preferred_element_type=jnp.float32
    )
    down_bias_grad = jnp.sum(branch_grad.astype(jnp.float32), axis=0)
    active_grad = jnp.einsum(
        "td,fd->tf", branch_grad, w_down, preferred_element_type=jnp.float32
    )
    hidden_grad = (active_grad * gelu_slope(hidden)).astype(jnp.bfloat16)
    up_weight_grad = jnp.einsum(
        "td,tf->df", normed_two, hidden_grad, preferred_element_type=jnp.float32
    )
    up_bias_grad = jnp.sum(hidden_grad.astype(jnp.float32), axis=0)
    normed_two_grad = jnp.einsum(
        "tf,df->td", hidden_grad, w_up, preferred_element_type=jnp.float32
    )
    middle_part, norm2_gain_grad, norm2_shift_grad = normalize_back(
        normed_two_grad, unit_two, factor_two, gain_two.astype(jnp.float32)
    )
    (
        norm2_gain_grad,
        norm2_shift_grad,
        up_weight_grad,
        up_bias_grad,
        down_weight_grad,
        down_bias_grad,
    ) = (
        scattered(norm2_gain_grad),
        scattered(norm2_shift_grad),
        scattered(up_weight_grad),
        scattered(up_bias_grad),
        scattered(down_weight_grad),
        scattered(down_bias_grad),
    )
    middle_grad = upstream + middle_part
    attention_grad = (column_mask * middle_grad).astype(jnp.bfloat16)
    out_weight_grad = jnp.einsum(
        "te,td->ed", mixture, attention_grad, preferred_element_type=jnp.float32
    )
    out_bias_grad = jnp.sum(attention_grad.astype(jnp.float32), axis=0)
    mixture_grad = jnp.einsum(
        "td,ed->te", attention_grad, w_out, preferred_element_type=jnp.float32
    ).astype(jnp.bfloat16)
    grad_groups = to_groups(mixture_grad, group_count)
    query_grad, key_grad, value_grad = lax.map(
        lambda items: attend_backward(items[0], items[1], items[2], items[3], items[4], key_live),
        (query_groups, key_groups, value_groups, grad_groups, logsum),
    )
    query_grad = from_groups(query_grad).astype(jnp.bfloat16)
    key_grad = from_groups(key_grad).astype(jnp.bfloat16)
    value_grad = from_groups(value_grad).astype(jnp.bfloat16)
    joined_grad = jnp.concatenate([query_grad, key_grad, value_grad], axis=1)
    qkv_weight_grad = jnp.einsum(
        "td,tc->dc", normed_one, joined_grad, preferred_element_type=jnp.float32
    )
    qv_bias_grad = jnp.concatenate(
        [
            jnp.sum(query_grad.astype(jnp.float32), axis=0),
            jnp.sum(value_grad.astype(jnp.float32), axis=0),
        ]
    )
    normed_one_grad = jnp.einsum(
        "tc,dc->td", joined_grad, w_qkv, preferred_element_type=jnp.float32
    )
    input_part, norm1_gain_grad, norm1_shift_grad = normalize_back(
        normed_one_grad, unit_one, factor_one, gain_one.astype(jnp.float32)
    )
    input_grad = (middle_grad + input_part).astype(jnp.bfloat16)
    (
        norm1_gain_grad,
        norm1_shift_grad,
        qkv_weight_grad,
        qv_bias_grad,
        out_weight_grad,
        out_bias_grad,
    ) = (
        scattered(norm1_gain_grad),
        scattered(norm1_shift_grad),
        scattered(qkv_weight_grad),
        scattered(qv_bias_grad),
        scattered(out_weight_grad),
        scattered(out_bias_grad),
    )
    return (
        output,
        input_grad,
        norm1_gain_grad,
        norm1_shift_grad,
        qkv_weight_grad,
        qv_bias_grad,
        out_weight_grad,
        out_bias_grad,
        norm2_gain_grad,
        norm2_shift_grad,
        up_weight_grad,
        up_bias_grad,
        down_weight_grad,
        down_bias_grad,
    )


MESH_ID = pl.DeviceIdType.MESH
VIA_X = (0, 2)
VIA_Y = (1, 3)
ORDER = (1, 3, 2)
SCORE_SCALE = math.log2(math.e) / math.sqrt(HEAD)
TILE = 768


class Place:
    def __init__(self):
        wide = lax.axis_index("wide")
        narrow = lax.axis_index("narrow")
        z, y = wide // 2, wide % 2
        x, c = narrow // 2, narrow % 2
        self.z, self.c = z, c
        self.zs = (z, z + 1 - 2 * (z % 2), (z + 2) % 4, 3 - z)
        self.q = y * 2 + x
        self.qx = y * 2 + (1 - x)
        self.qy = (1 - y) * 2 + x
        self.qd = (1 - y) * 2 + (1 - x)
        self.to_z = tuple((zz * 2 + y, x * 2 + c) for zz in self.zs)
        self.to_x = (z * 2 + y, (1 - x) * 2 + c)
        self.to_y = (z * 2 + 1 - y, x * 2 + c)
        self.to_c = (z * 2 + y, x * 2 + 1 - c)
        self.to_d = (z * 2 + 1 - y, (1 - x) * 2 + c)


def span(start, size, step):
    return pl.ds(pl.multiple_of(start, step), size)


def meet(place):
    barrier = pltpu.get_barrier_semaphore()
    peers = place.to_z[1:] + (place.to_x, place.to_y, place.to_d, place.to_c)
    for peer in peers:
        pl.semaphore_signal(barrier, inc=1, device_id=peer, device_id_type=MESH_ID)
    pl.semaphore_wait(barrier, len(peers))


def remote(source, target, send, recv, peer):
    return pltpu.make_async_remote_copy(
        src_ref=source,
        dst_ref=target,
        send_sem=send,
        recv_sem=recv,
        device_id=peer,
        device_id_type=MESH_ID,
    )


class Piece:
    COUNT = 19

    def __init__(self, place, send, recv, slots, z_send=None):
        self.p = place
        self.send, self.recv, self.slots, self.z_send = send, recv, slots, z_send
        self.sent = []

    def pair(self, index):
        own = self.send if index >= 3 or self.z_send is None else self.z_send
        return own.at[index], self.recv.at[self.slots[index]]

    def go(self, source, target, index, peer):
        remote(source(), target(), *self.pair(index), peer).start()
        self.sent.append((source, target, index, peer))

    def got(self, target, index, peer):
        remote(target, target, *self.pair(index), peer).wait_recv()

    def finish(self):
        for source, target, index, peer in self.sent:
            remote(source(), target(), *self.pair(index), peer).wait_send()
        self.sent = []


class Gather(Piece):
    SLOTS = (0, 1, 2, 3, 4, 5, 6, 11, 11, 7, 8, 9, 10, 11, 11, 12, 12, 12, 12)

    def __init__(self, place, block, column, others, send, recv, z_send):
        super().__init__(place, send, recv, self.SLOTS, z_send)
        self.block, self.column, self.others = block, column, others

    def own(self):
        return self.block(self.p.z, self.p.q)

    def start_z(self):
        p = self.p
        for k in ORDER:
            self.go(self.own, self.own, k - 1, p.to_z[k])

    def start_xy(self):
        p = self.p
        self.go(self.own, self.own, 3, p.to_x)
        self.go(self.own, self.own, 9, p.to_y)

    def z(self, k):
        p = self.p
        here = lambda: self.block(p.zs[k], p.q)
        self.got(here(), k - 1, p.to_z[k])
        self.go(here, here, 3 + k, p.to_x)
        self.go(here, here, 9 + k, p.to_y)

    def share(self, index, q):
        column = lambda: self.column(q)
        self.go(column, column, index, self.p.to_c)

    def own_column(self):
        self.share(15, self.p.q)

    def xy(self, k):
        p = self.p
        from_x = lambda: self.block(p.zs[k], p.qx)
        self.got(from_x(), 3 + k, p.to_x)
        if k in VIA_X:
            self.go(from_x, from_x, 13 + VIA_X.index(k), p.to_y)
        from_y = lambda: self.block(p.zs[k], p.qy)
        self.got(from_y(), 9 + k, p.to_y)
        if k in VIA_Y:
            self.go(from_y, from_y, 7 + VIA_Y.index(k), p.to_x)

    def xy_columns(self):
        self.share(16, self.p.qx)
        self.share(17, self.p.qy)

    def d(self):
        p = self.p
        self.got(self.column(p.qd), 13, p.to_y)
        self.share(18, p.qd)

    def c(self):
        self.got(self.others(), 15, self.p.to_c)


class Scatter(Piece):
    SLOTS = (13, 13, 13, 5, 6, 7, 8, 1, 2, 9, 10, 11, 12, 3, 4, 0, 0, 0, 0)

    def __init__(self, place, block, column, whole, bufs, send, recv):
        super().__init__(place, send, recv, self.SLOTS)
        self.block, self.column, self.whole = block, column, whole
        self.dx, self.dy, self.xr, self.yr, self.zr = bufs

    def add(self, target, other):
        target[...] = (target[...].astype(jnp.float32) + other[...].astype(jnp.float32)).astype(
            target.dtype
        )

    def give(self, other):
        p = self.p
        for i, q in enumerate((p.qd, p.qx, p.qy, p.q)):
            self.go(lambda q=q: other(q), lambda q=q: self.column(q), 15 + i, p.to_c)

    def arrive(self):
        self.got(self.whole(), 15, self.p.to_c)

    def diagonal(self):
        p = self.p
        for i in range(2):
            self.go(
                lambda i=i: self.block(p.zs[VIA_X[i]], p.qd), lambda i=i: self.dx.at[i], 7 + i, p.to_x
            )
            self.go(
                lambda i=i: self.block(p.zs[VIA_Y[i]], p.qd), lambda i=i: self.dy.at[i], 13 + i, p.to_y
            )

    def cross(self, k):
        p = self.p
        on_x = lambda: self.block(p.zs[k], p.qx)
        on_y = lambda: self.block(p.zs[k], p.qy)
        if k in VIA_Y:
            i = VIA_Y.index(k)
            self.go(on_y, lambda: self.yr.at[k], 9 + k, p.to_y)
            self.got(self.dy.at[i], 13 + i, p.to_y)
            self.add(on_x(), self.dy.at[i])
            self.go(on_x, lambda: self.xr.at[k], 3 + k, p.to_x)
        else:
            i = VIA_X.index(k)
            self.go(on_x, lambda: self.xr.at[k], 3 + k, p.to_x)
            self.got(self.dx.at[i], 7 + i, p.to_x)
            self.add(on_y(), self.dx.at[i])
            self.go(on_y, lambda: self.yr.at[k], 9 + k, p.to_y)

    def plane(self, k):
        p = self.p
        self.got(self.xr.at[k], 3 + k, p.to_x)
        self.got(self.yr.at[k], 9 + k, p.to_y)
        here = self.block(p.zs[k], p.q)
        return here, (
            here[...].astype(jnp.float32)
            + self.xr[k].astype(jnp.float32)
            + self.yr[k].astype(jnp.float32)
        )

    def spread(self, k):
        p = self.p
        here, value = self.plane(k)
        here[...] = value.astype(here.dtype)
        self.go(lambda: self.block(p.zs[k], p.q), lambda: self.zr.at[k - 1], k - 1, p.to_z[k])

    def last(self):
        _, value = self.plane(0)
        self.got(self.zr, 0, self.p.to_z[1])
        for k in ORDER:
            value = value + self.zr[k - 1].astype(jnp.float32)
        return value


class SmallScatter(Piece):
    SLOTS = (4, 4, 4, 1, 2, 3, 0, 0, 0, 0, 0, 0, 0, 0, 0, 0, 0, 0, 0)

    def __init__(self, place, total, arrived, send, recv):
        super().__init__(place, send, recv, self.SLOTS)
        self.total, self.arrived = total, arrived

    def give(self, other):
        self.go(other, lambda: self.total, 15, self.p.to_c)

    def arrive(self):
        self.got(self.total, 15, self.p.to_c)

    def neighbours(self):
        p = self.p
        return ((0, p.qx, p.to_x), (1, p.qy, p.to_y), (2, p.qd, p.to_d))

    def plane(self):
        for i, q, peer in self.neighbours():
            self.go(lambda q=q: self.total.at[:, q], lambda i=i: self.arrived.at[i], 3 + i, peer)

    def spread(self):
        p = self.p
        value = self.total[:, p.q]
        for i, _, peer in self.neighbours():
            self.got(self.arrived.at[i], 3 + i, peer)
            value = value + self.arrived[i]
        self.total[:, p.q] = value
        for k in ORDER:
            self.go(
                lambda k=k: self.total.at[p.zs[k], p.q],
                lambda k=k: self.arrived.at[3, k],
                k - 1,
                p.to_z[k],
            )

    def last(self):
        p = self.p
        self.got(self.arrived.at[3, pl.ds(1, 3)], 0, p.to_z[1])
        value = self.total[p.z, p.q]
        for k in ORDER:
            value = value + self.arrived[3, k]
        return value


def scatter_buffers(tail, kind):
    return [
        pltpu.VMEM((2,) + tail, kind),
        pltpu.VMEM((2,) + tail, kind),
        pltpu.VMEM((4,) + tail, kind),
        pltpu.VMEM((4,) + tail, kind),
        pltpu.VMEM((3,) + tail, kind),
    ]


MATRICES = ("qkv", "out", "up", "down")


def triples(**named):
    return [(name, one, two) for name, (one, two) in named.items()]


def pairs_of(**named):
    return list(named.items())


class Named:
    def __init__(self, names, refs):
        assert len(names) == len(refs)
        self.__dict__.update(zip(names, refs))


def loop(first, count, compute, slots=()):
    def step(i, carry):
        compute(i)
        for j, steps in enumerate(slots):
            if steps:

                @pl.when(i == first + j)
                def _(steps=steps):
                    for one in steps:
                        one()

        return carry

    lax.fori_loop(first, first + count, step, 0)


def follow(order, steps, loops):
    at = 0
    while at < len(order):
        kind = order[at][0]
        if kind not in loops:
            steps[order[at]]()
            at += 1
            continue
        first, slots, end = order[at][1], [[]], at + 1
        held = []
        while end < len(order) and (order[end][0] not in loops or order[end][0] == kind):
            if order[end][0] == kind:
                assert order[end][1] == first + len(slots)
                slots[-1] += held
                held = []
                slots.append([])
                at = end
            else:
                held.append(steps[order[end]])
            end += 1
        if len(slots) == 1:
            loops[kind](jnp.int32(first))
        else:
            loop(first, len(slots), loops[kind], slots)
        at += 1


def dot(left, right):
    return jnp.dot(left, right, preferred_element_type=jnp.float32)


def dot_nt(left, right):
    return lax.dot_general(
        left, right, (((1,), (1,)), ((), ())), preferred_element_type=jnp.float32
    )


def dot_tn(left, right):
    return lax.dot_general(
        left, right, (((0,), (0,)), ((), ())), preferred_element_type=jnp.float32
    )


def head_only(values, e):
    lane = lax.broadcasted_iota(jnp.int32, values.shape, 1)
    return jnp.where((lane // HEAD) == e, values, jnp.zeros_like(values))


def fill_present(present, mask):
    groups = mask.shape[1]
    rows = present.shape[0] // groups
    for g in range(groups):
        present[g * rows : (g + 1) * rows, :] = jnp.full(
            (rows, 128), mask[0, g].astype(jnp.float32)
        )


def segments(width):
    return ((0, width, width // 32), (width, 2 * width, width // 16), (3 * width, 4 * width, width // 8))


def selection(size, m):
    lane = lax.broadcasted_iota(jnp.int32, (1, size), 1).astype(jnp.float32)
    rest = lane - m * jnp.floor((lane + 0.5) * (1.0 / m))
    row = lax.broadcasted_iota(jnp.int32, (128, size), 0).astype(jnp.float32)
    return jnp.where(row == rest, 1.0, 0.0).astype(jnp.bfloat16)


def owners(width):
    parts = []
    for _, size, m in segments(width):
        lane = lax.broadcasted_iota(jnp.int32, (1, size), 1).astype(jnp.float32)
        parts.append(jnp.floor((lane + 0.5) * (1.0 / m)))
    return jnp.concatenate(parts, axis=1)


def unit(values):
    centred = values - jnp.mean(values, axis=1, keepdims=True)
    factor = lax.rsqrt(jnp.mean(centred * centred, axis=1, keepdims=True) + NORM_EPSILON)
    return centred * factor, factor


(
    ATTENTION,
    CLOSE,
    CROSS,
    C_GOT,
    DIAGONAL,
    DOWN_HIGH,
    DOWN_LOW,
    DRAIN,
    D_GOT,
    EXPAND_HIGH,
    EXPAND_LOW,
    FINISH,
    FIRST_BACK,
    FIRST_NORM,
    FORM,
    GIVE,
    HEADS,
    HEADS_BACK,
    LAST,
    MASK_GRAD,
    NARROW,
    OUT_BACK,
    OWN_COLUMN,
    OWN_PART,
    PACK,
    PREPARE,
    QKV_BACK,
    SECOND_BACK,
    SECOND_NORM,
    SETTLE,
    SMALL_PLANE,
    SMALL_SPREAD,
    SPREAD,
    START_XY,
    START_Z,
    UNPACK,
    UP_BACK,
    XY_COLUMNS,
    XY_GOT,
    Z_GOT,
) = range(40)
SEQUENCE = (
    (START_Z, 8),
    (START_XY, 8),
    (FORM, 0),
    (FORM, 1),
    (Z_GOT, 8, 1),
    (START_Z, 0),
    (START_Z, 1),
    (START_Z, 2),
    (START_Z, 3),
    (Z_GOT, 8, 3),
    (FORM, 2),
    (START_Z, 4),
    (FORM, 3),
    (START_Z, 5),
    (START_Z, 6),
    (START_Z, 7),
    (Z_GOT, 8, 2),
    (OWN_COLUMN, 8),
    (XY_GOT, 8, 1),
    (START_XY, 1),
    (START_XY, 2),
    (START_XY, 0),
    (XY_GOT, 8, 0),
    (XY_GOT, 8, 3),
    (PREPARE,),
    (XY_GOT, 8, 2),
    (XY_COLUMNS, 8),
    (Z_GOT, 0, 3),
    (START_XY, 3),
    (MASK_GRAD, 0),
    (XY_GOT, 1, 0),
    (MASK_GRAD, 1),
    (MASK_GRAD, 2),
    (Z_GOT, 0, 2),
    (XY_GOT, 2, 0),
    (Z_GOT, 0, 1),
    (OWN_COLUMN, 0),
    (MASK_GRAD, 3),
    (XY_GOT, 0, 0),
    (D_GOT, 8),
    (XY_GOT, 0, 3),
    (C_GOT, 8),
    (UNPACK,),
    (XY_GOT, 3, 0),
    (XY_GOT, 0, 2),
    (Z_GOT, 1, 3),
    (Z_GOT, 1, 1),
    (Z_GOT, 1, 2),
    (OWN_COLUMN, 1),
    (FIRST_NORM, 0),
    (FIRST_NORM, 1),
    (XY_GOT, 0, 1),
    (XY_COLUMNS, 0),
    (FIRST_NORM, 2),
    (FIRST_NORM, 3),
    (Z_GOT, 2, 3),
    (Z_GOT, 2, 2),
    (Z_GOT, 2, 1),
    (XY_GOT, 1, 3),
    (D_GOT, 0),
    (OWN_COLUMN, 2),
    (START_XY, 4),
    (XY_GOT, 1, 1),
    (XY_GOT, 1, 2),
    (C_GOT, 0),
    (XY_COLUMNS, 1),
    (HEADS, 0),
    (Z_GOT, 3, 1),
    (Z_GOT, 3, 3),
    (XY_GOT, 2, 1),
    (XY_GOT, 2, 2),
    (Z_GOT, 3, 2),
    (OWN_COLUMN, 3),
    (XY_GOT, 2, 3),
    (XY_COLUMNS, 2),
    (XY_GOT, 4, 0),
    (HEADS, 1),
    (D_GOT, 1),
    (START_XY, 5),
    (XY_GOT, 3, 1),
    (XY_GOT, 3, 3),
    (C_GOT, 1),
    (HEADS, 2),
    (Z_GOT, 4, 3),
    (D_GOT, 2),
    (Z_GOT, 4, 2),
    (XY_GOT, 3, 2),
    (XY_COLUMNS, 3),
    (HEADS, 3),
    (C_GOT, 2),
    (Z_GOT, 4, 1),
    (XY_GOT, 5, 0),
    (OWN_COLUMN, 4),
    (HEADS, 4),
    (XY_GOT, 4, 2),
    (XY_GOT, 4, 3),
    (START_XY, 6),
    (D_GOT, 3),
    (HEADS, 5),
    (XY_GOT, 4, 1),
    (XY_COLUMNS, 4),
    (Z_GOT, 5, 3),
    (C_GOT, 3),
    (ATTENTION,),
    (Z_GOT, 5, 2),
    (SECOND_NORM, 0),
    (SECOND_NORM, 1),
    (Z_GOT, 5, 1),
    (OWN_COLUMN, 5),
    (SECOND_NORM, 2),
    (SECOND_NORM, 3),
    (D_GOT, 4),
    (XY_GOT, 6, 0),
    (XY_GOT, 5, 3),
    (C_GOT, 4),
    (EXPAND_LOW, 0),
    (Z_GOT, 6, 3),
    (XY_GOT, 5, 2),
    (EXPAND_LOW, 1),
    (XY_GOT, 5, 1),
    (XY_COLUMNS, 5),
    (Z_GOT, 6, 2),
    (DOWN_LOW, 0),
    (DOWN_LOW, 1),
    (Z_GOT, 6, 1),
    (OWN_COLUMN, 6),
    (XY_GOT, 6, 3),
    (D_GOT, 5),
    (START_XY, 7),
    (XY_GOT, 6, 2),
    (C_GOT, 5),
    (EXPAND_HIGH, 0),
    (XY_GOT, 6, 1),
    (XY_COLUMNS, 6),
    (Z_GOT, 7, 3),
    (EXPAND_HIGH, 1),
    (Z_GOT, 7, 2),
    (DRAIN,),
    (Z_GOT, 7, 1),
    (OWN_COLUMN, 7),
    (XY_GOT, 7, 0),
    (DOWN_HIGH, 0),
    (DOWN_HIGH, 1),
    (D_GOT, 6),
    (GIVE, 0),
    (GIVE, 1),
    (XY_GOT, 7, 3),
    (C_GOT, 6),
    (XY_GOT, 7, 2),
    (XY_GOT, 7, 1),
    (XY_COLUMNS, 7),
    (OWN_PART, 0),
    (DIAGONAL, 0),
    (D_GOT, 7),
    (OWN_PART, 1),
    (DIAGONAL, 1),
    (CROSS, 0, 1),
    (CROSS, 0, 0),
    (C_GOT, 7),
    (CROSS, 0, 3),
    (NARROW, 0),
    (CROSS, 0, 2),
    (CROSS, 1, 0),
    (CROSS, 1, 1),
    (NARROW, 1),
    (CROSS, 1, 3),
    (CROSS, 1, 2),
    (NARROW, 2),
    (SPREAD, 0, 1),
    (NARROW, 3),
    (GIVE, 2),
    (SPREAD, 0, 3),
    (PACK, 2),
    (SPREAD, 0, 2),
    (GIVE, 3),
    (OWN_PART, 2),
    (DIAGONAL, 2),
    (SPREAD, 1, 1),
    (FINISH, 0),
    (FINISH, 1),
    (SPREAD, 1, 3),
    (FINISH, 2),
    (FINISH, 3),
    (UP_BACK,),
    (SPREAD, 1, 2),
    (LAST, 0),
    (CROSS, 2, 0),
    (CROSS, 2, 1),
    (OWN_PART, 3),
    (CROSS, 2, 3),
    (CROSS, 2, 2),
    (DIAGONAL, 3),
    (SECOND_BACK, 0),
    (SECOND_BACK, 1),
    (SECOND_BACK, 2),
    (SECOND_BACK, 3),
    (GIVE, 4),
    (SPREAD, 2, 1),
    (OUT_BACK,),
    (SPREAD, 2, 3),
    (HEADS_BACK, 0),
    (CROSS, 3, 0),
    (LAST, 1),
    (CLOSE, 3),
    (CROSS, 3, 2),
    (CROSS, 3, 1),
    (SPREAD, 2, 2),
    (CROSS, 3, 3),
    (OWN_PART, 4),
    (DIAGONAL, 4),
    (SETTLE, 3),
    (GIVE, 5),
    (HEADS_BACK, 1),
    (SPREAD, 3, 2),
    (LAST, 2),
    (SPREAD, 3, 1),
    (GIVE, 6),
    (SPREAD, 3, 3),
    (OWN_PART, 5),
    (CROSS, 4, 1),
    (CROSS, 4, 0),
    (CROSS, 4, 2),
    (CROSS, 4, 3),
    (DIAGONAL, 5),
    (HEADS_BACK, 2),
    (SPREAD, 4, 1),
    (SPREAD, 4, 3),
    (SPREAD, 4, 2),
    (CROSS, 5, 0),
    (CROSS, 5, 1),
    (GIVE, 7),
    (CROSS, 5, 2),
    (CROSS, 5, 3),
    (OWN_PART, 6),
    (DIAGONAL, 6),
    (PACK, 1),
    (LAST, 3),
    (CLOSE, 2),
    (SPREAD, 5, 1),
    (OWN_PART, 7),
    (DIAGONAL, 7),
    (SPREAD, 5, 2),
    (QKV_BACK,),
    (CROSS, 6, 2),
    (CROSS, 6, 0),
    (LAST, 4),
    (CROSS, 7, 0),
    (SPREAD, 5, 3),
    (CROSS, 7, 2),
    (CROSS, 7, 3),
    (CROSS, 6, 1),
    (CROSS, 6, 3),
    (CROSS, 7, 1),
    (CLOSE, 1),
    (SETTLE, 2),
    (FIRST_BACK, 0),
    (SPREAD, 6, 2),
    (FIRST_BACK, 1),
    (SETTLE, 1),
    (FIRST_BACK, 2),
    (FIRST_BACK, 3),
    (LAST, 5),
    (SPREAD, 7, 2),
    (PACK, 0),
    (GIVE, 8),
    (SPREAD, 7, 3),
    (SPREAD, 6, 1),
    (SPREAD, 6, 3),
    (OWN_PART, 8),
    (SMALL_PLANE,),
    (SPREAD, 7, 1),
    (SMALL_SPREAD,),
    (LAST, 6),
    (LAST, 7),
    (CLOSE, 0),
    (LAST, 8),
    (SETTLE, 0),
)


def layer_kernel(names, *refs):
    r = Named(names, refs)
    place = Place()
    c = place.c
    tokens, width = r.tokens.shape
    hidden = r.act.shape[1]
    third = width // 2
    tiles = hidden // TILE
    shards = (r.qkv_shard, r.out_shard, r.up_shard, r.down_shard)
    meet(place)

    moves = [(0, g * width, third, (g,)) for g in range(3)] + [
        (i, 0, shards[i].shape[1] // 2, ()) for i in (1, 2, 3)
    ]
    sibs = (r.qkv_sib, r.out_sib, r.up_sib, r.down_sib)
    wides = (r.qkv_wide, r.out_wide, r.up_wide, r.down_wide)

    def before(m):
        i, start, cols, at = moves[m]
        source = shards[i].at[:, span(start + (1 - c) * cols, cols, 128)]
        target = sibs[i].at[at] if at else sibs[i]
        return remote(source, target, r.pre_send.at[m], r.pre_recv.at[m], place.to_c)

    for m in range(6):
        before(m).start()
    r.small_wide[place.z, place.q, c] = jnp.zeros((8, 128), jnp.float32)
    for i in range(8):
        vector = getattr(r, "vector%d" % i)
        r.small_wide[place.z, place.q, c, i : i + 1, 0 : vector.shape[0]] = vector[...].reshape(1, -1)

    def gather(j, block, column, others):
        lane = 4 if j == 8 else j % 4
        return Gather(
            place, block, column, others, r.send.at[lane], r.gather_recv.at[j], r.gather_z.at[j]
        )

    every = slice(None)
    pieces = []
    for s in range(3):
        cols = lambda side, s=s: span(side * third + 128 * s, 128, 128)
        pieces.append(
            gather(
                s,
                lambda zz, q, cols=cols: r.qkv_wide.at[:, zz, q, :, cols(c)],
                lambda q, cols=cols: r.qkv_wide.at[:, :, q, :, cols(c)],
                lambda cols=cols: r.qkv_wide.at[:, :, :, :, cols(1 - c)],
            )
        )
    cuts = (
        (1, 0, 48, 0, 384),
        (2, 0, 48, 0, 768),
        (2, 0, 48, 768, 768),
        (3, 0, 96, 0, 384),
        (3, 96, 96, 0, 384),
    )
    for j, (i, row, rows, col, cols) in enumerate(cuts):
        half = shards[i].shape[1] // 2

        def at(side, row=row, rows=rows, col=col, cols=cols, half=half):
            return (pl.ds(row, rows), span(side * half + col, cols, 128))

        pieces.append(
            gather(
                3 + j,
                lambda zz, q, i=i, at=at: wides[i].at[(zz, q) + at(c)],
                lambda q, i=i, at=at: wides[i].at[(every, q) + at(c)],
                lambda i=i, at=at: wides[i].at[(every, every) + at(1 - c)],
            )
        )
    pieces.append(
        gather(
            8,
            lambda zz, q: r.small_wide.at[zz, q, c],
            lambda q: r.small_wide.at[:, q, c],
            lambda: r.small_wide.at[:, :, 1 - c],
        )
    )

    def form(i):
        for m, (weight, start, cols, at) in enumerate(moves):
            if weight == i:
                before(m).wait_recv()
                mine = shards[i][:, span(start + c * cols, cols, 128)]
                theirs = sibs[i][at] if at else sibs[i][...]
                wides[i][at + (place.z, place.q, every, span(c * cols, cols, 128))] = jnp.concatenate(
                    [jnp.where(c == 0, mine, theirs), jnp.where(c == 0, theirs, mine)], axis=0
                ).astype(jnp.bfloat16)

    def prepare():
        fill_present(r.present, r.mask)
        r.sums[...] = jnp.zeros_like(r.sums)
        r.owner[...] = owners(width)
        r.vec[...] = jnp.zeros_like(r.vec)
        r.small_part[...] = jnp.zeros_like(r.small_part)

    def unpack():
        for zz in range(4):
            rows = r.small_wide[zz].reshape(64, 128).astype(jnp.bfloat16)
            for start, size, m in segments(width):
                lanes = slice(start, start + size)
                picked = dot(rows, selection(size, m))
                total = r.vec[:, lanes]
                for d in range(8):
                    total = total + jnp.where(
                        r.owner[:, lanes] == zz * 8 + d, picked[d * 8 : d * 8 + 8], 0.0
                    )
                r.vec[:, lanes] = total
        for s in range(3):
            r.bias[s] = jnp.zeros((8, 6 * 128), jnp.float32)
            for e in range(2):
                at = 128 * s + third * e
                r.bias[s, 0:1, 128 * e : 128 * e + 128] = r.vec[2:3, width + at : width + at + 128]
                r.bias[s, 0:1, 512 + 128 * e : 640 + 128 * e] = r.vec[
                    2:3, 2 * width + at : 2 * width + at + 128
                ]

    def first_norm(t):
        rows = span(t * 128, 128, 128)
        normed, _ = unit(r.tokens[rows, :].astype(jnp.float32))
        value = normed * r.vec[0:1, 0:width] + r.vec[1:2, 0:width]
        r.normed[rows, :] = value.astype(jnp.bfloat16)
        r.turned_one[:, rows] = value.T.astype(jnp.bfloat16)

    def mask_grad(t):
        rows = span(t * 128, 128, 128)
        low = (r.present[rows, 0:1] * r.out_grad[rows, :].astype(jnp.float32)).astype(jnp.bfloat16)
        r.grad_low[rows, :] = low
        r.sums[7:8, 0:width] += jnp.sum(low.astype(jnp.float32), axis=0, keepdims=True)

    def heads(i):
        s, e = i // 2, i % 2

        @pl.when(e == 0)
        def _():
            weights = [
                r.qkv_wide[g, :, :, :, span(half * third + s * 128, 128, 128)].reshape(width, 128)
                for g in range(3)
                for half in range(2)
            ]
            value = dot(r.normed[...], jnp.concatenate(weights, axis=1)) + r.bias[s, 0:1, :]
            value = value.astype(jnp.bfloat16)
            for g in range(3):
                for half in range(2):
                    at = (2 * g + half) * 128
                    r.joined[s + 3 * half, g] = value[:, at : at + 128]

        hp = s + 3 * e
        cols = span(hp * 128, 128, 128)
        query, key, value = r.joined[hp, 0], r.joined[hp, 1], r.joined[hp, 2].T
        live = r.present[:, 0:1] > 0.5
        mixed = []
        for e in range(2):
            scores = dot_nt(head_only(key, e), query) * SCORE_SCALE
            scores = jnp.where(live, scores, -jnp.inf)
            largest = jnp.max(scores, axis=0, keepdims=True)
            expo = jnp.exp2(scores - largest)
            totals = jnp.sum(expo, axis=0, keepdims=True)
            probs = (expo * (1.0 / totals)).astype(jnp.bfloat16)
            mixed.append(dot(value[HEAD * e : HEAD * (e + 1)], probs))
            r.logsum[hp, e : e + 1, :] = largest + jnp.log2(totals)
        both = jnp.concatenate(mixed, axis=0)
        r.mixed_turned[cols, :] = both.astype(jnp.bfloat16)
        r.mixed[:, cols] = both.T.astype(jnp.bfloat16)

    def attention():
        r.middle[...] = dot(r.mixed[...], r.out_wide[...].reshape(width, width))

    def second_norm(t):
        rows = span(t * 128, 128, 128)
        present = r.present[rows, 0:1]
        middle = r.tokens[rows, :].astype(jnp.float32) + present * (
            r.middle[rows, :] + r.vec[3:4, 0:width]
        )
        r.middle[rows, :] = middle
        normed, _ = unit(middle)
        value = normed * r.vec[4:5, 0:width] + r.vec[5:6, 0:width]
        r.normed[rows, :] = value.astype(jnp.bfloat16)
        r.turned_two[:, rows] = value.T.astype(jnp.bfloat16)

    def slope_out(t, slot):
        return pltpu.make_async_copy(r.slope.at[slot], r.slope_far.at[t], r.slope_send.at[slot])

    def slope_in(t, slot):
        return pltpu.make_async_copy(r.slope_far.at[t], r.slope.at[slot], r.slope_recv.at[slot])

    def expand(t, u):
        slot = u % 2

        @pl.when(u >= 2)
        def _():
            slope_out(t, slot).wait()

        cols = span(t * TILE, TILE, 128)
        value = (
            dot(r.normed[...], r.up_wide[:, :, :, cols].reshape(width, TILE))
            + r.vec[6:7, span(3 * width + t * TILE, TILE, 128)]
        )
        cumulative = 0.5 * (1.0 + lax.erf(value * (1.0 / math.sqrt(2.0))))
        r.act[:, cols] = (value * cumulative).astype(jnp.bfloat16)
        r.slope[slot] = cumulative + value * jnp.exp(-0.5 * value * value) * (
            1.0 / math.sqrt(2.0 * math.pi)
        )
        slope_out(t, slot).start()

    def down_grad(t):
        cols = span(t * TILE, TILE, 128)
        grad = dot_tn(r.act[:, cols], r.grad_low[...]).astype(jnp.bfloat16)
        r.down_part[t] = grad.reshape(4, TILE // 4, width)

    low_tile = lambda u: 2 * u
    high_tile = lambda u: 2 * u + 1

    def scatter(j, block, column, whole):
        bufs = [getattr(r, "piece%d_%d" % (j, b)) for b in range(5)]
        lane = 4 if j == 8 else j % 4
        return Scatter(
            place, block, column, whole, bufs, r.send.at[lane], r.scatter_recv.at[j]
        )

    sums = []
    for s in range(2):
        rows = pl.ds(96 * s, 96)
        sums.append(
            scatter(
                s,
                lambda zz, q, rows=rows: r.down_total.at[zz, q, rows],
                lambda q, rows=rows: r.down_total.at[:, q, rows],
                lambda rows=rows: r.down_total.at[:, :, rows],
            )
        )
    for s in range(2):
        sums.append(
            scatter(
                2 + s,
                lambda zz, q, s=s: r.up_total.at[s, zz, q],
                lambda q, s=s: r.up_total.at[s, :, q],
                lambda s=s: r.up_total.at[s],
            )
        )
    sums.append(
        scatter(
            4,
            lambda zz, q: r.out_total.at[zz, q],
            lambda q: r.out_total.at[:, q],
            lambda: r.out_total,
        )
    )
    for s in range(3):
        sums.append(
            scatter(
                5 + s,
                lambda zz, q, s=s: r.qkv_total.at[s, zz, q],
                lambda q, s=s: r.qkv_total.at[s, :, q],
                lambda s=s: r.qkv_total.at[s],
            )
        )
    sums.append(SmallScatter(place, r.small_total, r.small_got, r.send.at[4], r.scatter_recv.at[8]))

    def up_part(side, s):
        cols = span(side * (hidden // 2) + 768 * s, 768, 128)
        return dot(r.turned_two[...], r.act[:, cols]).reshape(4, 4, 48, 768)

    def out_part(side):
        cols = span(side * third, third, 128)
        return dot(r.mixed_turned[...], r.normed[:, cols]).reshape(4, 4, 48, third)

    def qkv_part(side, s):
        hp = side * 3 + s
        grads = jnp.concatenate([r.joined[hp, g] for g in range(3)], axis=1)
        return dot(r.turned_one[...], grads)

    def other_part(p):
        if p in (2, 3):
            r.down_wide[:, :, 48 * (p - 2) : 48 * (p - 1), :] = up_part(1 - c, p - 2).astype(
                jnp.bfloat16
            )
        elif p == 4:
            r.down_wide[:, :, 96:144, 0:384] = out_part(1 - c).astype(jnp.bfloat16)
        else:
            value = qkv_part(1 - c, p - 5).astype(jnp.bfloat16)
            for g in range(3):
                r.down_part[:, :, 48 * g : 48 * g + 48, 128 * (p - 5) : 128 * (p - 4)] = value[
                    :, 128 * g : 128 * g + 128
                ].reshape(4, 4, 48, 128)

    def given(p):
        if p < 2:
            rows, cols = pl.ds(96 * p, 96), span((1 - c) * 384, 384, 128)
            return lambda q: r.down_part.at[:, q, rows, cols]
        if p < 4:
            return lambda q: r.down_wide.at[:, q, pl.ds(48 * (p - 2), 48)]
        if p == 4:
            return lambda q: r.down_wide.at[:, q, pl.ds(96, 48), pl.ds(0, 384)]
        if p < 8:
            return lambda q: r.down_part.at[:, q, pl.ds(0, 144), pl.ds(128 * (p - 5), 128)]
        return lambda: r.small_part.at[:, :, 1 - c]

    def wide_sum(total, value):
        total[...] = (total[...].astype(jnp.float32) + value).astype(total.dtype)

    def own_part(p):
        sums[p].arrive()
        if p < 2:
            rows = pl.ds(96 * p, 96)
            mine = r.down_part[:, :, rows, span(c * 384, 384, 128)].astype(jnp.float32)
            wide_sum(r.down_total.at[:, :, rows], mine)
        elif p < 4:
            wide_sum(r.up_total.at[p - 2], up_part(c, p - 2))
        elif p == 4:
            wide_sum(r.out_total, out_part(c))
        elif p < 8:
            value = qkv_part(c, p - 5)
            for g in range(3):
                wide_sum(
                    r.qkv_total.at[p - 5, :, :, pl.ds(48 * g, 48)],
                    value[:, 128 * g : 128 * g + 128].reshape(4, 4, 48, 128),
                )
        else:
            r.small_total[...] += r.small_part[:, :, c]

    def narrow(t):
        slot = t % 2

        @pl.when(t == 0)
        def _():
            slope_in(0, 0).start()
            r.acc[...] = jnp.zeros_like(r.acc)

        slope_in(t, slot).wait()

        @pl.when(t + 1 < tiles)
        def _():
            slope_in(t + 1, 1 - slot).start()

        cols = span(t * TILE, TILE, 128)
        weights = r.down_wide[t].reshape(TILE, width)
        r.acc[...] += dot(r.act[:, cols], weights)
        grad = (dot_nt(r.grad_low[...], weights) * r.slope[slot]).astype(jnp.bfloat16)
        r.act[:, cols] = grad
        r.sums[6:7, span(3 * width + t * TILE, TILE, 128)] = jnp.sum(
            grad.astype(jnp.float32), axis=0, keepdims=True
        )

    def drain_slope():
        for slot in range(2):
            slope_out(0, slot).wait()

    def finish_output(t):
        rows = span(t * 128, 128, 128)
        r.output[rows, :] = (
            r.middle[rows, :]
            + r.present[rows, 0:1] * (r.acc[rows, :] + r.vec[7:8, 0:width])
        ).astype(jnp.bfloat16)

    def up_back():
        r.acc[...] = dot_nt(r.act[...], r.up_wide[...].reshape(width, hidden))

    def norm_back(up, normed, factor, index):
        r.sums[index : index + 1, 0:width] += jnp.sum(up * normed, axis=0, keepdims=True)
        r.sums[index + 1 : index + 2, 0:width] += jnp.sum(up, axis=0, keepdims=True)
        scaled = up * r.vec[index : index + 1, 0:width]
        return factor * (
            scaled
            - jnp.mean(scaled, axis=1, keepdims=True)
            - normed * jnp.mean(scaled * normed, axis=1, keepdims=True)
        )

    def second_back(t):
        rows = span(t * 128, 128, 128)
        normed, factor = unit(r.middle[rows, :])
        grad = r.out_grad[rows, :].astype(jnp.float32) + norm_back(
            r.acc[rows, :], normed, factor, 4
        )
        r.middle[rows, :] = grad
        low = (r.present[rows, 0:1] * grad).astype(jnp.bfloat16)
        r.normed[rows, :] = low
        r.sums[3:4, 0:width] += jnp.sum(low.astype(jnp.float32), axis=0, keepdims=True)

    def out_back():
        r.mixed[...] = dot_nt(r.normed[...], r.out_wide[...].reshape(width, width)).astype(
            jnp.bfloat16
        )

    def heads_back(s):
        pair_back(s)
        pair_back(s + 3)

    def pair_back(hp):
        cols = span(hp * 128, 128, 128)
        query, key, value = r.joined[hp, 0], r.joined[hp, 1], r.joined[hp, 2]
        grad = r.mixed[:, cols]
        turned = key.T
        live = r.present[:, 0:1] > 0.5
        value_grad = jnp.zeros((tokens, 128), jnp.float32)
        key_grad = jnp.zeros((tokens, 128), jnp.float32)
        query_grad = []
        for e in range(2):
            scores = dot_nt(head_only(key, e), query) * SCORE_SCALE
            scores = jnp.where(live, scores, -jnp.inf)
            probs = jnp.exp2(scores - r.logsum[hp, e : e + 1, :])
            back = dot_nt(head_only(value, e), grad)
            inner = jnp.sum(probs * back, axis=0, keepdims=True)
            score_grad = (probs * (back - inner)).astype(jnp.bfloat16)
            value_grad = value_grad + dot(probs.astype(jnp.bfloat16), head_only(grad, e))
            key_grad = key_grad + dot(score_grad, head_only(query, e))
            query_grad.append(dot(turned[HEAD * e : HEAD * (e + 1)], score_grad))
        scale = 1.0 / math.sqrt(HEAD)
        query_low = (jnp.concatenate(query_grad, axis=0).T * scale).astype(jnp.bfloat16)
        value_low = value_grad.astype(jnp.bfloat16)
        r.joined[hp, 0] = query_low
        r.joined[hp, 1] = (key_grad * scale).astype(jnp.bfloat16)
        r.joined[hp, 2] = value_low
        r.sums[2:3, span(width + hp * 128, 128, 128)] = jnp.sum(
            query_low.astype(jnp.float32), axis=0, keepdims=True
        )
        r.sums[2:3, span(2 * width + hp * 128, 128, 128)] = jnp.sum(
            value_low.astype(jnp.float32), axis=0, keepdims=True
        )

    def qkv_back():
        total = jnp.zeros((tokens, width), jnp.float32)
        for g in range(3):
            grads = jnp.concatenate([r.joined[hp, g] for hp in range(6)], axis=1)
            total = total + dot_nt(grads, r.qkv_wide[g].reshape(width, width))
        r.acc[...] = total

    def first_back(t):
        rows = span(t * 128, 128, 128)
        normed, factor = unit(r.tokens[rows, :].astype(jnp.float32))
        part = norm_back(r.acc[rows, :], normed, factor, 0)
        r.input_grad[rows, :] = (r.middle[rows, :] + part).astype(jnp.bfloat16)

    def pack(index):
        start, size, m = segments(width)[index]
        row = (None, 2, 6)[index]
        lanes = slice(start, start + size)
        chosen = selection(size, m)
        for zz in range(4):
            left = r.sums[:, lanes] if row is None else r.sums[row : row + 1, lanes]
            tile = 0.0
            for _ in range(2):
                part = left.astype(jnp.bfloat16).astype(jnp.float32)
                left = left - part
                rows = jnp.concatenate(
                    [jnp.where(r.owner[:, lanes] == zz * 8 + d, part, 0.0) for d in range(8)], axis=0
                ).astype(jnp.bfloat16)
                tile = tile + dot_nt(rows, chosen)
            if row is None:
                r.small_part[zz] += tile.reshape(4, 2, 8, 128)
            else:
                for d in range(8):
                    r.small_part[zz, d // 2, d % 2, row : row + 1, :] += tile[d : d + 1, :]

    results = (r.qkv_result, r.out_result, r.up_result, r.down_result)
    finals = (r.qkv_final, r.out_final, r.up_final, r.down_final)

    def swap(m, side):
        i, start, cols, at = moves[m]
        rows = results[i].shape[0]
        return remote(
            finals[i].at[at + (span((1 - c) * rows, rows, 8),)],
            results[i].at[:, span(start + side * cols, cols, 128)],
            r.end_send.at[m],
            r.end_recv.at[m],
            place.to_c,
        )

    def close(i):
        for m, (weight, start, cols, at) in enumerate(moves):
            if weight == i:
                rows = results[i].shape[0]
                swap(m, c).start()
                results[i][:, span(start + c * cols, cols, 128)] = finals[i][
                    at + (span(c * rows, rows, 8),)
                ]

    def settle(i):
        for m, move in enumerate(moves):
            if move[0] == i:
                swap(m, 1 - c).wait_recv()

    def last(p):
        value = sums[p].last()
        if p < 2:
            r.down_final[96 * p : 96 * p + 96, :] = value
        elif p < 4:
            r.up_final[:, 768 * (p - 2) : 768 * (p - 1)] = value
        elif p == 4:
            r.out_final[...] = value
        elif p < 8:
            for g in range(3):
                r.qkv_final[g, :, 128 * (p - 5) : 128 * (p - 4)] = value[48 * g : 48 * g + 48]
        else:
            r.small_result[...] = value

    def start_xy(j):
        if 4 <= j < 8:
            pieces[j - 4].finish()
        pieces[j].start_xy()

    def give(p):
        before_it = pieces[8] if p == 8 else (sums[p - 4] if p >= 4 else pieces[p + 4])
        before_it.finish()
        if 2 <= p < 8:
            other_part(p)
        sums[p].give(given(p))

    steps = {(UNPACK,): unpack, (ATTENTION,): attention, (DRAIN,): drain_slope}
    steps.update({(UP_BACK,): up_back, (OUT_BACK,): out_back, (QKV_BACK,): qkv_back})
    steps[PREPARE,] = prepare
    for i in range(3):
        steps[PACK, i] = functools.partial(pack, i)
    for i in range(4):
        steps[FORM, i] = functools.partial(form, i)
        steps[CLOSE, i] = functools.partial(close, i)
        steps[SETTLE, i] = functools.partial(settle, i)
    for j in range(9):
        piece, total = pieces[j], sums[j]
        steps[START_Z, j] = piece.start_z
        steps[START_XY, j] = functools.partial(start_xy, j)
        steps[OWN_COLUMN, j] = piece.own_column
        steps[XY_COLUMNS, j] = piece.xy_columns
        steps[D_GOT, j] = piece.d
        steps[C_GOT, j] = piece.c
        steps[GIVE, j] = functools.partial(give, j)
        steps[OWN_PART, j] = functools.partial(own_part, j)
        steps[LAST, j] = functools.partial(last, j)
        for k in range(4):
            steps[Z_GOT, j, k] = functools.partial(piece.z, k)
            steps[XY_GOT, j, k] = functools.partial(piece.xy, k)
    for j, total in enumerate(sums[:8]):
        steps[DIAGONAL, j] = total.diagonal
        for k in range(4):
            steps[CROSS, j, k] = functools.partial(total.cross, k)
            steps[SPREAD, j, k] = functools.partial(total.spread, k)
    steps[SMALL_PLANE,] = sums[8].plane
    steps[SMALL_SPREAD,] = sums[8].spread
    loops = {
        FIRST_NORM: first_norm,
        MASK_GRAD: mask_grad,
        HEADS: heads,
        SECOND_NORM: second_norm,
        EXPAND_LOW: lambda u: expand(low_tile(u), u),
        EXPAND_HIGH: lambda u: expand(high_tile(u), u + 2),
        DOWN_LOW: lambda u: down_grad(low_tile(u)),
        DOWN_HIGH: lambda u: down_grad(high_tile(u)),
        NARROW: narrow,
        FINISH: finish_output,
        SECOND_BACK: second_back,
        HEADS_BACK: heads_back,
        FIRST_BACK: first_back,
    }
    follow(SEQUENCE, steps, loops)
    for m in range(6):
        before(m).wait_send()
        swap(m, c).wait_send()
    for piece in pieces + sums:
        piece.finish()


def layer_call(tokens, band_mask, out_grad, shards, smalls):
    bf16, f32 = jnp.bfloat16, jnp.float32
    count, width = tokens.shape
    shapes = [s.shape for s in shards]
    hidden = shapes[2][1]
    tiles = hidden // TILE
    vmem = pl.BlockSpec(memory_space=pltpu.VMEM)
    anywhere = pl.BlockSpec(memory_space=pl.ANY)
    inputs = triples(
        tokens=(tokens, vmem),
        mask=(band_mask, pl.BlockSpec(memory_space=pltpu.SMEM)),
        out_grad=(out_grad, vmem),
        qkv_shard=(shards[0], vmem),
        out_shard=(shards[1], vmem),
        up_shard=(shards[2], vmem),
        down_shard=(shards[3], vmem),
    ) + [("vector%d" % i, v, vmem) for i, v in enumerate(smalls)]
    outs = triples(
        slope_far=((tiles, count, TILE), f32),
        output=((count, width), bf16),
        input_grad=((count, width), bf16),
        qkv_result=(shapes[0], f32),
        out_result=(shapes[1], f32),
        up_result=(shapes[2], f32),
        down_result=(shapes[3], f32),
        small_result=((8, 128), f32),
    )
    tails = (
        [((96, 384), bf16)] * 2
        + [((48, 768), bf16)] * 2
        + [((48, 384), bf16)]
        + [((144, 128), bf16)] * 3
    )
    scratch = []
    for j, (tail, kind) in enumerate(tails):
        for b, one in enumerate(scatter_buffers(tail, kind)):
            scratch.append(("piece%d_%d" % (j, b), one))
    scratch += pairs_of(
        qkv_wide=pltpu.VMEM((3, 4, 4, 48, width), bf16),
        out_wide=pltpu.VMEM((4, 4, 48, width), bf16),
        up_wide=pltpu.VMEM((4, 4, 48, hidden), bf16),
        down_wide=pltpu.VMEM((4, 4, 192, width), bf16),
        qkv_sib=pltpu.VMEM((3, 24, width // 2), f32),
        out_sib=pltpu.VMEM((24, width // 2), f32),
        up_sib=pltpu.VMEM((24, hidden // 2), f32),
        down_sib=pltpu.VMEM((96, width // 2), f32),
        qkv_final=pltpu.VMEM((3, 48, width // 2), f32),
        out_final=pltpu.VMEM((48, width // 2), f32),
        up_final=pltpu.VMEM((48, hidden // 2), f32),
        down_final=pltpu.VMEM((192, width // 2), f32),
        small_wide=pltpu.VMEM((4, 4, 2, 8, 128), f32),
        small_part=pltpu.VMEM((4, 4, 2, 8, 128), f32),
        small_total=pltpu.VMEM((4, 4, 8, 128), f32),
        small_got=pltpu.VMEM((4, 4, 8, 128), f32),
        down_part=pltpu.VMEM((4, 4, 192, width), bf16),
        down_total=pltpu.VMEM((4, 4, 192, 384), bf16),
        up_total=pltpu.VMEM((2, 4, 4, 48, 768), bf16),
        out_total=pltpu.VMEM((4, 4, 48, 384), bf16),
        qkv_total=pltpu.VMEM((3, 4, 4, 144, 128), bf16),
        present=pltpu.VMEM((count, 128), f32),
        vec=pltpu.VMEM((8, 7 * width), f32),
        sums=pltpu.VMEM((8, 7 * width), f32),
        bias=pltpu.VMEM((3, 8, width), f32),
        owner=pltpu.VMEM((1, 7 * width), f32),
        logsum=pltpu.VMEM((width // 128, 8, count), f32),
        turned_one=pltpu.VMEM((width, count), bf16),
        turned_two=pltpu.VMEM((width, count), bf16),
        mixed_turned=pltpu.VMEM((width, count), bf16),
        normed=pltpu.VMEM((count, width), bf16),
        mixed=pltpu.VMEM((count, width), bf16),
        grad_low=pltpu.VMEM((count, width), bf16),
        joined=pltpu.VMEM((width // 128, 3, count, 128), bf16),
        middle=pltpu.VMEM((count, width), f32),
        acc=pltpu.VMEM((count, width), f32),
        act=pltpu.VMEM((count, hidden), bf16),
        slope=pltpu.VMEM((2, count, TILE), f32),
        send=pltpu.SemaphoreType.DMA((5, Piece.COUNT)),
        gather_z=pltpu.SemaphoreType.DMA((9, 3)),
        gather_recv=pltpu.SemaphoreType.DMA((9, 13)),
        scatter_recv=pltpu.SemaphoreType.DMA((9, 14)),
        pre_send=pltpu.SemaphoreType.DMA((6,)),
        pre_recv=pltpu.SemaphoreType.DMA((6,)),
        end_send=pltpu.SemaphoreType.DMA((6,)),
        end_recv=pltpu.SemaphoreType.DMA((6,)),
        slope_send=pltpu.SemaphoreType.DMA((2,)),
        slope_recv=pltpu.SemaphoreType.DMA((2,)),
    )
    names = (
        [name for name, _, _ in inputs] + [name for name, _, _ in outs] + [name for name, _ in scratch]
    )
    results = pl.pallas_call(
        functools.partial(layer_kernel, names),
        out_shape=tuple(jax.ShapeDtypeStruct(shape, kind) for _, shape, kind in outs),
        in_specs=[spec for _, _, spec in inputs],
        out_specs=(anywhere,) + (vmem,) * (len(outs) - 1),
        scratch_shapes=[kind for _, kind in scratch],
        compiler_params=pltpu.CompilerParams(
            collective_id=0, has_side_effects=True, vmem_limit_bytes=VMEM_BYTES
        ),
        name="layer",
    )(*[array for _, array, _ in inputs])
    return results[1:]


def deliver_kernel(count, *refs):
    sources, tile = refs[:count], refs[count]
    targets = refs[count + 1 : 2 * count + 1]
    vectors = refs[2 * count + 1 : -count - 2]
    stages = refs[-count - 2 : -2]
    get, put = refs[-2:]
    arriving = [
        pltpu.make_async_copy(sources[i], stages[i], get.at[i]) for i in range(count)
    ]
    leaving = [pltpu.make_async_copy(stages[i], targets[i], put.at[i]) for i in range(count)]
    for copy in arriving:
        copy.start()
    for i, vector in enumerate(vectors):
        vector[...] = tile[i, 0 : vector.shape[0]]
    for first, second in zip(arriving, leaving):
        first.wait()
        second.start()
    for copy in leaving:
        copy.wait()


def deliver(whole, tile, sizes):
    count = len(whole)
    anywhere = pl.BlockSpec(memory_space=pl.ANY)
    vmem = pl.BlockSpec(memory_space=pltpu.VMEM)
    return pl.pallas_call(
        functools.partial(deliver_kernel, count),
        out_shape=[jax.ShapeDtypeStruct(a.shape, a.dtype) for a in whole]
        + [jax.ShapeDtypeStruct((m,), jnp.float32) for m in sizes],
        in_specs=[anywhere] * count + [vmem],
        out_specs=[anywhere] * count + [vmem] * len(sizes),
        scratch_shapes=[pltpu.VMEM(a.shape, a.dtype) for a in whole]
        + [pltpu.SemaphoreType.DMA((count,))] * 2,
        compiler_params=pltpu.CompilerParams(vmem_limit_bytes=VMEM_BYTES),
        name="deliver",
    )(*whole, tile)


def body(
    tokens,
    band_mask,
    out_grad,
    norm1_gain,
    norm1_shift,
    qkv_weight,
    qv_bias,
    out_weight,
    out_bias,
    norm2_gain,
    norm2_shift,
    up_weight,
    up_bias,
    down_weight,
    down_bias,
):
    smalls = (norm1_gain, norm1_shift, qv_bias, out_bias, norm2_gain, norm2_shift, up_bias, down_bias)
    shards = (qkv_weight, out_weight, up_weight, down_weight)
    *whole, tile = layer_call(tokens, band_mask, out_grad, shards, smalls)
    output, input_grad, qkv, out, up, down, *grads = deliver(
        whole, tile, [v.shape[0] for v in smalls]
    )
    return (
        output,
        input_grad,
        grads[0],
        grads[1],
        qkv,
        grads[2],
        out,
        grads[3],
        grads[4],
        grads[5],
        up,
        grads[6],
        down,
        grads[7],
    )


def solution(mesh):
    rows, flat = P(AXES, None), P(AXES)
    params = (flat, flat, rows, flat, rows, flat, flat, flat, rows, flat, rows, flat)
    fitted = tuple(mesh.shape[axis] for axis in AXES) == (8, 4)
    return jax.shard_map(
        body if fitted else body_plain,
        mesh=mesh,
        in_specs=(rows, rows, rows) + params,
        out_specs=(rows, rows) + params,
        check_vma=False,
    )
```

```python
import functools
import math

import jax
import jax.numpy as jnp
from jax import lax
from jax.experimental import pallas as pl
from jax.experimental.pallas import tpu as pltpu
from jax.sharding import PartitionSpec as P

HEAD = 64
HEAD_GROUP = 4
QBLOCK = 512


NORM_EPSILON = 1e-05
VMEM_BYTES = 62 << 20
AXES = ("wide", "narrow")


def normalize(values, gain, shift):
    centre = jnp.mean(values, axis=1, keepdims=True)
    centred = values - centre
    factor = lax.rsqrt(jnp.mean(centred * centred, axis=1, keepdims=True) + NORM_EPSILON)
    normed = centred * factor
    return (normed * gain + shift, normed, factor)


def normalize_back(upstream, normed, factor, gain):
    gain_grad = jnp.sum(upstream * normed, axis=0)
    shift_grad = jnp.sum(upstream, axis=0)
    scaled = upstream * gain
    inner = (
        scaled
        - jnp.mean(scaled, axis=1, keepdims=True)
        - normed * jnp.mean(scaled * normed, axis=1, keepdims=True)
    )
    return (factor * inner, gain_grad, shift_grad)


def gelu_slope(values):
    cumulative = 0.5 * (1.0 + lax.erf(values * (1.0 / math.sqrt(2.0))))
    return cumulative + values * jnp.exp(-0.5 * values * values) * (1.0 / math.sqrt(2.0 * math.pi))


def to_groups(matrix, count):
    return matrix.reshape(matrix.shape[0], count, -1).transpose(1, 0, 2)


def from_groups(stacked):
    return stacked.transpose(1, 0, 2).reshape(stacked.shape[1], -1)


def attend_forward(query_cols, key_cols, value_cols, key_live):
    row_count, span_cols = key_cols.shape
    head_width = span_cols // HEAD_GROUP
    scaling = 1.0 / math.sqrt(head_width)
    key_rows = key_cols.reshape(row_count, HEAD_GROUP, head_width)
    value_rows = value_cols.reshape(row_count, HEAD_GROUP, head_width)
    query_blocks = query_cols.reshape(row_count // QBLOCK, QBLOCK, HEAD_GROUP, head_width)

    def one_block(query_rows):
        scores = (
            jnp.einsum("qhd,khd->hqk", query_rows, key_rows, preferred_element_type=jnp.float32)
            * scaling
        )
        scores = jnp.where(key_live[None, None, :], scores, -jnp.inf)
        largest = jnp.max(scores, axis=2, keepdims=True)
        expo = jnp.exp(scores - largest)
        totals = jnp.sum(expo, axis=2, keepdims=True)
        weights_low = (expo / totals).astype(jnp.bfloat16)
        mixture = jnp.einsum(
            "hqk,khd->qhd", weights_low, value_rows, preferred_element_type=jnp.float32
        )
        return (mixture.reshape(QBLOCK, span_cols), largest[:, :, 0] + jnp.log(totals[:, :, 0]))

    mixture, logsum = lax.map(one_block, query_blocks)
    return (mixture.reshape(row_count, span_cols), logsum)


def attend_backward(query_cols, key_cols, value_cols, grad_cols, logsum, key_live):
    row_count, span_cols = key_cols.shape
    head_width = span_cols // HEAD_GROUP
    scaling = 1.0 / math.sqrt(head_width)
    key_rows = key_cols.reshape(row_count, HEAD_GROUP, head_width)
    value_rows = value_cols.reshape(row_count, HEAD_GROUP, head_width)
    query_blocks = query_cols.reshape(row_count // QBLOCK, QBLOCK, HEAD_GROUP, head_width)
    grad_blocks = grad_cols.reshape(row_count // QBLOCK, QBLOCK, HEAD_GROUP, head_width)

    def one_block(carry, items):
        key_acc, value_acc = carry
        query_rows, grad_rows, block_logsum = items
        scores = (
            jnp.einsum("qhd,khd->hqk", query_rows, key_rows, preferred_element_type=jnp.float32)
            * scaling
        )
        scores = jnp.where(key_live[None, None, :], scores, -jnp.inf)
        probs = jnp.exp(scores - block_logsum[:, :, None])
        value_acc = value_acc + jnp.einsum(
            "hqk,qhd->khd",
            probs.astype(jnp.bfloat16),
            grad_rows,
            preferred_element_type=jnp.float32,
        )
        prob_grad = jnp.einsum(
            "qhd,khd->hqk", grad_rows, value_rows, preferred_element_type=jnp.float32
        )
        inner = jnp.sum(probs * prob_grad, axis=2, keepdims=True)
        score_grad = (probs * (prob_grad - inner)).astype(jnp.bfloat16)
        query_grad = (
            jnp.einsum("hqk,khd->qhd", score_grad, key_rows, preferred_element_type=jnp.float32)
            * scaling
        )
        key_acc = (
            key_acc
            + jnp.einsum("hqk,qhd->khd", score_grad, query_rows, preferred_element_type=jnp.float32)
            * scaling
        )
        return ((key_acc, value_acc), query_grad.reshape(QBLOCK, span_cols))

    empty = jnp.zeros((row_count, HEAD_GROUP, head_width), jnp.float32)
    (key_grad, value_grad), query_grad = lax.scan(
        one_block, (empty, empty), (query_blocks, grad_blocks, logsum)
    )
    return (
        query_grad.reshape(row_count, span_cols),
        key_grad.reshape(row_count, span_cols),
        value_grad.reshape(row_count, span_cols),
    )


def gathered(shard):
    return lax.all_gather(shard.astype(jnp.bfloat16), AXES, axis=0, tiled=True)


def scattered(part):
    return lax.psum_scatter(part, AXES, scatter_dimension=0, tiled=True)


def body_plain(
    tokens,
    band_mask,
    out_grad,
    norm1_gain,
    norm1_shift,
    qkv_weight,
    qv_bias,
    out_weight,
    out_bias,
    norm2_gain,
    norm2_shift,
    up_weight,
    up_bias,
    down_weight,
    down_bias,
):
    row_count, width = tokens.shape
    group_count = width // (HEAD_GROUP * HEAD)
    present = jnp.repeat(band_mask[0].astype(jnp.float32), row_count // band_mask.shape[1])
    key_live = present > 0.5
    column_mask = present[:, None]
    gain_one, shift_one, w_qkv, b_qv, w_out, b_out = (
        gathered(norm1_gain),
        gathered(norm1_shift),
        gathered(qkv_weight),
        gathered(qv_bias),
        gathered(out_weight),
        gathered(out_bias),
    )
    inputs = tokens.astype(jnp.float32)
    normed_one, unit_one, factor_one = normalize(
        inputs, gain_one.astype(jnp.float32), shift_one.astype(jnp.float32)
    )
    normed_one = normed_one.astype(jnp.bfloat16)
    bias_wide = b_qv.astype(jnp.float32)
    bias_full = jnp.concatenate(
        [bias_wide[:width], jnp.zeros((width,), jnp.float32), bias_wide[width:]]
    )
    joined = (jnp.dot(normed_one, w_qkv, preferred_element_type=jnp.float32) + bias_full).astype(
        jnp.bfloat16
    )
    query_groups = to_groups(joined[:, :width], group_count)
    key_groups = to_groups(joined[:, width : 2 * width], group_count)
    value_groups = to_groups(joined[:, 2 * width :], group_count)
    mixture, logsum = lax.map(
        lambda items: attend_forward(items[0], items[1], items[2], key_live),
        (query_groups, key_groups, value_groups),
    )
    mixture = from_groups(mixture).astype(jnp.bfloat16)
    attention = jnp.dot(mixture, w_out, preferred_element_type=jnp.float32) + b_out.astype(
        jnp.float32
    )
    middle = inputs + column_mask * attention
    gain_two, shift_two, w_up, b_up, w_down, b_down = (
        gathered(norm2_gain),
        gathered(norm2_shift),
        gathered(up_weight),
        gathered(up_bias),
        gathered(down_weight),
        gathered(down_bias),
    )
    normed_two, unit_two, factor_two = normalize(
        middle, gain_two.astype(jnp.float32), shift_two.astype(jnp.float32)
    )
    normed_two = normed_two.astype(jnp.bfloat16)
    hidden = jnp.dot(normed_two, w_up, preferred_element_type=jnp.float32) + b_up.astype(
        jnp.float32
    )
    active = jax.nn.gelu(hidden, approximate=False).astype(jnp.bfloat16)
    branch = jnp.dot(active, w_down, preferred_element_type=jnp.float32) + b_down.astype(
        jnp.float32
    )
    output = (middle + column_mask * branch).astype(jnp.bfloat16)
    upstream = out_grad.astype(jnp.float32)
    branch_grad = (column_mask * upstream).astype(jnp.bfloat16)
    down_weight_grad = jnp.einsum(
        "tf,td->fd", active, branch_grad, preferred_element_type=jnp.float32
    )
    down_bias_grad = jnp.sum(branch_grad.astype(jnp.float32), axis=0)
    active_grad = jnp.einsum(
        "td,fd->tf", branch_grad, w_down, preferred_element_type=jnp.float32
    )
    hidden_grad = (active_grad * gelu_slope(hidden)).astype(jnp.bfloat16)
    up_weight_grad = jnp.einsum(
        "td,tf->df", normed_two, hidden_grad, preferred_element_type=jnp.float32
    )
    up_bias_grad = jnp.sum(hidden_grad.astype(jnp.float32), axis=0)
    normed_two_grad = jnp.einsum(
        "tf,df->td", hidden_grad, w_up, preferred_element_type=jnp.float32
    )
    middle_part, norm2_gain_grad, norm2_shift_grad = normalize_back(
        normed_two_grad, unit_two, factor_two, gain_two.astype(jnp.float32)
    )
    (
        norm2_gain_grad,
        norm2_shift_grad,
        up_weight_grad,
        up_bias_grad,
        down_weight_grad,
        down_bias_grad,
    ) = (
        scattered(norm2_gain_grad),
        scattered(norm2_shift_grad),
        scattered(up_weight_grad),
        scattered(up_bias_grad),
        scattered(down_weight_grad),
        scattered(down_bias_grad),
    )
    middle_grad = upstream + middle_part
    attention_grad = (column_mask * middle_grad).astype(jnp.bfloat16)
    out_weight_grad = jnp.einsum(
        "te,td->ed", mixture, attention_grad, preferred_element_type=jnp.float32
    )
    out_bias_grad = jnp.sum(attention_grad.astype(jnp.float32), axis=0)
    mixture_grad = jnp.einsum(
        "td,ed->te", attention_grad, w_out, preferred_element_type=jnp.float32
    ).astype(jnp.bfloat16)
    grad_groups = to_groups(mixture_grad, group_count)
    query_grad, key_grad, value_grad = lax.map(
        lambda items: attend_backward(items[0], items[1], items[2], items[3], items[4], key_live),
        (query_groups, key_groups, value_groups, grad_groups, logsum),
    )
    query_grad = from_groups(query_grad).astype(jnp.bfloat16)
    key_grad = from_groups(key_grad).astype(jnp.bfloat16)
    value_grad = from_groups(value_grad).astype(jnp.bfloat16)
    joined_grad = jnp.concatenate([query_grad, key_grad, value_grad], axis=1)
    qkv_weight_grad = jnp.einsum(
        "td,tc->dc", normed_one, joined_grad, preferred_element_type=jnp.float32
    )
    qv_bias_grad = jnp.concatenate(
        [
            jnp.sum(query_grad.astype(jnp.float32), axis=0),
            jnp.sum(value_grad.astype(jnp.float32), axis=0),
        ]
    )
    normed_one_grad = jnp.einsum(
        "tc,dc->td", joined_grad, w_qkv, preferred_element_type=jnp.float32
    )
    input_part, norm1_gain_grad, norm1_shift_grad = normalize_back(
        normed_one_grad, unit_one, factor_one, gain_one.astype(jnp.float32)
    )
    input_grad = (middle_grad + input_part).astype(jnp.bfloat16)
    (
        norm1_gain_grad,
        norm1_shift_grad,
        qkv_weight_grad,
        qv_bias_grad,
        out_weight_grad,
        out_bias_grad,
    ) = (
        scattered(norm1_gain_grad),
        scattered(norm1_shift_grad),
        scattered(qkv_weight_grad),
        scattered(qv_bias_grad),
        scattered(out_weight_grad),
        scattered(out_bias_grad),
    )
    return (
        output,
        input_grad,
        norm1_gain_grad,
        norm1_shift_grad,
        qkv_weight_grad,
        qv_bias_grad,
        out_weight_grad,
        out_bias_grad,
        norm2_gain_grad,
        norm2_shift_grad,
        up_weight_grad,
        up_bias_grad,
        down_weight_grad,
        down_bias_grad,
    )


MESH_ID = pl.DeviceIdType.MESH
VIA_X = (0, 2)
VIA_Y = (1, 3)
ORDER = (1, 3, 2)
SCORE_SCALE = math.log2(math.e) / math.sqrt(HEAD)
TILE = 768


class Place:
    def __init__(self):
        wide = lax.axis_index("wide")
        narrow = lax.axis_index("narrow")
        z, y = wide // 2, wide % 2
        x, c = narrow // 2, narrow % 2
        self.z, self.c = z, c
        self.zs = (z, z + 1 - 2 * (z % 2), (z + 2) % 4, 3 - z)
        self.q = y * 2 + x
        self.qx = y * 2 + (1 - x)
        self.qy = (1 - y) * 2 + x
        self.qd = (1 - y) * 2 + (1 - x)
        self.to_z = tuple((zz * 2 + y, x * 2 + c) for zz in self.zs)
        self.to_x = (z * 2 + y, (1 - x) * 2 + c)
        self.to_y = (z * 2 + 1 - y, x * 2 + c)
        self.to_c = (z * 2 + y, x * 2 + 1 - c)
        self.to_d = (z * 2 + 1 - y, (1 - x) * 2 + c)


def span(start, size, step):
    return pl.ds(pl.multiple_of(start, step), size)


def meet(place):
    barrier = pltpu.get_barrier_semaphore()
    peers = place.to_z[1:] + (place.to_x, place.to_y, place.to_d, place.to_c)
    for peer in peers:
        pl.semaphore_signal(barrier, inc=1, device_id=peer, device_id_type=MESH_ID)
    pl.semaphore_wait(barrier, len(peers))


def remote(source, target, send, recv, peer):
    return pltpu.make_async_remote_copy(
        src_ref=source,
        dst_ref=target,
        send_sem=send,
        recv_sem=recv,
        device_id=peer,
        device_id_type=MESH_ID,
    )


class Piece:
    COUNT = 19

    def __init__(self, place, send, recv, slots, z_send=None):
        self.p = place
        self.send, self.recv, self.slots, self.z_send = send, recv, slots, z_send
        self.sent = []

    def pair(self, index):
        own = self.send if index >= 3 or self.z_send is None else self.z_send
        return own.at[index], self.recv.at[self.slots[index]]

    def go(self, source, target, index, peer):
        remote(source(), target(), *self.pair(index), peer).start()
        self.sent.append((source, target, index, peer))

    def got(self, target, index, peer):
        remote(target, target, *self.pair(index), peer).wait_recv()

    def finish(self):
        for source, target, index, peer in self.sent:
            remote(source(), target(), *self.pair(index), peer).wait_send()
        self.sent = []


class Gather(Piece):
    SLOTS = (0, 1, 2, 3, 4, 5, 6, 11, 11, 7, 8, 9, 10, 11, 11, 12, 12, 12, 12)

    def __init__(self, place, block, column, others, send, recv, z_send):
        super().__init__(place, send, recv, self.SLOTS, z_send)
        self.block, self.column, self.others = block, column, others

    def own(self):
        return self.block(self.p.z, self.p.q)

    def start_z(self):
        p = self.p
        for k in ORDER:
            self.go(self.own, self.own, k - 1, p.to_z[k])

    def start_xy(self):
        p = self.p
        self.go(self.own, self.own, 3, p.to_x)
        self.go(self.own, self.own, 9, p.to_y)

    def z(self, k):
        p = self.p
        here = lambda: self.block(p.zs[k], p.q)
        self.got(here(), k - 1, p.to_z[k])
        self.go(here, here, 3 + k, p.to_x)
        self.go(here, here, 9 + k, p.to_y)

    def share(self, index, q):
        column = lambda: self.column(q)
        self.go(column, column, index, self.p.to_c)

    def own_column(self):
        self.share(15, self.p.q)

    def xy(self, k):
        p = self.p
        from_x = lambda: self.block(p.zs[k], p.qx)
        self.got(from_x(), 3 + k, p.to_x)
        if k in VIA_X:
            self.go(from_x, from_x, 13 + VIA_X.index(k), p.to_y)
        from_y = lambda: self.block(p.zs[k], p.qy)
        self.got(from_y(), 9 + k, p.to_y)
        if k in VIA_Y:
            self.go(from_y, from_y, 7 + VIA_Y.index(k), p.to_x)

    def xy_columns(self):
        self.share(16, self.p.qx)
        self.share(17, self.p.qy)

    def d(self):
        p = self.p
        self.got(self.column(p.qd), 13, p.to_y)
        self.share(18, p.qd)

    def c(self):
        self.got(self.others(), 15, self.p.to_c)


class Scatter(Piece):
    SLOTS = (13, 13, 13, 5, 6, 7, 8, 1, 2, 9, 10, 11, 12, 3, 4, 0, 0, 0, 0)

    def __init__(self, place, block, column, whole, bufs, send, recv):
        super().__init__(place, send, recv, self.SLOTS)
        self.block, self.column, self.whole = block, column, whole
        self.dx, self.dy, self.xr, self.yr, self.zr = bufs

    def add(self, target, other):
        target[...] = (target[...].astype(jnp.float32) + other[...].astype(jnp.float32)).astype(
            target.dtype
        )

    def give(self, other):
        p = self.p
        for i, q in enumerate((p.qd, p.qx, p.qy, p.q)):
            self.go(lambda q=q: other(q), lambda q=q: self.column(q), 15 + i, p.to_c)

    def arrive(self):
        self.got(self.whole(), 15, self.p.to_c)

    def diagonal(self):
        p = self.p
        for i in range(2):
            self.go(
                lambda i=i: self.block(p.zs[VIA_X[i]], p.qd), lambda i=i: self.dx.at[i], 7 + i, p.to_x
            )
            self.go(
                lambda i=i: self.block(p.zs[VIA_Y[i]], p.qd), lambda i=i: self.dy.at[i], 13 + i, p.to_y
            )

    def cross(self, k):
        p = self.p
        on_x = lambda: self.block(p.zs[k], p.qx)
        on_y = lambda: self.block(p.zs[k], p.qy)
        if k in VIA_Y:
            i = VIA_Y.index(k)
            self.go(on_y, lambda: self.yr.at[k], 9 + k, p.to_y)
            self.got(self.dy.at[i], 13 + i, p.to_y)
            self.add(on_x(), self.dy.at[i])
            self.go(on_x, lambda: self.xr.at[k], 3 + k, p.to_x)
        else:
            i = VIA_X.index(k)
            self.go(on_x, lambda: self.xr.at[k], 3 + k, p.to_x)
            self.got(self.dx.at[i], 7 + i, p.to_x)
            self.add(on_y(), self.dx.at[i])
            self.go(on_y, lambda: self.yr.at[k], 9 + k, p.to_y)

    def plane(self, k):
        p = self.p
        self.got(self.xr.at[k], 3 + k, p.to_x)
        self.got(self.yr.at[k], 9 + k, p.to_y)
        here = self.block(p.zs[k], p.q)
        return here, (
            here[...].astype(jnp.float32)
            + self.xr[k].astype(jnp.float32)
            + self.yr[k].astype(jnp.float32)
        )

    def spread(self, k):
        p = self.p
        here, value = self.plane(k)
        here[...] = value.astype(here.dtype)
        self.go(lambda: self.block(p.zs[k], p.q), lambda: self.zr.at[k - 1], k - 1, p.to_z[k])

    def last(self):
        _, value = self.plane(0)
        self.got(self.zr, 0, self.p.to_z[1])
        for k in ORDER:
            value = value + self.zr[k - 1].astype(jnp.float32)
        return value


class SmallScatter(Piece):
    SLOTS = (4, 4, 4, 1, 2, 3, 0, 0, 0, 0, 0, 0, 0, 0, 0, 0, 0, 0, 0)

    def __init__(self, place, total, arrived, send, recv):
        super().__init__(place, send, recv, self.SLOTS)
        self.total, self.arrived = total, arrived

    def give(self, other):
        self.go(other, lambda: self.total, 15, self.p.to_c)

    def arrive(self):
        self.got(self.total, 15, self.p.to_c)

    def neighbours(self):
        p = self.p
        return ((0, p.qx, p.to_x), (1, p.qy, p.to_y), (2, p.qd, p.to_d))

    def plane(self):
        for i, q, peer in self.neighbours():
            self.go(lambda q=q: self.total.at[:, q], lambda i=i: self.arrived.at[i], 3 + i, peer)

    def spread(self):
        p = self.p
        value = self.total[:, p.q]
        for i, _, peer in self.neighbours():
            self.got(self.arrived.at[i], 3 + i, peer)
            value = value + self.arrived[i]
        self.total[:, p.q] = value
        for k in ORDER:
            self.go(
                lambda k=k: self.total.at[p.zs[k], p.q],
                lambda k=k: self.arrived.at[3, k],
                k - 1,
                p.to_z[k],
            )

    def last(self):
        p = self.p
        self.got(self.arrived.at[3, pl.ds(1, 3)], 0, p.to_z[1])
        value = self.total[p.z, p.q]
        for k in ORDER:
            value = value + self.arrived[3, k]
        return value


def scatter_buffers(tail, kind):
    return [
        pltpu.VMEM((2,) + tail, kind),
        pltpu.VMEM((2,) + tail, kind),
        pltpu.VMEM((4,) + tail, kind),
        pltpu.VMEM((4,) + tail, kind),
        pltpu.VMEM((3,) + tail, kind),
    ]


MATRICES = ("qkv", "out", "up", "down")


def triples(**named):
    return [(name, one, two) for name, (one, two) in named.items()]


def pairs_of(**named):
    return list(named.items())


class Named:
    def __init__(self, names, refs):
        assert len(names) == len(refs)
        self.__dict__.update(zip(names, refs))


def loop(first, count, compute, slots=()):
    def step(i, carry):
        compute(i)
        for j, steps in enumerate(slots):
            if steps:

                @pl.when(i == first + j)
                def _(steps=steps):
                    for one in steps:
                        one()

        return carry

    lax.fori_loop(first, first + count, step, 0)


def follow(order, steps, loops):
    at = 0
    while at < len(order):
        kind = order[at][0]
        if kind not in loops:
            steps[order[at]]()
            at += 1
            continue
        first, slots, end = order[at][1], [[]], at + 1
        held = []
        while end < len(order) and (order[end][0] not in loops or order[end][0] == kind):
            if order[end][0] == kind:
                assert order[end][1] == first + len(slots)
                slots[-1] += held
                held = []
                slots.append([])
                at = end
            else:
                held.append(steps[order[end]])
            end += 1
        if len(slots) == 1:
            loops[kind](jnp.int32(first))
        else:
            loop(first, len(slots), loops[kind], slots)
        at += 1


def dot(left, right):
    return jnp.dot(left, right, preferred_element_type=jnp.float32)


def dot_nt(left, right):
    return lax.dot_general(
        left, right, (((1,), (1,)), ((), ())), preferred_element_type=jnp.float32
    )


def dot_tn(left, right):
    return lax.dot_general(
        left, right, (((0,), (0,)), ((), ())), preferred_element_type=jnp.float32
    )


def head_only(values, e):
    lane = lax.broadcasted_iota(jnp.int32, values.shape, 1)
    return jnp.where((lane // HEAD) == e, values, jnp.zeros_like(values))


def fill_present(present, mask):
    groups = mask.shape[1]
    rows = present.shape[0] // groups
    for g in range(groups):
        present[g * rows : (g + 1) * rows, :] = jnp.full(
            (rows, 128), mask[0, g].astype(jnp.float32)
        )


def segments(width):
    return ((0, width, width // 32), (width, 2 * width, width // 16), (3 * width, 4 * width, width // 8))


def selection(size, m):
    lane = lax.broadcasted_iota(jnp.int32, (1, size), 1).astype(jnp.float32)
    rest = lane - m * jnp.floor((lane + 0.5) * (1.0 / m))
    row = lax.broadcasted_iota(jnp.int32, (128, size), 0).astype(jnp.float32)
    return jnp.where(row == rest, 1.0, 0.0).astype(jnp.bfloat16)


def owners(width):
    parts = []
    for _, size, m in segments(width):
        lane = lax.broadcasted_iota(jnp.int32, (1, size), 1).astype(jnp.float32)
        parts.append(jnp.floor((lane + 0.5) * (1.0 / m)))
    return jnp.concatenate(parts, axis=1)


def unit(values):
    centred = values - jnp.mean(values, axis=1, keepdims=True)
    factor = lax.rsqrt(jnp.mean(centred * centred, axis=1, keepdims=True) + NORM_EPSILON)
    return centred * factor, factor


(
    ATTENTION,
    CLOSE,
    CROSS,
    C_GOT,
    DIAGONAL,
    DOWN_HIGH,
    DOWN_LOW,
    DRAIN,
    D_GOT,
    EXPAND_HIGH,
    EXPAND_LOW,
    FINISH,
    FIRST_BACK,
    FIRST_NORM,
    FORM,
    GIVE,
    HEADS,
    HEADS_BACK,
    LAST,
    MASK_GRAD,
    NARROW,
    OUT_BACK,
    OWN_COLUMN,
    OWN_PART,
    PACK,
    PLANE_GOT,
    PLANE_START,
    PREPARE,
    QKV_BACK,
    SECOND_BACK,
    SECOND_NORM,
    SETTLE,
    SMALL_PLANE,
    SMALL_SPREAD,
    SPREAD,
    START_XY,
    START_Z,
    UNPACK,
    UP_BACK,
    XY_COLUMNS,
    XY_GOT,
    Z_GOT,
) = range(42)
SEQUENCE = (
    (START_Z, 8),
    (START_XY, 8),
    (FORM, 0),
    (START_Z, 0),
    (FORM, 1),
    (FORM, 2),
    (FORM, 3),
    (START_Z, 1),
    (START_Z, 2),
    (START_Z, 3),
    (START_Z, 4),
    (START_Z, 5),
    (START_Z, 6),
    (Z_GOT, 8, 3),
    (START_Z, 7),
    (Z_GOT, 8, 2),
    (START_XY, 1),
    (XY_GOT, 8, 0),
    (Z_GOT, 8, 1),
    (OWN_COLUMN, 8),
    (START_XY, 2),
    (START_XY, 0),
    (PREPARE,),
    (START_XY, 3),
    (MASK_GRAD, 0),
    (MASK_GRAD, 1),
    (Z_GOT, 0, 1),
    (XY_GOT, 8, 3),
    (MASK_GRAD, 2),
    (XY_GOT, 8, 2),
    (MASK_GRAD, 3),
    (XY_GOT, 1, 0),
    (XY_GOT, 8, 1),
    (XY_COLUMNS, 8),
    (Z_GOT, 0, 3),
    (Z_GOT, 0, 2),
    (OWN_COLUMN, 0),
    (XY_GOT, 2, 0),
    (XY_GOT, 0, 0),
    (XY_GOT, 3, 0),
    (Z_GOT, 1, 1),
    (XY_GOT, 0, 1),
    (D_GOT, 8),
    (Z_GOT, 1, 3),
    (C_GOT, 8),
    (UNPACK,),
    (XY_GOT, 0, 2),
    (Z_GOT, 1, 2),
    (OWN_COLUMN, 1),
    (XY_GOT, 0, 3),
    (XY_COLUMNS, 0),
    (FIRST_NORM, 0),
    (FIRST_NORM, 1),
    (FIRST_NORM, 2),
    (Z_GOT, 2, 1),
    (FIRST_NORM, 3),
    (XY_GOT, 1, 1),
    (Z_GOT, 2, 3),
    (Z_GOT, 2, 2),
    (OWN_COLUMN, 2),
    (XY_GOT, 1, 3),
    (D_GOT, 0),
    (XY_GOT, 1, 2),
    (START_XY, 4),
    (XY_COLUMNS, 1),
    (Z_GOT, 3, 1),
    (XY_GOT, 2, 1),
    (C_GOT, 0),
    (HEADS, 0),
    (Z_GOT, 3, 3),
    (XY_GOT, 2, 3),
    (Z_GOT, 3, 2),
    (OWN_COLUMN, 3),
    (D_GOT, 1),
    (XY_GOT, 2, 2),
    (XY_COLUMNS, 2),
    (HEADS, 1),
    (XY_GOT, 4, 0),
    (START_XY, 5),
    (XY_GOT, 3, 1),
    (C_GOT, 1),
    (HEADS, 2),
    (Z_GOT, 4, 1),
    (XY_GOT, 3, 3),
    (D_GOT, 2),
    (HEADS, 3),
    (XY_GOT, 3, 2),
    (XY_COLUMNS, 3),
    (Z_GOT, 4, 3),
    (C_GOT, 2),
    (HEADS, 4),
    (Z_GOT, 4, 2),
    (XY_GOT, 4, 1),
    (OWN_COLUMN, 4),
    (XY_GOT, 5, 0),
    (HEADS, 5),
    (D_GOT, 3),
    (XY_GOT, 4, 3),
    (Z_GOT, 5, 1),
    (C_GOT, 3),
    (ATTENTION,),
    (XY_GOT, 4, 2),
    (XY_COLUMNS, 4),
    (SECOND_NORM, 0),
    (START_XY, 7),
    (SECOND_NORM, 1),
    (SECOND_NORM, 2),
    (Z_GOT, 5, 3),
    (SECOND_NORM, 3),
    (Z_GOT, 5, 2),
    (OWN_COLUMN, 5),
    (XY_GOT, 5, 1),
    (D_GOT, 4),
    (XY_GOT, 7, 0),
    (C_GOT, 4),
    (EXPAND_LOW, 0),
    (START_XY, 6),
    (EXPAND_LOW, 1),
    (Z_GOT, 6, 1),
    (XY_GOT, 5, 3),
    (DOWN_LOW, 0),
    (XY_GOT, 5, 2),
    (XY_COLUMNS, 5),
    (DOWN_LOW, 1),
    (Z_GOT, 6, 3),
    (Z_GOT, 6, 2),
    (OWN_COLUMN, 6),
    (XY_GOT, 6, 0),
    (XY_GOT, 6, 1),
    (D_GOT, 5),
    (Z_GOT, 7, 1),
    (XY_GOT, 6, 3),
    (C_GOT, 5),
    (EXPAND_HIGH, 0),
    (EXPAND_HIGH, 1),
    (Z_GOT, 7, 3),
    (XY_GOT, 6, 2),
    (XY_COLUMNS, 6),
    (DRAIN,),
    (DOWN_HIGH, 0),
    (Z_GOT, 7, 2),
    (OWN_COLUMN, 7),
    (DOWN_HIGH, 1),
    (XY_GOT, 7, 1),
    (GIVE, 0),
    (GIVE, 1),
    (XY_GOT, 7, 3),
    (D_GOT, 6),
    (OWN_PART, 0),
    (XY_GOT, 7, 2),
    (XY_COLUMNS, 7),
    (DIAGONAL, 0),
    (OWN_PART, 1),
    (DIAGONAL, 1),
    (C_GOT, 6),
    (D_GOT, 7),
    (CROSS, 0, 0),
    (CROSS, 0, 1),
    (CROSS, 0, 2),
    (C_GOT, 7),
    (NARROW, 0),
    (NARROW, 1),
    (CROSS, 0, 3),
    (CROSS, 1, 0),
    (CROSS, 1, 1),
    (CROSS, 1, 2),
    (NARROW, 2),
    (CROSS, 1, 3),
    (NARROW, 3),
    (GIVE, 2),
    (SPREAD, 0, 1),
    (GIVE, 3),
    (PACK, 2),
    (SPREAD, 0, 2),
    (SPREAD, 0, 3),
    (OWN_PART, 2),
    (DIAGONAL, 2),
    (FINISH, 0),
    (FINISH, 1),
    (FINISH, 2),
    (FINISH, 3),
    (UP_BACK,),
    (SPREAD, 1, 2),
    (SPREAD, 1, 1),
    (OWN_PART, 3),
    (SPREAD, 1, 3),
    (DIAGONAL, 3),
    (CROSS, 2, 0),
    (SECOND_BACK, 0),
    (SECOND_BACK, 1),
    (SECOND_BACK, 2),
    (CROSS, 2, 2),
    (CROSS, 2, 1),
    (SECOND_BACK, 3),
    (GIVE, 4),
    (CROSS, 2, 3),
    (OUT_BACK,),
    (LAST, 0),
    (CROSS, 3, 0),
    (CROSS, 3, 1),
    (HEADS_BACK, 0),
    (CROSS, 3, 2),
    (CROSS, 3, 3),
    (GIVE, 5),
    (SPREAD, 2, 2),
    (OWN_PART, 4),
    (DIAGONAL, 4),
    (HEADS_BACK, 1),
    (SPREAD, 2, 3),
    (LAST, 1),
    (CLOSE, 3),
    (SPREAD, 2, 1),
    (OWN_PART, 5),
    (DIAGONAL, 5),
    (SPREAD, 3, 1),
    (GIVE, 6),
    (HEADS_BACK, 2),
    (SPREAD, 3, 3),
    (CROSS, 4, 1),
    (CROSS, 4, 3),
    (CROSS, 4, 2),
    (CROSS, 5, 0),
    (CROSS, 4, 0),
    (CROSS, 5, 1),
    (SPREAD, 3, 2),
    (SETTLE, 3),
    (OWN_PART, 6),
    (CROSS, 5, 3),
    (DIAGONAL, 6),
    (LAST, 2),
    (CROSS, 5, 2),
    (GIVE, 7),
    (PACK, 1),
    (SPREAD, 4, 1),
    (SPREAD, 4, 3),
    (SPREAD, 4, 2),
    (OWN_PART, 7),
    (DIAGONAL, 7),
    (QKV_BACK,),
    (SPREAD, 5, 1),
    (SPREAD, 5, 3),
    (FIRST_BACK, 0),
    (CROSS, 6, 0),
    (CROSS, 6, 1),
    (FIRST_BACK, 1),
    (CROSS, 6, 3),
    (CROSS, 6, 2),
    (LAST, 3),
    (CLOSE, 2),
    (FIRST_BACK, 2),
    (SPREAD, 5, 2),
    (FIRST_BACK, 3),
    (CROSS, 7, 0),
    (CROSS, 7, 1),
    (PACK, 0),
    (CROSS, 7, 3),
    (GIVE, 8),
    (CROSS, 7, 2),
    (SETTLE, 2),
    (LAST, 4),
    (CLOSE, 1),
    (SPREAD, 6, 1),
    (SPREAD, 6, 3),
    (OWN_PART, 8),
    (SMALL_PLANE,),
    (SETTLE, 1),
    (SPREAD, 6, 2),
    (LAST, 5),
    (SPREAD, 7, 1),
    (SPREAD, 7, 3),
    (SPREAD, 7, 2),
    (SMALL_SPREAD,),
    (LAST, 6),
    (LAST, 7),
    (CLOSE, 0),
    (LAST, 8),
    (SETTLE, 0),
)


FETCHED = ("qkv_shard", "out_shard", "up_shard", "down_shard", "tokens", "out_grad")
STORED = ("qkv_result", "out_result", "up_result", "down_result") + (
    ("output", "input_grad", "small_result")
)


def layer_kernel(names, *refs):
    r = Named(names, refs)
    place = Place()
    c = place.c
    tokens, width = r.tokens.shape
    hidden = r.act.shape[1]
    third = width // 2
    tiles = hidden // TILE
    shards = (r.qkv_shard, r.out_shard, r.up_shard, r.down_shard)

    def fetch(i):
        name = FETCHED[i]
        return pltpu.make_async_copy(getattr(r, name + "_in"), getattr(r, name), r.load.at[i])

    def store(i):
        name = STORED[i]
        return pltpu.make_async_copy(getattr(r, name), getattr(r, name + "_out"), r.save.at[i])

    for i in range(len(FETCHED)):
        fetch(i).start()
    meet(place)
    for i in range(4):
        fetch(i).wait()

    moves = [(0, g * width, third, (g,)) for g in range(3)] + [
        (i, 0, shards[i].shape[1] // 2, ()) for i in (1, 2, 3)
    ]
    sibs = (r.qkv_sib, r.out_sib, r.up_sib, r.down_sib)
    wides = (r.qkv_wide, r.out_wide, r.up_wide, r.down_wide)

    def before(m):
        i, start, cols, at = moves[m]
        source = shards[i].at[:, span(start + (1 - c) * cols, cols, 128)]
        target = sibs[i].at[at] if at else sibs[i]
        return remote(source, target, r.pre_send.at[m], r.pre_recv.at[m], place.to_c)

    for m in range(6):
        before(m).start()
    r.small_wide[place.z, place.q, c] = jnp.zeros((8, 128), jnp.float32)
    for i in range(8):
        vector = getattr(r, "vector%d" % i)
        r.small_wide[place.z, place.q, c, i : i + 1, 0 : vector.shape[0]] = vector[...].reshape(1, -1)

    def gather(j, block, column, others):
        lane = 4 if j == 8 else j % 4
        return Gather(
            place, block, column, others, r.send.at[lane], r.gather_recv.at[j], r.gather_z.at[j]
        )

    every = slice(None)
    pieces = []
    for s in range(3):
        cols = lambda side, s=s: span(side * third + 128 * s, 128, 128)
        pieces.append(
            gather(
                s,
                lambda zz, q, cols=cols: r.qkv_wide.at[:, zz, q, :, cols(c)],
                lambda q, cols=cols: r.qkv_wide.at[:, :, q, :, cols(c)],
                lambda cols=cols: r.qkv_wide.at[:, :, :, :, cols(1 - c)],
            )
        )
    cuts = (
        (1, 0, 48, 0, 384),
        (2, 0, 48, 0, 768),
        (2, 0, 48, 768, 768),
        (3, 0, 96, 0, 384),
        (3, 96, 96, 0, 384),
    )
    for j, (i, row, rows, col, cols) in enumerate(cuts):
        half = shards[i].shape[1] // 2

        def at(side, row=row, rows=rows, col=col, cols=cols, half=half):
            return (pl.ds(row, rows), span(side * half + col, cols, 128))

        pieces.append(
            gather(
                3 + j,
                lambda zz, q, i=i, at=at: wides[i].at[(zz, q) + at(c)],
                lambda q, i=i, at=at: wides[i].at[(every, q) + at(c)],
                lambda i=i, at=at: wides[i].at[(every, every) + at(1 - c)],
            )
        )
    pieces.append(
        gather(
            8,
            lambda zz, q: r.small_wide.at[zz, q, c],
            lambda q: r.small_wide.at[:, q, c],
            lambda: r.small_wide.at[:, :, 1 - c],
        )
    )

    def form(i):
        for m, (weight, start, cols, at) in enumerate(moves):
            if weight == i:
                before(m).wait_recv()
                mine = shards[i][:, span(start + c * cols, cols, 128)]
                theirs = sibs[i][at] if at else sibs[i][...]
                wides[i][at + (place.z, place.q, every, span(c * cols, cols, 128))] = jnp.concatenate(
                    [jnp.where(c == 0, mine, theirs), jnp.where(c == 0, theirs, mine)], axis=0
                ).astype(jnp.bfloat16)

    def prepare():
        for i in range(4, len(FETCHED)):
            fetch(i).wait()
        fill_present(r.present, r.mask)
        r.sums[...] = jnp.zeros_like(r.sums)
        r.owner[...] = owners(width)
        r.vec[...] = jnp.zeros_like(r.vec)
        r.small_part[...] = jnp.zeros_like(r.small_part)

    def unpack():
        for zz in range(4):
            rows = r.small_wide[zz].reshape(64, 128).astype(jnp.bfloat16)
            for start, size, m in segments(width):
                lanes = slice(start, start + size)
                picked = dot(rows, selection(size, m))
                total = r.vec[:, lanes]
                for d in range(8):
                    total = total + jnp.where(
                        r.owner[:, lanes] == zz * 8 + d, picked[d * 8 : d * 8 + 8], 0.0
                    )
                r.vec[:, lanes] = total
        for s in range(3):
            r.bias[s] = jnp.zeros((8, 6 * 128), jnp.float32)
            for e in range(2):
                at = 128 * s + third * e
                r.bias[s, 0:1, 128 * e : 128 * e + 128] = r.vec[2:3, width + at : width + at + 128]
                r.bias[s, 0:1, 512 + 128 * e : 640 + 128 * e] = r.vec[
                    2:3, 2 * width + at : 2 * width + at + 128
                ]

    def first_norm(t):
        rows = span(t * 128, 128, 128)
        normed, _ = unit(r.tokens[rows, :].astype(jnp.float32))
        value = normed * r.vec[0:1, 0:width] + r.vec[1:2, 0:width]
        r.normed[rows, :] = value.astype(jnp.bfloat16)
        r.turned_one[:, rows] = value.T.astype(jnp.bfloat16)

    def mask_grad(t):
        rows = span(t * 128, 128, 128)
        low = (r.present[rows, 0:1] * r.out_grad[rows, :].astype(jnp.float32)).astype(jnp.bfloat16)
        r.grad_low[rows, :] = low
        r.sums[7:8, 0:width] += jnp.sum(low.astype(jnp.float32), axis=0, keepdims=True)

    def heads(i):
        s, e = i // 2, i % 2

        @pl.when(e == 0)
        def _():
            weights = [
                r.qkv_wide[g, :, :, :, span(half * third + s * 128, 128, 128)].reshape(width, 128)
                for g in range(3)
                for half in range(2)
            ]
            value = dot(r.normed[...], jnp.concatenate(weights, axis=1)) + r.bias[s, 0:1, :]
            value = value.astype(jnp.bfloat16)
            for g in range(3):
                for half in range(2):
                    at = (2 * g + half) * 128
                    r.joined[s + 3 * half, g] = value[:, at : at + 128]

        hp = s + 3 * e
        cols = span(hp * 128, 128, 128)
        query, key, value = r.joined[hp, 0], r.joined[hp, 1], r.joined[hp, 2].T
        live = r.present[:, 0:1] > 0.5
        mixed = []
        for e in range(2):
            scores = dot_nt(head_only(key, e), query) * SCORE_SCALE
            scores = jnp.where(live, scores, -jnp.inf)
            largest = jnp.max(scores, axis=0, keepdims=True)
            expo = jnp.exp2(scores - largest)
            totals = jnp.sum(expo, axis=0, keepdims=True)
            probs = (expo * (1.0 / totals)).astype(jnp.bfloat16)
            mixed.append(dot(value[HEAD * e : HEAD * (e + 1)], probs))
            r.logsum[hp, e : e + 1, :] = largest + jnp.log2(totals)
        both = jnp.concatenate(mixed, axis=0)
        r.mixed_turned[cols, :] = both.astype(jnp.bfloat16)
        r.mixed[:, cols] = both.T.astype(jnp.bfloat16)

    def attention():
        r.middle[...] = dot(r.mixed[...], r.out_wide[...].reshape(width, width))

    def second_norm(t):
        rows = span(t * 128, 128, 128)
        present = r.present[rows, 0:1]
        middle = r.tokens[rows, :].astype(jnp.float32) + present * (
            r.middle[rows, :] + r.vec[3:4, 0:width]
        )
        r.middle[rows, :] = middle
        normed, _ = unit(middle)
        value = normed * r.vec[4:5, 0:width] + r.vec[5:6, 0:width]
        r.normed[rows, :] = value.astype(jnp.bfloat16)
        r.turned_two[:, rows] = value.T.astype(jnp.bfloat16)

    def slope_out(t, slot):
        return pltpu.make_async_copy(r.slope.at[slot], r.slope_far.at[t], r.slope_send.at[slot])

    def slope_in(t, slot):
        return pltpu.make_async_copy(r.slope_far.at[t], r.slope.at[slot], r.slope_recv.at[slot])

    def expand(t, u):
        slot = u % 2

        @pl.when(u >= 2)
        def _():
            slope_out(t, slot).wait()

        cols = span(t * TILE, TILE, 128)
        value = (
            dot(r.normed[...], r.up_wide[:, :, :, cols].reshape(width, TILE))
            + r.vec[6:7, span(3 * width + t * TILE, TILE, 128)]
        )
        cumulative = 0.5 * (1.0 + lax.erf(value * (1.0 / math.sqrt(2.0))))
        r.act[:, cols] = (value * cumulative).astype(jnp.bfloat16)
        r.slope[slot] = cumulative + value * jnp.exp(-0.5 * value * value) * (
            1.0 / math.sqrt(2.0 * math.pi)
        )
        slope_out(t, slot).start()

    def down_grad(t):
        cols = span(t * TILE, TILE, 128)
        grad = dot_tn(r.act[:, cols], r.grad_low[...]).astype(jnp.bfloat16)
        r.down_part[t] = grad.reshape(4, TILE // 4, width)

    low_tile = lambda u: 2 * u
    high_tile = lambda u: 2 * u + 1

    def scatter(j, block, column, whole):
        bufs = [getattr(r, "piece%d_%d" % (j, b)) for b in range(5)]
        lane = 4 if j == 8 else j % 4
        return Scatter(
            place, block, column, whole, bufs, r.send.at[lane], r.scatter_recv.at[j]
        )

    sums = []
    for s in range(2):
        rows = pl.ds(96 * s, 96)
        sums.append(
            scatter(
                s,
                lambda zz, q, rows=rows: r.down_total.at[zz, q, rows],
                lambda q, rows=rows: r.down_total.at[:, q, rows],
                lambda rows=rows: r.down_total.at[:, :, rows],
            )
        )
    for s in range(2):
        sums.append(
            scatter(
                2 + s,
                lambda zz, q, s=s: r.up_total.at[s, zz, q],
                lambda q, s=s: r.up_total.at[s, :, q],
                lambda s=s: r.up_total.at[s],
            )
        )
    sums.append(
        scatter(
            4,
            lambda zz, q: r.out_total.at[zz, q],
            lambda q: r.out_total.at[:, q],
            lambda: r.out_total,
        )
    )
    for s in range(3):
        sums.append(
            scatter(
                5 + s,
                lambda zz, q, s=s: r.qkv_total.at[s, zz, q],
                lambda q, s=s: r.qkv_total.at[s, :, q],
                lambda s=s: r.qkv_total.at[s],
            )
        )
    sums.append(SmallScatter(place, r.small_total, r.small_got, r.send.at[4], r.scatter_recv.at[8]))

    def up_part(side, s):
        cols = span(side * (hidden // 2) + 768 * s, 768, 128)
        return dot(r.turned_two[...], r.act[:, cols]).reshape(4, 4, 48, 768)

    def out_part(side):
        cols = span(side * third, third, 128)
        return dot(r.mixed_turned[...], r.normed[:, cols]).reshape(4, 4, 48, third)

    def qkv_part(side, s):
        hp = side * 3 + s
        grads = jnp.concatenate([r.joined[hp, g] for g in range(3)], axis=1)
        return dot(r.turned_one[...], grads)

    def other_part(p):
        if p in (2, 3):
            r.down_wide[:, :, 48 * (p - 2) : 48 * (p - 1), :] = up_part(1 - c, p - 2).astype(
                jnp.bfloat16
            )
        elif p == 4:
            r.down_wide[:, :, 96:144, 0:384] = out_part(1 - c).astype(jnp.bfloat16)
        else:
            value = qkv_part(1 - c, p - 5).astype(jnp.bfloat16)
            for g in range(3):
                r.down_part[:, :, 48 * g : 48 * g + 48, 128 * (p - 5) : 128 * (p - 4)] = value[
                    :, 128 * g : 128 * g + 128
                ].reshape(4, 4, 48, 128)

    def given(p):
        if p < 2:
            rows, cols = pl.ds(96 * p, 96), span((1 - c) * 384, 384, 128)
            return lambda q: r.down_part.at[:, q, rows, cols]
        if p < 4:
            return lambda q: r.down_wide.at[:, q, pl.ds(48 * (p - 2), 48)]
        if p == 4:
            return lambda q: r.down_wide.at[:, q, pl.ds(96, 48), pl.ds(0, 384)]
        if p < 8:
            return lambda q: r.down_part.at[:, q, pl.ds(0, 144), pl.ds(128 * (p - 5), 128)]
        return lambda: r.small_part.at[:, :, 1 - c]

    def wide_sum(total, value):
        total[...] = (total[...].astype(jnp.float32) + value).astype(total.dtype)

    def own_part(p):
        sums[p].arrive()
        if p < 2:
            rows = pl.ds(96 * p, 96)
            mine = r.down_part[:, :, rows, span(c * 384, 384, 128)].astype(jnp.float32)
            wide_sum(r.down_total.at[:, :, rows], mine)
        elif p < 4:
            wide_sum(r.up_total.at[p - 2], up_part(c, p - 2))
        elif p == 4:
            wide_sum(r.out_total, out_part(c))
        elif p < 8:
            value = qkv_part(c, p - 5)
            for g in range(3):
                wide_sum(
                    r.qkv_total.at[p - 5, :, :, pl.ds(48 * g, 48)],
                    value[:, 128 * g : 128 * g + 128].reshape(4, 4, 48, 128),
                )
        else:
            r.small_total[...] += r.small_part[:, :, c]

    def narrow(t):
        slot = t % 2

        @pl.when(t == 0)
        def _():
            slope_in(0, 0).start()
            r.acc[...] = jnp.zeros_like(r.acc)

        slope_in(t, slot).wait()

        @pl.when(t + 1 < tiles)
        def _():
            slope_in(t + 1, 1 - slot).start()

        cols = span(t * TILE, TILE, 128)
        weights = r.down_wide[t].reshape(TILE, width)
        r.acc[...] += dot(r.act[:, cols], weights)
        grad = (dot_nt(r.grad_low[...], weights) * r.slope[slot]).astype(jnp.bfloat16)
        r.act[:, cols] = grad
        r.sums[6:7, span(3 * width + t * TILE, TILE, 128)] = jnp.sum(
            grad.astype(jnp.float32), axis=0, keepdims=True
        )

    def drain_slope():
        for slot in range(2):
            slope_out(0, slot).wait()

    def finish_output(t):
        rows = span(t * 128, 128, 128)
        r.output[rows, :] = (
            r.middle[rows, :]
            + r.present[rows, 0:1] * (r.acc[rows, :] + r.vec[7:8, 0:width])
        ).astype(jnp.bfloat16)

        @pl.when(t == tokens // 128 - 1)
        def _():
            store(4).start()

    def up_back():
        r.acc[...] = dot_nt(r.act[...], r.up_wide[...].reshape(width, hidden))

    def norm_back(up, normed, factor, index):
        r.sums[index : index + 1, 0:width] += jnp.sum(up * normed, axis=0, keepdims=True)
        r.sums[index + 1 : index + 2, 0:width] += jnp.sum(up, axis=0, keepdims=True)
        scaled = up * r.vec[index : index + 1, 0:width]
        return factor * (
            scaled
            - jnp.mean(scaled, axis=1, keepdims=True)
            - normed * jnp.mean(scaled * normed, axis=1, keepdims=True)
        )

    def second_back(t):
        rows = span(t * 128, 128, 128)
        normed, factor = unit(r.middle[rows, :])
        grad = r.out_grad[rows, :].astype(jnp.float32) + norm_back(
            r.acc[rows, :], normed, factor, 4
        )
        r.middle[rows, :] = grad
        low = (r.present[rows, 0:1] * grad).astype(jnp.bfloat16)
        r.normed[rows, :] = low
        r.sums[3:4, 0:width] += jnp.sum(low.astype(jnp.float32), axis=0, keepdims=True)

    def out_back():
        r.mixed[...] = dot_nt(r.normed[...], r.out_wide[...].reshape(width, width)).astype(
            jnp.bfloat16
        )

    def heads_back(s):
        pair_back(s)
        pair_back(s + 3)

    def pair_back(hp):
        cols = span(hp * 128, 128, 128)
        query, key, value = r.joined[hp, 0], r.joined[hp, 1], r.joined[hp, 2]
        grad = r.mixed[:, cols]
        turned = key.T
        live = r.present[:, 0:1] > 0.5
        value_grad = jnp.zeros((tokens, 128), jnp.float32)
        key_grad = jnp.zeros((tokens, 128), jnp.float32)
        query_grad = []
        for e in range(2):
            scores = dot_nt(head_only(key, e), query) * SCORE_SCALE
            scores = jnp.where(live, scores, -jnp.inf)
            probs = jnp.exp2(scores - r.logsum[hp, e : e + 1, :])
            back = dot_nt(head_only(value, e), grad)
            inner = jnp.sum(probs * back, axis=0, keepdims=True)
            score_grad = (probs * (back - inner)).astype(jnp.bfloat16)
            value_grad = value_grad + dot(probs.astype(jnp.bfloat16), head_only(grad, e))
            key_grad = key_grad + dot(score_grad, head_only(query, e))
            query_grad.append(dot(turned[HEAD * e : HEAD * (e + 1)], score_grad))
        scale = 1.0 / math.sqrt(HEAD)
        query_low = (jnp.concatenate(query_grad, axis=0).T * scale).astype(jnp.bfloat16)
        value_low = value_grad.astype(jnp.bfloat16)
        r.joined[hp, 0] = query_low
        r.joined[hp, 1] = (key_grad * scale).astype(jnp.bfloat16)
        r.joined[hp, 2] = value_low
        r.sums[2:3, span(width + hp * 128, 128, 128)] = jnp.sum(
            query_low.astype(jnp.float32), axis=0, keepdims=True
        )
        r.sums[2:3, span(2 * width + hp * 128, 128, 128)] = jnp.sum(
            value_low.astype(jnp.float32), axis=0, keepdims=True
        )

    def qkv_back():
        total = jnp.zeros((tokens, width), jnp.float32)
        for g in range(3):
            grads = jnp.concatenate([r.joined[hp, g] for hp in range(6)], axis=1)
            total = total + dot_nt(grads, r.qkv_wide[g].reshape(width, width))
        r.acc[...] = total

    def first_back(t):
        rows = span(t * 128, 128, 128)
        normed, factor = unit(r.tokens[rows, :].astype(jnp.float32))
        part = norm_back(r.acc[rows, :], normed, factor, 0)
        r.input_grad[rows, :] = (r.middle[rows, :] + part).astype(jnp.bfloat16)

        @pl.when(t == tokens // 128 - 1)
        def _():
            store(5).start()

    def pack(index):
        start, size, m = segments(width)[index]
        row = (None, 2, 6)[index]
        lanes = slice(start, start + size)
        chosen = selection(size, m)
        for zz in range(4):
            left = r.sums[:, lanes] if row is None else r.sums[row : row + 1, lanes]
            tile = 0.0
            for _ in range(2):
                part = left.astype(jnp.bfloat16).astype(jnp.float32)
                left = left - part
                rows = jnp.concatenate(
                    [jnp.where(r.owner[:, lanes] == zz * 8 + d, part, 0.0) for d in range(8)], axis=0
                ).astype(jnp.bfloat16)
                tile = tile + dot_nt(rows, chosen)
            if row is None:
                r.small_part[zz] += tile.reshape(4, 2, 8, 128)
            else:
                for d in range(8):
                    r.small_part[zz, d // 2, d % 2, row : row + 1, :] += tile[d : d + 1, :]

    results = (r.qkv_result, r.out_result, r.up_result, r.down_result)
    finals = (r.qkv_final, r.out_final, r.up_final, r.down_final)

    def swap(m, side):
        i, start, cols, at = moves[m]
        rows = results[i].shape[0]
        return remote(
            finals[i].at[at + (span((1 - c) * rows, rows, 8),)],
            results[i].at[:, span(start + side * cols, cols, 128)],
            r.end_send.at[m],
            r.end_recv.at[m],
            place.to_c,
        )

    def close(i):
        for m, (weight, start, cols, at) in enumerate(moves):
            if weight == i:
                rows = results[i].shape[0]
                swap(m, c).start()
                results[i][:, span(start + c * cols, cols, 128)] = finals[i][
                    at + (span(c * rows, rows, 8),)
                ]

    def settle(i):
        for m, move in enumerate(moves):
            if move[0] == i:
                swap(m, 1 - c).wait_recv()
        store(i).start()

    def last(p):
        value = sums[p].last()
        if p < 2:
            r.down_final[96 * p : 96 * p + 96, :] = value
        elif p < 4:
            r.up_final[:, 768 * (p - 2) : 768 * (p - 1)] = value
        elif p == 4:
            r.out_final[...] = value
        elif p < 8:
            for g in range(3):
                r.qkv_final[g, :, 128 * (p - 5) : 128 * (p - 4)] = value[48 * g : 48 * g + 48]
        else:
            r.small_result[...] = value
            store(6).start()

    def start_xy(j):
        if 4 <= j < 8:
            pieces[j - 4].finish()
        pieces[j].start_xy()

    def give(p):
        before_it = pieces[8] if p == 8 else (sums[p - 4] if p >= 4 else pieces[p + 4])
        before_it.finish()
        if 2 <= p < 8:
            other_part(p)
        sums[p].give(given(p))

    steps = {(UNPACK,): unpack, (ATTENTION,): attention, (DRAIN,): drain_slope}
    steps.update({(UP_BACK,): up_back, (OUT_BACK,): out_back, (QKV_BACK,): qkv_back})
    steps[PREPARE,] = prepare
    for i in range(3):
        steps[PACK, i] = functools.partial(pack, i)
    for i in range(4):
        steps[FORM, i] = functools.partial(form, i)
        steps[CLOSE, i] = functools.partial(close, i)
        steps[SETTLE, i] = functools.partial(settle, i)
    for j in range(9):
        piece, total = pieces[j], sums[j]
        steps[START_Z, j] = piece.start_z
        steps[START_XY, j] = functools.partial(start_xy, j)
        steps[OWN_COLUMN, j] = piece.own_column
        steps[XY_COLUMNS, j] = piece.xy_columns
        steps[D_GOT, j] = piece.d
        steps[C_GOT, j] = piece.c
        steps[GIVE, j] = functools.partial(give, j)
        steps[OWN_PART, j] = functools.partial(own_part, j)
        steps[LAST, j] = functools.partial(last, j)
        for k in range(4):
            steps[Z_GOT, j, k] = functools.partial(piece.z, k)
            steps[XY_GOT, j, k] = functools.partial(piece.xy, k)
    for j, total in enumerate(sums[:8]):
        steps[DIAGONAL, j] = total.diagonal
        for k in range(4):
            steps[CROSS, j, k] = functools.partial(total.cross, k)
            steps[SPREAD, j, k] = functools.partial(total.spread, k)
    steps[SMALL_PLANE,] = sums[8].plane
    steps[SMALL_SPREAD,] = sums[8].spread
    loops = {
        FIRST_NORM: first_norm,
        MASK_GRAD: mask_grad,
        HEADS: heads,
        SECOND_NORM: second_norm,
        EXPAND_LOW: lambda u: expand(low_tile(u), u),
        EXPAND_HIGH: lambda u: expand(high_tile(u), u + 2),
        DOWN_LOW: lambda u: down_grad(low_tile(u)),
        DOWN_HIGH: lambda u: down_grad(high_tile(u)),
        NARROW: narrow,
        FINISH: finish_output,
        SECOND_BACK: second_back,
        HEADS_BACK: heads_back,
        FIRST_BACK: first_back,
    }
    follow(SEQUENCE, steps, loops)
    for m in range(6):
        before(m).wait_send()
        swap(m, c).wait_send()
    for piece in pieces + sums:
        piece.finish()
    for i in range(len(STORED)):
        store(i).wait()


def layer_call(tokens, band_mask, out_grad, shards, smalls):
    bf16, f32 = jnp.bfloat16, jnp.float32
    count, width = tokens.shape
    shapes = [s.shape for s in shards]
    hidden = shapes[2][1]
    tiles = hidden // TILE
    vmem = pl.BlockSpec(memory_space=pltpu.VMEM)
    anywhere = pl.BlockSpec(memory_space=pl.ANY)
    fetched = dict(zip(FETCHED, (*shards, tokens, out_grad)))
    inputs = [(name + "_in", array, anywhere) for name, array in fetched.items()]
    inputs += triples(mask=(band_mask, pl.BlockSpec(memory_space=pltpu.SMEM)))
    inputs += [("vector%d" % i, v, vmem) for i, v in enumerate(smalls)]
    stored = list(zip(STORED, shapes + [(count, width)] * 2 + [(8, 128)]))
    kinds = [f32] * 4 + [bf16] * 2 + [f32]
    outs = triples(slope_far=((tiles, count, TILE), f32)) + [
        (name + "_out", shape, kind) for (name, shape), kind in zip(stored, kinds)
    ]
    tails = (
        [((96, 384), bf16)] * 2
        + [((48, 768), bf16)] * 2
        + [((48, 384), bf16)]
        + [((144, 128), bf16)] * 3
    )
    scratch = [(name, pltpu.VMEM(a.shape, a.dtype)) for name, a in fetched.items()]
    scratch += [(name, pltpu.VMEM(shape, kind)) for (name, shape), kind in zip(stored, kinds)]
    for j, (tail, kind) in enumerate(tails):
        for b, one in enumerate(scatter_buffers(tail, kind)):
            scratch.append(("piece%d_%d" % (j, b), one))
    scratch += pairs_of(
        qkv_wide=pltpu.VMEM((3, 4, 4, 48, width), bf16),
        out_wide=pltpu.VMEM((4, 4, 48, width), bf16),
        up_wide=pltpu.VMEM((4, 4, 48, hidden), bf16),
        down_wide=pltpu.VMEM((4, 4, 192, width), bf16),
        qkv_sib=pltpu.VMEM((3, 24, width // 2), f32),
        out_sib=pltpu.VMEM((24, width // 2), f32),
        up_sib=pltpu.VMEM((24, hidden // 2), f32),
        down_sib=pltpu.VMEM((96, width // 2), f32),
        qkv_final=pltpu.VMEM((3, 48, width // 2), f32),
        out_final=pltpu.VMEM((48, width // 2), f32),
        up_final=pltpu.VMEM((48, hidden // 2), f32),
        down_final=pltpu.VMEM((192, width // 2), f32),
        small_wide=pltpu.VMEM((4, 4, 2, 8, 128), f32),
        small_part=pltpu.VMEM((4, 4, 2, 8, 128), f32),
        small_total=pltpu.VMEM((4, 4, 8, 128), f32),
        small_got=pltpu.VMEM((4, 4, 8, 128), f32),
        down_part=pltpu.VMEM((4, 4, 192, width), bf16),
        down_total=pltpu.VMEM((4, 4, 192, 384), bf16),
        up_total=pltpu.VMEM((2, 4, 4, 48, 768), bf16),
        out_total=pltpu.VMEM((4, 4, 48, 384), bf16),
        qkv_total=pltpu.VMEM((3, 4, 4, 144, 128), bf16),
        present=pltpu.VMEM((count, 128), f32),
        vec=pltpu.VMEM((8, 7 * width), f32),
        sums=pltpu.VMEM((8, 7 * width), f32),
        bias=pltpu.VMEM((3, 8, width), f32),
        owner=pltpu.VMEM((1, 7 * width), f32),
        logsum=pltpu.VMEM((width // 128, 8, count), f32),
        turned_one=pltpu.VMEM((width, count), bf16),
        turned_two=pltpu.VMEM((width, count), bf16),
        mixed_turned=pltpu.VMEM((width, count), bf16),
        normed=pltpu.VMEM((count, width), bf16),
        mixed=pltpu.VMEM((count, width), bf16),
        grad_low=pltpu.VMEM((count, width), bf16),
        joined=pltpu.VMEM((width // 128, 3, count, 128), bf16),
        middle=pltpu.VMEM((count, width), f32),
        acc=pltpu.VMEM((count, width), f32),
        act=pltpu.VMEM((count, hidden), bf16),
        slope=pltpu.VMEM((2, count, TILE), f32),
        send=pltpu.SemaphoreType.DMA((5, Piece.COUNT)),
        gather_z=pltpu.SemaphoreType.DMA((9, 3)),
        gather_recv=pltpu.SemaphoreType.DMA((9, 13)),
        scatter_recv=pltpu.SemaphoreType.DMA((9, 14)),
        pre_send=pltpu.SemaphoreType.DMA((6,)),
        pre_recv=pltpu.SemaphoreType.DMA((6,)),
        end_send=pltpu.SemaphoreType.DMA((6,)),
        end_recv=pltpu.SemaphoreType.DMA((6,)),
        load=pltpu.SemaphoreType.DMA((len(FETCHED),)),
        save=pltpu.SemaphoreType.DMA((len(STORED),)),
        slope_send=pltpu.SemaphoreType.DMA((2,)),
        slope_recv=pltpu.SemaphoreType.DMA((2,)),
    )
    names = (
        [name for name, _, _ in inputs] + [name for name, _, _ in outs] + [name for name, _ in scratch]
    )
    results = pl.pallas_call(
        functools.partial(layer_kernel, names),
        out_shape=tuple(jax.ShapeDtypeStruct(shape, kind) for _, shape, kind in outs),
        in_specs=[spec for _, _, spec in inputs],
        out_specs=(anywhere,) * len(outs),
        scratch_shapes=[kind for _, kind in scratch],
        compiler_params=pltpu.CompilerParams(
            collective_id=0, has_side_effects=True, vmem_limit_bytes=VMEM_BYTES
        ),
        name="layer",
    )(*[array for _, array, _ in inputs])
    qkv, out, up, down, output, input_grad, small = results[1:]
    return output, input_grad, qkv, out, up, down, small


def deliver_kernel(count, *refs):
    sources, tile = refs[:count], refs[count]
    targets = refs[count + 1 : 2 * count + 1]
    for source, target in zip(sources, targets):
        target[...] = source[...]
    for i, vector in enumerate(refs[2 * count + 1 :]):
        vector[...] = tile[i, 0 : vector.shape[0]]


def deliver(whole, tile, sizes):
    count = len(whole)
    vmem = pl.BlockSpec(memory_space=pltpu.VMEM)
    return pl.pallas_call(
        functools.partial(deliver_kernel, count),
        out_shape=[jax.ShapeDtypeStruct(a.shape, a.dtype) for a in whole]
        + [jax.ShapeDtypeStruct((m,), jnp.float32) for m in sizes],
        in_specs=[vmem] * (count + 1),
        out_specs=[vmem] * (count + len(sizes)),
        compiler_params=pltpu.CompilerParams(vmem_limit_bytes=VMEM_BYTES),
        name="deliver",
    )(*whole, tile)


def body(
    tokens,
    band_mask,
    out_grad,
    norm1_gain,
    norm1_shift,
    qkv_weight,
    qv_bias,
    out_weight,
    out_bias,
    norm2_gain,
    norm2_shift,
    up_weight,
    up_bias,
    down_weight,
    down_bias,
):
    smalls = (norm1_gain, norm1_shift, qv_bias, out_bias, norm2_gain, norm2_shift, up_bias, down_bias)
    shards = (qkv_weight, out_weight, up_weight, down_weight)
    *whole, tile = layer_call(tokens, band_mask, out_grad, shards, smalls)
    output, input_grad, qkv, out, up, down, *grads = deliver(
        whole, tile, [v.shape[0] for v in smalls]
    )
    return (
        output,
        input_grad,
        grads[0],
        grads[1],
        qkv,
        grads[2],
        out,
        grads[3],
        grads[4],
        grads[5],
        up,
        grads[6],
        down,
        grads[7],
    )


def solution(mesh):
    rows, flat = P(AXES, None), P(AXES)
    params = (flat, flat, rows, flat, rows, flat, flat, flat, rows, flat, rows, flat)
    fitted = tuple(mesh.shape[axis] for axis in AXES) == (8, 4)
    return jax.shard_map(
        body if fitted else body_plain,
        mesh=mesh,
        in_specs=(rows, rows, rows) + params,
        out_specs=(rows, rows) + params,
        check_vma=False,
    )
```

```python
import functools
import math

import jax
import jax.numpy as jnp
from jax import lax
from jax.experimental import pallas as pl
from jax.experimental.pallas import tpu as pltpu
from jax.sharding import PartitionSpec as P

HEAD = 64
HEAD_GROUP = 4
QBLOCK = 512


NORM_EPSILON = 1e-05
VMEM_BYTES = 62 << 20
AXES = ("wide", "narrow")


def normalize(values, gain, shift):
    centre = jnp.mean(values, axis=1, keepdims=True)
    centred = values - centre
    factor = lax.rsqrt(jnp.mean(centred * centred, axis=1, keepdims=True) + NORM_EPSILON)
    normed = centred * factor
    return (normed * gain + shift, normed, factor)


def normalize_back(upstream, normed, factor, gain):
    gain_grad = jnp.sum(upstream * normed, axis=0)
    shift_grad = jnp.sum(upstream, axis=0)
    scaled = upstream * gain
    inner = (
        scaled
        - jnp.mean(scaled, axis=1, keepdims=True)
        - normed * jnp.mean(scaled * normed, axis=1, keepdims=True)
    )
    return (factor * inner, gain_grad, shift_grad)


def gelu_slope(values):
    cumulative = 0.5 * (1.0 + lax.erf(values * (1.0 / math.sqrt(2.0))))
    return cumulative + values * jnp.exp(-0.5 * values * values) * (1.0 / math.sqrt(2.0 * math.pi))


def to_groups(matrix, count):
    return matrix.reshape(matrix.shape[0], count, -1).transpose(1, 0, 2)


def from_groups(stacked):
    return stacked.transpose(1, 0, 2).reshape(stacked.shape[1], -1)


def attend_forward(query_cols, key_cols, value_cols, key_live):
    row_count, span_cols = key_cols.shape
    head_width = span_cols // HEAD_GROUP
    scaling = 1.0 / math.sqrt(head_width)
    key_rows = key_cols.reshape(row_count, HEAD_GROUP, head_width)
    value_rows = value_cols.reshape(row_count, HEAD_GROUP, head_width)
    query_blocks = query_cols.reshape(row_count // QBLOCK, QBLOCK, HEAD_GROUP, head_width)

    def one_block(query_rows):
        scores = (
            jnp.einsum("qhd,khd->hqk", query_rows, key_rows, preferred_element_type=jnp.float32)
            * scaling
        )
        scores = jnp.where(key_live[None, None, :], scores, -jnp.inf)
        largest = jnp.max(scores, axis=2, keepdims=True)
        expo = jnp.exp(scores - largest)
        totals = jnp.sum(expo, axis=2, keepdims=True)
        weights_low = (expo / totals).astype(jnp.bfloat16)
        mixture = jnp.einsum(
            "hqk,khd->qhd", weights_low, value_rows, preferred_element_type=jnp.float32
        )
        return (mixture.reshape(QBLOCK, span_cols), largest[:, :, 0] + jnp.log(totals[:, :, 0]))

    mixture, logsum = lax.map(one_block, query_blocks)
    return (mixture.reshape(row_count, span_cols), logsum)


def attend_backward(query_cols, key_cols, value_cols, grad_cols, logsum, key_live):
    row_count, span_cols = key_cols.shape
    head_width = span_cols // HEAD_GROUP
    scaling = 1.0 / math.sqrt(head_width)
    key_rows = key_cols.reshape(row_count, HEAD_GROUP, head_width)
    value_rows = value_cols.reshape(row_count, HEAD_GROUP, head_width)
    query_blocks = query_cols.reshape(row_count // QBLOCK, QBLOCK, HEAD_GROUP, head_width)
    grad_blocks = grad_cols.reshape(row_count // QBLOCK, QBLOCK, HEAD_GROUP, head_width)

    def one_block(carry, items):
        key_acc, value_acc = carry
        query_rows, grad_rows, block_logsum = items
        scores = (
            jnp.einsum("qhd,khd->hqk", query_rows, key_rows, preferred_element_type=jnp.float32)
            * scaling
        )
        scores = jnp.where(key_live[None, None, :], scores, -jnp.inf)
        probs = jnp.exp(scores - block_logsum[:, :, None])
        value_acc = value_acc + jnp.einsum(
            "hqk,qhd->khd",
            probs.astype(jnp.bfloat16),
            grad_rows,
            preferred_element_type=jnp.float32,
        )
        prob_grad = jnp.einsum(
            "qhd,khd->hqk", grad_rows, value_rows, preferred_element_type=jnp.float32
        )
        inner = jnp.sum(probs * prob_grad, axis=2, keepdims=True)
        score_grad = (probs * (prob_grad - inner)).astype(jnp.bfloat16)
        query_grad = (
            jnp.einsum("hqk,khd->qhd", score_grad, key_rows, preferred_element_type=jnp.float32)
            * scaling
        )
        key_acc = (
            key_acc
            + jnp.einsum("hqk,qhd->khd", score_grad, query_rows, preferred_element_type=jnp.float32)
            * scaling
        )
        return ((key_acc, value_acc), query_grad.reshape(QBLOCK, span_cols))

    empty = jnp.zeros((row_count, HEAD_GROUP, head_width), jnp.float32)
    (key_grad, value_grad), query_grad = lax.scan(
        one_block, (empty, empty), (query_blocks, grad_blocks, logsum)
    )
    return (
        query_grad.reshape(row_count, span_cols),
        key_grad.reshape(row_count, span_cols),
        value_grad.reshape(row_count, span_cols),
    )


def gathered(shard):
    return lax.all_gather(shard.astype(jnp.bfloat16), AXES, axis=0, tiled=True)


def scattered(part):
    return lax.psum_scatter(part, AXES, scatter_dimension=0, tiled=True)


def body_plain(
    tokens,
    band_mask,
    out_grad,
    norm1_gain,
    norm1_shift,
    qkv_weight,
    qv_bias,
    out_weight,
    out_bias,
    norm2_gain,
    norm2_shift,
    up_weight,
    up_bias,
    down_weight,
    down_bias,
):
    row_count, width = tokens.shape
    group_count = width // (HEAD_GROUP * HEAD)
    present = jnp.repeat(band_mask[0].astype(jnp.float32), row_count // band_mask.shape[1])
    key_live = present > 0.5
    column_mask = present[:, None]
    gain_one, shift_one, w_qkv, b_qv, w_out, b_out = (
        gathered(norm1_gain),
        gathered(norm1_shift),
        gathered(qkv_weight),
        gathered(qv_bias),
        gathered(out_weight),
        gathered(out_bias),
    )
    inputs = tokens.astype(jnp.float32)
    normed_one, unit_one, factor_one = normalize(
        inputs, gain_one.astype(jnp.float32), shift_one.astype(jnp.float32)
    )
    normed_one = normed_one.astype(jnp.bfloat16)
    bias_wide = b_qv.astype(jnp.float32)
    bias_full = jnp.concatenate(
        [bias_wide[:width], jnp.zeros((width,), jnp.float32), bias_wide[width:]]
    )
    joined = (jnp.dot(normed_one, w_qkv, preferred_element_type=jnp.float32) + bias_full).astype(
        jnp.bfloat16
    )
    query_groups = to_groups(joined[:, :width], group_count)
    key_groups = to_groups(joined[:, width : 2 * width], group_count)
    value_groups = to_groups(joined[:, 2 * width :], group_count)
    mixture, logsum = lax.map(
        lambda items: attend_forward(items[0], items[1], items[2], key_live),
        (query_groups, key_groups, value_groups),
    )
    mixture = from_groups(mixture).astype(jnp.bfloat16)
    attention = jnp.dot(mixture, w_out, preferred_element_type=jnp.float32) + b_out.astype(
        jnp.float32
    )
    middle = inputs + column_mask * attention
    gain_two, shift_two, w_up, b_up, w_down, b_down = (
        gathered(norm2_gain),
        gathered(norm2_shift),
        gathered(up_weight),
        gathered(up_bias),
        gathered(down_weight),
        gathered(down_bias),
    )
    normed_two, unit_two, factor_two = normalize(
        middle, gain_two.astype(jnp.float32), shift_two.astype(jnp.float32)
    )
    normed_two = normed_two.astype(jnp.bfloat16)
    hidden = jnp.dot(normed_two, w_up, preferred_element_type=jnp.float32) + b_up.astype(
        jnp.float32
    )
    active = jax.nn.gelu(hidden, approximate=False).astype(jnp.bfloat16)
    branch = jnp.dot(active, w_down, preferred_element_type=jnp.float32) + b_down.astype(
        jnp.float32
    )
    output = (middle + column_mask * branch).astype(jnp.bfloat16)
    upstream = out_grad.astype(jnp.float32)
    branch_grad = (column_mask * upstream).astype(jnp.bfloat16)
    down_weight_grad = jnp.einsum(
        "tf,td->fd", active, branch_grad, preferred_element_type=jnp.float32
    )
    down_bias_grad = jnp.sum(branch_grad.astype(jnp.float32), axis=0)
    active_grad = jnp.einsum(
        "td,fd->tf", branch_grad, w_down, preferred_element_type=jnp.float32
    )
    hidden_grad = (active_grad * gelu_slope(hidden)).astype(jnp.bfloat16)
    up_weight_grad = jnp.einsum(
        "td,tf->df", normed_two, hidden_grad, preferred_element_type=jnp.float32
    )
    up_bias_grad = jnp.sum(hidden_grad.astype(jnp.float32), axis=0)
    normed_two_grad = jnp.einsum(
        "tf,df->td", hidden_grad, w_up, preferred_element_type=jnp.float32
    )
    middle_part, norm2_gain_grad, norm2_shift_grad = normalize_back(
        normed_two_grad, unit_two, factor_two, gain_two.astype(jnp.float32)
    )
    (
        norm2_gain_grad,
        norm2_shift_grad,
        up_weight_grad,
        up_bias_grad,
        down_weight_grad,
        down_bias_grad,
    ) = (
        scattered(norm2_gain_grad),
        scattered(norm2_shift_grad),
        scattered(up_weight_grad),
        scattered(up_bias_grad),
        scattered(down_weight_grad),
        scattered(down_bias_grad),
    )
    middle_grad = upstream + middle_part
    attention_grad = (column_mask * middle_grad).astype(jnp.bfloat16)
    out_weight_grad = jnp.einsum(
        "te,td->ed", mixture, attention_grad, preferred_element_type=jnp.float32
    )
    out_bias_grad = jnp.sum(attention_grad.astype(jnp.float32), axis=0)
    mixture_grad = jnp.einsum(
        "td,ed->te", attention_grad, w_out, preferred_element_type=jnp.float32
    ).astype(jnp.bfloat16)
    grad_groups = to_groups(mixture_grad, group_count)
    query_grad, key_grad, value_grad = lax.map(
        lambda items: attend_backward(items[0], items[1], items[2], items[3], items[4], key_live),
        (query_groups, key_groups, value_groups, grad_groups, logsum),
    )
    query_grad = from_groups(query_grad).astype(jnp.bfloat16)
    key_grad = from_groups(key_grad).astype(jnp.bfloat16)
    value_grad = from_groups(value_grad).astype(jnp.bfloat16)
    joined_grad = jnp.concatenate([query_grad, key_grad, value_grad], axis=1)
    qkv_weight_grad = jnp.einsum(
        "td,tc->dc", normed_one, joined_grad, preferred_element_type=jnp.float32
    )
    qv_bias_grad = jnp.concatenate(
        [
            jnp.sum(query_grad.astype(jnp.float32), axis=0),
            jnp.sum(value_grad.astype(jnp.float32), axis=0),
        ]
    )
    normed_one_grad = jnp.einsum(
        "tc,dc->td", joined_grad, w_qkv, preferred_element_type=jnp.float32
    )
    input_part, norm1_gain_grad, norm1_shift_grad = normalize_back(
        normed_one_grad, unit_one, factor_one, gain_one.astype(jnp.float32)
    )
    input_grad = (middle_grad + input_part).astype(jnp.bfloat16)
    (
        norm1_gain_grad,
        norm1_shift_grad,
        qkv_weight_grad,
        qv_bias_grad,
        out_weight_grad,
        out_bias_grad,
    ) = (
        scattered(norm1_gain_grad),
        scattered(norm1_shift_grad),
        scattered(qkv_weight_grad),
        scattered(qv_bias_grad),
        scattered(out_weight_grad),
        scattered(out_bias_grad),
    )
    return (
        output,
        input_grad,
        norm1_gain_grad,
        norm1_shift_grad,
        qkv_weight_grad,
        qv_bias_grad,
        out_weight_grad,
        out_bias_grad,
        norm2_gain_grad,
        norm2_shift_grad,
        up_weight_grad,
        up_bias_grad,
        down_weight_grad,
        down_bias_grad,
    )


MESH_ID = pl.DeviceIdType.MESH
VIA_X = (0, 2)
VIA_Y = (1, 3)
ORDER = (1, 3, 2)
SCORE_SCALE = math.log2(math.e) / math.sqrt(HEAD)
TILE = 768


class Place:
    def __init__(self):
        wide = lax.axis_index("wide")
        narrow = lax.axis_index("narrow")
        z, y = wide // 2, wide % 2
        x, c = narrow // 2, narrow % 2
        self.z, self.c = z, c
        self.zs = (z, z + 1 - 2 * (z % 2), (z + 2) % 4, 3 - z)
        self.q = y * 2 + x
        self.qx = y * 2 + (1 - x)
        self.qy = (1 - y) * 2 + x
        self.qd = (1 - y) * 2 + (1 - x)
        self.to_z = tuple((zz * 2 + y, x * 2 + c) for zz in self.zs)
        self.to_x = (z * 2 + y, (1 - x) * 2 + c)
        self.to_y = (z * 2 + 1 - y, x * 2 + c)
        self.to_c = (z * 2 + y, x * 2 + 1 - c)
        self.to_d = (z * 2 + 1 - y, (1 - x) * 2 + c)


def span(start, size, step):
    return pl.ds(pl.multiple_of(start, step), size)


def meet(place):
    barrier = pltpu.get_barrier_semaphore()
    peers = place.to_z[1:] + (place.to_x, place.to_y, place.to_d, place.to_c)
    for peer in peers:
        pl.semaphore_signal(barrier, inc=1, device_id=peer, device_id_type=MESH_ID)
    pl.semaphore_wait(barrier, len(peers))


def remote(source, target, send, recv, peer):
    return pltpu.make_async_remote_copy(
        src_ref=source,
        dst_ref=target,
        send_sem=send,
        recv_sem=recv,
        device_id=peer,
        device_id_type=MESH_ID,
    )


class Piece:
    COUNT = 19

    def __init__(self, place, send, recv, slots, z_send=None):
        self.p = place
        self.send, self.recv, self.slots, self.z_send = send, recv, slots, z_send
        self.sent = []

    def pair(self, index):
        own = self.send if index >= 3 or self.z_send is None else self.z_send
        return own.at[index], self.recv.at[self.slots[index]]

    def go(self, source, target, index, peer):
        remote(source(), target(), *self.pair(index), peer).start()
        self.sent.append((source, target, index, peer))

    def got(self, target, index, peer):
        remote(target, target, *self.pair(index), peer).wait_recv()

    def finish(self):
        for source, target, index, peer in self.sent:
            remote(source(), target(), *self.pair(index), peer).wait_send()
        self.sent = []


class Gather(Piece):
    SLOTS = (0, 1, 2, 3, 4, 5, 6, 11, 11, 7, 8, 9, 10, 11, 11, 12, 12, 12, 12)

    def __init__(self, place, block, column, others, send, recv, z_send):
        super().__init__(place, send, recv, self.SLOTS, z_send)
        self.block, self.column, self.others = block, column, others

    def own(self):
        return self.block(self.p.z, self.p.q)

    def start_z(self):
        p = self.p
        for k in ORDER:
            self.go(self.own, self.own, k - 1, p.to_z[k])

    def start_xy(self):
        p = self.p
        self.go(self.own, self.own, 3, p.to_x)
        self.go(self.own, self.own, 9, p.to_y)

    def z(self, k):
        p = self.p
        here = lambda: self.block(p.zs[k], p.q)
        self.got(here(), k - 1, p.to_z[k])
        self.go(here, here, 3 + k, p.to_x)
        self.go(here, here, 9 + k, p.to_y)

    def share(self, index, q):
        column = lambda: self.column(q)
        self.go(column, column, index, self.p.to_c)

    def own_column(self):
        self.share(15, self.p.q)

    def xy(self, k):
        p = self.p
        from_x = lambda: self.block(p.zs[k], p.qx)
        self.got(from_x(), 3 + k, p.to_x)
        if k in VIA_X:
            self.go(from_x, from_x, 13 + VIA_X.index(k), p.to_y)
        from_y = lambda: self.block(p.zs[k], p.qy)
        self.got(from_y(), 9 + k, p.to_y)
        if k in VIA_Y:
            self.go(from_y, from_y, 7 + VIA_Y.index(k), p.to_x)

    def xy_columns(self):
        self.share(16, self.p.qx)
        self.share(17, self.p.qy)

    def d(self):
        p = self.p
        self.got(self.column(p.qd), 13, p.to_y)
        self.share(18, p.qd)

    def c(self):
        self.got(self.others(), 15, self.p.to_c)


class Scatter(Piece):
    SLOTS = (13, 13, 13, 5, 6, 7, 8, 1, 2, 9, 10, 11, 12, 3, 4, 0, 0, 0, 0)

    def __init__(self, place, block, column, whole, bufs, send, recv):
        super().__init__(place, send, recv, self.SLOTS)
        self.block, self.column, self.whole = block, column, whole
        self.dx, self.dy, self.xr, self.yr, self.zr = bufs

    def add(self, target, other):
        target[...] = (target[...].astype(jnp.float32) + other[...].astype(jnp.float32)).astype(
            target.dtype
        )

    def give(self, other):
        p = self.p
        for i, q in enumerate((p.qd, p.qx, p.qy, p.q)):
            self.go(lambda q=q: other(q), lambda q=q: self.column(q), 15 + i, p.to_c)

    def arrive(self):
        self.got(self.whole(), 15, self.p.to_c)

    def diagonal(self):
        p = self.p
        for i in range(2):
            self.go(
                lambda i=i: self.block(p.zs[VIA_X[i]], p.qd), lambda i=i: self.dx.at[i], 7 + i, p.to_x
            )
            self.go(
                lambda i=i: self.block(p.zs[VIA_Y[i]], p.qd), lambda i=i: self.dy.at[i], 13 + i, p.to_y
            )

    def cross(self, k):
        p = self.p
        on_x = lambda: self.block(p.zs[k], p.qx)
        on_y = lambda: self.block(p.zs[k], p.qy)
        if k in VIA_Y:
            i = VIA_Y.index(k)
            self.go(on_y, lambda: self.yr.at[k], 9 + k, p.to_y)
            self.got(self.dy.at[i], 13 + i, p.to_y)
            self.add(on_x(), self.dy.at[i])
            self.go(on_x, lambda: self.xr.at[k], 3 + k, p.to_x)
        else:
            i = VIA_X.index(k)
            self.go(on_x, lambda: self.xr.at[k], 3 + k, p.to_x)
            self.got(self.dx.at[i], 7 + i, p.to_x)
            self.add(on_y(), self.dx.at[i])
            self.go(on_y, lambda: self.yr.at[k], 9 + k, p.to_y)

    def plane(self, k):
        p = self.p
        self.got(self.xr.at[k], 3 + k, p.to_x)
        self.got(self.yr.at[k], 9 + k, p.to_y)
        here = self.block(p.zs[k], p.q)
        return here, (
            here[...].astype(jnp.float32)
            + self.xr[k].astype(jnp.float32)
            + self.yr[k].astype(jnp.float32)
        )

    def spread(self, k):
        p = self.p
        here, value = self.plane(k)
        here[...] = value.astype(here.dtype)
        self.go(lambda: self.block(p.zs[k], p.q), lambda: self.zr.at[k - 1], k - 1, p.to_z[k])

    def last(self):
        _, value = self.plane(0)
        self.got(self.zr, 0, self.p.to_z[1])
        for k in ORDER:
            value = value + self.zr[k - 1].astype(jnp.float32)
        return value


class SmallScatter(Piece):
    SLOTS = (4, 4, 4, 1, 2, 3, 0, 0, 0, 0, 0, 0, 0, 0, 0, 0, 0, 0, 0)

    def __init__(self, place, total, arrived, send, recv):
        super().__init__(place, send, recv, self.SLOTS)
        self.total, self.arrived = total, arrived

    def give(self, other):
        self.go(other, lambda: self.total, 15, self.p.to_c)

    def arrive(self):
        self.got(self.total, 15, self.p.to_c)

    def neighbours(self):
        p = self.p
        return ((0, p.qx, p.to_x), (1, p.qy, p.to_y), (2, p.qd, p.to_d))

    def plane(self):
        for i, q, peer in self.neighbours():
            self.go(lambda q=q: self.total.at[:, q], lambda i=i: self.arrived.at[i], 3 + i, peer)

    def spread(self):
        p = self.p
        value = self.total[:, p.q]
        for i, _, peer in self.neighbours():
            self.got(self.arrived.at[i], 3 + i, peer)
            value = value + self.arrived[i]
        self.total[:, p.q] = value
        for k in ORDER:
            self.go(
                lambda k=k: self.total.at[p.zs[k], p.q],
                lambda k=k: self.arrived.at[3, k],
                k - 1,
                p.to_z[k],
            )

    def last(self):
        p = self.p
        self.got(self.arrived.at[3, pl.ds(1, 3)], 0, p.to_z[1])
        value = self.total[p.z, p.q]
        for k in ORDER:
            value = value + self.arrived[3, k]
        return value


def scatter_buffers(tail, kind):
    return [
        pltpu.VMEM((2,) + tail, kind),
        pltpu.VMEM((2,) + tail, kind),
        pltpu.VMEM((4,) + tail, kind),
        pltpu.VMEM((4,) + tail, kind),
        pltpu.VMEM((3,) + tail, kind),
    ]


MATRICES = ("qkv", "out", "up", "down")


def triples(**named):
    return [(name, one, two) for name, (one, two) in named.items()]


def pairs_of(**named):
    return list(named.items())


class Named:
    def __init__(self, names, refs):
        assert len(names) == len(refs)
        self.__dict__.update(zip(names, refs))


def loop(first, count, compute, slots=()):
    def step(i, carry):
        compute(i)
        for j, steps in enumerate(slots):
            if steps:

                @pl.when(i == first + j)
                def _(steps=steps):
                    for one in steps:
                        one()

        return carry

    lax.fori_loop(first, first + count, step, 0)


def follow(order, steps, loops):
    at = 0
    while at < len(order):
        kind = order[at][0]
        if kind not in loops:
            steps[order[at]]()
            at += 1
            continue
        first, slots, end = order[at][1], [[]], at + 1
        held = []
        while end < len(order) and (order[end][0] not in loops or order[end][0] == kind):
            if order[end][0] == kind:
                assert order[end][1] == first + len(slots)
                slots[-1] += held
                held = []
                slots.append([])
                at = end
            else:
                held.append(steps[order[end]])
            end += 1
        if len(slots) == 1:
            loops[kind](jnp.int32(first))
        else:
            loop(first, len(slots), loops[kind], slots)
        at += 1


def dot(left, right):
    return jnp.dot(left, right, preferred_element_type=jnp.float32)


def dot_nt(left, right):
    return lax.dot_general(
        left, right, (((1,), (1,)), ((), ())), preferred_element_type=jnp.float32
    )


def dot_tn(left, right):
    return lax.dot_general(
        left, right, (((0,), (0,)), ((), ())), preferred_element_type=jnp.float32
    )


def head_only(values, e):
    lane = lax.broadcasted_iota(jnp.int32, values.shape, 1)
    return jnp.where((lane // HEAD) == e, values, jnp.zeros_like(values))


def fill_present(present, mask):
    groups = mask.shape[1]
    rows = present.shape[0] // groups
    for g in range(groups):
        present[g * rows : (g + 1) * rows, :] = jnp.full(
            (rows, 128), mask[0, g].astype(jnp.float32)
        )


def segments(width):
    return ((0, width, width // 32), (width, 2 * width, width // 16), (3 * width, 4 * width, width // 8))


def selection(size, m):
    lane = lax.broadcasted_iota(jnp.int32, (1, size), 1).astype(jnp.float32)
    rest = lane - m * jnp.floor((lane + 0.5) * (1.0 / m))
    row = lax.broadcasted_iota(jnp.int32, (128, size), 0).astype(jnp.float32)
    return jnp.where(row == rest, 1.0, 0.0).astype(jnp.bfloat16)


def owners(width):
    parts = []
    for _, size, m in segments(width):
        lane = lax.broadcasted_iota(jnp.int32, (1, size), 1).astype(jnp.float32)
        parts.append(jnp.floor((lane + 0.5) * (1.0 / m)))
    return jnp.concatenate(parts, axis=1)


def unit(values):
    centred = values - jnp.mean(values, axis=1, keepdims=True)
    factor = lax.rsqrt(jnp.mean(centred * centred, axis=1, keepdims=True) + NORM_EPSILON)
    return centred * factor, factor


(
    ATTENTION,
    CLOSE,
    CROSS,
    C_GOT,
    DIAGONAL,
    DOWN_HIGH,
    DOWN_LOW,
    DRAIN,
    D_GOT,
    EXPAND_HIGH,
    EXPAND_LOW,
    FINISH,
    FIRST_BACK,
    FIRST_NORM,
    FORM,
    GIVE,
    HEADS,
    HEADS_BACK,
    LAST,
    MASK_GRAD,
    NARROW,
    OUT_BACK,
    OWN_COLUMN,
    OWN_PART,
    PACK,
    PLANE_GOT,
    PLANE_START,
    PREPARE,
    QKV_BACK,
    SECOND_BACK,
    SECOND_NORM,
    SETTLE,
    SMALL_PLANE,
    SMALL_SPREAD,
    SPREAD,
    START_XY,
    START_Z,
    UNPACK,
    UP_BACK,
    XY_COLUMNS,
    XY_GOT,
    Z_GOT,
) = range(42)
SEQUENCE = (
    (START_Z, 8),
    (START_XY, 8),
    (FORM, 0),
    (FORM, 1),
    (FORM, 2),
    (FORM, 3),
    (START_Z, 0),
    (START_Z, 1),
    (START_Z, 2),
    (START_XY, 0),
    (Z_GOT, 8, 1),
    (Z_GOT, 8, 3),
    (Z_GOT, 8, 2),
    (START_Z, 3),
    (START_Z, 4),
    (START_Z, 5),
    (START_Z, 6),
    (START_Z, 7),
    (START_XY, 3),
    (XY_GOT, 8, 0),
    (OWN_COLUMN, 8),
    (START_XY, 1),
    (START_XY, 2),
    (PREPARE,),
    (MASK_GRAD, 0),
    (MASK_GRAD, 1),
    (MASK_GRAD, 2),
    (XY_GOT, 8, 1),
    (XY_GOT, 0, 0),
    (XY_GOT, 8, 2),
    (XY_GOT, 8, 3),
    (XY_COLUMNS, 8),
    (MASK_GRAD, 3),
    (Z_GOT, 0, 1),
    (XY_GOT, 3, 0),
    (Z_GOT, 0, 2),
    (XY_GOT, 1, 0),
    (Z_GOT, 0, 3),
    (OWN_COLUMN, 0),
    (XY_GOT, 2, 0),
    (D_GOT, 8),
    (Z_GOT, 1, 1),
    (XY_GOT, 0, 1),
    (C_GOT, 8),
    (UNPACK,),
    (Z_GOT, 1, 3),
    (XY_GOT, 0, 2),
    (Z_GOT, 1, 2),
    (OWN_COLUMN, 1),
    (FIRST_NORM, 0),
    (FIRST_NORM, 1),
    (FIRST_NORM, 2),
    (Z_GOT, 2, 1),
    (XY_GOT, 0, 3),
    (XY_COLUMNS, 0),
    (FIRST_NORM, 3),
    (Z_GOT, 2, 2),
    (Z_GOT, 2, 3),
    (OWN_COLUMN, 2),
    (XY_GOT, 1, 1),
    (XY_GOT, 1, 3),
    (Z_GOT, 3, 1),
    (XY_GOT, 1, 2),
    (XY_COLUMNS, 1),
    (D_GOT, 0),
    (START_XY, 4),
    (Z_GOT, 3, 2),
    (Z_GOT, 3, 3),
    (OWN_COLUMN, 3),
    (XY_GOT, 2, 1),
    (XY_GOT, 2, 2),
    (XY_GOT, 2, 3),
    (XY_COLUMNS, 2),
    (C_GOT, 0),
    (HEADS, 0),
    (D_GOT, 1),
    (XY_GOT, 3, 1),
    (START_XY, 5),
    (HEADS, 1),
    (XY_GOT, 4, 0),
    (Z_GOT, 4, 1),
    (XY_GOT, 3, 2),
    (C_GOT, 1),
    (HEADS, 2),
    (Z_GOT, 4, 2),
    (D_GOT, 2),
    (Z_GOT, 4, 3),
    (OWN_COLUMN, 4),
    (XY_GOT, 3, 3),
    (XY_COLUMNS, 3),
    (HEADS, 3),
    (XY_GOT, 5, 0),
    (C_GOT, 2),
    (HEADS, 4),
    (Z_GOT, 5, 1),
    (XY_GOT, 4, 1),
    (Z_GOT, 5, 2),
    (HEADS, 5),
    (Z_GOT, 5, 3),
    (XY_GOT, 4, 2),
    (OWN_COLUMN, 5),
    (XY_GOT, 4, 3),
    (XY_COLUMNS, 4),
    (D_GOT, 3),
    (XY_GOT, 5, 1),
    (C_GOT, 3),
    (ATTENTION,),
    (START_XY, 7),
    (SECOND_NORM, 0),
    (SECOND_NORM, 1),
    (XY_GOT, 5, 2),
    (SECOND_NORM, 2),
    (SECOND_NORM, 3),
    (XY_GOT, 5, 3),
    (XY_COLUMNS, 5),
    (D_GOT, 4),
    (START_XY, 6),
    (Z_GOT, 6, 3),
    (Z_GOT, 6, 2),
    (Z_GOT, 6, 1),
    (OWN_COLUMN, 6),
    (Z_GOT, 7, 1),
    (C_GOT, 4),
    (EXPAND_LOW, 0),
    (Z_GOT, 7, 2),
    (Z_GOT, 7, 3),
    (XY_GOT, 7, 0),
    (OWN_COLUMN, 7),
    (EXPAND_LOW, 1),
    (D_GOT, 5),
    (DOWN_LOW, 0),
    (DOWN_LOW, 1),
    (XY_GOT, 6, 0),
    (C_GOT, 5),
    (EXPAND_HIGH, 0),
    (XY_GOT, 6, 3),
    (EXPAND_HIGH, 1),
    (XY_GOT, 6, 2),
    (DRAIN,),
    (DOWN_HIGH, 0),
    (XY_GOT, 6, 1),
    (XY_COLUMNS, 6),
    (DOWN_HIGH, 1),
    (GIVE, 0),
    (GIVE, 1),
    (XY_GOT, 7, 1),
    (XY_GOT, 7, 2),
    (XY_GOT, 7, 3),
    (XY_COLUMNS, 7),
    (OWN_PART, 0),
    (DIAGONAL, 0),
    (D_GOT, 6),
    (OWN_PART, 1),
    (DIAGONAL, 1),
    (CROSS, 0, 1),
    (D_GOT, 7),
    (C_GOT, 6),
    (CROSS, 0, 3),
    (CROSS, 0, 0),
    (C_GOT, 7),
    (NARROW, 0),
    (CROSS, 1, 1),
    (NARROW, 1),
    (CROSS, 0, 2),
    (CROSS, 1, 0),
    (CROSS, 1, 3),
    (NARROW, 2),
    (CROSS, 1, 2),
    (NARROW, 3),
    (SPREAD, 0, 1),
    (GIVE, 2),
    (SPREAD, 0, 3),
    (GIVE, 3),
    (PACK, 2),
    (SPREAD, 1, 1),
    (OWN_PART, 2),
    (DIAGONAL, 2),
    (SPREAD, 0, 2),
    (FINISH, 0),
    (FINISH, 1),
    (FINISH, 2),
    (FINISH, 3),
    (UP_BACK,),
    (SPREAD, 1, 3),
    (SECOND_BACK, 0),
    (SECOND_BACK, 1),
    (SPREAD, 1, 2),
    (CROSS, 2, 1),
    (SECOND_BACK, 2),
    (OWN_PART, 3),
    (CROSS, 2, 0),
    (CROSS, 2, 3),
    (DIAGONAL, 3),
    (LAST, 0),
    (SECOND_BACK, 3),
    (GIVE, 4),
    (CROSS, 2, 2),
    (OUT_BACK,),
    (SPREAD, 2, 1),
    (HEADS_BACK, 0),
    (SPREAD, 2, 3),
    (GIVE, 5),
    (LAST, 1),
    (CROSS, 3, 0),
    (CROSS, 3, 1),
    (CLOSE, 3),
    (OWN_PART, 4),
    (DIAGONAL, 4),
    (HEADS_BACK, 1),
    (CROSS, 3, 3),
    (CROSS, 3, 2),
    (SETTLE, 3),
    (SPREAD, 2, 2),
    (OWN_PART, 5),
    (DIAGONAL, 5),
    (SPREAD, 3, 1),
    (GIVE, 6),
    (CROSS, 4, 0),
    (CROSS, 4, 1),
    (HEADS_BACK, 2),
    (SPREAD, 3, 2),
    (CROSS, 4, 2),
    (SPREAD, 3, 3),
    (CROSS, 4, 3),
    (CROSS, 5, 0),
    (LAST, 2),
    (CROSS, 5, 1),
    (GIVE, 7),
    (CROSS, 5, 3),
    (CROSS, 5, 2),
    (OWN_PART, 6),
    (DIAGONAL, 6),
    (PACK, 1),
    (SPREAD, 4, 1),
    (SPREAD, 4, 2),
    (OWN_PART, 7),
    (SPREAD, 4, 3),
    (DIAGONAL, 7),
    (QKV_BACK,),
    (SPREAD, 5, 1),
    (SPREAD, 5, 3),
    (FIRST_BACK, 0),
    (SPREAD, 5, 2),
    (FIRST_BACK, 1),
    (CROSS, 6, 0),
    (CROSS, 6, 1),
    (FIRST_BACK, 2),
    (FIRST_BACK, 3),
    (CROSS, 6, 3),
    (CROSS, 6, 2),
    (PACK, 0),
    (GIVE, 8),
    (CROSS, 7, 0),
    (CROSS, 7, 1),
    (LAST, 3),
    (CROSS, 7, 3),
    (CLOSE, 2),
    (CROSS, 7, 2),
    (OWN_PART, 8),
    (SMALL_PLANE,),
    (SPREAD, 6, 1),
    (LAST, 4),
    (CLOSE, 1),
    (SPREAD, 6, 3),
    (SETTLE, 2),
    (SPREAD, 6, 2),
    (SETTLE, 1),
    (SPREAD, 7, 1),
    (LAST, 5),
    (SPREAD, 7, 3),
    (SPREAD, 7, 2),
    (SMALL_SPREAD,),
    (LAST, 6),
    (LAST, 7),
    (CLOSE, 0),
    (LAST, 8),
    (SETTLE, 0),
)


FETCHED = ("qkv_shard", "out_shard", "up_shard", "down_shard", "tokens", "out_grad")
STORED = ("qkv_result", "out_result", "up_result", "down_result") + (
    ("output", "input_grad", "small_result")
)


def layer_kernel(names, *refs):
    r = Named(names, refs)
    place = Place()
    c = place.c
    tokens, width = r.tokens.shape
    hidden = r.act.shape[1]
    third = width // 2
    tiles = hidden // TILE
    shards = (r.qkv_shard, r.out_shard, r.up_shard, r.down_shard)

    def fetch(i):
        name = FETCHED[i]
        return pltpu.make_async_copy(getattr(r, name + "_in"), getattr(r, name), r.load.at[i])

    def store(i):
        name = STORED[i]
        return pltpu.make_async_copy(getattr(r, name), getattr(r, name + "_out"), r.save.at[i])

    for i in range(len(FETCHED)):
        fetch(i).start()
    meet(place)
    for i in range(4):
        fetch(i).wait()

    moves = [(0, g * width, third, (g,)) for g in range(3)] + [
        (i, 0, shards[i].shape[1] // 2, ()) for i in (1, 2, 3)
    ]
    sibs = (r.qkv_sib, r.out_sib, r.up_sib, r.down_sib)
    wides = (r.qkv_wide, r.out_wide, r.up_wide, r.down_wide)

    def before(m):
        i, start, cols, at = moves[m]
        source = shards[i].at[:, span(start + (1 - c) * cols, cols, 128)]
        target = sibs[i].at[at] if at else sibs[i]
        return remote(source, target, r.pre_send.at[m], r.pre_recv.at[m], place.to_c)

    for m in range(6):
        before(m).start()
    r.small_wide[place.z, place.q, c] = jnp.zeros((8, 128), jnp.float32)
    for i in range(8):
        vector = getattr(r, "vector%d" % i)
        r.small_wide[place.z, place.q, c, i : i + 1, 0 : vector.shape[0]] = vector[...].reshape(1, -1)

    def gather(j, block, column, others):
        lane = 4 if j == 8 else j % 4
        return Gather(
            place, block, column, others, r.send.at[lane], r.gather_recv.at[j], r.gather_z.at[j]
        )

    every = slice(None)
    pieces = []
    for s in range(3):
        cols = lambda side, s=s: span(side * third + 128 * s, 128, 128)
        pieces.append(
            gather(
                s,
                lambda zz, q, cols=cols: r.qkv_wide.at[:, zz, q, :, cols(c)],
                lambda q, cols=cols: r.qkv_wide.at[:, :, q, :, cols(c)],
                lambda cols=cols: r.qkv_wide.at[:, :, :, :, cols(1 - c)],
            )
        )
    cuts = (
        (1, 0, 48, 0, 384),
        (2, 0, 48, 0, 768),
        (2, 0, 48, 768, 768),
        (3, 0, 96, 0, 384),
        (3, 96, 96, 0, 384),
    )
    for j, (i, row, rows, col, cols) in enumerate(cuts):
        half = shards[i].shape[1] // 2

        def at(side, row=row, rows=rows, col=col, cols=cols, half=half):
            return (pl.ds(row, rows), span(side * half + col, cols, 128))

        pieces.append(
            gather(
                3 + j,
                lambda zz, q, i=i, at=at: wides[i].at[(zz, q) + at(c)],
                lambda q, i=i, at=at: wides[i].at[(every, q) + at(c)],
                lambda i=i, at=at: wides[i].at[(every, every) + at(1 - c)],
            )
        )
    pieces.append(
        gather(
            8,
            lambda zz, q: r.small_wide.at[zz, q, c],
            lambda q: r.small_wide.at[:, q, c],
            lambda: r.small_wide.at[:, :, 1 - c],
        )
    )

    def form(i):
        for m, (weight, start, cols, at) in enumerate(moves):
            if weight == i:
                before(m).wait_recv()
                mine = shards[i][:, span(start + c * cols, cols, 128)]
                theirs = sibs[i][at] if at else sibs[i][...]
                wides[i][at + (place.z, place.q, every, span(c * cols, cols, 128))] = jnp.concatenate(
                    [jnp.where(c == 0, mine, theirs), jnp.where(c == 0, theirs, mine)], axis=0
                ).astype(jnp.bfloat16)

    def prepare():
        for i in range(4, len(FETCHED)):
            fetch(i).wait()
        fill_present(r.present, r.mask)
        r.sums[...] = jnp.zeros_like(r.sums)
        r.owner[...] = owners(width)
        r.vec[...] = jnp.zeros_like(r.vec)
        r.small_part[...] = jnp.zeros_like(r.small_part)

    def unpack():
        for zz in range(4):
            rows = r.small_wide[zz].reshape(64, 128).astype(jnp.bfloat16)
            for start, size, m in segments(width):
                lanes = slice(start, start + size)
                picked = dot(rows, selection(size, m))
                total = r.vec[:, lanes]
                for d in range(8):
                    total = total + jnp.where(
                        r.owner[:, lanes] == zz * 8 + d, picked[d * 8 : d * 8 + 8], 0.0
                    )
                r.vec[:, lanes] = total
        for s in range(3):
            r.bias[s] = jnp.zeros((8, 6 * 128), jnp.float32)
            for e in range(2):
                at = 128 * s + third * e
                r.bias[s, 0:1, 128 * e : 128 * e + 128] = r.vec[2:3, width + at : width + at + 128]
                r.bias[s, 0:1, 512 + 128 * e : 640 + 128 * e] = r.vec[
                    2:3, 2 * width + at : 2 * width + at + 128
                ]

    def first_norm(t):
        rows = span(t * 128, 128, 128)
        normed, _ = unit(r.tokens[rows, :].astype(jnp.float32))
        value = normed * r.vec[0:1, 0:width] + r.vec[1:2, 0:width]
        r.normed[rows, :] = value.astype(jnp.bfloat16)
        r.turned_one[:, rows] = value.T.astype(jnp.bfloat16)

    def mask_grad(t):
        rows = span(t * 128, 128, 128)
        low = (r.present[rows, 0:1] * r.out_grad[rows, :].astype(jnp.float32)).astype(jnp.bfloat16)
        r.grad_low[rows, :] = low
        r.sums[7:8, 0:width] += jnp.sum(low.astype(jnp.float32), axis=0, keepdims=True)

    def heads(i):
        s, e = i // 2, i % 2

        @pl.when(e == 0)
        def _():
            weights = [
                r.qkv_wide[g, :, :, :, span(half * third + s * 128, 128, 128)].reshape(width, 128)
                for g in range(3)
                for half in range(2)
            ]
            value = dot(r.normed[...], jnp.concatenate(weights, axis=1)) + r.bias[s, 0:1, :]
            value = value.astype(jnp.bfloat16)
            for g in range(3):
                for half in range(2):
                    at = (2 * g + half) * 128
                    r.joined[s + 3 * half, g] = value[:, at : at + 128]

        hp = s + 3 * e
        cols = span(hp * 128, 128, 128)
        query, key, value = r.joined[hp, 0], r.joined[hp, 1], r.joined[hp, 2].T
        live = r.present[:, 0:1] > 0.5
        mixed = []
        for e in range(2):
            scores = dot_nt(head_only(key, e), query) * SCORE_SCALE
            scores = jnp.where(live, scores, -jnp.inf)
            largest = jnp.max(scores, axis=0, keepdims=True)
            expo = jnp.exp2(scores - largest)
            totals = jnp.sum(expo, axis=0, keepdims=True)
            probs = (expo * (1.0 / totals)).astype(jnp.bfloat16)
            mixed.append(dot(value[HEAD * e : HEAD * (e + 1)], probs))
            r.logsum[hp, e : e + 1, :] = largest + jnp.log2(totals)
        both = jnp.concatenate(mixed, axis=0)
        r.mixed_turned[cols, :] = both.astype(jnp.bfloat16)
        r.mixed[:, cols] = both.T.astype(jnp.bfloat16)

    def attention():
        r.middle[...] = dot(r.mixed[...], r.out_wide[...].reshape(width, width))

    def second_norm(t):
        rows = span(t * 128, 128, 128)
        present = r.present[rows, 0:1]
        middle = r.tokens[rows, :].astype(jnp.float32) + present * (
            r.middle[rows, :] + r.vec[3:4, 0:width]
        )
        r.middle[rows, :] = middle
        normed, _ = unit(middle)
        value = normed * r.vec[4:5, 0:width] + r.vec[5:6, 0:width]
        r.normed[rows, :] = value.astype(jnp.bfloat16)
        r.turned_two[:, rows] = value.T.astype(jnp.bfloat16)

    def slope_out(t, slot):
        return pltpu.make_async_copy(r.slope.at[slot], r.slope_far.at[t], r.slope_send.at[slot])

    def slope_in(t, slot):
        return pltpu.make_async_copy(r.slope_far.at[t], r.slope.at[slot], r.slope_recv.at[slot])

    def expand(t, u):
        slot = u % 2

        @pl.when(u >= 2)
        def _():
            slope_out(t, slot).wait()

        cols = span(t * TILE, TILE, 128)
        value = (
            dot(r.normed[...], r.up_wide[:, :, :, cols].reshape(width, TILE))
            + r.vec[6:7, span(3 * width + t * TILE, TILE, 128)]
        )
        cumulative = 0.5 * (1.0 + lax.erf(value * (1.0 / math.sqrt(2.0))))
        r.act[:, cols] = (value * cumulative).astype(jnp.bfloat16)
        r.slope[slot] = cumulative + value * jnp.exp(-0.5 * value * value) * (
            1.0 / math.sqrt(2.0 * math.pi)
        )
        slope_out(t, slot).start()

    def down_grad(t):
        cols = span(t * TILE, TILE, 128)
        grad = dot_tn(r.act[:, cols], r.grad_low[...]).astype(jnp.bfloat16)
        r.down_part[t] = grad.reshape(4, TILE // 4, width)

    low_tile = lambda u: 2 * u
    high_tile = lambda u: 2 * u + 1

    def scatter(j, block, column, whole):
        bufs = [getattr(r, "piece%d_%d" % (j, b)) for b in range(5)]
        lane = 4 if j == 8 else j % 4
        return Scatter(
            place, block, column, whole, bufs, r.send.at[lane], r.scatter_recv.at[j]
        )

    sums = []
    for s in range(2):
        rows = pl.ds(96 * s, 96)
        sums.append(
            scatter(
                s,
                lambda zz, q, rows=rows: r.down_total.at[zz, q, rows],
                lambda q, rows=rows: r.down_total.at[:, q, rows],
                lambda rows=rows: r.down_total.at[:, :, rows],
            )
        )
    for s in range(2):
        sums.append(
            scatter(
                2 + s,
                lambda zz, q, s=s: r.up_total.at[s, zz, q],
                lambda q, s=s: r.up_total.at[s, :, q],
                lambda s=s: r.up_total.at[s],
            )
        )
    sums.append(
        scatter(
            4,
            lambda zz, q: r.out_total.at[zz, q],
            lambda q: r.out_total.at[:, q],
            lambda: r.out_total,
        )
    )
    for s in range(3):
        sums.append(
            scatter(
                5 + s,
                lambda zz, q, s=s: r.qkv_total.at[s, zz, q],
                lambda q, s=s: r.qkv_total.at[s, :, q],
                lambda s=s: r.qkv_total.at[s],
            )
        )
    sums.append(SmallScatter(place, r.small_total, r.small_got, r.send.at[4], r.scatter_recv.at[8]))

    def up_part(side, s):
        cols = span(side * (hidden // 2) + 768 * s, 768, 128)
        return dot(r.turned_two[...], r.act[:, cols]).reshape(4, 4, 48, 768)

    def out_part(side):
        cols = span(side * third, third, 128)
        return dot(r.mixed_turned[...], r.normed[:, cols]).reshape(4, 4, 48, third)

    def qkv_part(side, s):
        hp = side * 3 + s
        grads = jnp.concatenate([r.joined[hp, g] for g in range(3)], axis=1)
        return dot(r.turned_one[...], grads)

    def other_part(p):
        if p in (2, 3):
            r.down_wide[:, :, 48 * (p - 2) : 48 * (p - 1), :] = up_part(1 - c, p - 2).astype(
                jnp.bfloat16
            )
        elif p == 4:
            r.down_wide[:, :, 96:144, 0:384] = out_part(1 - c).astype(jnp.bfloat16)
        else:
            value = qkv_part(1 - c, p - 5).astype(jnp.bfloat16)
            for g in range(3):
                r.down_part[:, :, 48 * g : 48 * g + 48, 128 * (p - 5) : 128 * (p - 4)] = value[
                    :, 128 * g : 128 * g + 128
                ].reshape(4, 4, 48, 128)

    def given(p):
        if p < 2:
            rows, cols = pl.ds(96 * p, 96), span((1 - c) * 384, 384, 128)
            return lambda q: r.down_part.at[:, q, rows, cols]
        if p < 4:
            return lambda q: r.down_wide.at[:, q, pl.ds(48 * (p - 2), 48)]
        if p == 4:
            return lambda q: r.down_wide.at[:, q, pl.ds(96, 48), pl.ds(0, 384)]
        if p < 8:
            return lambda q: r.down_part.at[:, q, pl.ds(0, 144), pl.ds(128 * (p - 5), 128)]
        return lambda: r.small_part.at[:, :, 1 - c]

    def wide_sum(total, value):
        total[...] = (total[...].astype(jnp.float32) + value).astype(total.dtype)

    def own_part(p):
        sums[p].arrive()
        if p < 2:
            rows = pl.ds(96 * p, 96)
            mine = r.down_part[:, :, rows, span(c * 384, 384, 128)].astype(jnp.float32)
            wide_sum(r.down_total.at[:, :, rows], mine)
        elif p < 4:
            wide_sum(r.up_total.at[p - 2], up_part(c, p - 2))
        elif p == 4:
            wide_sum(r.out_total, out_part(c))
        elif p < 8:
            value = qkv_part(c, p - 5)
            for g in range(3):
                wide_sum(
                    r.qkv_total.at[p - 5, :, :, pl.ds(48 * g, 48)],
                    value[:, 128 * g : 128 * g + 128].reshape(4, 4, 48, 128),
                )
        else:
            r.small_total[...] += r.small_part[:, :, c]

    def narrow(t):
        slot = t % 2

        @pl.when(t == 0)
        def _():
            slope_in(0, 0).start()
            r.acc[...] = jnp.zeros_like(r.acc)

        slope_in(t, slot).wait()

        @pl.when(t + 1 < tiles)
        def _():
            slope_in(t + 1, 1 - slot).start()

        cols = span(t * TILE, TILE, 128)
        weights = r.down_wide[t].reshape(TILE, width)
        r.acc[...] += dot(r.act[:, cols], weights)
        grad = (dot_nt(r.grad_low[...], weights) * r.slope[slot]).astype(jnp.bfloat16)
        r.act[:, cols] = grad
        r.sums[6:7, span(3 * width + t * TILE, TILE, 128)] = jnp.sum(
            grad.astype(jnp.float32), axis=0, keepdims=True
        )

    def drain_slope():
        for slot in range(2):
            slope_out(0, slot).wait()

    def finish_output(t):
        rows = span(t * 128, 128, 128)
        r.output[rows, :] = (
            r.middle[rows, :]
            + r.present[rows, 0:1] * (r.acc[rows, :] + r.vec[7:8, 0:width])
        ).astype(jnp.bfloat16)

        @pl.when(t == tokens // 128 - 1)
        def _():
            store(4).start()

    def up_back():
        r.acc[...] = dot_nt(r.act[...], r.up_wide[...].reshape(width, hidden))

    def norm_back(up, normed, factor, index):
        r.sums[index : index + 1, 0:width] += jnp.sum(up * normed, axis=0, keepdims=True)
        r.sums[index + 1 : index + 2, 0:width] += jnp.sum(up, axis=0, keepdims=True)
        scaled = up * r.vec[index : index + 1, 0:width]
        return factor * (
            scaled
            - jnp.mean(scaled, axis=1, keepdims=True)
            - normed * jnp.mean(scaled * normed, axis=1, keepdims=True)
        )

    def second_back(t):
        rows = span(t * 128, 128, 128)
        normed, factor = unit(r.middle[rows, :])
        grad = r.out_grad[rows, :].astype(jnp.float32) + norm_back(
            r.acc[rows, :], normed, factor, 4
        )
        r.middle[rows, :] = grad
        low = (r.present[rows, 0:1] * grad).astype(jnp.bfloat16)
        r.normed[rows, :] = low
        r.sums[3:4, 0:width] += jnp.sum(low.astype(jnp.float32), axis=0, keepdims=True)

    def out_back():
        r.mixed[...] = dot_nt(r.normed[...], r.out_wide[...].reshape(width, width)).astype(
            jnp.bfloat16
        )

    def heads_back(s):
        pair_back(s)
        pair_back(s + 3)

    def pair_back(hp):
        cols = span(hp * 128, 128, 128)
        query, key, value = r.joined[hp, 0], r.joined[hp, 1], r.joined[hp, 2]
        grad = r.mixed[:, cols]
        turned = key.T
        live = r.present[:, 0:1] > 0.5
        value_grad = jnp.zeros((tokens, 128), jnp.float32)
        key_grad = jnp.zeros((tokens, 128), jnp.float32)
        query_grad = []
        for e in range(2):
            scores = dot_nt(head_only(key, e), query) * SCORE_SCALE
            scores = jnp.where(live, scores, -jnp.inf)
            probs = jnp.exp2(scores - r.logsum[hp, e : e + 1, :])
            back = dot_nt(head_only(value, e), grad)
            inner = jnp.sum(probs * back, axis=0, keepdims=True)
            score_grad = (probs * (back - inner)).astype(jnp.bfloat16)
            value_grad = value_grad + dot(probs.astype(jnp.bfloat16), head_only(grad, e))
            key_grad = key_grad + dot(score_grad, head_only(query, e))
            query_grad.append(dot(turned[HEAD * e : HEAD * (e + 1)], score_grad))
        scale = 1.0 / math.sqrt(HEAD)
        query_low = (jnp.concatenate(query_grad, axis=0).T * scale).astype(jnp.bfloat16)
        value_low = value_grad.astype(jnp.bfloat16)
        r.joined[hp, 0] = query_low
        r.joined[hp, 1] = (key_grad * scale).astype(jnp.bfloat16)
        r.joined[hp, 2] = value_low
        r.sums[2:3, span(width + hp * 128, 128, 128)] = jnp.sum(
            query_low.astype(jnp.float32), axis=0, keepdims=True
        )
        r.sums[2:3, span(2 * width + hp * 128, 128, 128)] = jnp.sum(
            value_low.astype(jnp.float32), axis=0, keepdims=True
        )

    def qkv_back():
        total = jnp.zeros((tokens, width), jnp.float32)
        for g in range(3):
            grads = jnp.concatenate([r.joined[hp, g] for hp in range(6)], axis=1)
            total = total + dot_nt(grads, r.qkv_wide[g].reshape(width, width))
        r.acc[...] = total

    def first_back(t):
        rows = span(t * 128, 128, 128)
        normed, factor = unit(r.tokens[rows, :].astype(jnp.float32))
        part = norm_back(r.acc[rows, :], normed, factor, 0)
        r.input_grad[rows, :] = (r.middle[rows, :] + part).astype(jnp.bfloat16)

        @pl.when(t == tokens // 128 - 1)
        def _():
            store(5).start()

    def pack(index):
        start, size, m = segments(width)[index]
        row = (None, 2, 6)[index]
        lanes = slice(start, start + size)
        chosen = selection(size, m)
        for zz in range(4):
            left = r.sums[:, lanes] if row is None else r.sums[row : row + 1, lanes]
            tile = 0.0
            for _ in range(2):
                part = left.astype(jnp.bfloat16).astype(jnp.float32)
                left = left - part
                rows = jnp.concatenate(
                    [jnp.where(r.owner[:, lanes] == zz * 8 + d, part, 0.0) for d in range(8)], axis=0
                ).astype(jnp.bfloat16)
                tile = tile + dot_nt(rows, chosen)
            if row is None:
                r.small_part[zz] += tile.reshape(4, 2, 8, 128)
            else:
                for d in range(8):
                    r.small_part[zz, d // 2, d % 2, row : row + 1, :] += tile[d : d + 1, :]

    results = (r.qkv_result, r.out_result, r.up_result, r.down_result)
    finals = (r.qkv_final, r.out_final, r.up_final, r.down_final)

    def swap(m, side):
        i, start, cols, at = moves[m]
        rows = results[i].shape[0]
        return remote(
            finals[i].at[at + (span((1 - c) * rows, rows, 8),)],
            results[i].at[:, span(start + side * cols, cols, 128)],
            r.end_send.at[m],
            r.end_recv.at[m],
            place.to_c,
        )

    def close(i):
        for m, (weight, start, cols, at) in enumerate(moves):
            if weight == i:
                rows = results[i].shape[0]
                swap(m, c).start()
                results[i][:, span(start + c * cols, cols, 128)] = finals[i][
                    at + (span(c * rows, rows, 8),)
                ]

    def settle(i):
        for m, move in enumerate(moves):
            if move[0] == i:
                swap(m, 1 - c).wait_recv()
        store(i).start()

    def last(p):
        value = sums[p].last()
        if p < 2:
            r.down_final[96 * p : 96 * p + 96, :] = value
        elif p < 4:
            r.up_final[:, 768 * (p - 2) : 768 * (p - 1)] = value
        elif p == 4:
            r.out_final[...] = value
        elif p < 8:
            for g in range(3):
                r.qkv_final[g, :, 128 * (p - 5) : 128 * (p - 4)] = value[48 * g : 48 * g + 48]
        else:
            r.small_result[...] = value
            store(6).start()

    def start_xy(j):
        if 4 <= j < 8:
            pieces[j - 4].finish()
        pieces[j].start_xy()

    def give(p):
        before_it = pieces[8] if p == 8 else (sums[p - 4] if p >= 4 else pieces[p + 4])
        before_it.finish()
        if 2 <= p < 8:
            other_part(p)
        sums[p].give(given(p))

    steps = {(UNPACK,): unpack, (ATTENTION,): attention, (DRAIN,): drain_slope}
    steps.update({(UP_BACK,): up_back, (OUT_BACK,): out_back, (QKV_BACK,): qkv_back})
    steps[PREPARE,] = prepare
    for i in range(3):
        steps[PACK, i] = functools.partial(pack, i)
    for i in range(4):
        steps[FORM, i] = functools.partial(form, i)
        steps[CLOSE, i] = functools.partial(close, i)
        steps[SETTLE, i] = functools.partial(settle, i)
    for j in range(9):
        piece, total = pieces[j], sums[j]
        steps[START_Z, j] = piece.start_z
        steps[START_XY, j] = functools.partial(start_xy, j)
        steps[OWN_COLUMN, j] = piece.own_column
        steps[XY_COLUMNS, j] = piece.xy_columns
        steps[D_GOT, j] = piece.d
        steps[C_GOT, j] = piece.c
        steps[GIVE, j] = functools.partial(give, j)
        steps[OWN_PART, j] = functools.partial(own_part, j)
        steps[LAST, j] = functools.partial(last, j)
        for k in range(4):
            steps[Z_GOT, j, k] = functools.partial(piece.z, k)
            steps[XY_GOT, j, k] = functools.partial(piece.xy, k)
    for j, total in enumerate(sums[:8]):
        steps[DIAGONAL, j] = total.diagonal
        for k in range(4):
            steps[CROSS, j, k] = functools.partial(total.cross, k)
            steps[SPREAD, j, k] = functools.partial(total.spread, k)
    steps[SMALL_PLANE,] = sums[8].plane
    steps[SMALL_SPREAD,] = sums[8].spread
    loops = {
        FIRST_NORM: first_norm,
        MASK_GRAD: mask_grad,
        HEADS: heads,
        SECOND_NORM: second_norm,
        EXPAND_LOW: lambda u: expand(low_tile(u), u),
        EXPAND_HIGH: lambda u: expand(high_tile(u), u + 2),
        DOWN_LOW: lambda u: down_grad(low_tile(u)),
        DOWN_HIGH: lambda u: down_grad(high_tile(u)),
        NARROW: narrow,
        FINISH: finish_output,
        SECOND_BACK: second_back,
        HEADS_BACK: heads_back,
        FIRST_BACK: first_back,
    }
    follow(SEQUENCE, steps, loops)
    for m in range(6):
        before(m).wait_send()
        swap(m, c).wait_send()
    for piece in pieces + sums:
        piece.finish()
    for i in range(len(STORED)):
        store(i).wait()


def layer_call(tokens, band_mask, out_grad, shards, smalls):
    bf16, f32 = jnp.bfloat16, jnp.float32
    count, width = tokens.shape
    shapes = [s.shape for s in shards]
    hidden = shapes[2][1]
    tiles = hidden // TILE
    vmem = pl.BlockSpec(memory_space=pltpu.VMEM)
    anywhere = pl.BlockSpec(memory_space=pl.ANY)
    fetched = dict(zip(FETCHED, (*shards, tokens, out_grad)))
    inputs = [(name + "_in", array, anywhere) for name, array in fetched.items()]
    inputs += triples(mask=(band_mask, pl.BlockSpec(memory_space=pltpu.SMEM)))
    inputs += [("vector%d" % i, v, vmem) for i, v in enumerate(smalls)]
    stored = list(zip(STORED, shapes + [(count, width)] * 2 + [(8, 128)]))
    kinds = [f32] * 4 + [bf16] * 2 + [f32]
    outs = triples(slope_far=((tiles, count, TILE), f32)) + [
        (name + "_out", shape, kind) for (name, shape), kind in zip(stored, kinds)
    ]
    tails = (
        [((96, 384), bf16)] * 2
        + [((48, 768), bf16)] * 2
        + [((48, 384), bf16)]
        + [((144, 128), bf16)] * 3
    )
    scratch = [(name, pltpu.VMEM(a.shape, a.dtype)) for name, a in fetched.items()]
    scratch += [(name, pltpu.VMEM(shape, kind)) for (name, shape), kind in zip(stored, kinds)]
    for j, (tail, kind) in enumerate(tails):
        for b, one in enumerate(scatter_buffers(tail, kind)):
            scratch.append(("piece%d_%d" % (j, b), one))
    scratch += pairs_of(
        qkv_wide=pltpu.VMEM((3, 4, 4, 48, width), bf16),
        out_wide=pltpu.VMEM((4, 4, 48, width), bf16),
        up_wide=pltpu.VMEM((4, 4, 48, hidden), bf16),
        down_wide=pltpu.VMEM((4, 4, 192, width), bf16),
        qkv_sib=pltpu.VMEM((3, 24, width // 2), f32),
        out_sib=pltpu.VMEM((24, width // 2), f32),
        up_sib=pltpu.VMEM((24, hidden // 2), f32),
        down_sib=pltpu.VMEM((96, width // 2), f32),
        qkv_final=pltpu.VMEM((3, 48, width // 2), f32),
        out_final=pltpu.VMEM((48, width // 2), f32),
        up_final=pltpu.VMEM((48, hidden // 2), f32),
        down_final=pltpu.VMEM((192, width // 2), f32),
        small_wide=pltpu.VMEM((4, 4, 2, 8, 128), f32),
        small_part=pltpu.VMEM((4, 4, 2, 8, 128), f32),
        small_total=pltpu.VMEM((4, 4, 8, 128), f32),
        small_got=pltpu.VMEM((4, 4, 8, 128), f32),
        down_part=pltpu.VMEM((4, 4, 192, width), bf16),
        down_total=pltpu.VMEM((4, 4, 192, 384), bf16),
        up_total=pltpu.VMEM((2, 4, 4, 48, 768), bf16),
        out_total=pltpu.VMEM((4, 4, 48, 384), bf16),
        qkv_total=pltpu.VMEM((3, 4, 4, 144, 128), bf16),
        present=pltpu.VMEM((count, 128), f32),
        vec=pltpu.VMEM((8, 7 * width), f32),
        sums=pltpu.VMEM((8, 7 * width), f32),
        bias=pltpu.VMEM((3, 8, width), f32),
        owner=pltpu.VMEM((1, 7 * width), f32),
        logsum=pltpu.VMEM((width // 128, 8, count), f32),
        turned_one=pltpu.VMEM((width, count), bf16),
        turned_two=pltpu.VMEM((width, count), bf16),
        mixed_turned=pltpu.VMEM((width, count), bf16),
        normed=pltpu.VMEM((count, width), bf16),
        mixed=pltpu.VMEM((count, width), bf16),
        grad_low=pltpu.VMEM((count, width), bf16),
        joined=pltpu.VMEM((width // 128, 3, count, 128), bf16),
        middle=pltpu.VMEM((count, width), f32),
        acc=pltpu.VMEM((count, width), f32),
        act=pltpu.VMEM((count, hidden), bf16),
        slope=pltpu.VMEM((2, count, TILE), f32),
        send=pltpu.SemaphoreType.DMA((5, Piece.COUNT)),
        gather_z=pltpu.SemaphoreType.DMA((9, 3)),
        gather_recv=pltpu.SemaphoreType.DMA((9, 13)),
        scatter_recv=pltpu.SemaphoreType.DMA((9, 14)),
        pre_send=pltpu.SemaphoreType.DMA((6,)),
        pre_recv=pltpu.SemaphoreType.DMA((6,)),
        end_send=pltpu.SemaphoreType.DMA((6,)),
        end_recv=pltpu.SemaphoreType.DMA((6,)),
        load=pltpu.SemaphoreType.DMA((len(FETCHED),)),
        save=pltpu.SemaphoreType.DMA((len(STORED),)),
        slope_send=pltpu.SemaphoreType.DMA((2,)),
        slope_recv=pltpu.SemaphoreType.DMA((2,)),
    )
    names = (
        [name for name, _, _ in inputs] + [name for name, _, _ in outs] + [name for name, _ in scratch]
    )
    results = pl.pallas_call(
        functools.partial(layer_kernel, names),
        out_shape=tuple(jax.ShapeDtypeStruct(shape, kind) for _, shape, kind in outs),
        in_specs=[spec for _, _, spec in inputs],
        out_specs=(anywhere,) * len(outs),
        scratch_shapes=[kind for _, kind in scratch],
        compiler_params=pltpu.CompilerParams(
            collective_id=0, has_side_effects=True, vmem_limit_bytes=VMEM_BYTES
        ),
        name="layer",
    )(*[array for _, array, _ in inputs])
    qkv, out, up, down, output, input_grad, small = results[1:]
    return output, input_grad, qkv, out, up, down, small


def deliver_kernel(count, *refs):
    sources, tile = refs[:count], refs[count]
    targets = refs[count + 1 : 2 * count + 1]
    for source, target in zip(sources, targets):
        target[...] = source[...]
    for i, vector in enumerate(refs[2 * count + 1 :]):
        vector[...] = tile[i, 0 : vector.shape[0]]


def deliver(whole, tile, sizes):
    count = len(whole)
    vmem = pl.BlockSpec(memory_space=pltpu.VMEM)
    return pl.pallas_call(
        functools.partial(deliver_kernel, count),
        out_shape=[jax.ShapeDtypeStruct(a.shape, a.dtype) for a in whole]
        + [jax.ShapeDtypeStruct((m,), jnp.float32) for m in sizes],
        in_specs=[vmem] * (count + 1),
        out_specs=[vmem] * (count + len(sizes)),
        compiler_params=pltpu.CompilerParams(vmem_limit_bytes=VMEM_BYTES),
        name="deliver",
    )(*whole, tile)


def body(
    tokens,
    band_mask,
    out_grad,
    norm1_gain,
    norm1_shift,
    qkv_weight,
    qv_bias,
    out_weight,
    out_bias,
    norm2_gain,
    norm2_shift,
    up_weight,
    up_bias,
    down_weight,
    down_bias,
):
    smalls = (norm1_gain, norm1_shift, qv_bias, out_bias, norm2_gain, norm2_shift, up_bias, down_bias)
    shards = (qkv_weight, out_weight, up_weight, down_weight)
    *whole, tile = layer_call(tokens, band_mask, out_grad, shards, smalls)
    output, input_grad, qkv, out, up, down, *grads = deliver(
        whole, tile, [v.shape[0] for v in smalls]
    )
    return (
        output,
        input_grad,
        grads[0],
        grads[1],
        qkv,
        grads[2],
        out,
        grads[3],
        grads[4],
        grads[5],
        up,
        grads[6],
        down,
        grads[7],
    )


def solution(mesh):
    rows, flat = P(AXES, None), P(AXES)
    params = (flat, flat, rows, flat, rows, flat, flat, flat, rows, flat, rows, flat)
    fitted = tuple(mesh.shape[axis] for axis in AXES) == (8, 4)
    return jax.shard_map(
        body if fitted else body_plain,
        mesh=mesh,
        in_specs=(rows, rows, rows) + params,
        out_specs=(rows, rows) + params,
        check_vma=False,
    )
```

```python
import functools
import math

import jax
import jax.numpy as jnp
from jax import lax
from jax.experimental import pallas as pl
from jax.experimental.pallas import tpu as pltpu
from jax.sharding import PartitionSpec as P

HEAD = 64
HEAD_GROUP = 4
QBLOCK = 512


NORM_EPSILON = 1e-05
VMEM_BYTES = 62 << 20
AXES = ("wide", "narrow")


def normalize(values, gain, shift):
    centre = jnp.mean(values, axis=1, keepdims=True)
    centred = values - centre
    factor = lax.rsqrt(jnp.mean(centred * centred, axis=1, keepdims=True) + NORM_EPSILON)
    normed = centred * factor
    return (normed * gain + shift, normed, factor)


def normalize_back(upstream, normed, factor, gain):
    gain_grad = jnp.sum(upstream * normed, axis=0)
    shift_grad = jnp.sum(upstream, axis=0)
    scaled = upstream * gain
    inner = (
        scaled
        - jnp.mean(scaled, axis=1, keepdims=True)
        - normed * jnp.mean(scaled * normed, axis=1, keepdims=True)
    )
    return (factor * inner, gain_grad, shift_grad)


def gelu_slope(values):
    cumulative = 0.5 * (1.0 + lax.erf(values * (1.0 / math.sqrt(2.0))))
    return cumulative + values * jnp.exp(-0.5 * values * values) * (1.0 / math.sqrt(2.0 * math.pi))


def to_groups(matrix, count):
    return matrix.reshape(matrix.shape[0], count, -1).transpose(1, 0, 2)


def from_groups(stacked):
    return stacked.transpose(1, 0, 2).reshape(stacked.shape[1], -1)


def attend_forward(query_cols, key_cols, value_cols, key_live):
    row_count, span_cols = key_cols.shape
    head_width = span_cols // HEAD_GROUP
    scaling = 1.0 / math.sqrt(head_width)
    key_rows = key_cols.reshape(row_count, HEAD_GROUP, head_width)
    value_rows = value_cols.reshape(row_count, HEAD_GROUP, head_width)
    query_blocks = query_cols.reshape(row_count // QBLOCK, QBLOCK, HEAD_GROUP, head_width)

    def one_block(query_rows):
        scores = (
            jnp.einsum("qhd,khd->hqk", query_rows, key_rows, preferred_element_type=jnp.float32)
            * scaling
        )
        scores = jnp.where(key_live[None, None, :], scores, -jnp.inf)
        largest = jnp.max(scores, axis=2, keepdims=True)
        expo = jnp.exp(scores - largest)
        totals = jnp.sum(expo, axis=2, keepdims=True)
        weights_low = (expo / totals).astype(jnp.bfloat16)
        mixture = jnp.einsum(
            "hqk,khd->qhd", weights_low, value_rows, preferred_element_type=jnp.float32
        )
        return (mixture.reshape(QBLOCK, span_cols), largest[:, :, 0] + jnp.log(totals[:, :, 0]))

    mixture, logsum = lax.map(one_block, query_blocks)
    return (mixture.reshape(row_count, span_cols), logsum)


def attend_backward(query_cols, key_cols, value_cols, grad_cols, logsum, key_live):
    row_count, span_cols = key_cols.shape
    head_width = span_cols // HEAD_GROUP
    scaling = 1.0 / math.sqrt(head_width)
    key_rows = key_cols.reshape(row_count, HEAD_GROUP, head_width)
    value_rows = value_cols.reshape(row_count, HEAD_GROUP, head_width)
    query_blocks = query_cols.reshape(row_count // QBLOCK, QBLOCK, HEAD_GROUP, head_width)
    grad_blocks = grad_cols.reshape(row_count // QBLOCK, QBLOCK, HEAD_GROUP, head_width)

    def one_block(carry, items):
        key_acc, value_acc = carry
        query_rows, grad_rows, block_logsum = items
        scores = (
            jnp.einsum("qhd,khd->hqk", query_rows, key_rows, preferred_element_type=jnp.float32)
            * scaling
        )
        scores = jnp.where(key_live[None, None, :], scores, -jnp.inf)
        probs = jnp.exp(scores - block_logsum[:, :, None])
        value_acc = value_acc + jnp.einsum(
            "hqk,qhd->khd",
            probs.astype(jnp.bfloat16),
            grad_rows,
            preferred_element_type=jnp.float32,
        )
        prob_grad = jnp.einsum(
            "qhd,khd->hqk", grad_rows, value_rows, preferred_element_type=jnp.float32
        )
        inner = jnp.sum(probs * prob_grad, axis=2, keepdims=True)
        score_grad = (probs * (prob_grad - inner)).astype(jnp.bfloat16)
        query_grad = (
            jnp.einsum("hqk,khd->qhd", score_grad, key_rows, preferred_element_type=jnp.float32)
            * scaling
        )
        key_acc = (
            key_acc
            + jnp.einsum("hqk,qhd->khd", score_grad, query_rows, preferred_element_type=jnp.float32)
            * scaling
        )
        return ((key_acc, value_acc), query_grad.reshape(QBLOCK, span_cols))

    empty = jnp.zeros((row_count, HEAD_GROUP, head_width), jnp.float32)
    (key_grad, value_grad), query_grad = lax.scan(
        one_block, (empty, empty), (query_blocks, grad_blocks, logsum)
    )
    return (
        query_grad.reshape(row_count, span_cols),
        key_grad.reshape(row_count, span_cols),
        value_grad.reshape(row_count, span_cols),
    )


def gathered(shard):
    return lax.all_gather(shard.astype(jnp.bfloat16), AXES, axis=0, tiled=True)


def scattered(part):
    return lax.psum_scatter(part, AXES, scatter_dimension=0, tiled=True)


def body_plain(
    tokens,
    band_mask,
    out_grad,
    norm1_gain,
    norm1_shift,
    qkv_weight,
    qv_bias,
    out_weight,
    out_bias,
    norm2_gain,
    norm2_shift,
    up_weight,
    up_bias,
    down_weight,
    down_bias,
):
    row_count, width = tokens.shape
    group_count = width // (HEAD_GROUP * HEAD)
    present = jnp.repeat(band_mask[0].astype(jnp.float32), row_count // band_mask.shape[1])
    key_live = present > 0.5
    column_mask = present[:, None]
    gain_one, shift_one, w_qkv, b_qv, w_out, b_out = (
        gathered(norm1_gain),
        gathered(norm1_shift),
        gathered(qkv_weight),
        gathered(qv_bias),
        gathered(out_weight),
        gathered(out_bias),
    )
    inputs = tokens.astype(jnp.float32)
    normed_one, unit_one, factor_one = normalize(
        inputs, gain_one.astype(jnp.float32), shift_one.astype(jnp.float32)
    )
    normed_one = normed_one.astype(jnp.bfloat16)
    bias_wide = b_qv.astype(jnp.float32)
    bias_full = jnp.concatenate(
        [bias_wide[:width], jnp.zeros((width,), jnp.float32), bias_wide[width:]]
    )
    joined = (jnp.dot(normed_one, w_qkv, preferred_element_type=jnp.float32) + bias_full).astype(
        jnp.bfloat16
    )
    query_groups = to_groups(joined[:, :width], group_count)
    key_groups = to_groups(joined[:, width : 2 * width], group_count)
    value_groups = to_groups(joined[:, 2 * width :], group_count)
    mixture, logsum = lax.map(
        lambda items: attend_forward(items[0], items[1], items[2], key_live),
        (query_groups, key_groups, value_groups),
    )
    mixture = from_groups(mixture).astype(jnp.bfloat16)
    attention = jnp.dot(mixture, w_out, preferred_element_type=jnp.float32) + b_out.astype(
        jnp.float32
    )
    middle = inputs + column_mask * attention
    gain_two, shift_two, w_up, b_up, w_down, b_down = (
        gathered(norm2_gain),
        gathered(norm2_shift),
        gathered(up_weight),
        gathered(up_bias),
        gathered(down_weight),
        gathered(down_bias),
    )
    normed_two, unit_two, factor_two = normalize(
        middle, gain_two.astype(jnp.float32), shift_two.astype(jnp.float32)
    )
    normed_two = normed_two.astype(jnp.bfloat16)
    hidden = jnp.dot(normed_two, w_up, preferred_element_type=jnp.float32) + b_up.astype(
        jnp.float32
    )
    active = jax.nn.gelu(hidden, approximate=False).astype(jnp.bfloat16)
    branch = jnp.dot(active, w_down, preferred_element_type=jnp.float32) + b_down.astype(
        jnp.float32
    )
    output = (middle + column_mask * branch).astype(jnp.bfloat16)
    upstream = out_grad.astype(jnp.float32)
    branch_grad = (column_mask * upstream).astype(jnp.bfloat16)
    down_weight_grad = jnp.einsum(
        "tf,td->fd", active, branch_grad, preferred_element_type=jnp.float32
    )
    down_bias_grad = jnp.sum(branch_grad.astype(jnp.float32), axis=0)
    active_grad = jnp.einsum(
        "td,fd->tf", branch_grad, w_down, preferred_element_type=jnp.float32
    )
    hidden_grad = (active_grad * gelu_slope(hidden)).astype(jnp.bfloat16)
    up_weight_grad = jnp.einsum(
        "td,tf->df", normed_two, hidden_grad, preferred_element_type=jnp.float32
    )
    up_bias_grad = jnp.sum(hidden_grad.astype(jnp.float32), axis=0)
    normed_two_grad = jnp.einsum(
        "tf,df->td", hidden_grad, w_up, preferred_element_type=jnp.float32
    )
    middle_part, norm2_gain_grad, norm2_shift_grad = normalize_back(
        normed_two_grad, unit_two, factor_two, gain_two.astype(jnp.float32)
    )
    (
        norm2_gain_grad,
        norm2_shift_grad,
        up_weight_grad,
        up_bias_grad,
        down_weight_grad,
        down_bias_grad,
    ) = (
        scattered(norm2_gain_grad),
        scattered(norm2_shift_grad),
        scattered(up_weight_grad),
        scattered(up_bias_grad),
        scattered(down_weight_grad),
        scattered(down_bias_grad),
    )
    middle_grad = upstream + middle_part
    attention_grad = (column_mask * middle_grad).astype(jnp.bfloat16)
    out_weight_grad = jnp.einsum(
        "te,td->ed", mixture, attention_grad, preferred_element_type=jnp.float32
    )
    out_bias_grad = jnp.sum(attention_grad.astype(jnp.float32), axis=0)
    mixture_grad = jnp.einsum(
        "td,ed->te", attention_grad, w_out, preferred_element_type=jnp.float32
    ).astype(jnp.bfloat16)
    grad_groups = to_groups(mixture_grad, group_count)
    query_grad, key_grad, value_grad = lax.map(
        lambda items: attend_backward(items[0], items[1], items[2], items[3], items[4], key_live),
        (query_groups, key_groups, value_groups, grad_groups, logsum),
    )
    query_grad = from_groups(query_grad).astype(jnp.bfloat16)
    key_grad = from_groups(key_grad).astype(jnp.bfloat16)
    value_grad = from_groups(value_grad).astype(jnp.bfloat16)
    joined_grad = jnp.concatenate([query_grad, key_grad, value_grad], axis=1)
    qkv_weight_grad = jnp.einsum(
        "td,tc->dc", normed_one, joined_grad, preferred_element_type=jnp.float32
    )
    qv_bias_grad = jnp.concatenate(
        [
            jnp.sum(query_grad.astype(jnp.float32), axis=0),
            jnp.sum(value_grad.astype(jnp.float32), axis=0),
        ]
    )
    normed_one_grad = jnp.einsum(
        "tc,dc->td", joined_grad, w_qkv, preferred_element_type=jnp.float32
    )
    input_part, norm1_gain_grad, norm1_shift_grad = normalize_back(
        normed_one_grad, unit_one, factor_one, gain_one.astype(jnp.float32)
    )
    input_grad = (middle_grad + input_part).astype(jnp.bfloat16)
    (
        norm1_gain_grad,
        norm1_shift_grad,
        qkv_weight_grad,
        qv_bias_grad,
        out_weight_grad,
        out_bias_grad,
    ) = (
        scattered(norm1_gain_grad),
        scattered(norm1_shift_grad),
        scattered(qkv_weight_grad),
        scattered(qv_bias_grad),
        scattered(out_weight_grad),
        scattered(out_bias_grad),
    )
    return (
        output,
        input_grad,
        norm1_gain_grad,
        norm1_shift_grad,
        qkv_weight_grad,
        qv_bias_grad,
        out_weight_grad,
        out_bias_grad,
        norm2_gain_grad,
        norm2_shift_grad,
        up_weight_grad,
        up_bias_grad,
        down_weight_grad,
        down_bias_grad,
    )


MESH_ID = pl.DeviceIdType.MESH
VIA_X = (0, 2)
VIA_Y = (1, 3)
ORDER = (1, 3, 2)
SCORE_SCALE = math.log2(math.e) / math.sqrt(HEAD)
TILE = 768


class Place:
    def __init__(self):
        wide = lax.axis_index("wide")
        narrow = lax.axis_index("narrow")
        z, y = wide // 2, wide % 2
        x, c = narrow // 2, narrow % 2
        self.z, self.c = z, c
        self.zs = (z, z + 1 - 2 * (z % 2), (z + 2) % 4, 3 - z)
        self.q = y * 2 + x
        self.qx = y * 2 + (1 - x)
        self.qy = (1 - y) * 2 + x
        self.qd = (1 - y) * 2 + (1 - x)
        self.to_z = tuple((zz * 2 + y, x * 2 + c) for zz in self.zs)
        self.to_x = (z * 2 + y, (1 - x) * 2 + c)
        self.to_y = (z * 2 + 1 - y, x * 2 + c)
        self.to_c = (z * 2 + y, x * 2 + 1 - c)
        self.to_d = (z * 2 + 1 - y, (1 - x) * 2 + c)


def span(start, size, step):
    return pl.ds(pl.multiple_of(start, step), size)


def meet(place):
    barrier = pltpu.get_barrier_semaphore()
    peers = place.to_z[1:] + (place.to_x, place.to_y, place.to_d, place.to_c)
    for peer in peers:
        pl.semaphore_signal(barrier, inc=1, device_id=peer, device_id_type=MESH_ID)
    pl.semaphore_wait(barrier, len(peers))


def remote(source, target, send, recv, peer):
    return pltpu.make_async_remote_copy(
        src_ref=source,
        dst_ref=target,
        send_sem=send,
        recv_sem=recv,
        device_id=peer,
        device_id_type=MESH_ID,
    )


class Piece:
    COUNT = 19

    def __init__(self, place, send, recv, slots, z_send=None):
        self.p = place
        self.send, self.recv, self.slots, self.z_send = send, recv, slots, z_send
        self.sent = []

    def pair(self, index):
        own = self.send if index >= 3 or self.z_send is None else self.z_send
        return own.at[index], self.recv.at[self.slots[index]]

    def go(self, source, target, index, peer):
        remote(source(), target(), *self.pair(index), peer).start()
        self.sent.append((source, target, index, peer))

    def got(self, target, index, peer):
        remote(target, target, *self.pair(index), peer).wait_recv()

    def finish(self):
        for source, target, index, peer in self.sent:
            remote(source(), target(), *self.pair(index), peer).wait_send()
        self.sent = []


class Gather(Piece):
    SLOTS = (0, 1, 2, 3, 4, 5, 6, 11, 11, 7, 8, 9, 10, 11, 11, 12, 12, 12, 12)

    def __init__(self, place, block, column, others, send, recv, z_send):
        super().__init__(place, send, recv, self.SLOTS, z_send)
        self.block, self.column, self.others = block, column, others

    def own(self):
        return self.block(self.p.z, self.p.q)

    def start_z(self):
        p = self.p
        for k in ORDER:
            self.go(self.own, self.own, k - 1, p.to_z[k])

    def start_xy(self):
        p = self.p
        self.go(self.own, self.own, 3, p.to_x)
        self.go(self.own, self.own, 9, p.to_y)

    def z(self, k):
        p = self.p
        here = lambda: self.block(p.zs[k], p.q)
        self.got(here(), k - 1, p.to_z[k])
        self.go(here, here, 3 + k, p.to_x)
        self.go(here, here, 9 + k, p.to_y)

    def share(self, index, q):
        column = lambda: self.column(q)
        self.go(column, column, index, self.p.to_c)

    def own_column(self):
        self.share(15, self.p.q)

    def xy(self, k):
        p = self.p
        from_x = lambda: self.block(p.zs[k], p.qx)
        self.got(from_x(), 3 + k, p.to_x)
        if k in VIA_X:
            self.go(from_x, from_x, 13 + VIA_X.index(k), p.to_y)
        from_y = lambda: self.block(p.zs[k], p.qy)
        self.got(from_y(), 9 + k, p.to_y)
        if k in VIA_Y:
            self.go(from_y, from_y, 7 + VIA_Y.index(k), p.to_x)

    def xy_columns(self):
        self.share(16, self.p.qx)
        self.share(17, self.p.qy)

    def d(self):
        p = self.p
        self.got(self.column(p.qd), 13, p.to_y)
        self.share(18, p.qd)

    def c(self):
        self.got(self.others(), 15, self.p.to_c)


class Scatter(Piece):
    SLOTS = (13, 13, 13, 5, 6, 7, 8, 1, 2, 9, 10, 11, 12, 3, 4, 0, 0, 0, 0)

    def __init__(self, place, block, column, whole, bufs, send, recv):
        super().__init__(place, send, recv, self.SLOTS)
        self.block, self.column, self.whole = block, column, whole
        self.dx, self.dy, self.xr, self.yr, self.zr = bufs

    def add(self, target, other):
        target[...] = (target[...].astype(jnp.float32) + other[...].astype(jnp.float32)).astype(
            target.dtype
        )

    def give(self, other):
        p = self.p
        for i, q in enumerate((p.qd, p.qx, p.qy, p.q)):
            self.go(lambda q=q: other(q), lambda q=q: self.column(q), 15 + i, p.to_c)

    def arrive(self):
        self.got(self.whole(), 15, self.p.to_c)

    def diagonal(self):
        p = self.p
        for i in range(2):
            self.go(
                lambda i=i: self.block(p.zs[VIA_X[i]], p.qd), lambda i=i: self.dx.at[i], 7 + i, p.to_x
            )
            self.go(
                lambda i=i: self.block(p.zs[VIA_Y[i]], p.qd), lambda i=i: self.dy.at[i], 13 + i, p.to_y
            )

    def cross(self, k):
        p = self.p
        on_x = lambda: self.block(p.zs[k], p.qx)
        on_y = lambda: self.block(p.zs[k], p.qy)
        if k in VIA_Y:
            i = VIA_Y.index(k)
            self.go(on_y, lambda: self.yr.at[k], 9 + k, p.to_y)
            self.got(self.dy.at[i], 13 + i, p.to_y)
            self.add(on_x(), self.dy.at[i])
            self.go(on_x, lambda: self.xr.at[k], 3 + k, p.to_x)
        else:
            i = VIA_X.index(k)
            self.go(on_x, lambda: self.xr.at[k], 3 + k, p.to_x)
            self.got(self.dx.at[i], 7 + i, p.to_x)
            self.add(on_y(), self.dx.at[i])
            self.go(on_y, lambda: self.yr.at[k], 9 + k, p.to_y)

    def plane(self, k):
        p = self.p
        self.got(self.xr.at[k], 3 + k, p.to_x)
        self.got(self.yr.at[k], 9 + k, p.to_y)
        here = self.block(p.zs[k], p.q)
        return here, (
            here[...].astype(jnp.float32)
            + self.xr[k].astype(jnp.float32)
            + self.yr[k].astype(jnp.float32)
        )

    def spread(self, k):
        p = self.p
        here, value = self.plane(k)
        here[...] = value.astype(here.dtype)
        self.go(lambda: self.block(p.zs[k], p.q), lambda: self.zr.at[k - 1], k - 1, p.to_z[k])

    def last(self):
        _, value = self.plane(0)
        self.got(self.zr, 0, self.p.to_z[1])
        for k in ORDER:
            value = value + self.zr[k - 1].astype(jnp.float32)
        return value


class SmallScatter(Piece):
    SLOTS = (4, 4, 4, 1, 2, 3, 0, 0, 0, 0, 0, 0, 0, 0, 0, 0, 0, 0, 0)

    def __init__(self, place, total, arrived, send, recv):
        super().__init__(place, send, recv, self.SLOTS)
        self.total, self.arrived = total, arrived

    def give(self, other):
        self.go(other, lambda: self.total, 15, self.p.to_c)

    def arrive(self):
        self.got(self.total, 15, self.p.to_c)

    def neighbours(self):
        p = self.p
        return ((0, p.qx, p.to_x), (1, p.qy, p.to_y), (2, p.qd, p.to_d))

    def plane(self):
        for i, q, peer in self.neighbours():
            self.go(lambda q=q: self.total.at[:, q], lambda i=i: self.arrived.at[i], 3 + i, peer)

    def spread(self):
        p = self.p
        value = self.total[:, p.q]
        for i, _, peer in self.neighbours():
            self.got(self.arrived.at[i], 3 + i, peer)
            value = value + self.arrived[i]
        self.total[:, p.q] = value
        for k in ORDER:
            self.go(
                lambda k=k: self.total.at[p.zs[k], p.q],
                lambda k=k: self.arrived.at[3, k],
                k - 1,
                p.to_z[k],
            )

    def last(self):
        p = self.p
        self.got(self.arrived.at[3, pl.ds(1, 3)], 0, p.to_z[1])
        value = self.total[p.z, p.q]
        for k in ORDER:
            value = value + self.arrived[3, k]
        return value


def scatter_buffers(tail, kind):
    return [
        pltpu.VMEM((2,) + tail, kind),
        pltpu.VMEM((2,) + tail, kind),
        pltpu.VMEM((4,) + tail, kind),
        pltpu.VMEM((4,) + tail, kind),
        pltpu.VMEM((3,) + tail, kind),
    ]


MATRICES = ("qkv", "out", "up", "down")


def triples(**named):
    return [(name, one, two) for name, (one, two) in named.items()]


def pairs_of(**named):
    return list(named.items())


class Named:
    def __init__(self, names, refs):
        assert len(names) == len(refs)
        self.__dict__.update(zip(names, refs))


def loop(first, count, compute, slots=()):
    def step(i, carry):
        compute(i)
        for j, steps in enumerate(slots):
            if steps:

                @pl.when(i == first + j)
                def _(steps=steps):
                    for one in steps:
                        one()

        return carry

    lax.fori_loop(first, first + count, step, 0)


def follow(order, steps, loops):
    at = 0
    while at < len(order):
        kind = order[at][0]
        if kind not in loops:
            steps[order[at]]()
            at += 1
            continue
        first, slots, end = order[at][1], [[]], at + 1
        held = []
        while end < len(order) and (order[end][0] not in loops or order[end][0] == kind):
            if order[end][0] == kind:
                assert order[end][1] == first + len(slots)
                slots[-1] += held
                held = []
                slots.append([])
                at = end
            else:
                held.append(steps[order[end]])
            end += 1
        if len(slots) == 1:
            loops[kind](jnp.int32(first))
        else:
            loop(first, len(slots), loops[kind], slots)
        at += 1


def dot(left, right):
    return jnp.dot(left, right, preferred_element_type=jnp.float32)


def dot_nt(left, right):
    return lax.dot_general(
        left, right, (((1,), (1,)), ((), ())), preferred_element_type=jnp.float32
    )


def dot_tn(left, right):
    return lax.dot_general(
        left, right, (((0,), (0,)), ((), ())), preferred_element_type=jnp.float32
    )


def head_only(values, e):
    lane = lax.broadcasted_iota(jnp.int32, values.shape, 1)
    return jnp.where((lane // HEAD) == e, values, jnp.zeros_like(values))


def fill_present(present, mask):
    groups = mask.shape[1]
    rows = present.shape[0] // groups
    for g in range(groups):
        present[g * rows : (g + 1) * rows, :] = jnp.full(
            (rows, 128), mask[0, g].astype(jnp.float32)
        )


def segments(width):
    return ((0, width, width // 32), (width, 2 * width, width // 16), (3 * width, 4 * width, width // 8))


def selection(size, m):
    lane = lax.broadcasted_iota(jnp.int32, (1, size), 1).astype(jnp.float32)
    rest = lane - m * jnp.floor((lane + 0.5) * (1.0 / m))
    row = lax.broadcasted_iota(jnp.int32, (128, size), 0).astype(jnp.float32)
    return jnp.where(row == rest, 1.0, 0.0).astype(jnp.bfloat16)


def owners(width):
    parts = []
    for _, size, m in segments(width):
        lane = lax.broadcasted_iota(jnp.int32, (1, size), 1).astype(jnp.float32)
        parts.append(jnp.floor((lane + 0.5) * (1.0 / m)))
    return jnp.concatenate(parts, axis=1)


def unit(values):
    centred = values - jnp.mean(values, axis=1, keepdims=True)
    factor = lax.rsqrt(jnp.mean(centred * centred, axis=1, keepdims=True) + NORM_EPSILON)
    return centred * factor, factor


(
    ATTENTION,
    CLOSE,
    CROSS,
    C_GOT,
    DIAGONAL,
    DOWN_HIGH,
    DOWN_LOW,
    DRAIN,
    D_GOT,
    EXPAND_HIGH,
    EXPAND_LOW,
    FINISH,
    FIRST_BACK,
    FIRST_NORM,
    FORM,
    GIVE,
    HEADS,
    HEADS_BACK,
    LAST,
    MASK_GRAD,
    NARROW,
    OUT_BACK,
    OWN_COLUMN,
    OWN_PART,
    PACK,
    PLANE_GOT,
    PLANE_START,
    PREPARE,
    QKV_BACK,
    SECOND_BACK,
    SECOND_NORM,
    SETTLE,
    SMALL_PLANE,
    SMALL_SPREAD,
    SPREAD,
    START_XY,
    START_Z,
    UNPACK,
    UP_BACK,
    XY_COLUMNS,
    XY_GOT,
    Z_GOT,
) = range(42)
SEQUENCE = (
    (START_Z, 8),
    (START_XY, 8),
    (FORM, 0),
    (START_Z, 0),
    (FORM, 1),
    (FORM, 2),
    (FORM, 3),
    (START_Z, 1),
    (START_Z, 2),
    (START_Z, 3),
    (START_Z, 4),
    (START_XY, 2),
    (START_XY, 1),
    (Z_GOT, 8, 3),
    (XY_GOT, 8, 0),
    (Z_GOT, 8, 1),
    (Z_GOT, 8, 2),
    (OWN_COLUMN, 8),
    (START_Z, 5),
    (START_Z, 6),
    (START_Z, 7),
    (START_XY, 0),
    (START_XY, 3),
    (PREPARE,),
    (MASK_GRAD, 0),
    (MASK_GRAD, 1),
    (MASK_GRAD, 2),
    (MASK_GRAD, 3),
    (Z_GOT, 0, 1),
    (XY_GOT, 2, 0),
    (Z_GOT, 0, 2),
    (XY_GOT, 1, 0),
    (XY_GOT, 8, 3),
    (Z_GOT, 0, 3),
    (OWN_COLUMN, 0),
    (XY_GOT, 8, 1),
    (XY_GOT, 8, 2),
    (XY_COLUMNS, 8),
    (XY_GOT, 0, 0),
    (XY_GOT, 3, 0),
    (Z_GOT, 1, 1),
    (XY_GOT, 0, 1),
    (Z_GOT, 1, 2),
    (Z_GOT, 1, 3),
    (OWN_COLUMN, 1),
    (XY_GOT, 0, 2),
    (Z_GOT, 2, 1),
    (XY_GOT, 0, 3),
    (XY_COLUMNS, 0),
    (D_GOT, 8),
    (Z_GOT, 2, 2),
    (Z_GOT, 2, 3),
    (OWN_COLUMN, 2),
    (C_GOT, 8),
    (UNPACK,),
    (XY_GOT, 1, 1),
    (Z_GOT, 3, 1),
    (FIRST_NORM, 0),
    (XY_GOT, 1, 2),
    (FIRST_NORM, 1),
    (FIRST_NORM, 2),
    (Z_GOT, 3, 2),
    (XY_GOT, 1, 3),
    (XY_COLUMNS, 1),
    (Z_GOT, 3, 3),
    (D_GOT, 0),
    (OWN_COLUMN, 3),
    (FIRST_NORM, 3),
    (START_XY, 4),
    (XY_GOT, 2, 1),
    (XY_GOT, 2, 2),
    (XY_GOT, 2, 3),
    (XY_COLUMNS, 2),
    (XY_GOT, 3, 1),
    (C_GOT, 0),
    (HEADS, 0),
    (Z_GOT, 4, 1),
    (D_GOT, 1),
    (START_XY, 5),
    (XY_GOT, 3, 2),
    (HEADS, 1),
    (XY_GOT, 3, 3),
    (Z_GOT, 4, 3),
    (Z_GOT, 4, 2),
    (XY_COLUMNS, 3),
    (OWN_COLUMN, 4),
    (XY_GOT, 4, 0),
    (C_GOT, 1),
    (HEADS, 2),
    (D_GOT, 2),
    (HEADS, 3),
    (XY_GOT, 4, 1),
    (Z_GOT, 5, 1),
    (XY_GOT, 5, 0),
    (C_GOT, 2),
    (HEADS, 4),
    (Z_GOT, 5, 2),
    (Z_GOT, 5, 3),
    (OWN_COLUMN, 5),
    (D_GOT, 3),
    (XY_GOT, 4, 3),
    (HEADS, 5),
    (XY_GOT, 4, 2),
    (XY_COLUMNS, 4),
    (C_GOT, 3),
    (ATTENTION,),
    (SECOND_NORM, 0),
    (SECOND_NORM, 1),
    (SECOND_NORM, 2),
    (START_XY, 7),
    (XY_GOT, 5, 1),
    (SECOND_NORM, 3),
    (XY_GOT, 5, 2),
    (XY_GOT, 5, 3),
    (XY_COLUMNS, 5),
    (Z_GOT, 7, 1),
    (D_GOT, 4),
    (XY_GOT, 7, 0),
    (Z_GOT, 7, 2),
    (C_GOT, 4),
    (EXPAND_LOW, 0),
    (Z_GOT, 7, 3),
    (OWN_COLUMN, 7),
    (EXPAND_LOW, 1),
    (DOWN_LOW, 0),
    (D_GOT, 5),
    (START_XY, 6),
    (Z_GOT, 6, 2),
    (Z_GOT, 6, 3),
    (Z_GOT, 6, 1),
    (OWN_COLUMN, 6),
    (XY_GOT, 7, 1),
    (DOWN_LOW, 1),
    (XY_GOT, 7, 2),
    (C_GOT, 5),
    (EXPAND_HIGH, 0),
    (EXPAND_HIGH, 1),
    (XY_GOT, 7, 3),
    (XY_COLUMNS, 7),
    (DRAIN,),
    (DOWN_HIGH, 0),
    (XY_GOT, 6, 0),
    (DOWN_HIGH, 1),
    (GIVE, 0),
    (XY_GOT, 6, 2),
    (GIVE, 1),
    (XY_GOT, 6, 3),
    (XY_GOT, 6, 1),
    (XY_COLUMNS, 6),
    (OWN_PART, 0),
    (DIAGONAL, 0),
    (D_GOT, 7),
    (OWN_PART, 1),
    (DIAGONAL, 1),
    (D_GOT, 6),
    (CROSS, 0, 1),
    (C_GOT, 7),
    (CROSS, 0, 0),
    (CROSS, 0, 3),
    (C_GOT, 6),
    (NARROW, 0),
    (NARROW, 1),
    (CROSS, 0, 2),
    (CROSS, 1, 1),
    (NARROW, 2),
    (CROSS, 1, 3),
    (CROSS, 1, 2),
    (CROSS, 1, 0),
    (NARROW, 3),
    (SPREAD, 0, 1),
    (GIVE, 2),
    (GIVE, 3),
    (PACK, 2),
    (SPREAD, 0, 3),
    (SPREAD, 0, 2),
    (OWN_PART, 2),
    (DIAGONAL, 2),
    (SPREAD, 1, 1),
    (FINISH, 0),
    (FINISH, 1),
    (FINISH, 2),
    (FINISH, 3),
    (UP_BACK,),
    (SPREAD, 1, 3),
    (SPREAD, 1, 2),
    (OWN_PART, 3),
    (DIAGONAL, 3),
    (CROSS, 2, 1),
    (SECOND_BACK, 0),
    (SECOND_BACK, 1),
    (SECOND_BACK, 2),
    (CROSS, 2, 0),
    (CROSS, 2, 3),
    (SECOND_BACK, 3),
    (GIVE, 4),
    (CROSS, 2, 2),
    (OUT_BACK,),
    (LAST, 0),
    (HEADS_BACK, 0),
    (CROSS, 3, 1),
    (CROSS, 3, 2),
    (CROSS, 3, 0),
    (SPREAD, 2, 1),
    (CROSS, 3, 3),
    (OWN_PART, 4),
    (DIAGONAL, 4),
    (GIVE, 5),
    (LAST, 1),
    (CLOSE, 3),
    (HEADS_BACK, 1),
    (SPREAD, 2, 3),
    (SPREAD, 3, 1),
    (SETTLE, 3),
    (SPREAD, 2, 2),
    (OWN_PART, 5),
    (DIAGONAL, 5),
    (SPREAD, 3, 2),
    (GIVE, 6),
    (HEADS_BACK, 2),
    (CROSS, 4, 3),
    (CROSS, 4, 0),
    (CROSS, 4, 2),
    (SPREAD, 3, 3),
    (CROSS, 5, 0),
    (CROSS, 4, 1),
    (CROSS, 5, 1),
    (OWN_PART, 6),
    (CROSS, 5, 2),
    (DIAGONAL, 6),
    (CROSS, 5, 3),
    (GIVE, 7),
    (PACK, 1),
    (SPREAD, 4, 3),
    (LAST, 2),
    (OWN_PART, 7),
    (SPREAD, 4, 2),
    (DIAGONAL, 7),
    (QKV_BACK,),
    (SPREAD, 4, 1),
    (SPREAD, 5, 1),
    (SPREAD, 5, 2),
    (FIRST_BACK, 0),
    (FIRST_BACK, 1),
    (CROSS, 6, 0),
    (CROSS, 6, 1),
    (FIRST_BACK, 2),
    (CROSS, 6, 2),
    (CROSS, 6, 3),
    (FIRST_BACK, 3),
    (SPREAD, 5, 3),
    (PACK, 0),
    (GIVE, 8),
    (CROSS, 7, 1),
    (CROSS, 7, 0),
    (LAST, 3),
    (CROSS, 7, 3),
    (CROSS, 7, 2),
    (CLOSE, 2),
    (SPREAD, 6, 1),
    (OWN_PART, 8),
    (SMALL_PLANE,),
    (LAST, 4),
    (CLOSE, 1),
    (SPREAD, 6, 2),
    (SETTLE, 2),
    (SPREAD, 6, 3),
    (SETTLE, 1),
    (SPREAD, 7, 1),
    (LAST, 5),
    (SPREAD, 7, 3),
    (SPREAD, 7, 2),
    (SMALL_SPREAD,),
    (LAST, 6),
    (LAST, 7),
    (CLOSE, 0),
    (LAST, 8),
    (SETTLE, 0),
)


FETCHED = ("qkv_shard", "out_shard", "up_shard", "down_shard", "tokens", "out_grad")
STORED = ("qkv_result", "out_result", "up_result", "down_result") + (
    ("output", "input_grad", "small_result")
)


def layer_kernel(names, *refs):
    r = Named(names, refs)
    place = Place()
    c = place.c
    tokens, width = r.tokens.shape
    hidden = r.act.shape[1]
    third = width // 2
    tiles = hidden // TILE
    shards = (r.qkv_shard, r.out_shard, r.up_shard, r.down_shard)

    def fetch(i):
        name = FETCHED[i]
        return pltpu.make_async_copy(getattr(r, name + "_in"), getattr(r, name), r.load.at[i])

    def store(i):
        name = STORED[i]
        return pltpu.make_async_copy(getattr(r, name), getattr(r, name + "_out"), r.save.at[i])

    for i in range(len(FETCHED)):
        fetch(i).start()
    meet(place)
    for i in range(4):
        fetch(i).wait()

    moves = [(0, g * width, third, (g,)) for g in range(3)] + [
        (i, 0, shards[i].shape[1] // 2, ()) for i in (1, 2, 3)
    ]
    sibs = (r.qkv_sib, r.out_sib, r.up_sib, r.down_sib)
    wides = (r.qkv_wide, r.out_wide, r.up_wide, r.down_wide)

    def before(m):
        i, start, cols, at = moves[m]
        source = shards[i].at[:, span(start + (1 - c) * cols, cols, 128)]
        target = sibs[i].at[at] if at else sibs[i]
        return remote(source, target, r.pre_send.at[m], r.pre_recv.at[m], place.to_c)

    for m in range(6):
        before(m).start()
    r.small_wide[place.z, place.q, c] = jnp.zeros((8, 128), jnp.float32)
    for i in range(8):
        vector = getattr(r, "vector%d" % i)
        r.small_wide[place.z, place.q, c, i : i + 1, 0 : vector.shape[0]] = vector[...].reshape(1, -1)

    def gather(j, block, column, others):
        lane = 4 if j == 8 else j % 4
        return Gather(
            place, block, column, others, r.send.at[lane], r.gather_recv.at[j], r.gather_z.at[j]
        )

    every = slice(None)
    pieces = []
    for s in range(3):
        cols = lambda side, s=s: span(side * third + 128 * s, 128, 128)
        pieces.append(
            gather(
                s,
                lambda zz, q, cols=cols: r.qkv_wide.at[:, zz, q, :, cols(c)],
                lambda q, cols=cols: r.qkv_wide.at[:, :, q, :, cols(c)],
                lambda cols=cols: r.qkv_wide.at[:, :, :, :, cols(1 - c)],
            )
        )
    cuts = (
        (1, 0, 48, 0, 384),
        (2, 0, 48, 0, 768),
        (2, 0, 48, 768, 768),
        (3, 0, 96, 0, 384),
        (3, 96, 96, 0, 384),
    )
    for j, (i, row, rows, col, cols) in enumerate(cuts):
        half = shards[i].shape[1] // 2

        def at(side, row=row, rows=rows, col=col, cols=cols, half=half):
            return (pl.ds(row, rows), span(side * half + col, cols, 128))

        pieces.append(
            gather(
                3 + j,
                lambda zz, q, i=i, at=at: wides[i].at[(zz, q) + at(c)],
                lambda q, i=i, at=at: wides[i].at[(every, q) + at(c)],
                lambda i=i, at=at: wides[i].at[(every, every) + at(1 - c)],
            )
        )
    pieces.append(
        gather(
            8,
            lambda zz, q: r.small_wide.at[zz, q, c],
            lambda q: r.small_wide.at[:, q, c],
            lambda: r.small_wide.at[:, :, 1 - c],
        )
    )

    def form(i):
        for m, (weight, start, cols, at) in enumerate(moves):
            if weight == i:
                before(m).wait_recv()
                mine = shards[i][:, span(start + c * cols, cols, 128)]
                theirs = sibs[i][at] if at else sibs[i][...]
                wides[i][at + (place.z, place.q, every, span(c * cols, cols, 128))] = jnp.concatenate(
                    [jnp.where(c == 0, mine, theirs), jnp.where(c == 0, theirs, mine)], axis=0
                ).astype(jnp.bfloat16)

    def prepare():
        for i in range(4, len(FETCHED)):
            fetch(i).wait()
        fill_present(r.present, r.mask)
        r.sums[...] = jnp.zeros_like(r.sums)
        r.owner[...] = owners(width)
        r.vec[...] = jnp.zeros_like(r.vec)
        r.small_part[...] = jnp.zeros_like(r.small_part)

    def unpack():
        for zz in range(4):
            rows = r.small_wide[zz].reshape(64, 128).astype(jnp.bfloat16)
            for start, size, m in segments(width):
                lanes = slice(start, start + size)
                picked = dot(rows, selection(size, m))
                total = r.vec[:, lanes]
                for d in range(8):
                    total = total + jnp.where(
                        r.owner[:, lanes] == zz * 8 + d, picked[d * 8 : d * 8 + 8], 0.0
                    )
                r.vec[:, lanes] = total
        for s in range(3):
            r.bias[s] = jnp.zeros((8, 6 * 128), jnp.float32)
            for e in range(2):
                at = 128 * s + third * e
                r.bias[s, 0:1, 128 * e : 128 * e + 128] = r.vec[2:3, width + at : width + at + 128]
                r.bias[s, 0:1, 512 + 128 * e : 640 + 128 * e] = r.vec[
                    2:3, 2 * width + at : 2 * width + at + 128
                ]

    def first_norm(t):
        rows = span(t * 128, 128, 128)
        normed, _ = unit(r.tokens[rows, :].astype(jnp.float32))
        value = normed * r.vec[0:1, 0:width] + r.vec[1:2, 0:width]
        r.normed[rows, :] = value.astype(jnp.bfloat16)
        r.turned_one[:, rows] = value.T.astype(jnp.bfloat16)

    def mask_grad(t):
        rows = span(t * 128, 128, 128)
        low = (r.present[rows, 0:1] * r.out_grad[rows, :].astype(jnp.float32)).astype(jnp.bfloat16)
        r.grad_low[rows, :] = low
        r.sums[7:8, 0:width] += jnp.sum(low.astype(jnp.float32), axis=0, keepdims=True)

    def heads(i):
        s, e = i // 2, i % 2

        @pl.when(e == 0)
        def _():
            weights = [
                r.qkv_wide[g, :, :, :, span(half * third + s * 128, 128, 128)].reshape(width, 128)
                for g in range(3)
                for half in range(2)
            ]
            value = dot(r.normed[...], jnp.concatenate(weights, axis=1)) + r.bias[s, 0:1, :]
            value = value.astype(jnp.bfloat16)
            for g in range(3):
                for half in range(2):
                    at = (2 * g + half) * 128
                    r.joined[s + 3 * half, g] = value[:, at : at + 128]

        hp = s + 3 * e
        cols = span(hp * 128, 128, 128)
        query, key, value = r.joined[hp, 0], r.joined[hp, 1], r.joined[hp, 2].T
        live = r.present[:, 0:1] > 0.5
        mixed = []
        for e in range(2):
            scores = dot_nt(head_only(key, e), query) * SCORE_SCALE
            scores = jnp.where(live, scores, -jnp.inf)
            largest = jnp.max(scores, axis=0, keepdims=True)
            expo = jnp.exp2(scores - largest)
            totals = jnp.sum(expo, axis=0, keepdims=True)
            probs = (expo * (1.0 / totals)).astype(jnp.bfloat16)
            mixed.append(dot(value[HEAD * e : HEAD * (e + 1)], probs))
            r.logsum[hp, e : e + 1, :] = largest + jnp.log2(totals)
        both = jnp.concatenate(mixed, axis=0)
        r.mixed_turned[cols, :] = both.astype(jnp.bfloat16)
        r.mixed[:, cols] = both.T.astype(jnp.bfloat16)

    def attention():
        r.middle[...] = dot(r.mixed[...], r.out_wide[...].reshape(width, width))

    def second_norm(t):
        rows = span(t * 128, 128, 128)
        present = r.present[rows, 0:1]
        middle = r.tokens[rows, :].astype(jnp.float32) + present * (
            r.middle[rows, :] + r.vec[3:4, 0:width]
        )
        r.middle[rows, :] = middle
        normed, _ = unit(middle)
        value = normed * r.vec[4:5, 0:width] + r.vec[5:6, 0:width]
        r.normed[rows, :] = value.astype(jnp.bfloat16)
        r.turned_two[:, rows] = value.T.astype(jnp.bfloat16)

    def slope_out(t, slot):
        return pltpu.make_async_copy(r.slope.at[slot], r.slope_far.at[t], r.slope_send.at[slot])

    def slope_in(t, slot):
        return pltpu.make_async_copy(r.slope_far.at[t], r.slope.at[slot], r.slope_recv.at[slot])

    def expand(t, u):
        slot = u % 2

        @pl.when(u >= 2)
        def _():
            slope_out(t, slot).wait()

        cols = span(t * TILE, TILE, 128)
        value = (
            dot(r.normed[...], r.up_wide[:, :, :, cols].reshape(width, TILE))
            + r.vec[6:7, span(3 * width + t * TILE, TILE, 128)]
        )
        cumulative = 0.5 * (1.0 + lax.erf(value * (1.0 / math.sqrt(2.0))))
        r.act[:, cols] = (value * cumulative).astype(jnp.bfloat16)
        r.slope[slot] = cumulative + value * jnp.exp(-0.5 * value * value) * (
            1.0 / math.sqrt(2.0 * math.pi)
        )
        slope_out(t, slot).start()

    def down_grad(t):
        cols = span(t * TILE, TILE, 128)
        grad = dot_tn(r.act[:, cols], r.grad_low[...]).astype(jnp.bfloat16)
        r.down_part[t] = grad.reshape(4, TILE // 4, width)

    low_tile = lambda u: 2 * u
    high_tile = lambda u: 2 * u + 1

    def scatter(j, block, column, whole):
        bufs = [getattr(r, "piece%d_%d" % (j, b)) for b in range(5)]
        lane = 4 if j == 8 else j % 4
        return Scatter(
            place, block, column, whole, bufs, r.send.at[lane], r.scatter_recv.at[j]
        )

    sums = []
    for s in range(2):
        rows = pl.ds(96 * s, 96)
        sums.append(
            scatter(
                s,
                lambda zz, q, rows=rows: r.down_total.at[zz, q, rows],
                lambda q, rows=rows: r.down_total.at[:, q, rows],
                lambda rows=rows: r.down_total.at[:, :, rows],
            )
        )
    for s in range(2):
        sums.append(
            scatter(
                2 + s,
                lambda zz, q, s=s: r.up_total.at[s, zz, q],
                lambda q, s=s: r.up_total.at[s, :, q],
                lambda s=s: r.up_total.at[s],
            )
        )
    sums.append(
        scatter(
            4,
            lambda zz, q: r.out_total.at[zz, q],
            lambda q: r.out_total.at[:, q],
            lambda: r.out_total,
        )
    )
    for s in range(3):
        sums.append(
            scatter(
                5 + s,
                lambda zz, q, s=s: r.qkv_total.at[s, zz, q],
                lambda q, s=s: r.qkv_total.at[s, :, q],
                lambda s=s: r.qkv_total.at[s],
            )
        )
    sums.append(SmallScatter(place, r.small_total, r.small_got, r.send.at[4], r.scatter_recv.at[8]))

    def up_part(side, s):
        cols = span(side * (hidden // 2) + 768 * s, 768, 128)
        return dot(r.turned_two[...], r.act[:, cols]).reshape(4, 4, 48, 768)

    def out_part(side):
        cols = span(side * third, third, 128)
        return dot(r.mixed_turned[...], r.normed[:, cols]).reshape(4, 4, 48, third)

    def qkv_part(side, s):
        hp = side * 3 + s
        grads = jnp.concatenate([r.joined[hp, g] for g in range(3)], axis=1)
        return dot(r.turned_one[...], grads)

    def other_part(p):
        if p in (2, 3):
            r.down_wide[:, :, 48 * (p - 2) : 48 * (p - 1), :] = up_part(1 - c, p - 2).astype(
                jnp.bfloat16
            )
        elif p == 4:
            r.down_wide[:, :, 96:144, 0:384] = out_part(1 - c).astype(jnp.bfloat16)
        else:
            value = qkv_part(1 - c, p - 5).astype(jnp.bfloat16)
            for g in range(3):
                r.down_part[:, :, 48 * g : 48 * g + 48, 128 * (p - 5) : 128 * (p - 4)] = value[
                    :, 128 * g : 128 * g + 128
                ].reshape(4, 4, 48, 128)

    def given(p):
        if p < 2:
            rows, cols = pl.ds(96 * p, 96), span((1 - c) * 384, 384, 128)
            return lambda q: r.down_part.at[:, q, rows, cols]
        if p < 4:
            return lambda q: r.down_wide.at[:, q, pl.ds(48 * (p - 2), 48)]
        if p == 4:
            return lambda q: r.down_wide.at[:, q, pl.ds(96, 48), pl.ds(0, 384)]
        if p < 8:
            return lambda q: r.down_part.at[:, q, pl.ds(0, 144), pl.ds(128 * (p - 5), 128)]
        return lambda: r.small_part.at[:, :, 1 - c]

    def wide_sum(total, value):
        total[...] = (total[...].astype(jnp.float32) + value).astype(total.dtype)

    def own_part(p):
        sums[p].arrive()
        if p < 2:
            rows = pl.ds(96 * p, 96)
            mine = r.down_part[:, :, rows, span(c * 384, 384, 128)].astype(jnp.float32)
            wide_sum(r.down_total.at[:, :, rows], mine)
        elif p < 4:
            wide_sum(r.up_total.at[p - 2], up_part(c, p - 2))
        elif p == 4:
            wide_sum(r.out_total, out_part(c))
        elif p < 8:
            value = qkv_part(c, p - 5)
            for g in range(3):
                wide_sum(
                    r.qkv_total.at[p - 5, :, :, pl.ds(48 * g, 48)],
                    value[:, 128 * g : 128 * g + 128].reshape(4, 4, 48, 128),
                )
        else:
            r.small_total[...] += r.small_part[:, :, c]

    def narrow(t):
        slot = t % 2

        @pl.when(t == 0)
        def _():
            slope_in(0, 0).start()
            r.acc[...] = jnp.zeros_like(r.acc)

        slope_in(t, slot).wait()

        @pl.when(t + 1 < tiles)
        def _():
            slope_in(t + 1, 1 - slot).start()

        cols = span(t * TILE, TILE, 128)
        weights = r.down_wide[t].reshape(TILE, width)
        r.acc[...] += dot(r.act[:, cols], weights)
        grad = (dot_nt(r.grad_low[...], weights) * r.slope[slot]).astype(jnp.bfloat16)
        r.act[:, cols] = grad
        r.sums[6:7, span(3 * width + t * TILE, TILE, 128)] = jnp.sum(
            grad.astype(jnp.float32), axis=0, keepdims=True
        )

    def drain_slope():
        for slot in range(2):
            slope_out(0, slot).wait()

    def finish_output(t):
        rows = span(t * 128, 128, 128)
        r.output[rows, :] = (
            r.middle[rows, :]
            + r.present[rows, 0:1] * (r.acc[rows, :] + r.vec[7:8, 0:width])
        ).astype(jnp.bfloat16)

        @pl.when(t == tokens // 128 - 1)
        def _():
            store(4).start()

    def up_back():
        r.acc[...] = dot_nt(r.act[...], r.up_wide[...].reshape(width, hidden))

    def norm_back(up, normed, factor, index):
        r.sums[index : index + 1, 0:width] += jnp.sum(up * normed, axis=0, keepdims=True)
        r.sums[index + 1 : index + 2, 0:width] += jnp.sum(up, axis=0, keepdims=True)
        scaled = up * r.vec[index : index + 1, 0:width]
        return factor * (
            scaled
            - jnp.mean(scaled, axis=1, keepdims=True)
            - normed * jnp.mean(scaled * normed, axis=1, keepdims=True)
        )

    def second_back(t):
        rows = span(t * 128, 128, 128)
        normed, factor = unit(r.middle[rows, :])
        grad = r.out_grad[rows, :].astype(jnp.float32) + norm_back(
            r.acc[rows, :], normed, factor, 4
        )
        r.middle[rows, :] = grad
        low = (r.present[rows, 0:1] * grad).astype(jnp.bfloat16)
        r.normed[rows, :] = low
        r.sums[3:4, 0:width] += jnp.sum(low.astype(jnp.float32), axis=0, keepdims=True)

    def out_back():
        r.mixed[...] = dot_nt(r.normed[...], r.out_wide[...].reshape(width, width)).astype(
            jnp.bfloat16
        )

    def heads_back(s):
        pair_back(s)
        pair_back(s + 3)

    def pair_back(hp):
        cols = span(hp * 128, 128, 128)
        query, key, value = r.joined[hp, 0], r.joined[hp, 1], r.joined[hp, 2]
        grad = r.mixed[:, cols]
        turned = key.T
        live = r.present[:, 0:1] > 0.5
        value_grad = jnp.zeros((tokens, 128), jnp.float32)
        key_grad = jnp.zeros((tokens, 128), jnp.float32)
        query_grad = []
        for e in range(2):
            scores = dot_nt(head_only(key, e), query) * SCORE_SCALE
            scores = jnp.where(live, scores, -jnp.inf)
            probs = jnp.exp2(scores - r.logsum[hp, e : e + 1, :])
            back = dot_nt(head_only(value, e), grad)
            inner = jnp.sum(probs * back, axis=0, keepdims=True)
            score_grad = (probs * (back - inner)).astype(jnp.bfloat16)
            value_grad = value_grad + dot(probs.astype(jnp.bfloat16), head_only(grad, e))
            key_grad = key_grad + dot(score_grad, head_only(query, e))
            query_grad.append(dot(turned[HEAD * e : HEAD * (e + 1)], score_grad))
        scale = 1.0 / math.sqrt(HEAD)
        query_low = (jnp.concatenate(query_grad, axis=0).T * scale).astype(jnp.bfloat16)
        value_low = value_grad.astype(jnp.bfloat16)
        r.joined[hp, 0] = query_low
        r.joined[hp, 1] = (key_grad * scale).astype(jnp.bfloat16)
        r.joined[hp, 2] = value_low
        r.sums[2:3, span(width + hp * 128, 128, 128)] = jnp.sum(
            query_low.astype(jnp.float32), axis=0, keepdims=True
        )
        r.sums[2:3, span(2 * width + hp * 128, 128, 128)] = jnp.sum(
            value_low.astype(jnp.float32), axis=0, keepdims=True
        )

    def qkv_back():
        total = jnp.zeros((tokens, width), jnp.float32)
        for g in range(3):
            grads = jnp.concatenate([r.joined[hp, g] for hp in range(6)], axis=1)
            total = total + dot_nt(grads, r.qkv_wide[g].reshape(width, width))
        r.acc[...] = total

    def first_back(t):
        rows = span(t * 128, 128, 128)
        normed, factor = unit(r.tokens[rows, :].astype(jnp.float32))
        part = norm_back(r.acc[rows, :], normed, factor, 0)
        r.input_grad[rows, :] = (r.middle[rows, :] + part).astype(jnp.bfloat16)

        @pl.when(t == tokens // 128 - 1)
        def _():
            store(5).start()

    def pack(index):
        start, size, m = segments(width)[index]
        row = (None, 2, 6)[index]
        lanes = slice(start, start + size)
        chosen = selection(size, m)
        for zz in range(4):
            left = r.sums[:, lanes] if row is None else r.sums[row : row + 1, lanes]
            tile = 0.0
            for _ in range(2):
                part = left.astype(jnp.bfloat16).astype(jnp.float32)
                left = left - part
                rows = jnp.concatenate(
                    [jnp.where(r.owner[:, lanes] == zz * 8 + d, part, 0.0) for d in range(8)], axis=0
                ).astype(jnp.bfloat16)
                tile = tile + dot_nt(rows, chosen)
            if row is None:
                r.small_part[zz] += tile.reshape(4, 2, 8, 128)
            else:
                for d in range(8):
                    r.small_part[zz, d // 2, d % 2, row : row + 1, :] += tile[d : d + 1, :]

    results = (r.qkv_result, r.out_result, r.up_result, r.down_result)
    finals = (r.qkv_final, r.out_final, r.up_final, r.down_final)

    def swap(m, side):
        i, start, cols, at = moves[m]
        rows = results[i].shape[0]
        return remote(
            finals[i].at[at + (span((1 - c) * rows, rows, 8),)],
            results[i].at[:, span(start + side * cols, cols, 128)],
            r.end_send.at[m],
            r.end_recv.at[m],
            place.to_c,
        )

    def close(i):
        for m, (weight, start, cols, at) in enumerate(moves):
            if weight == i:
                rows = results[i].shape[0]
                swap(m, c).start()
                results[i][:, span(start + c * cols, cols, 128)] = finals[i][
                    at + (span(c * rows, rows, 8),)
                ]

    def settle(i):
        for m, move in enumerate(moves):
            if move[0] == i:
                swap(m, 1 - c).wait_recv()
        store(i).start()

    def last(p):
        value = sums[p].last()
        if p < 2:
            r.down_final[96 * p : 96 * p + 96, :] = value
        elif p < 4:
            r.up_final[:, 768 * (p - 2) : 768 * (p - 1)] = value
        elif p == 4:
            r.out_final[...] = value
        elif p < 8:
            for g in range(3):
                r.qkv_final[g, :, 128 * (p - 5) : 128 * (p - 4)] = value[48 * g : 48 * g + 48]
        else:
            r.small_result[...] = value
            store(6).start()

    def start_xy(j):
        if 4 <= j < 8:
            pieces[j - 4].finish()
        pieces[j].start_xy()

    def give(p):
        before_it = pieces[8] if p == 8 else (sums[p - 4] if p >= 4 else pieces[p + 4])
        before_it.finish()
        if 2 <= p < 8:
            other_part(p)
        sums[p].give(given(p))

    steps = {(UNPACK,): unpack, (ATTENTION,): attention, (DRAIN,): drain_slope}
    steps.update({(UP_BACK,): up_back, (OUT_BACK,): out_back, (QKV_BACK,): qkv_back})
    steps[PREPARE,] = prepare
    for i in range(3):
        steps[PACK, i] = functools.partial(pack, i)
    for i in range(4):
        steps[FORM, i] = functools.partial(form, i)
        steps[CLOSE, i] = functools.partial(close, i)
        steps[SETTLE, i] = functools.partial(settle, i)
    for j in range(9):
        piece, total = pieces[j], sums[j]
        steps[START_Z, j] = piece.start_z
        steps[START_XY, j] = functools.partial(start_xy, j)
        steps[OWN_COLUMN, j] = piece.own_column
        steps[XY_COLUMNS, j] = piece.xy_columns
        steps[D_GOT, j] = piece.d
        steps[C_GOT, j] = piece.c
        steps[GIVE, j] = functools.partial(give, j)
        steps[OWN_PART, j] = functools.partial(own_part, j)
        steps[LAST, j] = functools.partial(last, j)
        for k in range(4):
            steps[Z_GOT, j, k] = functools.partial(piece.z, k)
            steps[XY_GOT, j, k] = functools.partial(piece.xy, k)
    for j, total in enumerate(sums[:8]):
        steps[DIAGONAL, j] = total.diagonal
        for k in range(4):
            steps[CROSS, j, k] = functools.partial(total.cross, k)
            steps[SPREAD, j, k] = functools.partial(total.spread, k)
    steps[SMALL_PLANE,] = sums[8].plane
    steps[SMALL_SPREAD,] = sums[8].spread
    loops = {
        FIRST_NORM: first_norm,
        MASK_GRAD: mask_grad,
        HEADS: heads,
        SECOND_NORM: second_norm,
        EXPAND_LOW: lambda u: expand(low_tile(u), u),
        EXPAND_HIGH: lambda u: expand(high_tile(u), u + 2),
        DOWN_LOW: lambda u: down_grad(low_tile(u)),
        DOWN_HIGH: lambda u: down_grad(high_tile(u)),
        NARROW: narrow,
        FINISH: finish_output,
        SECOND_BACK: second_back,
        HEADS_BACK: heads_back,
        FIRST_BACK: first_back,
    }
    follow(SEQUENCE, steps, loops)
    for m in range(6):
        before(m).wait_send()
        swap(m, c).wait_send()
    for piece in pieces + sums:
        piece.finish()
    for i in range(len(STORED)):
        store(i).wait()


def layer_call(tokens, band_mask, out_grad, shards, smalls):
    bf16, f32 = jnp.bfloat16, jnp.float32
    count, width = tokens.shape
    shapes = [s.shape for s in shards]
    hidden = shapes[2][1]
    tiles = hidden // TILE
    vmem = pl.BlockSpec(memory_space=pltpu.VMEM)
    anywhere = pl.BlockSpec(memory_space=pl.ANY)
    fetched = dict(zip(FETCHED, (*shards, tokens, out_grad)))
    inputs = [(name + "_in", array, anywhere) for name, array in fetched.items()]
    inputs += triples(mask=(band_mask, pl.BlockSpec(memory_space=pltpu.SMEM)))
    inputs += [("vector%d" % i, v, vmem) for i, v in enumerate(smalls)]
    stored = list(zip(STORED, shapes + [(count, width)] * 2 + [(8, 128)]))
    kinds = [f32] * 4 + [bf16] * 2 + [f32]
    outs = triples(slope_far=((tiles, count, TILE), f32)) + [
        (name + "_out", shape, kind) for (name, shape), kind in zip(stored, kinds)
    ]
    tails = (
        [((96, 384), bf16)] * 2
        + [((48, 768), bf16)] * 2
        + [((48, 384), bf16)]
        + [((144, 128), bf16)] * 3
    )
    scratch = [(name, pltpu.VMEM(a.shape, a.dtype)) for name, a in fetched.items()]
    scratch += [(name, pltpu.VMEM(shape, kind)) for (name, shape), kind in zip(stored, kinds)]
    for j, (tail, kind) in enumerate(tails):
        for b, one in enumerate(scatter_buffers(tail, kind)):
            scratch.append(("piece%d_%d" % (j, b), one))
    scratch += pairs_of(
        qkv_wide=pltpu.VMEM((3, 4, 4, 48, width), bf16),
        out_wide=pltpu.VMEM((4, 4, 48, width), bf16),
        up_wide=pltpu.VMEM((4, 4, 48, hidden), bf16),
        down_wide=pltpu.VMEM((4, 4, 192, width), bf16),
        qkv_sib=pltpu.VMEM((3, 24, width // 2), f32),
        out_sib=pltpu.VMEM((24, width // 2), f32),
        up_sib=pltpu.VMEM((24, hidden // 2), f32),
        down_sib=pltpu.VMEM((96, width // 2), f32),
        qkv_final=pltpu.VMEM((3, 48, width // 2), f32),
        out_final=pltpu.VMEM((48, width // 2), f32),
        up_final=pltpu.VMEM((48, hidden // 2), f32),
        down_final=pltpu.VMEM((192, width // 2), f32),
        small_wide=pltpu.VMEM((4, 4, 2, 8, 128), f32),
        small_part=pltpu.VMEM((4, 4, 2, 8, 128), f32),
        small_total=pltpu.VMEM((4, 4, 8, 128), f32),
        small_got=pltpu.VMEM((4, 4, 8, 128), f32),
        down_part=pltpu.VMEM((4, 4, 192, width), bf16),
        down_total=pltpu.VMEM((4, 4, 192, 384), bf16),
        up_total=pltpu.VMEM((2, 4, 4, 48, 768), bf16),
        out_total=pltpu.VMEM((4, 4, 48, 384), bf16),
        qkv_total=pltpu.VMEM((3, 4, 4, 144, 128), bf16),
        present=pltpu.VMEM((count, 128), f32),
        vec=pltpu.VMEM((8, 7 * width), f32),
        sums=pltpu.VMEM((8, 7 * width), f32),
        bias=pltpu.VMEM((3, 8, width), f32),
        owner=pltpu.VMEM((1, 7 * width), f32),
        logsum=pltpu.VMEM((width // 128, 8, count), f32),
        turned_one=pltpu.VMEM((width, count), bf16),
        turned_two=pltpu.VMEM((width, count), bf16),
        mixed_turned=pltpu.VMEM((width, count), bf16),
        normed=pltpu.VMEM((count, width), bf16),
        mixed=pltpu.VMEM((count, width), bf16),
        grad_low=pltpu.VMEM((count, width), bf16),
        joined=pltpu.VMEM((width // 128, 3, count, 128), bf16),
        middle=pltpu.VMEM((count, width), f32),
        acc=pltpu.VMEM((count, width), f32),
        act=pltpu.VMEM((count, hidden), bf16),
        slope=pltpu.VMEM((2, count, TILE), f32),
        send=pltpu.SemaphoreType.DMA((5, Piece.COUNT)),
        gather_z=pltpu.SemaphoreType.DMA((9, 3)),
        gather_recv=pltpu.SemaphoreType.DMA((9, 13)),
        scatter_recv=pltpu.SemaphoreType.DMA((9, 14)),
        pre_send=pltpu.SemaphoreType.DMA((6,)),
        pre_recv=pltpu.SemaphoreType.DMA((6,)),
        end_send=pltpu.SemaphoreType.DMA((6,)),
        end_recv=pltpu.SemaphoreType.DMA((6,)),
        load=pltpu.SemaphoreType.DMA((len(FETCHED),)),
        save=pltpu.SemaphoreType.DMA((len(STORED),)),
        slope_send=pltpu.SemaphoreType.DMA((2,)),
        slope_recv=pltpu.SemaphoreType.DMA((2,)),
    )
    names = (
        [name for name, _, _ in inputs] + [name for name, _, _ in outs] + [name for name, _ in scratch]
    )
    results = pl.pallas_call(
        functools.partial(layer_kernel, names),
        out_shape=tuple(jax.ShapeDtypeStruct(shape, kind) for _, shape, kind in outs),
        in_specs=[spec for _, _, spec in inputs],
        out_specs=(anywhere,) * len(outs),
        scratch_shapes=[kind for _, kind in scratch],
        compiler_params=pltpu.CompilerParams(
            collective_id=0, has_side_effects=True, vmem_limit_bytes=VMEM_BYTES
        ),
        name="layer",
    )(*[array for _, array, _ in inputs])
    qkv, out, up, down, output, input_grad, small = results[1:]
    return output, input_grad, qkv, out, up, down, small


def deliver_kernel(count, *refs):
    sources, tile = refs[:count], refs[count]
    targets = refs[count + 1 : 2 * count + 1]
    for source, target in zip(sources, targets):
        target[...] = source[...]
    for i, vector in enumerate(refs[2 * count + 1 :]):
        vector[...] = tile[i, 0 : vector.shape[0]]


def deliver(whole, tile, sizes):
    count = len(whole)
    vmem = pl.BlockSpec(memory_space=pltpu.VMEM)
    return pl.pallas_call(
        functools.partial(deliver_kernel, count),
        out_shape=[jax.ShapeDtypeStruct(a.shape, a.dtype) for a in whole]
        + [jax.ShapeDtypeStruct((m,), jnp.float32) for m in sizes],
        in_specs=[vmem] * (count + 1),
        out_specs=[vmem] * (count + len(sizes)),
        compiler_params=pltpu.CompilerParams(vmem_limit_bytes=VMEM_BYTES),
        name="deliver",
    )(*whole, tile)


def body(
    tokens,
    band_mask,
    out_grad,
    norm1_gain,
    norm1_shift,
    qkv_weight,
    qv_bias,
    out_weight,
    out_bias,
    norm2_gain,
    norm2_shift,
    up_weight,
    up_bias,
    down_weight,
    down_bias,
):
    smalls = (norm1_gain, norm1_shift, qv_bias, out_bias, norm2_gain, norm2_shift, up_bias, down_bias)
    shards = (qkv_weight, out_weight, up_weight, down_weight)
    *whole, tile = layer_call(tokens, band_mask, out_grad, shards, smalls)
    output, input_grad, qkv, out, up, down, *grads = deliver(
        whole, tile, [v.shape[0] for v in smalls]
    )
    return (
        output,
        input_grad,
        grads[0],
        grads[1],
        qkv,
        grads[2],
        out,
        grads[3],
        grads[4],
        grads[5],
        up,
        grads[6],
        down,
        grads[7],
    )


def solution(mesh):
    rows, flat = P(AXES, None), P(AXES)
    params = (flat, flat, rows, flat, rows, flat, flat, flat, rows, flat, rows, flat)
    fitted = tuple(mesh.shape[axis] for axis in AXES) == (8, 4)
    return jax.shard_map(
        body if fitted else body_plain,
        mesh=mesh,
        in_specs=(rows, rows, rows) + params,
        out_specs=(rows, rows) + params,
        check_vma=False,
    )
```
